32 devices in a mesh: seq: 4 (over x, core), chan: 8 (over z, y).
Axes of the slice: x: 2, y: 2, z: 4, core: 2. Of those that a mesh axis runs over, the one named last changes fastest.
Arguments:
- hidden_in: bfloat16 [2, 1024, 2048], P(None, 'seq', 'chan'), may hold values from -6 to 6
- norm_gain: float32 [2, 2048], P(None, 'chan'), may hold values from 0.1 to 1.9
- in_weight: bfloat16 [2, 2048, 2, 4096], P(None, None, None, 'chan'), may hold values from -0.125 to 0.125
- conv_weight: float32 [2, 4, 4096], P(None, None, 'chan'), may hold values from -3 to 3
- conv_bias: float32 [2, 4096], P(None, 'chan'), may hold values from -3 to 3
- xproj_weight: bfloat16 [2, 4096, 160], P(None, 'chan'), may hold values from -0.09375 to 0.09375
- dtproj_weight: bfloat16 [2, 128, 4096], P(None, None, 'chan'), may hold values from -0.5 to 0.5
- dt_bias: float32 [2, 4096], P(None, 'chan'), may hold values from -5.5 to -3
- decay_log: float32 [2, 16, 4096], P(None, None, 'chan'), may hold values from -3.5 to 1
- skip_gain: float32 [2, 4096], P(None, 'chan'), may hold values from 0.5 to 1.5
- out_weight: bfloat16 [2, 4096, 2048], P(None, 'chan'), may hold values from -0.1875 to 0.1875
- conv_state: float32 [2, 2, 3, 4096], P(None, None, None, 'chan'), may hold values from -6 to 6
- scan_state: float32 [2, 2, 16, 4096], P(None, None, None, 'chan'), may hold values from -6 to 6
- out_cotangent: bfloat16 [2, 1024, 2048], P(None, 'seq', 'chan'), may hold values from -6 to 6
Outputs:
- hidden_out: float32 [2, 1024, 2048], P(None, 'seq', 'chan')
- input_grad: float32 [2, 1024, 2048], P(None, 'seq', 'chan')
- gain_grad: float32 [2, 2048], P(None, 'chan')
- in_weight_grad: float32 [2, 2048, 2, 4096], P(None, None, None, 'chan')
- conv_weight_grad: float32 [2, 4, 4096], P(None, None, 'chan')
- conv_bias_grad: float32 [2, 4096], P(None, 'chan')
- xproj_grad: float32 [2, 4096, 160], P(None, 'chan')
- dtproj_grad: float32 [2, 128, 4096], P(None, None, 'chan')
- dt_bias_grad: float32 [2, 4096], P(None, 'chan')
- decay_log_grad: float32 [2, 16, 4096], P(None, None, 'chan')
- skip_gain_grad: float32 [2, 4096], P(None, 'chan')
- out_weight_grad: float32 [2, 4096, 2048], P(None, 'chan')
- conv_state_grad: float32 [2, 2, 3, 4096], P(None, None, None, 'chan')
- scan_state_grad: float32 [2, 2, 16, 4096], P(None, None, None, 'chan')
The draws below stay inside these ranges and needn't reach their ends.
All inputs are finite; a program needn't handle non-finite values.
Results may differ from the reference program's by a relative error of at most 0.018.
Values may be sent and summed in bfloat16 or wider, within the bound.
A program may use at most 768 MiB of HBM per device.

```python
import math
import jax
import jax.numpy as jnp
from jax import lax

D = 2048
DI = 4096
R = 128
N = 16
KC = 4
LAYERS = 2
SEQS = 2
LENGTH = 1024
XW = 160


def steps_of(stream_key, extent, pieces, low, largest):
    gain, own = 1.0, jax.random.fold_in(stream_key, 6)
    for position, blocks in pieces:
        heights = jnp.exp(jax.random.uniform(jax.random.fold_in(own, position), (blocks,), jnp.float32, low / len(pieces), largest / len(pieces)))
        gain = gain * jnp.repeat(heights, extent[position] // blocks).reshape([-1 if axis == position else 1 for axis in range(len(extent))])
    return gain


def noise(stream_key, dims, deviation, limit, split=(), held_as=jnp.bfloat16):
    drawn = deviation * jax.random.normal(stream_key, dims, jnp.float32)
    if split:
        drawn = drawn * steps_of(stream_key, dims, split, -0.22, 0.18)
    return jnp.clip(drawn, -limit, limit).astype(held_as)


def setup_inputs(seed: int = 0) -> dict:
    key_of = jax.random.split(jax.random.key(seed), 15)
    return {
        "hidden_in": noise(key_of[0], (SEQS, LENGTH, D), 1.0, 6.0, ((1, 4), (2, 8))),
        "norm_gain": jnp.clip(1.0 + 0.18 * jax.random.normal(key_of[1], (LAYERS, D), jnp.float32), 0.1, 1.9),
        "in_weight": noise(key_of[2], (LAYERS, D, 2, DI), D ** -0.5, 0.125, ((3, 8),)),
        "conv_weight": noise(key_of[3], (LAYERS, KC, DI), 0.5, 3.0, ((2, 8),), jnp.float32),
        "conv_bias": noise(key_of[4], (LAYERS, DI), 0.5, 3.0, ((1, 8),), jnp.float32),
        "xproj_weight": noise(key_of[5], (LAYERS, DI, XW), DI ** -0.5, 0.09375, ((1, 8),)),
        "dtproj_weight": noise(key_of[6], (LAYERS, R, DI), R ** -0.5, 0.5, ((2, 8),)),
        "dt_bias": jnp.clip(-5.5 + 2.5 * jax.random.uniform(key_of[7], (LAYERS, DI), jnp.float32) ** steps_of(key_of[7], (LAYERS, DI), ((1, 8),), -0.2, 0.2), -5.5, -3.0),
        "decay_log": jnp.clip(-3.5 + 4.5 * jax.random.uniform(key_of[8], (LAYERS, N, DI), jnp.float32) ** steps_of(key_of[8], (LAYERS, N, DI), ((2, 8),), -0.2, 0.2), -3.5, 1.0),
        "skip_gain": jnp.clip(0.5 + 1.0 * jax.random.uniform(key_of[9], (LAYERS, DI), jnp.float32) ** steps_of(key_of[9], (LAYERS, DI), ((1, 8),), -0.2, 0.2), 0.5, 1.5),
        "out_weight": noise(key_of[10], (LAYERS, DI, D), (DI // 4) ** -0.5, 0.1875, ((1, 8),)),
        "conv_state": noise(key_of[11], (LAYERS, SEQS, KC - 1, DI), 1.0, 6.0, ((3, 8),), jnp.float32),
        "scan_state": noise(key_of[12], (LAYERS, SEQS, N, DI), 1.0, 6.0, ((3, 8),), jnp.float32),
        "out_cotangent": noise(key_of[13], (SEQS, LENGTH, D), 1.0, 6.0, ((1, 4), (2, 8))),
    }


HIGHEST = lax.Precision.HIGHEST
EPS = 1e-05

@jax.custom_vjp
def low(v):
    return lax.optimization_barrier(v.astype(jnp.bfloat16)).astype(jnp.float32)

@jax.custom_vjp
def low_back(v):
    return v

def low_keep(v):
    return (low(v), None)

def low_pass(kept, grad):
    return (grad,)

def back_keep(v):
    return (v, None)

def back_low(kept, grad):
    return (low(grad),)
low.defvjp(low_keep, low_pass)
low_back.defvjp(back_keep, back_low)

def selective(activation, step_size, input_map, output_map, decay_rate, initial):
    length = activation.shape[0]
    block_len = math.gcd(length, 64)

    def scan_step(carried, inputs):
        act_now, step_now, input_now, output_now = inputs
        carried = jnp.exp(step_now[None, :] * decay_rate) * carried + input_now[:, None] * (step_now * act_now)[None, :]
        return (carried, lax.optimization_barrier(jnp.sum(output_now[:, None] * carried, axis=0)))

    @jax.checkpoint
    def scan_block(carried, inputs):
        return lax.scan(scan_step, carried, inputs)
    shaped = tuple((value.reshape(length // block_len, block_len, value.shape[1]) for value in (activation, step_size, input_map, output_map)))
    last_state, outputs = lax.scan(scan_block, initial, shaped)
    return outputs.reshape(length, activation.shape[1])

def mixer_layer(hidden, norm_scale, weight_in, conv_taps, conv_shift, weight_proj, weight_step, step_bias, decay_log, skip_gain, weight_out, conv_init, state_init):
    length = hidden.shape[0]
    model_width = hidden.shape[1]
    inverse = lax.rsqrt(lax.optimization_barrier(jnp.mean(hidden * hidden, axis=-1, keepdims=True)) + EPS)
    normed = low(hidden * inverse * norm_scale)
    mixed_pair = low_back(jnp.dot(normed, weight_in.reshape(model_width, -1), precision=HIGHEST)).reshape(length, 2, -1)
    inner_part = mixed_pair[:, 0]
    gate_in = mixed_pair[:, 1]
    padded = jnp.concatenate([conv_init, inner_part], axis=0)
    conv_total = conv_shift + conv_taps[0] * padded[0:length]
    for offset in range(1, KC):
        conv_total = conv_total + conv_taps[offset] * padded[offset:offset + length]
    activation = jax.nn.silu(conv_total)
    projected = low_back(jnp.dot(low(activation), weight_proj, precision=HIGHEST))
    rank_part = low(projected[:, :R])
    input_map = projected[:, R:R + N]
    output_map = projected[:, R + N:]
    delta_pre = low_back(jnp.dot(rank_part, weight_step, precision=HIGHEST) + step_bias)
    step_size = jax.nn.softplus(delta_pre)
    outputs = selective(activation, step_size, input_map, output_map, -jnp.exp(decay_log), state_init) + skip_gain * activation
    gated_out = low(outputs * jax.nn.silu(gate_in))
    branch = low_back(jnp.dot(gated_out, weight_out, precision=HIGHEST))
    return hidden + branch

def forward(hidden, gains, weight_in, conv_taps, conv_shift, weight_proj, weight_step, step_bias, decay_log, skip_gain, weight_out, conv_init, state_init):
    batched = jax.vmap(mixer_layer, in_axes=(0, None, None, None, None, None, None, None, None, None, None, 0, 0))
    for layer_index in range(LAYERS):
        hidden = batched(hidden, gains[layer_index], weight_in[layer_index], conv_taps[layer_index], conv_shift[layer_index], weight_proj[layer_index], weight_step[layer_index], step_bias[layer_index], decay_log[layer_index], skip_gain[layer_index], weight_out[layer_index], conv_init[layer_index], state_init[layer_index])
    return hidden

def reference(hidden_in, norm_gain, in_weight, conv_weight, conv_bias, xproj_weight, dtproj_weight, dt_bias, decay_log, skip_gain, out_weight, conv_state, scan_state, out_cotangent):
    primals = (hidden_in.astype(jnp.float32), norm_gain, in_weight.astype(jnp.float32), conv_weight, conv_bias, xproj_weight.astype(jnp.float32), dtproj_weight.astype(jnp.float32), dt_bias, decay_log, skip_gain, out_weight.astype(jnp.float32), conv_state, scan_state)
    result, pullback = jax.vjp(forward, *primals)
    gradients = pullback(out_cotangent.astype(jnp.float32))
    return (result, gradients[0], gradients[1], gradients[2], gradients[3], gradients[4], gradients[5], gradients[6], gradients[7], gradients[8], gradients[9], gradients[10], gradients[11], gradients[12])
```

```python
import functools
import math

import jax
import jax.numpy as jnp
from jax import lax
from jax.experimental import pallas as pl
from jax.experimental.pallas import tpu as pltpu
from jax.sharding import PartitionSpec as P

EPS = 1e-05
G = 8
LANES = 128
LOG2E = 1.4426950408889634
LN2 = 0.6931471805599453
F32 = jnp.float32
BF16 = jnp.bfloat16
VMEM_LIMIT = 48 * 1024 * 1024


def params(*semantics):
    return pltpu.CompilerParams(dimension_semantics=semantics, vmem_limit_bytes=VMEM_LIMIT)


def spread_maps(maps_ref, first, count, out_ref):
    def one(l, carry):
        tile = maps_ref[0, l]
        for n in range(count):
            out_ref[l, n] = jnp.broadcast_to(tile[:, first + n : first + n + 1], (G, LANES))
        return carry

    lax.fori_loop(0, maps_ref.shape[1], one, 0)


def spread_rate(decay_ref, rate_ref):
    rate = jnp.exp(decay_ref[...]) * (-LOG2E)
    for n in range(rate.shape[0]):
        rate_ref[n] = jnp.broadcast_to(rate[n : n + 1, :], (G, LANES))


def shifted(value, by, fill):
    row = lax.broadcasted_iota(jnp.int32, value.shape, 0)
    moved = pltpu.roll(value, by % G, 0)
    inside = row >= by if by > 0 else row < G + by
    return jnp.where(inside, moved, fill)


def segment_prefix(ends, span, rate_ref, direction):
    step = 1
    while step < G:
        moved_span = shifted(span, direction * step, 0.0)
        ends = [
            e + jnp.exp2(span * rate_ref[n]) * shifted(e, direction * step, 0.0)
            for n, e in enumerate(ends)
        ]
        span = span + moved_span
        step *= 2
    return ends, span


def ends_kernel(act_ref, step_ref, maps_ref, decay_ref, prefix_ref, span_ref, pack_ref, b_ref, rate_ref):
    length, states = act_ref.shape[1], decay_ref.shape[0]

    @pl.when(pl.program_id(1) == 0)
    def _():
        spread_maps(maps_ref, 0, states, b_ref)

    spread_rate(decay_ref, rate_ref)

    def one(l, carry):
        h, total = carry
        st = step_ref[0, l]
        u = st * act_ref[0, l]
        h = tuple(
            jnp.exp2(st * rate_ref[n]) * h[n] + u * b_ref[l, n] for n in range(states)
        )
        return h, total + st

    zero = jnp.zeros((G, LANES), F32)
    h, total = lax.fori_loop(0, length, one, ((zero,) * states, zero))
    ends, span = segment_prefix(list(h), total, rate_ref, 1)
    for n in range(states):
        prefix_ref[0, n] = shifted(ends[n], 1, 0.0)
        pack_ref[0, n : n + 1, :] = ends[n][G - 1 : G, :]
    span_ref[0, 0] = shifted(span, 1, 0.0)
    span_ref[0, 1] = jnp.broadcast_to(span[G - 1 : G, :], (G, LANES)) - span
    pack_ref[0, states:, :] = jnp.broadcast_to(span[G - 1 : G, :], (8, LANES))


def scan_ends(act, step, maps, decay):
    seqs, length, _, chans = act.shape
    states = decay.shape[0]
    token = pl.BlockSpec((1, length, G, LANES), lambda s, j: (s, 0, 0, j))
    return pl.pallas_call(
        ends_kernel,
        grid=(seqs, chans // LANES),
        in_specs=[
            token,
            token,
            pl.BlockSpec((1, length, G, maps.shape[3]), lambda s, j: (s, 0, 0, 0)),
            pl.BlockSpec((states, LANES), lambda s, j: (0, j)),
        ],
        out_specs=[
            pl.BlockSpec((1, states, G, LANES), lambda s, j: (s, 0, 0, j)),
            pl.BlockSpec((1, 2, G, LANES), lambda s, j: (s, 0, 0, j)),
            pl.BlockSpec((1, states + 8, LANES), lambda s, j: (s, 0, j)),
        ],
        out_shape=[
            jax.ShapeDtypeStruct((seqs, states, G, chans), F32),
            jax.ShapeDtypeStruct((seqs, 2, G, chans), F32),
            jax.ShapeDtypeStruct((seqs, states + 8, chans), F32),
        ],
        scratch_shapes=[
            pltpu.VMEM((length, states, G, LANES), F32),
            pltpu.VMEM((states, G, LANES), F32),
        ],
        compiler_params=params("arbitrary", "arbitrary"),
        name="scan_ends",
    )(act, step, maps, decay)


def forward_kernel(
    act_ref, step_ref, gate_ref, maps_ref, decay_ref, prefix_ref, span_ref, packs_ref, init_ref, skip_ref,
    y_ref, gated_ref, start_ref, b_ref, c_ref, rate_ref,
):
    length, states = act_ref.shape[1], decay_ref.shape[0]

    @pl.when(pl.program_id(1) == 0)
    def _():
        spread_maps(maps_ref, 0, states, b_ref)
        spread_maps(maps_ref, states, states, c_ref)

    spread_rate(decay_ref, rate_ref)
    rate = jnp.exp(decay_ref[...]) * (-LOG2E)
    me = lax.axis_index("seq")
    entry = init_ref[0]
    for d in range(packs_ref.shape[0]):
        joined = jnp.exp2(rate * packs_ref[d, 0, states : states + 1, :]) * entry + packs_ref[d, 0, :states, :]
        entry = jnp.where(d < me, joined, entry)
    span = span_ref[0, 0]
    h = []
    for n in range(states):
        first = prefix_ref[0, n] + jnp.exp2(rate_ref[n] * span) * entry[n : n + 1, :]
        start_ref[0, n] = first
        h.append(first)
    skip = jnp.broadcast_to(skip_ref[...], (G, LANES))

    def one(k, h):
        h = list(h)
        halves = []
        for i in range(2):
            l = 2 * k + i
            st = step_ref[0, l]
            act = act_ref[0, l]
            u = st * act
            y = skip * act
            for n in range(states):
                h[n] = jnp.exp2(st * rate_ref[n]) * h[n] + u * b_ref[l, n]
                y = y + c_ref[l, n] * h[n]
            y_ref[0, l] = y
            gate = gate_ref[0, l]
            halves.append(y * (gate / (1.0 + jnp.exp(-gate))))
        gated_ref[0, pl.ds(pl.multiple_of(k * 2 * G, 2 * G), 2 * G), :] = jnp.concatenate(halves, axis=0).astype(BF16)
        return tuple(h)

    lax.fori_loop(0, length // 2, one, tuple(h))


def scan_forward(act, step, gate, maps, decay, prefix, span, packs, init, skip):
    seqs, length, _, chans = act.shape
    states = decay.shape[0]
    token = pl.BlockSpec((1, length, G, LANES), lambda s, j: (s, 0, 0, j))
    per_state = pl.BlockSpec((1, states, G, LANES), lambda s, j: (s, 0, 0, j))
    return pl.pallas_call(
        forward_kernel,
        grid=(seqs, chans // LANES),
        in_specs=[
            token,
            token,
            token,
            pl.BlockSpec((1, length, G, maps.shape[3]), lambda s, j: (s, 0, 0, 0)),
            pl.BlockSpec((states, LANES), lambda s, j: (0, j)),
            per_state,
            pl.BlockSpec((1, 2, G, LANES), lambda s, j: (s, 0, 0, j)),
            pl.BlockSpec((packs.shape[0], 1, states + 8, LANES), lambda s, j: (0, s, 0, j)),
            pl.BlockSpec((1, states, LANES), lambda s, j: (s, 0, j)),
            pl.BlockSpec((1, LANES), lambda s, j: (0, j)),
        ],
        out_specs=[
            token,
            pl.BlockSpec((1, length * G, LANES), lambda s, j: (s, 0, j)),
            per_state,
        ],
        out_shape=[
            jax.ShapeDtypeStruct(act.shape, F32),
            jax.ShapeDtypeStruct((seqs, length * G, chans), BF16),
            jax.ShapeDtypeStruct((seqs, states, G, chans), F32),
        ],
        scratch_shapes=[
            pltpu.VMEM((length, states, G, LANES), F32),
            pltpu.VMEM((length, states, G, LANES), F32),
            pltpu.VMEM((states, G, LANES), F32),
        ],
        compiler_params=params("arbitrary", "arbitrary"),
        name="scan_forward",
    )(act, step, gate, maps, decay, prefix, span, packs, init, skip)


def adjoint_kernel(step_ref, gate_ref, grad_ref, maps_ref, decay_ref, span_ref, suffix_ref, pack_ref, c_ref, rate_ref):
    length, states = step_ref.shape[1], decay_ref.shape[0]

    @pl.when(pl.program_id(1) == 0)
    def _():
        spread_maps(maps_ref, states, states, c_ref)

    spread_rate(decay_ref, rate_ref)

    def one(k, carry):
        l = length - 1 - k
        st = step_ref[0, l]
        gate = gate_ref[0, l]
        gy = grad_ref[0, l] * (gate / (1.0 + jnp.exp(-gate)))
        return tuple(
            jnp.exp2(st * rate_ref[n]) * (carry[n] + gy * c_ref[l, n]) for n in range(states)
        )

    zero = jnp.zeros((G, LANES), F32)
    carry = lax.fori_loop(0, length, one, (zero,) * states)
    own = span_ref[0, 1, 0:1, :] + span_ref[0, 0, 1:2, :] - span_ref[0, 0] - span_ref[0, 1]
    ends, _ = segment_prefix(list(carry), own, rate_ref, -1)
    for n in range(states):
        suffix_ref[0, n] = shifted(ends[n], -1, 0.0)
        pack_ref[0, n : n + 1, :] = ends[n][0:1, :]


def scan_adjoint(step, gate, grad, maps, decay, span):
    seqs, length, _, chans = step.shape
    states = decay.shape[0]
    token = pl.BlockSpec((1, length, G, LANES), lambda s, j: (s, 0, 0, j))
    return pl.pallas_call(
        adjoint_kernel,
        grid=(seqs, chans // LANES),
        in_specs=[
            token,
            token,
            token,
            pl.BlockSpec((1, length, G, maps.shape[3]), lambda s, j: (s, 0, 0, 0)),
            pl.BlockSpec((states, LANES), lambda s, j: (0, j)),
            pl.BlockSpec((1, 2, G, LANES), lambda s, j: (s, 0, 0, j)),
        ],
        out_specs=[
            pl.BlockSpec((1, states, G, LANES), lambda s, j: (s, 0, 0, j)),
            pl.BlockSpec((1, states, LANES), lambda s, j: (s, 0, j)),
        ],
        out_shape=[
            jax.ShapeDtypeStruct((seqs, states, G, chans), F32),
            jax.ShapeDtypeStruct((seqs, states, chans), F32),
        ],
        scratch_shapes=[
            pltpu.VMEM((length, states, G, LANES), F32),
            pltpu.VMEM((states, G, LANES), F32),
        ],
        compiler_params=params("arbitrary", "arbitrary"),
        name="scan_adjoint",
    )(step, gate, grad, maps, decay, span)


def backward_kernel(
    act_ref, step_ref, delta_ref, gate_ref, y_ref, grad_ref, maps_ref, decay_ref, start_ref, suffix_ref, span_ref,
    packs_ref, forward_packs_ref, skip_ref,
    gact_ref, gpre_ref, ggate_ref, gmaps_ref, gdecay_ref, gskip_ref, ginit_ref,
    b_ref, c_ref, rate_ref, h_ref, product_ref, select_ref,
):
    length, states = act_ref.shape[1], decay_ref.shape[0]
    wide = states * LANES

    @pl.when(pl.program_id(1) == 0)
    def _():
        spread_maps(maps_ref, 0, states, b_ref)
        spread_maps(maps_ref, states, states, c_ref)
        row = lax.broadcasted_iota(jnp.int32, select_ref.shape, 0) // LANES
        col = lax.broadcasted_iota(jnp.int32, select_ref.shape, 1)
        select_ref[...] = jnp.where(row == col, 1.0, 0.0).astype(BF16)

    spread_rate(decay_ref, rate_ref)
    rate = jnp.exp(decay_ref[...]) * (-LOG2E)
    me = lax.axis_index("seq")
    count = packs_ref.shape[0]
    entry = jnp.zeros((states, LANES), F32)
    for d in reversed(range(count)):
        joined = jnp.exp2(rate * forward_packs_ref[d, 0, states : states + 1, :]) * entry + packs_ref[d, 0]
        entry = jnp.where(d > me, joined, entry)
    after = span_ref[0, 1]
    skip = jnp.broadcast_to(skip_ref[...], (G, LANES))

    def forward(l, h):
        st = step_ref[0, l]
        u = st * act_ref[0, l]
        for n in range(states):
            h_ref[l, n] = h[n]
        return tuple(
            jnp.exp2(st * rate_ref[n]) * h[n] + u * b_ref[l, n] for n in range(states)
        )

    h = lax.fori_loop(0, length, forward, tuple(start_ref[0, n] for n in range(states)))
    for n in range(states):
        h_ref[length, n] = h[n]

    def back(k, state):
        carry, gdecay, gskip = list(state[0]), list(state[1]), state[2]
        lines = [length - 1 - 2 * k, length - 2 - 2 * k]
        st, act, u, gy, q, r = [], [], [], [], [], []
        ggate = []
        for l in lines:
            st.append(step_ref[0, l])
            act.append(act_ref[0, l])
            u.append(st[-1] * act[-1])
            gate = gate_ref[0, l]
            grad = grad_ref[0, l]
            sig = 1.0 / (1.0 + jnp.exp(-gate))
            silu = gate * sig
            gy.append(grad * silu)
            ggate.append(grad * y_ref[0, l] * (sig + silu * (1.0 - sig)))
            gskip = gskip + gy[-1] * act[-1]
            q.append(jnp.zeros((G, LANES), F32))
            r.append(jnp.zeros((G, LANES), F32))
        row = pl.multiple_of((length - 2 - 2 * k) * G, 2 * G)
        for n in range(states):
            late, early = [], []
            for i, l in enumerate(lines):
                lam = c_ref[l, n] * gy[i] + carry[n]
                early.append(lam * u[i])
                late.append(gy[i] * h_ref[l + 1, n])
                q[i] = q[i] + lam * b_ref[l, n]
                carry[n] = jnp.exp2(st[i] * rate_ref[n]) * lam
                w = carry[n] * h_ref[l, n]
                r[i] = r[i] + rate_ref[n] * w
                gdecay[n] = gdecay[n] + st[i] * w
            product_ref[pl.ds(row, 2 * G), n * LANES : (n + 1) * LANES] = jnp.concatenate(early[::-1], axis=0).astype(BF16)
            product_ref[pl.ds(row, 2 * G), wide + n * LANES : wide + (n + 1) * LANES] = jnp.concatenate(late[::-1], axis=0).astype(BF16)
        gpre = []
        for i, l in enumerate(lines):
            gact_ref[0, l] = skip * gy[i] + st[i] * q[i]
            gstep = LN2 * r[i] + act[i] * q[i]
            gpre.append(gstep / (1.0 + jnp.exp(-delta_ref[0, l])))
        gpre_ref[0, pl.ds(row, 2 * G), :] = jnp.concatenate(gpre[::-1], axis=0).astype(BF16)
        ggate_ref[0, pl.ds(row, 2 * G), :] = jnp.concatenate(ggate[::-1], axis=0).astype(BF16)
        return tuple(carry), tuple(gdecay), gskip

    zero = jnp.zeros((G, LANES), F32)
    first = tuple(
        suffix_ref[0, n] + jnp.exp2(rate_ref[n] * after) * entry[n : n + 1, :] for n in range(states)
    )
    carry, gdecay, gskip = lax.fori_loop(0, length // 2, back, (first, (zero,) * states, zero))
    for n in range(states):
        ginit_ref[0, n : n + 1, :] = carry[n][0:1, :]
        total = jnp.sum(gdecay[n] * rate_ref[n], axis=0, keepdims=True)
        gdecay_ref[0, n : n + 1, :] = total * LN2
    gskip_ref[0] = jnp.broadcast_to(jnp.sum(gskip, axis=0, keepdims=True), (8, LANES))
    sums = jnp.dot(product_ref[...], select_ref[...], preferred_element_type=F32)

    @pl.when(pl.program_id(1) == 0)
    def _():
        gmaps_ref[0] = sums

    @pl.when(pl.program_id(1) > 0)
    def _():
        gmaps_ref[0] += sums


def scan_backward(act, step, delta, gate, y, grad, maps, decay, start, suffix, span, packs, forward_packs, skip):
    seqs, length, _, chans = act.shape
    states = decay.shape[0]
    token = pl.BlockSpec((1, length, G, LANES), lambda s, j: (s, 0, 0, j))
    rows = pl.BlockSpec((1, length * G, LANES), lambda s, j: (s, 0, j))
    per_state = pl.BlockSpec((1, states, G, LANES), lambda s, j: (s, 0, 0, j))
    total = pl.BlockSpec((1, states, LANES), lambda s, j: (s, 0, j))
    return pl.pallas_call(
        backward_kernel,
        grid=(seqs, chans // LANES),
        in_specs=[
            token,
            token,
            token,
            token,
            token,
            token,
            pl.BlockSpec((1, length, G, maps.shape[3]), lambda s, j: (s, 0, 0, 0)),
            pl.BlockSpec((states, LANES), lambda s, j: (0, j)),
            per_state,
            per_state,
            pl.BlockSpec((1, 2, G, LANES), lambda s, j: (s, 0, 0, j)),
            pl.BlockSpec((packs.shape[0], 1, states, LANES), lambda s, j: (0, s, 0, j)),
            pl.BlockSpec((packs.shape[0], 1, states + 8, LANES), lambda s, j: (0, s, 0, j)),
            pl.BlockSpec((1, LANES), lambda s, j: (0, j)),
        ],
        out_specs=[
            token,
            rows,
            rows,
            pl.BlockSpec((1, length * G, LANES), lambda s, j: (s, 0, 0)),
            total,
            pl.BlockSpec((1, 8, LANES), lambda s, j: (s, 0, j)),
            total,
        ],
        out_shape=[
            jax.ShapeDtypeStruct(act.shape, F32),
            jax.ShapeDtypeStruct((seqs, length * G, chans), BF16),
            jax.ShapeDtypeStruct((seqs, length * G, chans), BF16),
            jax.ShapeDtypeStruct((seqs, length * G, LANES), F32),
            jax.ShapeDtypeStruct((seqs, states, chans), F32),
            jax.ShapeDtypeStruct((seqs, 8, chans), F32),
            jax.ShapeDtypeStruct((seqs, states, chans), F32),
        ],
        scratch_shapes=[
            pltpu.VMEM((length, states, G, LANES), F32),
            pltpu.VMEM((length, states, G, LANES), F32),
            pltpu.VMEM((states, G, LANES), F32),
            pltpu.VMEM((length + 1, states, G, LANES), F32),
            pltpu.VMEM((length * G, 2 * states * LANES), BF16),
            pltpu.VMEM((2 * states * LANES, LANES), BF16),
        ],
        compiler_params=params("arbitrary", "arbitrary"),
        name="scan_backward",
    )(act, step, delta, gate, y, grad, maps, decay, start, suffix, span, packs, forward_packs, skip)


def passed_along(value, axis, by):
    peers = lax.axis_size(axis)
    pairs = [(i, i + by) for i in range(peers) if 0 <= i + by < peers]
    return lax.ppermute(value, axis, pairs)


def to_segments(value):
    seqs, tokens, width = value.shape
    return value.reshape(seqs, G, tokens // G, width).transpose(0, 2, 1, 3)


def from_segments(value):
    seqs, length, _, width = value.shape
    return value.transpose(0, 2, 1, 3).reshape(seqs, length * G, width)


def dot(a, b, dims):
    return lax.dot_general(a, b, (dims, ((), ())), preferred_element_type=F32)


def local(
    hidden_in,
    norm_gain,
    in_weight,
    conv_weight,
    conv_bias,
    xproj_weight,
    dtproj_weight,
    dt_bias,
    decay_log,
    skip_gain,
    out_weight,
    conv_state,
    scan_state,
    out_cotangent,
):
    layers = in_weight.shape[0]
    rank = dtproj_weight.shape[1]
    states = decay_log.shape[1]
    seqs, tokens, _ = hidden_in.shape
    length = tokens // G
    rows = seqs * tokens
    chans = in_weight.shape[3]
    model = hidden_in.shape[2] * lax.axis_size("chan")
    taps = conv_weight.shape[1]
    is_first = lax.axis_index("seq") == 0

    hidden = to_segments(hidden_in).astype(F32).reshape(rows, -1)
    saved = []
    for i in range(layers):
        square = jnp.sum(hidden * hidden, axis=1, keepdims=True)
        inverse = lax.rsqrt(lax.psum(square, "chan") / model + EPS)
        part = (hidden * inverse * norm_gain[i]).astype(BF16)
        normed = lax.all_gather(part, "chan", axis=1, tiled=True)
        flat_in = in_weight[i].reshape(model, -1)
        mixed = dot(normed, flat_in, ((1,), (0,)))
        inner = mixed[:, :chans].reshape(seqs, length, G, chans)
        gate = mixed[:, chans:].reshape(seqs, length, G, chans)
        tail = inner[:, length - taps + 1 :]
        received = passed_along(tail[:, :, G - 1], "seq", 1)
        before = jnp.where(is_first, conv_state[i], received)
        head = jnp.concatenate([before[:, :, None], tail[:, :, : G - 1]], axis=2)
        padded = jnp.concatenate([head, inner], axis=1)
        pre = conv_bias[i] + sum(conv_weight[i, k] * padded[:, k : k + length] for k in range(taps))
        act = jax.nn.silu(pre)
        act_low = act.astype(BF16).reshape(rows, chans)
        projected = lax.psum(dot(act_low, xproj_weight[i], ((1,), (0,))), "chan")
        rank_part = projected[:, :rank].astype(BF16)
        maps = projected[:, rank:].reshape(seqs, length, G, 2 * states)
        delta = dot(rank_part, dtproj_weight[i], ((1,), (0,))) + dt_bias[i]
        delta = delta.reshape(seqs, length, G, chans)
        step = jax.nn.softplus(delta)
        prefix, span, pack = scan_ends(act, step, maps, decay_log[i])
        packs = lax.all_gather(pack, "seq")
        y, gated, start = scan_forward(
            act, step, gate, maps, decay_log[i], prefix, span, packs, scan_state[i], skip_gain[i : i + 1]
        )
        gated = gated.reshape(rows, chans)
        branch = lax.psum_scatter(
            dot(gated, out_weight[i], ((1,), (0,))).astype(BF16), "chan", scatter_dimension=1, tiled=True
        )
        saved.append(
            (hidden, inverse, normed, flat_in, mixed, gate, padded, pre, act, act_low, rank_part, maps, delta, step,
             span, packs, y, gated, start)
        )
        hidden = hidden + branch.astype(F32)

    grad = to_segments(out_cotangent).astype(F32).reshape(rows, -1)
    per_layer = []
    for i in reversed(range(layers)):
        (hidden_i, inverse, normed, flat_in, mixed, gate, padded, pre, act, act_low, rank_part, maps, delta, step,
         span, packs, y, gated, start) = saved[i]
        grad_rows = lax.all_gather(grad.astype(BF16), "chan", axis=1, tiled=True)
        grad_gated = dot(grad_rows, out_weight[i], ((1,), (1,))).reshape(seqs, length, G, chans)
        out_grad = dot(gated, grad_rows, ((0,), (0,)))
        suffix, back_pack = scan_adjoint(step, gate, grad_gated, maps, decay_log[i], span)
        back_packs = lax.all_gather(back_pack, "seq")
        gact, gpre, ggate, gmaps, gdecay, gskip, ginit = scan_backward(
            act, step, delta, gate, y, grad_gated, maps, decay_log[i], start, suffix, span, back_packs, packs,
            skip_gain[i : i + 1],
        )
        gpre = gpre.reshape(rows, chans)
        dtproj_grad = dot(rank_part, gpre, ((0,), (0,)))
        grad_rank = dot(gpre, dtproj_weight[i], ((1,), (1,)))
        bias_grad = jnp.sum(gpre.astype(F32), axis=0)
        grad_proj = lax.psum(
            jnp.concatenate([grad_rank, gmaps.reshape(rows, -1)[:, : 2 * states]], axis=1), "chan"
        ).astype(BF16)
        xproj_grad = dot(act_low, grad_proj, ((0,), (0,)))
        gact = gact + dot(grad_proj, xproj_weight[i], ((1,), (1,))).reshape(gact.shape)
        sig = jax.nn.sigmoid(pre)
        gconv = gact * (sig + pre * sig * (1.0 - sig))
        shift_grad = jnp.sum(gconv, axis=(0, 1, 2))
        taps_grad = jnp.stack(
            [jnp.sum(gconv * padded[:, k : k + length], axis=(0, 1, 2)) for k in range(taps)]
        )
        early = jnp.stack(
            [sum(conv_weight[i, k] * gconv[:, j - k] for k in range(j + 1)) for j in range(taps - 1)], axis=1
        )
        from_next = passed_along(early[:, :, 0], "seq", -1)
        over = jnp.concatenate([early[:, :, 1:], from_next[:, :, None]], axis=2)
        tailed = jnp.concatenate([gconv, jnp.zeros_like(gconv[:, : taps - 1])], axis=1)
        ginner = sum(conv_weight[i, k] * tailed[:, taps - 1 - k : taps - 1 - k + length] for k in range(taps))
        ginner = jnp.concatenate([ginner[:, : length - taps + 1], ginner[:, length - taps + 1 :] + over], axis=1)
        gmixed = jnp.concatenate([ginner.astype(BF16).reshape(rows, chans), ggate.reshape(rows, chans)], axis=1)
        in_grad = dot(normed, gmixed, ((0,), (0,))).reshape(in_weight.shape[1:])
        gnormed = lax.psum_scatter(
            dot(gmixed, flat_in, ((1,), (1,))).astype(BF16), "chan", scatter_dimension=1, tiled=True
        ).astype(F32)
        weighted = gnormed * norm_gain[i]
        inner_sums = lax.psum(jnp.sum(gmixed.astype(F32) * mixed, axis=1, keepdims=True), "chan")
        grad = grad + inverse * weighted - hidden_i * (inverse * inverse * inner_sums / model)
        gain_grad = jnp.sum(gnormed * hidden_i * inverse, axis=0)
        conv_init = jnp.where(is_first, early[:, :, 0], 0.0)
        scan_init = jnp.where(is_first, ginit, 0.0)
        summed = lax.psum(
            (
                gain_grad,
                in_grad,
                taps_grad,
                shift_grad,
                xproj_grad,
                dtproj_grad,
                bias_grad,
                jnp.sum(gdecay, axis=0),
                jnp.sum(gskip[:, 0], axis=0),
                out_grad,
                conv_init,
                scan_init,
            ),
            "seq",
        )
        per_layer.insert(0, summed)
    stacked = [jnp.stack([per_layer[i][m] for i in range(layers)]) for m in range(12)]

    def back_out(value):
        return from_segments(value.reshape(seqs, length, G, -1))

    return (back_out(hidden), back_out(grad), *stacked)


def solution(mesh):
    return jax.shard_map(
        local,
        mesh=mesh,
        in_specs=(
            P(None, "seq", "chan"),
            P(None, "chan"),
            P(None, None, None, "chan"),
            P(None, None, "chan"),
            P(None, "chan"),
            P(None, "chan", None),
            P(None, None, "chan"),
            P(None, "chan"),
            P(None, None, "chan"),
            P(None, "chan"),
            P(None, "chan", None),
            P(None, None, None, "chan"),
            P(None, None, None, "chan"),
            P(None, "seq", "chan"),
        ),
        out_specs=(
            P(None, "seq", "chan"),
            P(None, "seq", "chan"),
            P(None, "chan"),
            P(None, None, None, "chan"),
            P(None, None, "chan"),
            P(None, "chan"),
            P(None, "chan", None),
            P(None, None, "chan"),
            P(None, "chan"),
            P(None, None, "chan"),
            P(None, "chan"),
            P(None, "chan", None),
            P(None, None, None, "chan"),
            P(None, None, None, "chan"),
        ),
        check_vma=False,
    )
```

```python
import functools
import math

import jax
import jax.numpy as jnp
from jax import lax
from jax.experimental import pallas as pl
from jax.experimental.pallas import tpu as pltpu
from jax.sharding import PartitionSpec as P

EPS = 1e-05
G = 8
LANES = 128
LOG2E = 1.4426950408889634
LN2 = 0.6931471805599453
F32 = jnp.float32
BF16 = jnp.bfloat16
VMEM_LIMIT = 48 * 1024 * 1024


def params(*semantics):
    return pltpu.CompilerParams(dimension_semantics=semantics, vmem_limit_bytes=VMEM_LIMIT)


def spread_maps(maps_ref, first, count, out_ref):
    shape = (maps_ref.shape[2], count * LANES)
    row = lax.broadcasted_iota(jnp.int32, shape, 0)
    col = lax.broadcasted_iota(jnp.int32, shape, 1) // LANES
    choice = jnp.where(row == col + first, 1.0, 0.0).astype(BF16)
    out_ref[...] = jnp.dot(maps_ref[0], choice, preferred_element_type=F32)


def part(ref, l, n):
    return ref[pl.ds(pl.multiple_of(l * G, G), G), n * LANES : (n + 1) * LANES]


def spread_rate(decay_ref, rate_ref):
    rate = jnp.exp(decay_ref[...]) * (-LOG2E)
    for n in range(rate.shape[0]):
        rate_ref[n] = jnp.broadcast_to(rate[n : n + 1, :], (G, LANES))


def shifted(value, by, fill):
    row = lax.broadcasted_iota(jnp.int32, value.shape, 0)
    moved = pltpu.roll(value, by % G, 0)
    inside = row >= by if by > 0 else row < G + by
    return jnp.where(inside, moved, fill)


def segment_prefix(ends, span, rate_ref, direction):
    step = 1
    while step < G:
        moved_span = shifted(span, direction * step, 0.0)
        ends = [
            e + jnp.exp2(span * rate_ref[n]) * shifted(e, direction * step, 0.0)
            for n, e in enumerate(ends)
        ]
        span = span + moved_span
        step *= 2
    return ends, span


def ends_kernel(act_ref, step_ref, maps_ref, decay_ref, prefix_ref, span_ref, pack_ref, b_ref, rate_ref):
    length, states = act_ref.shape[1], decay_ref.shape[0]

    @pl.when(pl.program_id(1) == 0)
    def _():
        spread_maps(maps_ref, 0, states, b_ref)

    spread_rate(decay_ref, rate_ref)

    def one(l, carry):
        h, total = carry
        st = step_ref[0, l]
        u = st * act_ref[0, l]
        h = tuple(
            jnp.exp2(st * rate_ref[n]) * h[n] + u * part(b_ref, l, n) for n in range(states)
        )
        return h, total + st

    zero = jnp.zeros((G, LANES), F32)
    h, total = lax.fori_loop(0, length, one, ((zero,) * states, zero))
    ends, span = segment_prefix(list(h), total, rate_ref, 1)
    for n in range(states):
        prefix_ref[0, n] = shifted(ends[n], 1, 0.0)
        pack_ref[0, n : n + 1, :] = ends[n][G - 1 : G, :]
    span_ref[0, 0] = shifted(span, 1, 0.0)
    span_ref[0, 1] = jnp.broadcast_to(span[G - 1 : G, :], (G, LANES)) - span
    pack_ref[0, states:, :] = jnp.broadcast_to(span[G - 1 : G, :], (8, LANES))


def scan_ends(act, step, maps, decay):
    seqs, length, _, chans = act.shape
    states = decay.shape[0]
    token = pl.BlockSpec((1, length, G, LANES), lambda s, j: (s, 0, 0, j))
    return pl.pallas_call(
        ends_kernel,
        grid=(seqs, chans // LANES),
        in_specs=[
            token,
            token,
            pl.BlockSpec((1, length * G, maps.shape[2]), lambda s, j: (s, 0, 0)),
            pl.BlockSpec((states, LANES), lambda s, j: (0, j)),
        ],
        out_specs=[
            pl.BlockSpec((1, states, G, LANES), lambda s, j: (s, 0, 0, j)),
            pl.BlockSpec((1, 2, G, LANES), lambda s, j: (s, 0, 0, j)),
            pl.BlockSpec((1, states + 8, LANES), lambda s, j: (s, 0, j)),
        ],
        out_shape=[
            jax.ShapeDtypeStruct((seqs, states, G, chans), F32),
            jax.ShapeDtypeStruct((seqs, 2, G, chans), F32),
            jax.ShapeDtypeStruct((seqs, states + 8, chans), F32),
        ],
        scratch_shapes=[
            pltpu.VMEM((length * G, states * LANES), F32),
            pltpu.VMEM((states, G, LANES), F32),
        ],
        compiler_params=params("arbitrary", "arbitrary"),
        cost_estimate=estimate(12),
        name="scan_ends",
    )(act, step, maps, decay)


def forward_kernel(
    act_ref, step_ref, gate_ref, maps_ref, decay_ref, prefix_ref, span_ref, packs_ref, init_ref, skip_ref,
    y_ref, gated_ref, start_ref, b_ref, c_ref, rate_ref,
):
    length, states = act_ref.shape[1], decay_ref.shape[0]

    @pl.when(pl.program_id(1) == 0)
    def _():
        spread_maps(maps_ref, 0, states, b_ref)
        spread_maps(maps_ref, states, states, c_ref)

    spread_rate(decay_ref, rate_ref)
    rate = jnp.exp(decay_ref[...]) * (-LOG2E)
    me = lax.axis_index("seq")
    entry = init_ref[0]
    for d in range(packs_ref.shape[0]):
        joined = jnp.exp2(rate * packs_ref[d, 0, states : states + 1, :]) * entry + packs_ref[d, 0, :states, :]
        entry = jnp.where(d < me, joined, entry)
    span = span_ref[0, 0]
    h = []
    for n in range(states):
        first = prefix_ref[0, n] + jnp.exp2(rate_ref[n] * span) * entry[n : n + 1, :]
        start_ref[0, n] = first
        h.append(first)
    skip = jnp.broadcast_to(skip_ref[...], (G, LANES))

    def one(k, h):
        h = list(h)
        halves = []
        for i in range(2):
            l = 2 * k + i
            st = step_ref[0, l]
            act = act_ref[0, l]
            u = st * act
            y = skip * act
            for n in range(states):
                h[n] = jnp.exp2(st * rate_ref[n]) * h[n] + u * part(b_ref, l, n)
                y = y + part(c_ref, l, n) * h[n]
            y_ref[0, l] = y
            gate = gate_ref[0, l]
            halves.append(y * (gate / (1.0 + jnp.exp(-gate))))
        gated_ref[0, pl.ds(pl.multiple_of(k * 2 * G, 2 * G), 2 * G), :] = jnp.concatenate(halves, axis=0).astype(BF16)
        return tuple(h)

    lax.fori_loop(0, length // 2, one, tuple(h))


def scan_forward(act, step, gate, maps, decay, prefix, span, packs, init, skip):
    seqs, length, _, chans = act.shape
    states = decay.shape[0]
    token = pl.BlockSpec((1, length, G, LANES), lambda s, j: (s, 0, 0, j))
    per_state = pl.BlockSpec((1, states, G, LANES), lambda s, j: (s, 0, 0, j))
    return pl.pallas_call(
        forward_kernel,
        grid=(seqs, chans // LANES),
        in_specs=[
            token,
            token,
            token,
            pl.BlockSpec((1, length * G, maps.shape[2]), lambda s, j: (s, 0, 0)),
            pl.BlockSpec((states, LANES), lambda s, j: (0, j)),
            per_state,
            pl.BlockSpec((1, 2, G, LANES), lambda s, j: (s, 0, 0, j)),
            pl.BlockSpec((packs.shape[0], 1, states + 8, LANES), lambda s, j: (0, s, 0, j)),
            pl.BlockSpec((1, states, LANES), lambda s, j: (s, 0, j)),
            pl.BlockSpec((1, LANES), lambda s, j: (0, j)),
        ],
        out_specs=[
            token,
            pl.BlockSpec((1, length * G, LANES), lambda s, j: (s, 0, j)),
            per_state,
        ],
        out_shape=[
            jax.ShapeDtypeStruct(act.shape, F32),
            jax.ShapeDtypeStruct((seqs, length * G, chans), BF16),
            jax.ShapeDtypeStruct((seqs, states, G, chans), F32),
        ],
        scratch_shapes=[
            pltpu.VMEM((length * G, states * LANES), F32),
            pltpu.VMEM((length * G, states * LANES), F32),
            pltpu.VMEM((states, G, LANES), F32),
        ],
        compiler_params=params("arbitrary", "arbitrary"),
        cost_estimate=estimate(20),
        name="scan_forward",
    )(act, step, gate, maps, decay, prefix, span, packs, init, skip)


def adjoint_kernel(step_ref, gate_ref, grad_ref, maps_ref, decay_ref, span_ref, suffix_ref, pack_ref, c_ref, rate_ref):
    length, states = step_ref.shape[1], decay_ref.shape[0]

    @pl.when(pl.program_id(1) == 0)
    def _():
        spread_maps(maps_ref, states, states, c_ref)

    spread_rate(decay_ref, rate_ref)

    def one(k, carry):
        l = length - 1 - k
        st = step_ref[0, l]
        gate = gate_ref[0, l]
        gy = grad_ref[0, l] * (gate / (1.0 + jnp.exp(-gate)))
        return tuple(
            jnp.exp2(st * rate_ref[n]) * (carry[n] + gy * part(c_ref, l, n)) for n in range(states)
        )

    zero = jnp.zeros((G, LANES), F32)
    carry = lax.fori_loop(0, length, one, (zero,) * states)
    own = span_ref[0, 1, 0:1, :] + span_ref[0, 0, 1:2, :] - span_ref[0, 0] - span_ref[0, 1]
    ends, _ = segment_prefix(list(carry), own, rate_ref, -1)
    for n in range(states):
        suffix_ref[0, n] = shifted(ends[n], -1, 0.0)
        pack_ref[0, n : n + 1, :] = ends[n][0:1, :]


def scan_adjoint(step, gate, grad, maps, decay, span):
    seqs, length, _, chans = step.shape
    states = decay.shape[0]
    token = pl.BlockSpec((1, length, G, LANES), lambda s, j: (s, 0, 0, j))
    return pl.pallas_call(
        adjoint_kernel,
        grid=(seqs, chans // LANES),
        in_specs=[
            token,
            token,
            token,
            pl.BlockSpec((1, length * G, maps.shape[2]), lambda s, j: (s, 0, 0)),
            pl.BlockSpec((states, LANES), lambda s, j: (0, j)),
            pl.BlockSpec((1, 2, G, LANES), lambda s, j: (s, 0, 0, j)),
        ],
        out_specs=[
            pl.BlockSpec((1, states, G, LANES), lambda s, j: (s, 0, 0, j)),
            pl.BlockSpec((1, states, LANES), lambda s, j: (s, 0, j)),
        ],
        out_shape=[
            jax.ShapeDtypeStruct((seqs, states, G, chans), F32),
            jax.ShapeDtypeStruct((seqs, states, chans), F32),
        ],
        scratch_shapes=[
            pltpu.VMEM((length * G, states * LANES), F32),
            pltpu.VMEM((states, G, LANES), F32),
        ],
        compiler_params=params("arbitrary", "arbitrary"),
        cost_estimate=estimate(15),
        name="scan_adjoint",
    )(step, gate, grad, maps, decay, span)


def backward_kernel(
    act_ref, step_ref, delta_ref, gate_ref, y_ref, grad_ref, maps_ref, decay_ref, start_ref, suffix_ref, span_ref,
    packs_ref, forward_packs_ref, skip_ref,
    gact_ref, gpre_ref, ggate_ref, gmaps_ref, gdecay_ref, gskip_ref, ginit_ref,
    b_ref, c_ref, rate_ref, h_ref, product_ref, select_ref,
):
    length, states = act_ref.shape[1], decay_ref.shape[0]
    wide = states * LANES

    @pl.when(pl.program_id(1) == 0)
    def _():
        spread_maps(maps_ref, 0, states, b_ref)
        spread_maps(maps_ref, states, states, c_ref)
        row = lax.broadcasted_iota(jnp.int32, select_ref.shape, 0) // LANES
        col = lax.broadcasted_iota(jnp.int32, select_ref.shape, 1)
        select_ref[...] = jnp.where(row == col, 1.0, 0.0).astype(BF16)

    spread_rate(decay_ref, rate_ref)
    rate = jnp.exp(decay_ref[...]) * (-LOG2E)
    me = lax.axis_index("seq")
    count = packs_ref.shape[0]
    entry = jnp.zeros((states, LANES), F32)
    for d in reversed(range(count)):
        joined = jnp.exp2(rate * forward_packs_ref[d, 0, states : states + 1, :]) * entry + packs_ref[d, 0]
        entry = jnp.where(d > me, joined, entry)
    after = span_ref[0, 1]
    skip = jnp.broadcast_to(skip_ref[...], (G, LANES))

    def forward(l, h):
        st = step_ref[0, l]
        u = st * act_ref[0, l]
        for n in range(states):
            h_ref[l, n] = h[n]
        return tuple(
            jnp.exp2(st * rate_ref[n]) * h[n] + u * part(b_ref, l, n) for n in range(states)
        )

    h = lax.fori_loop(0, length, forward, tuple(start_ref[0, n] for n in range(states)))
    for n in range(states):
        h_ref[length, n] = h[n]

    def back(k, state):
        carry, gdecay, gskip = list(state[0]), list(state[1]), state[2]
        lines = [length - 1 - 2 * k, length - 2 - 2 * k]
        st, act, u, gy, q, r = [], [], [], [], [], []
        ggate = []
        for l in lines:
            st.append(step_ref[0, l])
            act.append(act_ref[0, l])
            u.append(st[-1] * act[-1])
            gate = gate_ref[0, l]
            grad = grad_ref[0, l]
            sig = 1.0 / (1.0 + jnp.exp(-gate))
            silu = gate * sig
            gy.append(grad * silu)
            ggate.append(grad * y_ref[0, l] * (sig + silu * (1.0 - sig)))
            gskip = gskip + gy[-1] * act[-1]
            q.append(jnp.zeros((G, LANES), F32))
            r.append(jnp.zeros((G, LANES), F32))
        row = pl.multiple_of((length - 2 - 2 * k) * G, 2 * G)
        for n in range(states):
            late, early = [], []
            for i, l in enumerate(lines):
                lam = part(c_ref, l, n) * gy[i] + carry[n]
                early.append(lam * u[i])
                late.append(gy[i] * h_ref[l + 1, n])
                q[i] = q[i] + lam * part(b_ref, l, n)
                carry[n] = jnp.exp2(st[i] * rate_ref[n]) * lam
                w = carry[n] * h_ref[l, n]
                r[i] = r[i] + rate_ref[n] * w
                gdecay[n] = gdecay[n] + st[i] * w
            product_ref[pl.ds(row, 2 * G), n * LANES : (n + 1) * LANES] = jnp.concatenate(early[::-1], axis=0).astype(BF16)
            product_ref[pl.ds(row, 2 * G), wide + n * LANES : wide + (n + 1) * LANES] = jnp.concatenate(late[::-1], axis=0).astype(BF16)
        gpre = []
        for i, l in enumerate(lines):
            gact_ref[0, l] = skip * gy[i] + st[i] * q[i]
            gstep = LN2 * r[i] + act[i] * q[i]
            gpre.append(gstep / (1.0 + jnp.exp(-delta_ref[0, l])))
        gpre_ref[0, pl.ds(row, 2 * G), :] = jnp.concatenate(gpre[::-1], axis=0).astype(BF16)
        ggate_ref[0, pl.ds(row, 2 * G), :] = jnp.concatenate(ggate[::-1], axis=0).astype(BF16)
        return tuple(carry), tuple(gdecay), gskip

    zero = jnp.zeros((G, LANES), F32)
    first = tuple(
        suffix_ref[0, n] + jnp.exp2(rate_ref[n] * after) * entry[n : n + 1, :] for n in range(states)
    )
    carry, gdecay, gskip = lax.fori_loop(0, length // 2, back, (first, (zero,) * states, zero))
    for n in range(states):
        ginit_ref[0, n : n + 1, :] = carry[n][0:1, :]
        total = jnp.sum(gdecay[n] * rate_ref[n], axis=0, keepdims=True)
        gdecay_ref[0, n : n + 1, :] = total * LN2
    gskip_ref[0] = jnp.broadcast_to(jnp.sum(gskip, axis=0, keepdims=True), (8, LANES))
    sums = jnp.dot(product_ref[...], select_ref[...], preferred_element_type=F32)

    @pl.when(pl.program_id(1) == 0)
    def _():
        gmaps_ref[0] = sums

    @pl.when(pl.program_id(1) > 0)
    def _():
        gmaps_ref[0] += sums


def scan_backward(act, step, delta, gate, y, grad, maps, decay, start, suffix, span, packs, forward_packs, skip):
    seqs, length, _, chans = act.shape
    states = decay.shape[0]
    token = pl.BlockSpec((1, length, G, LANES), lambda s, j: (s, 0, 0, j))
    rows = pl.BlockSpec((1, length * G, LANES), lambda s, j: (s, 0, j))
    per_state = pl.BlockSpec((1, states, G, LANES), lambda s, j: (s, 0, 0, j))
    total = pl.BlockSpec((1, states, LANES), lambda s, j: (s, 0, j))
    return pl.pallas_call(
        backward_kernel,
        grid=(seqs, chans // LANES),
        in_specs=[
            token,
            token,
            token,
            token,
            token,
            token,
            pl.BlockSpec((1, length * G, maps.shape[2]), lambda s, j: (s, 0, 0)),
            pl.BlockSpec((states, LANES), lambda s, j: (0, j)),
            per_state,
            per_state,
            pl.BlockSpec((1, 2, G, LANES), lambda s, j: (s, 0, 0, j)),
            pl.BlockSpec((packs.shape[0], 1, states, LANES), lambda s, j: (0, s, 0, j)),
            pl.BlockSpec((packs.shape[0], 1, states + 8, LANES), lambda s, j: (0, s, 0, j)),
            pl.BlockSpec((1, LANES), lambda s, j: (0, j)),
        ],
        out_specs=[
            token,
            rows,
            rows,
            pl.BlockSpec((1, length * G, LANES), lambda s, j: (s, 0, 0)),
            total,
            pl.BlockSpec((1, 8, LANES), lambda s, j: (s, 0, j)),
            total,
        ],
        out_shape=[
            jax.ShapeDtypeStruct(act.shape, F32),
            jax.ShapeDtypeStruct((seqs, length * G, chans), BF16),
            jax.ShapeDtypeStruct((seqs, length * G, chans), BF16),
            jax.ShapeDtypeStruct((seqs, length * G, LANES), F32),
            jax.ShapeDtypeStruct((seqs, states, chans), F32),
            jax.ShapeDtypeStruct((seqs, 8, chans), F32),
            jax.ShapeDtypeStruct((seqs, states, chans), F32),
        ],
        scratch_shapes=[
            pltpu.VMEM((length * G, states * LANES), F32),
            pltpu.VMEM((length * G, states * LANES), F32),
            pltpu.VMEM((states, G, LANES), F32),
            pltpu.VMEM((length + 1, states, G, LANES), F32),
            pltpu.VMEM((length * G, 2 * states * LANES), BF16),
            pltpu.VMEM((2 * states * LANES, LANES), BF16),
        ],
        compiler_params=params("arbitrary", "arbitrary"),
        cost_estimate=estimate(39),
        name="scan_backward",
    )(act, step, delta, gate, y, grad, maps, decay, start, suffix, span, packs, forward_packs, skip)


MESH = pl.DeviceIdType.MESH


def remote(src, dst, send, recv, to):
    return pltpu.make_async_remote_copy(
        src_ref=src, dst_ref=dst, send_sem=send, recv_sem=recv, device_id={"chan": to}, device_id_type=MESH
    )


class Line:
    def __init__(self, count):
        self.me = lax.axis_index("chan")
        self.half = count // 2
        self.at = self.me // 2
        self.low = self.me % 2
        self.pair = self.at * 2 + 1 - self.low
        self.right = jnp.minimum(self.at + 1, self.half - 1) * 2 + self.low
        self.left = jnp.maximum(self.at - 1, 0) * 2 + self.low
        self.has_right = self.at < self.half - 1
        self.has_left = self.at > 0

    def greet(self):
        barrier = pltpu.get_barrier_semaphore()

        def signal(to):
            pl.semaphore_signal(barrier, inc=1, device_id={"chan": to}, device_id_type=MESH)

        signal(self.pair)
        pl.when(self.has_right)(lambda: signal(self.right))
        pl.when(self.has_left)(lambda: signal(self.left))
        pl.semaphore_wait(barrier, 1 + jnp.minimum(self.at, 1) + jnp.minimum(self.half - 1 - self.at, 1))


def gather_steps(line, out_ref, width, chunks, sems):
    pair_send, pair_recv, right_send, right_recv, left_send, left_recv = sems
    half = line.half
    rows = out_ref.shape[0] // chunks

    def place(owner, c):
        return out_ref.at[pl.ds(c * rows, rows), pl.ds(pl.multiple_of(owner * width, width), width)]

    def to_pair(owner, slot, c):
        return remote(place(owner, c), place(owner, c), pair_send.at[slot, c], pair_recv.at[slot, c], line.pair)

    def to_right(owner, j, c):
        return remote(place(owner, c), place(owner, c), right_send.at[j, c], right_recv.at[j, c], line.right)

    def to_left(owner, j, c):
        return remote(place(owner, c), place(owner, c), left_send.at[j, c], left_recv.at[j, c], line.left)

    def begin(c):
        pl.when(line.has_right)(lambda: to_right(line.me, 0, c).start())
        pl.when(line.has_left)(lambda: to_left(line.me, 0, c).start())
        to_pair(line.me, 0, c).start()

    def middle():
        for j in range(1, half):
            for c in range(chunks):
                @pl.when(line.at >= j)
                def _():
                    owner = line.me - 2 * j
                    to_right(owner, j - 1, c).wait_recv()
                    pl.when(line.has_right)(lambda: to_right(owner, j, c).start())
                    to_pair(owner, j, c).start()

                @pl.when(line.at + j < half)
                def _():
                    owner = line.me + 2 * j
                    to_left(owner, j - 1, c).wait_recv()
                    pl.when(line.has_left)(lambda: to_left(owner, j, c).start())
                    to_pair(owner, half + j, c).start()

    def end():
        for c in range(chunks):
            to_pair(line.me, 0, c).wait()
            pl.when(line.has_right)(lambda: to_right(line.me, 0, c).wait_send())
            pl.when(line.has_left)(lambda: to_left(line.me, 0, c).wait_send())
            for j in range(1, half):
                @pl.when(line.at >= j)
                def _():
                    owner = line.me - 2 * j
                    to_pair(owner, j, c).wait()
                    pl.when(line.has_right)(lambda: to_right(owner, j, c).wait_send())

                @pl.when(line.at + j < half)
                def _():
                    owner = line.me + 2 * j
                    to_pair(owner, half + j, c).wait()
                    pl.when(line.has_left)(lambda: to_left(owner, j, c).wait_send())

    return begin, middle, end


def gather_sems(count, chunks):
    half = count // 2
    return [pltpu.SemaphoreType.DMA((2 * half, chunks))] * 2 + [pltpu.SemaphoreType.DMA((half, chunks))] * 4


def estimate(us):
    return pl.CostEstimate(flops=int(us * 5e8), bytes_accessed=1 << 20, transcendentals=0)


def remote_params(ident):
    return pltpu.CompilerParams(collective_id=ident, has_side_effects=True, vmem_limit_bytes=VMEM_LIMIT)


def whole(count):
    return [pl.BlockSpec(memory_space=pltpu.VMEM)] * count


def chunks_of(rows):
    return next(c for c in (3, 2, 1) if rows % (16 * c) == 0)


def gather_kernel(count, chunks, part_ref, gain_ref, out_ref, *sems):
    line = Line(count)
    rows, width = part_ref.shape
    mine = pl.ds(pl.multiple_of(line.me * width, width), width)
    out_ref[:rows, mine] = part_ref[...]
    layers = gain_ref.shape[0]
    gain = gain_ref[...]
    terms = []
    for _ in range(3):
        term = gain.astype(BF16).astype(F32)
        terms.append(term)
        gain = gain - term
    terms.append(jnp.zeros((16 - 3 * layers, width), F32))
    out_ref[rows:, mine] = jnp.concatenate(terms, axis=0).astype(BF16)
    line.greet()
    begin, middle, end = gather_steps(line, out_ref, width, chunks, sems)
    for c in range(chunks):
        begin(c)
    middle()
    end()


def gather_first(part, gain):
    count = lax.axis_size("chan")
    rows, width = part.shape
    layers = gain.shape[0]
    chunks = chunks_of(rows + 16)
    full = pl.pallas_call(
        functools.partial(gather_kernel, count, chunks),
        in_specs=whole(2),
        out_specs=whole(1)[0],
        out_shape=jax.ShapeDtypeStruct((rows + 16, count * width), BF16),
        scratch_shapes=gather_sems(count, chunks),
        compiler_params=remote_params(0),
        cost_estimate=estimate(25),
        name="gather_first",
    )(part, gain)
    terms = full[rows : rows + 3 * layers].astype(F32)
    return full, terms[:layers] + terms[layers : 2 * layers] + terms[2 * layers :]


def scatter_steps(line, part_ref, pair_buf, right_buf, left_buf, stage, width, chunks, sems):
    pair_send, pair_recv, right_send, right_recv, left_send, left_recv = sems
    half = line.half
    rows = part_ref.shape[0] // chunks

    def block(owner, c):
        return part_ref.at[pl.ds(c * rows, rows), pl.ds(pl.multiple_of(owner * width, width), width)]

    def piece(ref, slot, c):
        return ref.at[slot, pl.ds(c * rows, rows)]

    def to_pair(at, c):
        return remote(block(at * 2 + 1 - line.low, c), pair_buf.at[at, pl.ds(c * rows, rows)], pair_send.at[at, c], pair_recv.at[at, c], line.pair)

    def to_right(j, c):
        return remote(piece(stage, j, c), piece(right_buf, j - 1, c), right_send.at[j - 1, c], right_recv.at[j - 1, c], line.right)

    def to_left(j, c):
        return remote(piece(stage, half + j, c), piece(left_buf, j - 1, c), left_send.at[j - 1, c], left_recv.at[j - 1, c], line.left)

    def begin():
        for c in range(chunks):
            for j in range(half - 1, 0, -1):
                pl.when(line.at + j < half)(lambda: to_pair(line.at + j, c).start())
                pl.when(line.at >= j)(lambda: to_pair(line.at - j, c).start())
            to_pair(line.at, c).start()

    def own_and_pair(at, c):
        to_pair(at, c).wait_recv()
        return block(at * 2 + line.low, c)[...].astype(F32) + pair_buf[at, pl.ds(c * rows, rows)].astype(F32)

    def middle(c):
        for j in range(half - 1, 0, -1):
            @pl.when(line.at + j < half)
            def _():
                stage[j, pl.ds(c * rows, rows)] = own_and_pair(line.at + j, c).astype(BF16)

                @pl.when(line.has_left)
                def _():
                    arrived = remote(piece(stage, j, c), piece(right_buf, j, c), right_send.at[j, c], right_recv.at[j, c], line.right)
                    arrived.wait_recv()
                    total = stage[j, pl.ds(c * rows, rows)].astype(F32) + right_buf[j, pl.ds(c * rows, rows)].astype(F32)
                    stage[j, pl.ds(c * rows, rows)] = total.astype(BF16)

                to_right(j, c).start()

            @pl.when(line.at >= j)
            def _():
                stage[half + j, pl.ds(c * rows, rows)] = own_and_pair(line.at - j, c).astype(BF16)

                @pl.when(line.has_right)
                def _():
                    arrived = remote(piece(stage, half + j, c), piece(left_buf, j, c), left_send.at[j, c], left_recv.at[j, c], line.left)
                    arrived.wait_recv()
                    total = stage[half + j, pl.ds(c * rows, rows)].astype(F32) + left_buf[j, pl.ds(c * rows, rows)].astype(F32)
                    stage[half + j, pl.ds(c * rows, rows)] = total.astype(BF16)

                to_left(j, c).start()

    def finish(c, out_ref):
        here = pl.ds(c * rows, rows)
        out_ref[here, :] = own_and_pair(line.at, c)

        @pl.when(line.has_left)
        def _():
            remote(piece(stage, 0, c), piece(right_buf, 0, c), right_send.at[0, c], right_recv.at[0, c], line.right).wait_recv()
            out_ref[here, :] += right_buf[0, here].astype(F32)

        @pl.when(line.has_right)
        def _():
            remote(piece(stage, 0, c), piece(left_buf, 0, c), left_send.at[0, c], left_recv.at[0, c], line.left).wait_recv()
            out_ref[here, :] += left_buf[0, here].astype(F32)

    def end():
        for c in range(chunks):
            for at in range(half):
                to_pair(at, c).wait_send()
            for j in range(1, half):
                pl.when(line.at + j < half)(lambda: to_right(j, c).wait_send())
                pl.when(line.at >= j)(lambda: to_left(j, c).wait_send())

    return begin, middle, finish, end


def scatter_scratch(count, chunks, rows, width):
    half = count // 2
    return (
        [pltpu.VMEM((half, rows, width), BF16)] * 3
        + [pltpu.VMEM((2 * half, rows, width), BF16)]
        + [pltpu.SemaphoreType.DMA((half, chunks))] * 6
    )


def boundary_kernel(count, chunks, part_ref, hidden_ref, new_ref, full_ref, pair_buf, right_buf, left_buf, stage, *sems):
    line = Line(count)
    rows, width = hidden_ref.shape
    mine = pl.ds(pl.multiple_of(line.me * width, width), width)
    line.greet()
    begin, middle, finish, end = scatter_steps(
        line, part_ref, pair_buf, right_buf, left_buf, stage, width, chunks, sems[:6]
    )
    gather_begin, gather_middle, gather_end = gather_steps(line, full_ref, width, chunks, sems[6:])
    begin()
    for c in range(chunks):
        here = pl.ds(c * (rows // chunks), rows // chunks)
        middle(c)
        finish(c, new_ref)
        new_ref[here, :] += hidden_ref[here, :]
        full_ref[here, mine] = new_ref[here, :].astype(BF16)
        gather_begin(c)
    gather_middle()
    gather_end()
    end()


def forward_boundary(part, hidden):
    count = lax.axis_size("chan")
    rows, width = hidden.shape
    chunks = 2
    return pl.pallas_call(
        functools.partial(boundary_kernel, count, chunks),
        in_specs=whole(2),
        out_specs=whole(2),
        out_shape=[jax.ShapeDtypeStruct((rows, width), F32), jax.ShapeDtypeStruct((rows, count * width), BF16)],
        scratch_shapes=scatter_scratch(count, chunks, rows, width) + gather_sems(count, chunks),
        compiler_params=remote_params(1),
        cost_estimate=estimate(50),
        name="forward_boundary",
    )(part, hidden)


def back_kernel(
    count, chunks, gathers, part_ref, grad_ref, hidden_ref, inverse_ref, gain_ref, inner_ref, new_ref, ggain_ref, *more
):
    full_ref, more = (more[0], more[1:]) if gathers else (None, more)
    pair_buf, right_buf, left_buf, stage, inner_buf, column_ref, inner_send, inner_recv = more[:8]
    sems = more[8:]
    line = Line(count)
    rows, width = grad_ref.shape
    model = width * count
    mine = pl.ds(pl.multiple_of(line.me * width, width), width)
    others = [lax.rem(line.me + k, count) for k in range(1, count)]
    barrier = pltpu.get_barrier_semaphore()
    for other in others:
        pl.semaphore_signal(barrier, inc=1, device_id={"chan": other}, device_id_type=MESH)
    pl.semaphore_wait(barrier, count - 1)
    begin, middle, finish, end = scatter_steps(
        line, part_ref, pair_buf, right_buf, left_buf, stage, width, chunks, sems[:6]
    )
    if gathers:
        gather_begin, gather_middle, gather_end = gather_steps(line, full_ref, width, chunks, sems[6:])
    sums = [
        remote(inner_ref, inner_buf.at[k], inner_send.at[k], inner_recv.at[k], others[k]) for k in range(count - 1)
    ]
    for copy in sums:
        copy.start()
    begin()
    eye = lax.broadcasted_iota(jnp.int32, (LANES, LANES), 0) == lax.broadcasted_iota(jnp.int32, (LANES, LANES), 1)
    ggain_ref[...] = jnp.zeros_like(ggain_ref)
    for c in range(chunks):
        here = pl.ds(c * (rows // chunks), rows // chunks)
        middle(c)
        if c == 0:
            inner = inner_ref[...]
            for k in range(count - 1):
                sums[k].wait_recv()
                inner = inner + inner_buf[k]
            for b in range(rows // LANES):
                column_ref[pl.ds(b * LANES, LANES), :] = jnp.sum(
                    jnp.where(eye, jnp.broadcast_to(inner[b : b + 1, :], (LANES, LANES)), 0.0), axis=1, keepdims=True
                )
        finish(c, new_ref)
        gnormed = new_ref[here, :]
        inverse = inverse_ref[here, :]
        hidden = hidden_ref[here, :]
        factor = inverse * inverse * column_ref[here, :] * (1.0 / model)
        ggain_ref[0:1, :] += jnp.sum(gnormed * hidden * inverse, axis=0, keepdims=True)
        new = grad_ref[here, :] + inverse * (gain_ref[...] * gnormed) - hidden * factor
        new_ref[here, :] = new
        if gathers:
            full_ref[here, mine] = new.astype(BF16)
            gather_begin(c)
    if gathers:
        gather_middle()
        gather_end()
    end()
    for copy in sums:
        copy.wait_send()


def backward_boundary(part, grad, hidden, inverse, gain, inner, gathers):
    count = lax.axis_size("chan")
    rows, width = hidden.shape
    chunks = 2
    out_shape = [jax.ShapeDtypeStruct((rows, width), F32), jax.ShapeDtypeStruct((8, width), F32)]
    scratch = scatter_scratch(count, chunks, rows, width)
    scratch += [
        pltpu.VMEM((count - 1, rows // LANES, LANES), F32),
        pltpu.VMEM((rows, 1), F32),
        pltpu.SemaphoreType.DMA((count - 1,)),
        pltpu.SemaphoreType.DMA((count - 1,)),
    ]
    order = scratch[:4] + scratch[10:] + scratch[4:10]
    if gathers:
        out_shape.append(jax.ShapeDtypeStruct((rows, count * width), BF16))
        order += gather_sems(count, chunks)
    return pl.pallas_call(
        functools.partial(back_kernel, count, chunks, gathers),
        in_specs=whole(6),
        out_specs=whole(len(out_shape)),
        out_shape=out_shape,
        scratch_shapes=order,
        compiler_params=remote_params(2 if gathers else 3),
        cost_estimate=estimate(50 if gathers else 27),
        name="backward_boundary" if gathers else "backward_last",
    )(part, grad, hidden, inverse, gain, inner.reshape(rows // LANES, LANES))


def sum_kernel(count, part_ref, out_ref, arrived, total_ref, send1, recv1, send2, recv2):
    me = lax.axis_index("chan")
    rows = part_ref.shape[0] // count
    others = [lax.rem(me + k, count) for k in range(1, count)]
    barrier = pltpu.get_barrier_semaphore()
    for other in others:
        pl.semaphore_signal(barrier, inc=1, device_id={"chan": other}, device_id_type=MESH)
    pl.semaphore_wait(barrier, count - 1)

    def piece(ref, owner):
        return ref.at[pl.ds(pl.multiple_of(owner * rows, rows), rows)]

    first, second = [], []
    for k, other in enumerate(others):
        first.append(remote(piece(part_ref, other), arrived.at[k], send1.at[k], recv1.at[k], other))
        first[k].start()
    acc = piece(part_ref, me)[...].astype(F32)
    for k in range(count - 1):
        first[k].wait_recv()
        acc = acc + arrived[k].astype(F32)
    total_ref[...] = acc.astype(BF16)
    for k, other in enumerate(others):
        second.append(remote(total_ref, piece(out_ref, me), send2.at[k], recv2.at[k], other))
        second[k].start()
    piece(out_ref, me)[...] = total_ref[...]
    for copy in second:
        copy.wait()
    for copy in first:
        copy.wait_send()


def sum_chan(part):
    count = lax.axis_size("chan")
    rows, width = part.shape
    return pl.pallas_call(
        functools.partial(sum_kernel, count),
        in_specs=whole(1),
        out_specs=whole(1)[0],
        out_shape=jax.ShapeDtypeStruct((rows, width), BF16),
        scratch_shapes=[pltpu.VMEM((count - 1, rows // count, width), BF16), pltpu.VMEM((rows // count, width), BF16)]
        + [pltpu.SemaphoreType.DMA((count - 1,))] * 4,
        compiler_params=remote_params(4),
        cost_estimate=estimate(14),
        name="sum_chan",
    )(part)


def exchanged(value, bit):
    return lax.ppermute(value, "seq", [(i, i ^ bit) for i in range(lax.axis_size("seq"))])


class Summed:
    def __init__(self, value, halves):
        self.halves = halves
        self.bit = 1
        self.keep = value
        give = value
        if halves:
            half = value.shape[0] // 2
            core = lax.axis_index("seq") % 2
            self.keep = lax.dynamic_slice_in_dim(value, core * half, half, 0)
            give = lax.dynamic_slice_in_dim(value, (1 - core) * half, half, 0)
        self.wire = exchanged(give, 1)

    def step(self):
        total = self.keep.astype(F32) + self.wire.astype(F32)
        self.bit *= 2
        if self.bit < lax.axis_size("seq"):
            self.keep = total.astype(BF16)
            self.wire = exchanged(self.keep, self.bit)
        elif self.halves:
            self.keep = total.astype(BF16)
            self.wire = exchanged(self.keep, 1)
        else:
            self.keep = total

    def across(self):
        while self.bit * 2 < lax.axis_size("seq"):
            self.step()

    def last(self):
        while self.bit * 2 < lax.axis_size("seq"):
            self.step()
        return self.keep, self.wire

    def total(self):
        while self.bit < lax.axis_size("seq"):
            self.step()
        return (self.keep, self.wire) if self.halves else self.keep


def after(value, *sums):
    value, wires = lax.optimization_barrier((value, [one.wire for one in sums]))
    for one, wire in zip(sums, wires):
        one.wire = wire
    return value


def place_pairs_kernel(core_ref, *refs):
    *ins, out_ref = refs[-5:]
    own = pl.program_id(0) == 0
    for j in range(2):
        out_ref[0, :, j, :] = jnp.where(own, ins[2 * j][...].astype(F32), ins[2 * j + 1][...].astype(F32))


def place_rows_kernel(core_ref, *refs):
    mine, other, out_ref = refs[-3:]
    own = pl.program_id(0) == 0
    out_ref[0] = jnp.where(own, mine[...].astype(F32), other[...].astype(F32))


def place(kernel, parts, base, layer, layers, block, middle):
    half, width = parts[0].shape
    core = (lax.axis_index("seq") % 2).reshape(1)
    steps = half // block

    def where(kept):
        if kept:
            return lambda k, b, core: (jnp.where(k == 0, b, steps - 1), 0)
        return lambda k, b, core: (jnp.where(k == 1, b, 0), 0)

    def out(k, b, core):
        return (layer, (core[0] + k - 2 * core[0] * k) * steps + b) + (0,) * (1 + len(middle))

    ins = [pl.BlockSpec((block, width), where(p % 2 == 0)) for p in range(len(parts))]
    shape = (layers, 2 * half) + middle + (width,)
    args = list(parts)
    aliases = {}
    if base is not None:
        ins.insert(0, pl.BlockSpec(memory_space=pl.ANY))
        args.insert(0, base)
        aliases = {1: 0}
    return pl.pallas_call(
        kernel,
        grid_spec=pltpu.PrefetchScalarGridSpec(
            num_scalar_prefetch=1,
            grid=(2, steps),
            in_specs=ins,
            out_specs=pl.BlockSpec((1, block) + middle + (width,), out),
        ),
        out_shape=jax.ShapeDtypeStruct(shape, F32),
        input_output_aliases=aliases,
        compiler_params=params("arbitrary", "arbitrary"),
        cost_estimate=estimate(5),
        name="place",
    )(core, *args)


def dot(a, b, dims):
    return lax.dot_general(a, b, (dims, ((), ())), preferred_element_type=F32)


def rows_of_packed(rank_columns, rank, states, seqs, taps):
    names = [("xproj", rank_columns), ("dtproj", rank), ("decay", states), ("init", seqs * states)]
    names += [("taps", taps), ("shift", 1), ("bias", 1), ("skip", 1), ("conv", (taps - 1) * seqs)]
    places, row = {}, 0
    for name, size in names:
        places[name] = (row, row + size)
        row += size
    return places, row + (-row) % 16


def mid_kernel(
    gproj_ref, xproj_ref, gact_ref, inner_ref, head_ref, low_ref, taps_ref, shift_ref, rank_ref, gpre_ref, ggate_ref,
    gdecay_ref, gskip_ref, ginit_ref,
    gmixed_ref, packed_ref,
    dotted_ref, pad_ref, gconv_ref, tail_ref, give_ref, got_ref, send_sem, recv_sem,
):
    seqs, length = gact_ref.shape[:2]
    tokens = length * G
    count = gmixed_ref.shape[1] // (2 * LANES)
    taps = taps_ref.shape[0]
    over = taps - 1
    j = pl.program_id(0)
    place, peers = lax.axis_index("seq"), lax.axis_size("seq")
    states = gdecay_ref.shape[1]
    places, _ = rows_of_packed(gproj_ref.shape[1], rank_ref.shape[1], states, seqs, taps)

    def to_previous(t):
        return pltpu.make_async_remote_copy(
            src_ref=give_ref.at[t], dst_ref=got_ref.at[t], send_sem=send_sem.at[t], recv_sem=recv_sem.at[t],
            device_id={"seq": jnp.maximum(place - 1, 0)}, device_id_type=MESH,
        )

    @pl.when(j == 0)
    def _():
        barrier = pltpu.get_barrier_semaphore()

        @pl.when(place < peers - 1)
        def _():
            pl.semaphore_signal(barrier, inc=1, device_id={"seq": place + 1}, device_id_type=MESH)

        pl.when(place > 0)(lambda: pl.semaphore_wait(barrier, 1))

    columns = pl.ds(pl.multiple_of(j * LANES, LANES), LANES)
    gate_columns = pl.ds(pl.multiple_of((count + j) * LANES, LANES), LANES)
    gmixed_ref[:, gate_columns] = ggate_ref[...]
    dotted_ref[...] = jnp.dot(gproj_ref[...], xproj_ref[...], preferred_element_type=F32)
    zero = jnp.zeros((G, LANES), F32)
    weights = [jnp.broadcast_to(taps_ref[k : k + 1, :], (G, LANES)) for k in range(taps)]
    shift = jnp.broadcast_to(shift_ref[...], (G, LANES))
    sums = (zero,) * (taps + 1)
    early = [[None] * seqs for _ in range(over)]
    for s in range(seqs):
        for k in range(over):
            pad_ref[k] = head_ref[s, k]

        def fill(l, carry):
            pad_ref[l + over] = inner_ref[s, l]
            return carry

        lax.fori_loop(0, length, fill, 0)

        def one(l, sums):
            parts = [pad_ref[l + k] for k in range(taps)]
            pre = shift
            for k in range(taps):
                pre = pre + weights[k] * parts[k]
            sig = 1.0 / (1.0 + jnp.exp(-pre))
            here = dotted_ref[pl.ds(pl.multiple_of(s * tokens + l * G, G), G), :]
            gconv = (gact_ref[s, l] + here) * (sig + pre * sig * (1.0 - sig))
            gconv_ref[l] = gconv
            return tuple(sums[k] + gconv * parts[k] for k in range(taps)) + (sums[taps] + gconv,)

        sums = lax.fori_loop(0, length, one, sums)
        for k in range(over):
            gconv_ref[length + k] = shifted(gconv_ref[k], -1, 0.0)
            total = weights[0] * gconv_ref[k]
            for i in range(1, k + 1):
                total = total + weights[i] * gconv_ref[k - i]
            early[k][s] = total[0:1, :]
            give_ref[j, s, k : k + 1, :] = total[0:1, :]

        def inner_of(l):
            total = weights[0] * gconv_ref[l + over]
            for k in range(1, taps):
                total = total + weights[k] * gconv_ref[l + over - k]
            return total

        def pair(p, carry):
            both = jnp.concatenate([inner_of(2 * p), inner_of(2 * p + 1)], axis=0)
            gmixed_ref[pl.ds(pl.multiple_of(s * tokens + 2 * p * G, 2 * G), 2 * G), columns] = both.astype(BF16)
            return carry

        lax.fori_loop(0, length // 2 - 2, pair, 0)
        for q in range(4):
            tail_ref[j, s, q] = inner_of(length - 4 + q)
    pl.when(place > 0)(lambda: to_previous(j).start())

    def put(name, value):
        first, last = places[name]
        packed_ref[first:last, :] = value.astype(BF16)

    put("xproj", dot(gproj_ref[...], low_ref[...], ((0,), (0,))))
    put("dtproj", dot(rank_ref[...], gpre_ref[...], ((0,), (0,))))
    bias = jnp.dot(jnp.ones((16, seqs * tokens), BF16), gpre_ref[...], preferred_element_type=F32)[0:1, :]
    decay, skip = gdecay_ref[0], gskip_ref[0, 0:1, :]
    for s in range(1, seqs):
        decay = decay + gdecay_ref[s]
        skip = skip + gskip_ref[s, 0:1, :]
    put("decay", decay)
    first = place == 0
    for s in range(seqs):
        row = places["init"][0] + s * states
        packed_ref[row : row + states, :] = jnp.where(first, ginit_ref[s], 0.0).astype(BF16)
    rest = [jnp.sum(value, axis=0, keepdims=True) for value in sums]
    rest += [bias, skip]
    rest += [jnp.where(first, early[k][s], 0.0) for k in range(over) for s in range(seqs)]
    row = places["taps"][0]
    rest += [jnp.zeros((1, LANES), F32)] * (packed_ref.shape[0] - row - len(rest))
    packed_ref[row:, :] = jnp.concatenate(rest, axis=0).astype(BF16)

    @pl.when(j == count - 1)
    def _():
        last_row = lax.broadcasted_iota(jnp.int32, (G, LANES), 0) == G - 1
        inside = place < peers - 1
        for t in range(count):
            pl.when(place < peers - 1)(lambda: to_previous(t).wait_recv())
            for s in range(seqs):
                values = []
                for q in range(4):
                    value = tail_ref[t, s, q]
                    k = q - 4 + over
                    if k >= 0:
                        given = jnp.broadcast_to(got_ref[t, s, k : k + 1, :], (G, LANES))
                        value = value + jnp.where(jnp.logical_and(last_row, inside), given, 0.0)
                    values.append(value)
                for q in (0, 2):
                    row = s * tokens + (length - 4 + q) * G
                    both = jnp.concatenate(values[q : q + 2], axis=0)
                    gmixed_ref[row : row + 2 * G, t * LANES : (t + 1) * LANES] = both.astype(BF16)
            pl.when(place > 0)(lambda: to_previous(t).wait_send())


def mid_backward(
    gproj, xproj, gact, mixed, head, low, taps, shift, rank_part, gpre, ggate, gdecay, gskip, ginit
):
    seqs, length, _, chans = gact.shape
    rows = seqs * length * G
    count = chans // LANES
    states = gdecay.shape[1]
    over = taps.shape[0] - 1
    _, packed_rows = rows_of_packed(gproj.shape[1], rank_part.shape[1], states, seqs, taps.shape[0])
    token = pl.BlockSpec((seqs, length, G, LANES), lambda j: (0, 0, 0, j))
    row = pl.BlockSpec((rows, LANES), lambda j: (0, j))

    def column(height):
        return pl.BlockSpec((height, LANES), lambda j: (0, j))

    def stack(height):
        return pl.BlockSpec((seqs, height, LANES), lambda j: (0, 0, j))

    return pl.pallas_call(
        mid_kernel,
        grid=(count,),
        in_specs=[
            pl.BlockSpec(gproj.shape, lambda j: (0, 0)),
            column(xproj.shape[0]),
            token,
            token,
            pl.BlockSpec((seqs, over, G, LANES), lambda j: (0, 0, 0, j)),
            row,
            column(over + 1),
            column(1),
            pl.BlockSpec(rank_part.shape, lambda j: (0, 0)),
            row,
            row,
            stack(states),
            stack(8),
            stack(states),
        ],
        out_specs=[pl.BlockSpec((rows, 2 * chans), lambda j: (0, 0)), column(packed_rows)],
        out_shape=[
            jax.ShapeDtypeStruct((rows, 2 * chans), BF16),
            jax.ShapeDtypeStruct((packed_rows, chans), BF16),
        ],
        scratch_shapes=[
            pltpu.VMEM((rows, LANES), F32),
            pltpu.VMEM((length + over, G, LANES), F32),
            pltpu.VMEM((length + over, G, LANES), F32),
            pltpu.VMEM((count, seqs, 4, G, LANES), F32),
            pltpu.VMEM((count, seqs, 8, LANES), F32),
            pltpu.VMEM((count, seqs, 8, LANES), F32),
            pltpu.SemaphoreType.DMA((count,)),
            pltpu.SemaphoreType.DMA((count,)),
        ],
        compiler_params=pltpu.CompilerParams(
            dimension_semantics=("arbitrary",), collective_id=5, has_side_effects=True, vmem_limit_bytes=VMEM_LIMIT
        ),
        cost_estimate=estimate(8),
        name="mid_backward",
    )(gproj, xproj, gact, mixed, head, low, taps, shift, rank_part, gpre, ggate, gdecay, gskip, ginit)


def unpack_kernel(layers, places, seqs, *refs):
    smalls, gains, outs = refs[: 2 * layers], refs[2 * layers : 4 * layers], refs[4 * layers :]
    gain, taps, shift, xproj, dtproj, bias, decay, skip, conv, init = outs
    for i in range(layers):
        def rows(name):
            first, last = places[name]
            return smalls[2 * i][first:last, :].astype(F32) + smalls[2 * i + 1][first:last, :].astype(F32)

        gain[i : i + 1, :] = gains[2 * i][0:1, :].astype(F32) + gains[2 * i + 1][0:1, :].astype(F32)
        xproj[i], dtproj[i], decay[i] = rows("xproj"), rows("dtproj"), rows("decay")
        init[i] = rows("init")
        low, high = places["taps"][0], smalls[0].shape[0]
        rest = smalls[2 * i][low:high, :].astype(F32) + smalls[2 * i + 1][low:high, :].astype(F32)

        def of(name):
            first, last = places[name]
            return rest[first - low : last - low, :]

        taps[i] = of("taps")
        shift[i : i + 1, :], bias[i : i + 1, :], skip[i : i + 1, :] = of("shift"), of("bias"), of("skip")
        for k in range(conv.shape[1]):
            conv[i, k] = of("conv")[k * seqs : (k + 1) * seqs, :]


def unpack(smalls, gains, places, seqs, width):
    layers = len(smalls)
    chans = smalls[0][0].shape[1]

    def size(name):
        return places[name][1] - places[name][0]

    shapes = [
        (layers, width), (layers, size("taps"), chans), (layers, chans), (layers, size("xproj"), chans),
        (layers, size("dtproj"), chans), (layers, chans), (layers, size("decay"), chans), (layers, chans),
        (layers, size("conv") // seqs, seqs, chans), (layers, size("init"), chans),
    ]
    args = [value for pair in smalls for value in pair] + [value for pair in gains for value in pair]
    return pl.pallas_call(
        functools.partial(unpack_kernel, layers, places, seqs),
        in_specs=whole(len(args)),
        out_specs=whole(len(shapes)),
        out_shape=[jax.ShapeDtypeStruct(shape, F32) for shape in shapes],
        compiler_params=params(),
        cost_estimate=estimate(3),
        name="unpack",
    )(*args)


def passed_along(value, axis, by):
    peers = lax.axis_size(axis)
    pairs = [(i, i + by) for i in range(peers) if 0 <= i + by < peers]
    return lax.ppermute(value, axis, pairs)


def to_segments(value):
    seqs, tokens, width = value.shape
    return value.reshape(seqs, G, tokens // G, width).transpose(0, 2, 1, 3)


def from_segments(value):
    seqs, length, _, width = value.shape
    return value.transpose(0, 2, 1, 3).reshape(seqs, length * G, width)


def local(
    hidden_in,
    norm_gain,
    in_weight,
    conv_weight,
    conv_bias,
    xproj_weight,
    dtproj_weight,
    dt_bias,
    decay_log,
    skip_gain,
    out_weight,
    conv_state,
    scan_state,
    out_cotangent,
):
    layers = in_weight.shape[0]
    rank = dtproj_weight.shape[1]
    states = decay_log.shape[1]
    seqs, tokens, _ = hidden_in.shape
    length = tokens // G
    rows = seqs * tokens
    chans = in_weight.shape[3]
    model = hidden_in.shape[2] * lax.axis_size("chan")
    taps = conv_weight.shape[1]
    is_first = lax.axis_index("seq") == 0

    flat_all = in_weight.reshape(layers, model, -1)
    first = to_segments(hidden_in).reshape(rows, -1)
    hidden = first.astype(F32)
    grad = to_segments(out_cotangent).reshape(rows, -1)
    grad_rows = lax.all_gather(grad, "chan", axis=1, tiled=True)
    grad = grad.astype(F32)
    full, gains = gather_first(first, norm_gain)
    saved = []
    for i in range(layers):
        wide = full[:rows].astype(F32)
        inverse = lax.rsqrt(jnp.sum(wide * wide, axis=1, keepdims=True) / model + EPS)
        normed = (wide * inverse * gains[i]).astype(BF16)
        flat_in = flat_all[i]
        mixed = dot(normed, flat_in, ((1,), (0,)))
        inner = mixed[:, :chans].reshape(seqs, length, G, chans)
        gate = mixed[:, chans:].reshape(seqs, length, G, chans)
        tail = inner[:, length - taps + 1 :]
        received = passed_along(tail[:, :, G - 1], "seq", 1)
        before = jnp.where(is_first, conv_state[i], received)
        head = jnp.concatenate([before[:, :, None], tail[:, :, : G - 1]], axis=2)
        padded = jnp.concatenate([head, inner], axis=1)
        pre = conv_bias[i] + sum(conv_weight[i, k] * padded[:, k : k + length] for k in range(taps))
        act = jax.nn.silu(pre)
        act_low = act.astype(BF16).reshape(rows, chans)
        projected = sum_chan(dot(act_low, xproj_weight[i], ((1,), (0,))).astype(BF16))
        rank_part = projected[:, :rank]
        maps = projected[:, rank:].reshape(seqs, tokens, 2 * states)
        delta = dot(rank_part, dtproj_weight[i], ((1,), (0,))) + dt_bias[i]
        delta = delta.reshape(seqs, length, G, chans)
        step = jax.nn.softplus(delta)
        prefix, span, pack = scan_ends(act, step, maps, decay_log[i])
        packs = lax.all_gather(pack, "seq")
        y, gated, start = scan_forward(
            act, step, gate, maps, decay_log[i], prefix, span, packs, scan_state[i], skip_gain[i : i + 1]
        )
        gated = gated.reshape(rows, chans)
        branch = dot(gated, out_weight[i], ((1,), (0,))).astype(BF16)
        saved.append(
            (hidden, inverse, normed, flat_in, mixed, gate, head, act, act_low, rank_part, maps, delta, step,
             span, packs, y, gated, start)
        )
        if i + 1 < layers:
            hidden, full = forward_boundary(branch, hidden)
        else:
            branch_sum = lax.psum_scatter(branch, "chan", scatter_dimension=1, tiled=True)

    def finish(i, sums):
        nonlocal in_grads, out_grads
        in_grads = place(
            place_pairs_kernel, [*sums["inner"].total(), *sums["gate"].total()], in_grads, i, layers, model // 8, (2,)
        )
        out_grads = place(place_rows_kernel, list(sums["out"].total()), out_grads, i, layers, chans // 4, ())

    smalls = [None] * layers
    in_grads = out_grads = None
    before_sums = None
    for i in reversed(range(layers)):
        (hidden_i, inverse, normed, flat_in, mixed, gate, head, act, act_low, rank_part, maps, delta, step,
         span, packs, y, gated, start) = saved[i]
        sums = {}
        sums["out"] = Summed(dot(gated, grad_rows, ((0,), (0,))).astype(BF16), True)
        grad_gated = dot(grad_rows, out_weight[i], ((1,), (1,)))
        grad_gated = grad_gated.reshape(seqs, length, G, chans)
        suffix, back_pack = scan_adjoint(step, gate, grad_gated, maps, decay_log[i], span)
        back_packs = after(lax.all_gather(back_pack, "seq"), sums["out"])
        sums["out"].across()
        scanned = scan_backward(
            act, step, delta, gate, y, grad_gated, maps, decay_log[i], start, suffix, span, back_packs, packs,
            skip_gain[i : i + 1],
        )
        gact, gpre, ggate, gmaps, gdecay, gskip, ginit = after(scanned, sums["out"])
        sums["out"].step()
        gpre = gpre.reshape(rows, chans)
        ggate = ggate.reshape(rows, chans)
        grad_rank = dot(gpre, dtproj_weight[i], ((1,), (1,)))
        proj_part = jnp.concatenate([grad_rank, gmaps.reshape(rows, -1)[:, : 2 * states]], axis=1).astype(BF16)
        sums["gate"] = Summed(dot(normed, ggate, ((0,), (0,))).astype(BF16), True)
        grad_proj = sum_chan(proj_part)
        grad_proj = after(grad_proj, sums["gate"], sums["out"])
        sums["gate"].across()
        gmixed, packed = mid_backward(
            grad_proj, xproj_weight[i].T, gact, mixed.reshape(seqs, length, G, -1), head, act_low, conv_weight[i],
            conv_bias[i : i + 1], rank_part, gpre, ggate, gdecay, gskip, ginit,
        )
        sums["small"] = Summed(packed, False)
        sums["inner"] = Summed(dot(normed, gmixed[:, :chans], ((0,), (0,))).astype(BF16), True)
        inner_sums = jnp.sum(gmixed.astype(F32) * mixed, axis=1)
        gnormed = dot(gmixed, flat_in, ((1,), (1,))).astype(BF16)
        gnormed = after(gnormed, sums["inner"], sums["small"])
        sums["inner"].across()
        sums["small"].across()
        outs = backward_boundary(gnormed, grad, hidden_i, inverse, norm_gain[i : i + 1], inner_sums, i > 0)
        if i == layers - 1:
            outs, branch_sum = lax.optimization_barrier((outs, branch_sum))
            hidden = hidden + branch_sum.astype(F32)
        outs = after(outs, sums["gate"], sums["inner"], sums["small"])
        grad = outs[0]
        if i > 0:
            grad_rows = outs[2]
        sums["gate"].step()
        sums["inner"].step()
        sums["gain"] = Summed(outs[1].astype(BF16), False)
        smalls[i] = sums
        if before_sums is not None:
            finish(i + 1, before_sums)
        before_sums = sums
    finish(0, before_sums)
    places, _ = rows_of_packed(xproj_weight.shape[2], rank, states, seqs, taps)
    gain, taps_grad, shift, xproj, dtproj, bias, decay, skip, conv, init = unpack(
        [one["small"].last() for one in smalls], [one["gain"].last() for one in smalls], places, seqs,
        norm_gain.shape[1],
    )

    def back_out(value):
        return from_segments(value.reshape(seqs, length, G, -1))

    return (
        back_out(hidden),
        back_out(grad),
        gain,
        in_grads,
        taps_grad,
        shift,
        xproj.transpose(0, 2, 1),
        dtproj,
        bias,
        decay,
        skip,
        out_grads,
        conv.transpose(0, 2, 1, 3),
        init.reshape(scan_state.shape),
    )


def solution(mesh):
    return jax.shard_map(
        local,
        mesh=mesh,
        in_specs=(
            P(None, "seq", "chan"),
            P(None, "chan"),
            P(None, None, None, "chan"),
            P(None, None, "chan"),
            P(None, "chan"),
            P(None, "chan", None),
            P(None, None, "chan"),
            P(None, "chan"),
            P(None, None, "chan"),
            P(None, "chan"),
            P(None, "chan", None),
            P(None, None, None, "chan"),
            P(None, None, None, "chan"),
            P(None, "seq", "chan"),
        ),
        out_specs=(
            P(None, "seq", "chan"),
            P(None, "seq", "chan"),
            P(None, "chan"),
            P(None, None, None, "chan"),
            P(None, None, "chan"),
            P(None, "chan"),
            P(None, "chan", None),
            P(None, None, "chan"),
            P(None, "chan"),
            P(None, None, "chan"),
            P(None, "chan"),
            P(None, "chan", None),
            P(None, None, None, "chan"),
            P(None, None, None, "chan"),
        ),
        check_vma=False,
    )
```

```python
import functools
import math

import jax
import jax.numpy as jnp
from jax import lax
from jax.experimental import pallas as pl
from jax.experimental.pallas import tpu as pltpu
from jax.sharding import PartitionSpec as P

EPS = 1e-05
G = 8
LANES = 128
LOG2E = 1.4426950408889634
LN2 = 0.6931471805599453
F32 = jnp.float32
BF16 = jnp.bfloat16
VMEM_LIMIT = 48 * 1024 * 1024
MESH = pl.DeviceIdType.MESH


def params(*semantics):
    return pltpu.CompilerParams(dimension_semantics=semantics, vmem_limit_bytes=VMEM_LIMIT)


def spread_maps(maps_ref, first, count, out_ref):
    shape = (maps_ref.shape[2], count * LANES)
    row = lax.broadcasted_iota(jnp.int32, shape, 0)
    col = lax.broadcasted_iota(jnp.int32, shape, 1) // LANES
    choice = jnp.where(row == col + first, 1.0, 0.0).astype(BF16)
    out_ref[...] = jnp.dot(maps_ref[0], choice, preferred_element_type=F32)


def part(ref, l, n):
    return ref[pl.ds(pl.multiple_of(l * G, G), G), n * LANES : (n + 1) * LANES]


def spread_rate(decay_ref, rate_ref):
    rate = jnp.exp(decay_ref[...]) * (-LOG2E)
    for n in range(rate.shape[0]):
        rate_ref[n] = jnp.broadcast_to(rate[n : n + 1, :], (G, LANES))


def shifted(value, by, fill):
    row = lax.broadcasted_iota(jnp.int32, value.shape, 0)
    moved = pltpu.roll(value, by % G, 0)
    inside = row >= by if by > 0 else row < G + by
    return jnp.where(inside, moved, fill)


def segment_prefix(ends, span, rate_ref, direction):
    step = 1
    while step < G:
        moved_span = shifted(span, direction * step, 0.0)
        ends = [
            e + jnp.exp2(span * rate_ref[n]) * shifted(e, direction * step, 0.0)
            for n, e in enumerate(ends)
        ]
        span = span + moved_span
        step *= 2
    return ends, span


class SeqExchange:
    def __init__(self, give_ref, got_ref, send_sem, recv_sem):
        self.refs = give_ref, got_ref
        self.sems = send_sem, recv_sem
        self.me, self.peers = lax.axis_index("seq"), lax.axis_size("seq")
        self.others = [lax.rem(self.me + k, self.peers) for k in range(1, self.peers)]

    def signal(self):
        barrier = pltpu.get_barrier_semaphore()
        for other in self.others:
            pl.semaphore_signal(barrier, inc=1, device_id={"seq": other}, device_id_type=MESH)

    def meet(self):
        if self.others:
            pl.semaphore_wait(pltpu.get_barrier_semaphore(), len(self.others))

    def copy(self, step, k):
        give, got = self.refs
        send, recv = self.sems
        return pltpu.make_async_remote_copy(
            src_ref=give.at[step], dst_ref=got.at[self.me, step], send_sem=send.at[step, k], recv_sem=recv.at[step, k],
            device_id={"seq": self.others[k]}, device_id_type=MESH,
        )

    def start(self, step):
        for k in range(len(self.others)):
            self.copy(step, k).start()

    def finish(self, steps):
        for step in range(steps):
            for k in range(len(self.others)):
                self.copy(step, k).wait()


def exchange_scratch(steps, rows):
    peers = lax.axis_size("seq")
    sems = pltpu.SemaphoreType.DMA((steps, max(peers - 1, 1)))
    return [pltpu.VMEM((steps, rows, LANES), F32), pltpu.VMEM((peers, steps, rows, LANES), F32), sems, sems]


def exchange_params(ident):
    return pltpu.CompilerParams(
        dimension_semantics=("arbitrary", "arbitrary"), collective_id=ident, has_side_effects=True,
        vmem_limit_bytes=VMEM_LIMIT,
    )


def exchange_step(exchange, packs_ref, give_ref, got_ref, rows):
    seqs, tiles = pl.num_programs(0), pl.num_programs(1)
    step = pl.program_id(0) * tiles + pl.program_id(1)
    total = give_ref.shape[0]
    wide = packs_ref.shape[3] // LANES
    give_ref[step] = rows
    pl.when(step == 0)(exchange.meet)
    exchange.start(step)

    @pl.when(step == total - 1)
    def _():
        exchange.finish(total)
        for i in range(total):
            for d in range(got_ref.shape[0]):
                packs_ref[d, i // wide, :, (i % wide) * LANES : (i % wide + 1) * LANES] = jnp.where(
                    exchange.me == d, give_ref[i], got_ref[d, i]
                )


def ends_kernel(
    act_ref, step_ref, maps_ref, decay_ref, prefix_ref, span_ref, packs_ref, b_ref, rate_ref, give_ref, got_ref, *sems
):
    length, states = act_ref.shape[1], decay_ref.shape[0]
    exchange = SeqExchange(give_ref, got_ref, *sems)
    pl.when(pl.program_id(0) + pl.program_id(1) == 0)(exchange.signal)

    @pl.when(pl.program_id(1) == 0)
    def _():
        spread_maps(maps_ref, 0, states, b_ref)

    spread_rate(decay_ref, rate_ref)

    def one(l, carry):
        h, total = carry
        st = step_ref[0, l]
        u = st * act_ref[0, l]
        h = tuple(
            jnp.exp2(st * rate_ref[n]) * h[n] + u * part(b_ref, l, n) for n in range(states)
        )
        return h, total + st

    zero = jnp.zeros((G, LANES), F32)
    h, total = lax.fori_loop(0, length, one, ((zero,) * states, zero), unroll=math.gcd(length, 8))
    ends, span = segment_prefix(list(h), total, rate_ref, 1)
    for n in range(states):
        prefix_ref[0, n] = shifted(ends[n], 1, 0.0)
    span_ref[0, 0] = shifted(span, 1, 0.0)
    span_ref[0, 1] = jnp.broadcast_to(span[G - 1 : G, :], (G, LANES)) - span
    rows = [e[G - 1 : G, :] for e in ends] + [jnp.broadcast_to(span[G - 1 : G, :], (8, LANES))]
    exchange_step(exchange, packs_ref, give_ref, got_ref, jnp.concatenate(rows, axis=0))


def scan_ends(act, step, maps, decay):
    seqs, length, _, chans = act.shape
    states = decay.shape[0]
    peers = lax.axis_size("seq")
    token = pl.BlockSpec((1, length, G, LANES), lambda s, j: (s, 0, 0, j))
    return pl.pallas_call(
        ends_kernel,
        grid=(seqs, chans // LANES),
        in_specs=[
            token,
            token,
            pl.BlockSpec((1, length * G, maps.shape[2]), lambda s, j: (s, 0, 0)),
            pl.BlockSpec((states, LANES), lambda s, j: (0, j)),
        ],
        out_specs=[
            pl.BlockSpec((1, states, G, LANES), lambda s, j: (s, 0, 0, j)),
            pl.BlockSpec((1, 2, G, LANES), lambda s, j: (s, 0, 0, j)),
            pl.BlockSpec((peers, seqs, states + 8, chans), lambda s, j: (0, 0, 0, 0)),
        ],
        out_shape=[
            jax.ShapeDtypeStruct((seqs, states, G, chans), F32),
            jax.ShapeDtypeStruct((seqs, 2, G, chans), F32),
            jax.ShapeDtypeStruct((peers, seqs, states + 8, chans), F32),
        ],
        scratch_shapes=[
            pltpu.VMEM((length * G, states * LANES), F32),
            pltpu.VMEM((states, G, LANES), F32),
        ]
        + exchange_scratch(seqs * chans // LANES, states + 8),
        compiler_params=exchange_params(6),
        cost_estimate=estimate(12),
        name="scan_ends",
    )(act, step, maps, decay)


def forward_kernel(
    act_ref, step_ref, gate_ref, maps_ref, decay_ref, prefix_ref, span_ref, packs_ref, init_ref, skip_ref,
    y_ref, gated_ref, start_ref, b_ref, c_ref, rate_ref,
):
    length, states = act_ref.shape[1], decay_ref.shape[0]

    @pl.when(pl.program_id(1) == 0)
    def _():
        spread_maps(maps_ref, 0, states, b_ref)
        spread_maps(maps_ref, states, states, c_ref)

    spread_rate(decay_ref, rate_ref)
    rate = jnp.exp(decay_ref[...]) * (-LOG2E)
    me = lax.axis_index("seq")
    entry = init_ref[0]
    for d in range(packs_ref.shape[0]):
        joined = jnp.exp2(rate * packs_ref[d, 0, states : states + 1, :]) * entry + packs_ref[d, 0, :states, :]
        entry = jnp.where(d < me, joined, entry)
    span = span_ref[0, 0]
    h = []
    for n in range(states):
        first = prefix_ref[0, n] + jnp.exp2(rate_ref[n] * span) * entry[n : n + 1, :]
        start_ref[0, n] = first
        h.append(first)
    skip = jnp.broadcast_to(skip_ref[...], (G, LANES))

    def one(k, h):
        h = list(h)
        halves = []
        for i in range(2):
            l = 2 * k + i
            st = step_ref[0, l]
            act = act_ref[0, l]
            u = st * act
            y = skip * act
            for n in range(states):
                h[n] = jnp.exp2(st * rate_ref[n]) * h[n] + u * part(b_ref, l, n)
                y = y + part(c_ref, l, n) * h[n]
            y_ref[0, l] = y
            gate = gate_ref[0, l]
            halves.append(y * (gate / (1.0 + jnp.exp(-gate))))
        gated_ref[0, pl.ds(pl.multiple_of(k * 2 * G, 2 * G), 2 * G), :] = jnp.concatenate(halves, axis=0).astype(BF16)
        return tuple(h)

    lax.fori_loop(0, length // 2, one, tuple(h), unroll=math.gcd(length // 2, 4))


def scan_forward(act, step, gate, maps, decay, prefix, span, packs, init, skip):
    seqs, length, _, chans = act.shape
    states = decay.shape[0]
    token = pl.BlockSpec((1, length, G, LANES), lambda s, j: (s, 0, 0, j))
    per_state = pl.BlockSpec((1, states, G, LANES), lambda s, j: (s, 0, 0, j))
    return pl.pallas_call(
        forward_kernel,
        grid=(seqs, chans // LANES),
        in_specs=[
            token,
            token,
            token,
            pl.BlockSpec((1, length * G, maps.shape[2]), lambda s, j: (s, 0, 0)),
            pl.BlockSpec((states, LANES), lambda s, j: (0, j)),
            per_state,
            pl.BlockSpec((1, 2, G, LANES), lambda s, j: (s, 0, 0, j)),
            pl.BlockSpec((packs.shape[0], 1, states + 8, LANES), lambda s, j: (0, s, 0, j)),
            pl.BlockSpec((1, states, LANES), lambda s, j: (s, 0, j)),
            pl.BlockSpec((1, LANES), lambda s, j: (0, j)),
        ],
        out_specs=[
            token,
            pl.BlockSpec((1, length * G, LANES), lambda s, j: (s, 0, j)),
            per_state,
        ],
        out_shape=[
            jax.ShapeDtypeStruct(act.shape, F32),
            jax.ShapeDtypeStruct((seqs, length * G, chans), BF16),
            jax.ShapeDtypeStruct((seqs, states, G, chans), F32),
        ],
        scratch_shapes=[
            pltpu.VMEM((length * G, states * LANES), F32),
            pltpu.VMEM((length * G, states * LANES), F32),
            pltpu.VMEM((states, G, LANES), F32),
        ],
        compiler_params=params("arbitrary", "arbitrary"),
        cost_estimate=estimate(20),
        name="scan_forward",
    )(act, step, gate, maps, decay, prefix, span, packs, init, skip)


def adjoint_kernel(
    step_ref, gate_ref, grad_ref, maps_ref, decay_ref, span_ref, suffix_ref, packs_ref, c_ref, rate_ref, give_ref,
    got_ref, *sems,
):
    length, states = step_ref.shape[1], decay_ref.shape[0]
    exchange = SeqExchange(give_ref, got_ref, *sems)
    pl.when(pl.program_id(0) + pl.program_id(1) == 0)(exchange.signal)

    @pl.when(pl.program_id(1) == 0)
    def _():
        spread_maps(maps_ref, states, states, c_ref)

    spread_rate(decay_ref, rate_ref)

    def one(k, carry):
        l = length - 1 - k
        st = step_ref[0, l]
        gate = gate_ref[0, l]
        gy = grad_ref[0, l] * (gate / (1.0 + jnp.exp(-gate)))
        return tuple(
            jnp.exp2(st * rate_ref[n]) * (carry[n] + gy * part(c_ref, l, n)) for n in range(states)
        )

    zero = jnp.zeros((G, LANES), F32)
    carry = lax.fori_loop(0, length, one, (zero,) * states, unroll=math.gcd(length, 8))
    own = span_ref[0, 1, 0:1, :] + span_ref[0, 0, 1:2, :] - span_ref[0, 0] - span_ref[0, 1]
    ends, _ = segment_prefix(list(carry), own, rate_ref, -1)
    for n in range(states):
        suffix_ref[0, n] = shifted(ends[n], -1, 0.0)
    rows = jnp.concatenate([e[0:1, :] for e in ends], axis=0)
    exchange_step(exchange, packs_ref, give_ref, got_ref, rows)


def scan_adjoint(step, gate, grad, maps, decay, span):
    seqs, length, _, chans = step.shape
    states = decay.shape[0]
    peers = lax.axis_size("seq")
    token = pl.BlockSpec((1, length, G, LANES), lambda s, j: (s, 0, 0, j))
    return pl.pallas_call(
        adjoint_kernel,
        grid=(seqs, chans // LANES),
        in_specs=[
            token,
            token,
            token,
            pl.BlockSpec((1, length * G, maps.shape[2]), lambda s, j: (s, 0, 0)),
            pl.BlockSpec((states, LANES), lambda s, j: (0, j)),
            pl.BlockSpec((1, 2, G, LANES), lambda s, j: (s, 0, 0, j)),
        ],
        out_specs=[
            pl.BlockSpec((1, states, G, LANES), lambda s, j: (s, 0, 0, j)),
            pl.BlockSpec((peers, seqs, states, chans), lambda s, j: (0, 0, 0, 0)),
        ],
        out_shape=[
            jax.ShapeDtypeStruct((seqs, states, G, chans), F32),
            jax.ShapeDtypeStruct((peers, seqs, states, chans), F32),
        ],
        scratch_shapes=[
            pltpu.VMEM((length * G, states * LANES), F32),
            pltpu.VMEM((states, G, LANES), F32),
        ]
        + exchange_scratch(seqs * chans // LANES, states),
        compiler_params=exchange_params(7),
        cost_estimate=estimate(15),
        name="scan_adjoint",
    )(step, gate, grad, maps, decay, span)


def backward_kernel(
    act_ref, step_ref, delta_ref, gate_ref, y_ref, grad_ref, maps_ref, decay_ref, start_ref, suffix_ref, span_ref,
    packs_ref, forward_packs_ref, skip_ref,
    gact_ref, gpre_ref, ggate_ref, gmaps_ref, gdecay_ref, gskip_ref, ginit_ref,
    b_ref, c_ref, rate_ref, h_ref, product_ref, select_ref,
):
    length, states = act_ref.shape[1], decay_ref.shape[0]
    wide = states * LANES

    @pl.when(pl.program_id(1) == 0)
    def _():
        spread_maps(maps_ref, 0, states, b_ref)
        spread_maps(maps_ref, states, states, c_ref)
        row = lax.broadcasted_iota(jnp.int32, select_ref.shape, 0) // LANES
        col = lax.broadcasted_iota(jnp.int32, select_ref.shape, 1)
        product_ref[...] = jnp.zeros_like(product_ref)
        select_ref[...] = jnp.where(row == col, 1.0, 0.0).astype(BF16)

    spread_rate(decay_ref, rate_ref)
    rate = jnp.exp(decay_ref[...]) * (-LOG2E)
    me = lax.axis_index("seq")
    count = packs_ref.shape[0]
    entry = jnp.zeros((states, LANES), F32)
    for d in reversed(range(count)):
        joined = jnp.exp2(rate * forward_packs_ref[d, 0, states : states + 1, :]) * entry + packs_ref[d, 0]
        entry = jnp.where(d > me, joined, entry)
    after = span_ref[0, 1]
    skip = jnp.broadcast_to(skip_ref[...], (G, LANES))

    def forward(l, h):
        st = step_ref[0, l]
        u = st * act_ref[0, l]
        for n in range(states):
            h_ref[l, n] = h[n]
        return tuple(
            jnp.exp2(st * rate_ref[n]) * h[n] + u * part(b_ref, l, n) for n in range(states)
        )

    h = lax.fori_loop(
        0, length, forward, tuple(start_ref[0, n] for n in range(states)), unroll=math.gcd(length, 4)
    )
    for n in range(states):
        h_ref[length, n] = h[n]

    def back(k, state):
        carry, gdecay, gskip = list(state[0]), list(state[1]), state[2]
        lines = [length - 1 - 2 * k, length - 2 - 2 * k]
        st, act, u, gy, q, r = [], [], [], [], [], []
        ggate = []
        for l in lines:
            st.append(step_ref[0, l])
            act.append(act_ref[0, l])
            u.append(st[-1] * act[-1])
            gate = gate_ref[0, l]
            grad = grad_ref[0, l]
            sig = 1.0 / (1.0 + jnp.exp(-gate))
            silu = gate * sig
            gy.append(grad * silu)
            ggate.append(grad * y_ref[0, l] * (sig + silu * (1.0 - sig)))
            gskip = gskip + gy[-1] * act[-1]
            q.append(jnp.zeros((G, LANES), F32))
            r.append(jnp.zeros((G, LANES), F32))
        row = pl.multiple_of((length - 2 - 2 * k) * G, 2 * G)
        for n in range(states):
            late, early = [], []
            for i, l in enumerate(lines):
                lam = part(c_ref, l, n) * gy[i] + carry[n]
                early.append(lam * u[i])
                late.append(gy[i] * h_ref[l + 1, n])
                q[i] = q[i] + lam * part(b_ref, l, n)
                carry[n] = jnp.exp2(st[i] * rate_ref[n]) * lam
                w = carry[n] * h_ref[l, n]
                r[i] = r[i] + rate_ref[n] * w
                gdecay[n] = gdecay[n] + st[i] * w
            product_ref[pl.ds(row, 2 * G), n * LANES : (n + 1) * LANES] += jnp.concatenate(early[::-1], axis=0)
            product_ref[pl.ds(row, 2 * G), wide + n * LANES : wide + (n + 1) * LANES] += jnp.concatenate(late[::-1], axis=0)
        gpre = []
        for i, l in enumerate(lines):
            gact_ref[0, l] = skip * gy[i] + st[i] * q[i]
            gstep = LN2 * r[i] + act[i] * q[i]
            gpre.append(gstep / (1.0 + jnp.exp(-delta_ref[0, l])))
        gpre_ref[0, pl.ds(row, 2 * G), :] = jnp.concatenate(gpre[::-1], axis=0).astype(BF16)
        ggate_ref[0, pl.ds(row, 2 * G), :] = jnp.concatenate(ggate[::-1], axis=0).astype(BF16)
        return tuple(carry), tuple(gdecay), gskip

    zero = jnp.zeros((G, LANES), F32)
    first = tuple(
        suffix_ref[0, n] + jnp.exp2(rate_ref[n] * after) * entry[n : n + 1, :] for n in range(states)
    )
    carry, gdecay, gskip = lax.fori_loop(
        0, length // 2, back, (first, (zero,) * states, zero), unroll=math.gcd(length // 2, 2)
    )
    for n in range(states):
        ginit_ref[0, n : n + 1, :] = carry[n][0:1, :]
        total = jnp.sum(gdecay[n] * rate_ref[n], axis=0, keepdims=True)
        gdecay_ref[0, n : n + 1, :] = total * LN2
    gskip_ref[0] = jnp.broadcast_to(jnp.sum(gskip, axis=0, keepdims=True), (8, LANES))

    @pl.when(pl.program_id(1) == pl.num_programs(1) - 1)
    def _():
        gmaps_ref[0] = jnp.dot(product_ref[...].astype(BF16), select_ref[...], preferred_element_type=F32)


def scan_backward(act, step, delta, gate, y, grad, maps, decay, start, suffix, span, packs, forward_packs, skip):
    seqs, length, _, chans = act.shape
    states = decay.shape[0]
    token = pl.BlockSpec((1, length, G, LANES), lambda s, j: (s, 0, 0, j))
    rows = pl.BlockSpec((1, length * G, LANES), lambda s, j: (s, 0, j))
    per_state = pl.BlockSpec((1, states, G, LANES), lambda s, j: (s, 0, 0, j))
    total = pl.BlockSpec((1, states, LANES), lambda s, j: (s, 0, j))
    return pl.pallas_call(
        backward_kernel,
        grid=(seqs, chans // LANES),
        in_specs=[
            token,
            token,
            token,
            token,
            token,
            token,
            pl.BlockSpec((1, length * G, maps.shape[2]), lambda s, j: (s, 0, 0)),
            pl.BlockSpec((states, LANES), lambda s, j: (0, j)),
            per_state,
            per_state,
            pl.BlockSpec((1, 2, G, LANES), lambda s, j: (s, 0, 0, j)),
            pl.BlockSpec((packs.shape[0], 1, states, LANES), lambda s, j: (0, s, 0, j)),
            pl.BlockSpec((packs.shape[0], 1, states + 8, LANES), lambda s, j: (0, s, 0, j)),
            pl.BlockSpec((1, LANES), lambda s, j: (0, j)),
        ],
        out_specs=[
            token,
            rows,
            rows,
            pl.BlockSpec((1, length * G, LANES), lambda s, j: (s, 0, 0)),
            total,
            pl.BlockSpec((1, 8, LANES), lambda s, j: (s, 0, j)),
            total,
        ],
        out_shape=[
            jax.ShapeDtypeStruct(act.shape, F32),
            jax.ShapeDtypeStruct((seqs, length * G, chans), BF16),
            jax.ShapeDtypeStruct((seqs, length * G, chans), BF16),
            jax.ShapeDtypeStruct((seqs, length * G, LANES), F32),
            jax.ShapeDtypeStruct((seqs, states, chans), F32),
            jax.ShapeDtypeStruct((seqs, 8, chans), F32),
            jax.ShapeDtypeStruct((seqs, states, chans), F32),
        ],
        scratch_shapes=[
            pltpu.VMEM((length * G, states * LANES), F32),
            pltpu.VMEM((length * G, states * LANES), F32),
            pltpu.VMEM((states, G, LANES), F32),
            pltpu.VMEM((length + 1, states, G, LANES), F32),
            pltpu.VMEM((length * G, 2 * states * LANES), F32),
            pltpu.VMEM((2 * states * LANES, LANES), BF16),
        ],
        compiler_params=params("arbitrary", "arbitrary"),
        cost_estimate=estimate(39),
        name="scan_backward",
    )(act, step, delta, gate, y, grad, maps, decay, start, suffix, span, packs, forward_packs, skip)


def remote(src, dst, send, recv, to):
    return pltpu.make_async_remote_copy(
        src_ref=src, dst_ref=dst, send_sem=send, recv_sem=recv, device_id={"chan": to}, device_id_type=MESH
    )


class Line:
    def __init__(self, count):
        self.me = lax.axis_index("chan")
        self.half = count // 2
        self.at = self.me // 2
        self.low = self.me % 2
        self.pair = self.at * 2 + 1 - self.low
        self.right = jnp.minimum(self.at + 1, self.half - 1) * 2 + self.low
        self.left = jnp.maximum(self.at - 1, 0) * 2 + self.low
        self.has_right = self.at < self.half - 1
        self.has_left = self.at > 0

    def greet(self):
        barrier = pltpu.get_barrier_semaphore()

        def signal(to):
            pl.semaphore_signal(barrier, inc=1, device_id={"chan": to}, device_id_type=MESH)

        signal(self.pair)
        pl.when(self.has_right)(lambda: signal(self.right))
        pl.when(self.has_left)(lambda: signal(self.left))
        pl.semaphore_wait(barrier, 1 + jnp.minimum(self.at, 1) + jnp.minimum(self.half - 1 - self.at, 1))


def gather_steps(line, out_ref, width, chunks, sems):
    pair_send, pair_recv, right_send, right_recv, left_send, left_recv = sems
    half = line.half
    rows = out_ref.shape[0] // chunks

    def place(owner, c):
        return out_ref.at[pl.ds(c * rows, rows), pl.ds(pl.multiple_of(owner * width, width), width)]

    def to_pair(owner, slot, c):
        return remote(place(owner, c), place(owner, c), pair_send.at[slot, c], pair_recv.at[slot, c], line.pair)

    def to_right(owner, j, c):
        return remote(place(owner, c), place(owner, c), right_send.at[j, c], right_recv.at[j, c], line.right)

    def to_left(owner, j, c):
        return remote(place(owner, c), place(owner, c), left_send.at[j, c], left_recv.at[j, c], line.left)

    def begin(c):
        pl.when(line.has_right)(lambda: to_right(line.me, 0, c).start())
        pl.when(line.has_left)(lambda: to_left(line.me, 0, c).start())
        to_pair(line.me, 0, c).start()

    def middle():
        for j in range(1, half):
            for c in range(chunks):
                @pl.when(line.at >= j)
                def _():
                    owner = line.me - 2 * j
                    to_right(owner, j - 1, c).wait_recv()
                    pl.when(line.has_right)(lambda: to_right(owner, j, c).start())
                    to_pair(owner, j, c).start()

                @pl.when(line.at + j < half)
                def _():
                    owner = line.me + 2 * j
                    to_left(owner, j - 1, c).wait_recv()
                    pl.when(line.has_left)(lambda: to_left(owner, j, c).start())
                    to_pair(owner, half + j, c).start()

    def end():
        for c in range(chunks):
            to_pair(line.me, 0, c).wait()
            pl.when(line.has_right)(lambda: to_right(line.me, 0, c).wait_send())
            pl.when(line.has_left)(lambda: to_left(line.me, 0, c).wait_send())
            for j in range(1, half):
                @pl.when(line.at >= j)
                def _():
                    owner = line.me - 2 * j
                    to_pair(owner, j, c).wait()
                    pl.when(line.has_right)(lambda: to_right(owner, j, c).wait_send())

                @pl.when(line.at + j < half)
                def _():
                    owner = line.me + 2 * j
                    to_pair(owner, half + j, c).wait()
                    pl.when(line.has_left)(lambda: to_left(owner, j, c).wait_send())

    return begin, middle, end


def gather_sems(count, chunks):
    half = count // 2
    return [pltpu.SemaphoreType.DMA((2 * half, chunks))] * 2 + [pltpu.SemaphoreType.DMA((half, chunks))] * 4


def estimate(us):
    return pl.CostEstimate(flops=int(us * 1e8), bytes_accessed=1 << 20, transcendentals=0)


def remote_params(ident):
    return pltpu.CompilerParams(collective_id=ident, has_side_effects=True, vmem_limit_bytes=VMEM_LIMIT)


def whole(count):
    return [pl.BlockSpec(memory_space=pltpu.VMEM)] * count


def chunks_of(rows):
    return next(c for c in (3, 2, 1) if rows % (16 * c) == 0)


def gather_kernel(count, chunks, part_ref, gain_ref, out_ref, *sems):
    line = Line(count)
    rows, width = part_ref.shape
    mine = pl.ds(pl.multiple_of(line.me * width, width), width)
    out_ref[:rows, mine] = part_ref[...]
    layers = gain_ref.shape[0]
    gain = gain_ref[...]
    terms = []
    for _ in range(3):
        term = gain.astype(BF16).astype(F32)
        terms.append(term)
        gain = gain - term
    terms.append(jnp.zeros((16 - 3 * layers, width), F32))
    out_ref[rows:, mine] = jnp.concatenate(terms, axis=0).astype(BF16)
    line.greet()
    begin, middle, end = gather_steps(line, out_ref, width, chunks, sems)
    for c in range(chunks):
        begin(c)
    middle()
    end()


def gather_first(part, gain):
    count = lax.axis_size("chan")
    rows, width = part.shape
    layers = gain.shape[0]
    chunks = chunks_of(rows + 16)
    full = pl.pallas_call(
        functools.partial(gather_kernel, count, chunks),
        in_specs=whole(2),
        out_specs=whole(1)[0],
        out_shape=jax.ShapeDtypeStruct((rows + 16, count * width), BF16),
        scratch_shapes=gather_sems(count, chunks),
        compiler_params=remote_params(0),
        cost_estimate=estimate(25),
        name="gather_first",
    )(part, gain)
    terms = full[rows : rows + 3 * layers].astype(F32)
    return full, terms[:layers] + terms[layers : 2 * layers] + terms[2 * layers :]


def scatter_steps(line, part_ref, pair_buf, right_buf, left_buf, stage, width, chunks, sems):
    pair_send, pair_recv, right_send, right_recv, left_send, left_recv = sems
    half = line.half
    rows = part_ref.shape[0] // chunks

    def block(owner, c):
        return part_ref.at[pl.ds(c * rows, rows), pl.ds(pl.multiple_of(owner * width, width), width)]

    def piece(ref, slot, c):
        return ref.at[slot, pl.ds(c * rows, rows)]

    def to_pair(at, c):
        return remote(block(at * 2 + 1 - line.low, c), pair_buf.at[at, pl.ds(c * rows, rows)], pair_send.at[at, c], pair_recv.at[at, c], line.pair)

    def to_right(j, c):
        return remote(piece(stage, j, c), piece(right_buf, j - 1, c), right_send.at[j - 1, c], right_recv.at[j - 1, c], line.right)

    def to_left(j, c):
        return remote(piece(stage, half + j, c), piece(left_buf, j - 1, c), left_send.at[j - 1, c], left_recv.at[j - 1, c], line.left)

    def begin(produce):
        for c in range(chunks):

            def send(at):
                if c == 0:
                    produce(at * 2 + 1 - line.low)
                to_pair(at, c).start()

            for j in range(half - 1, 0, -1):
                pl.when(line.at + j < half)(lambda: send(line.at + j))
                pl.when(line.at >= j)(lambda: send(line.at - j))
            send(line.at)
        for at in range(half):
            produce(at * 2 + line.low)

    def own_and_pair(at, c):
        to_pair(at, c).wait_recv()
        return block(at * 2 + line.low, c)[...].astype(F32) + pair_buf[at, pl.ds(c * rows, rows)].astype(F32)

    def middle(c):
        for j in range(half - 1, 0, -1):
            @pl.when(line.at + j < half)
            def _():
                stage[j, pl.ds(c * rows, rows)] = own_and_pair(line.at + j, c).astype(BF16)

                @pl.when(line.has_left)
                def _():
                    arrived = remote(piece(stage, j, c), piece(right_buf, j, c), right_send.at[j, c], right_recv.at[j, c], line.right)
                    arrived.wait_recv()
                    total = stage[j, pl.ds(c * rows, rows)].astype(F32) + right_buf[j, pl.ds(c * rows, rows)].astype(F32)
                    stage[j, pl.ds(c * rows, rows)] = total.astype(BF16)

                to_right(j, c).start()

            @pl.when(line.at >= j)
            def _():
                stage[half + j, pl.ds(c * rows, rows)] = own_and_pair(line.at - j, c).astype(BF16)

                @pl.when(line.has_right)
                def _():
                    arrived = remote(piece(stage, half + j, c), piece(left_buf, j, c), left_send.at[j, c], left_recv.at[j, c], line.left)
                    arrived.wait_recv()
                    total = stage[half + j, pl.ds(c * rows, rows)].astype(F32) + left_buf[j, pl.ds(c * rows, rows)].astype(F32)
                    stage[half + j, pl.ds(c * rows, rows)] = total.astype(BF16)

                to_left(j, c).start()

    def finish(c, out_ref):
        here = pl.ds(c * rows, rows)
        out_ref[here, :] = own_and_pair(line.at, c)

        @pl.when(line.has_left)
        def _():
            remote(piece(stage, 0, c), piece(right_buf, 0, c), right_send.at[0, c], right_recv.at[0, c], line.right).wait_recv()
            out_ref[here, :] += right_buf[0, here].astype(F32)

        @pl.when(line.has_right)
        def _():
            remote(piece(stage, 0, c), piece(left_buf, 0, c), left_send.at[0, c], left_recv.at[0, c], line.left).wait_recv()
            out_ref[here, :] += left_buf[0, here].astype(F32)

    def end():
        for c in range(chunks):
            for at in range(half):
                to_pair(at, c).wait_send()
            for j in range(1, half):
                pl.when(line.at + j < half)(lambda: to_right(j, c).wait_send())
                pl.when(line.at >= j)(lambda: to_left(j, c).wait_send())

    return begin, middle, finish, end


def scatter_scratch(count, chunks, rows, width):
    half = count // 2
    return (
        [pltpu.VMEM((half, rows, width), BF16)] * 3
        + [pltpu.VMEM((2 * half, rows, width), BF16)]
        + [pltpu.SemaphoreType.DMA((half, chunks))] * 6
    )


def boundary_kernel(
    count, chunks, layer, gated_ref, weights_ref, hidden_ref, new_ref, full_ref, pair_buf, right_buf, left_buf, stage,
    part_ref, weight_ref, weight_sem, *sems,
):
    line = Line(count)
    rows, width = hidden_ref.shape
    mine = pl.ds(pl.multiple_of(line.me * width, width), width)
    fetch = pltpu.make_async_copy(weights_ref.at[layer], weight_ref, weight_sem)
    fetch.start()
    line.greet()
    fetch.wait()

    def produce(owner):
        columns = pl.ds(pl.multiple_of(owner * width, width), width)
        block = jnp.dot(gated_ref[...], weight_ref[:, columns], preferred_element_type=F32)
        part_ref[:, columns] = block.astype(BF16)

    begin, middle, finish, end = scatter_steps(
        line, part_ref, pair_buf, right_buf, left_buf, stage, width, chunks, sems[:6]
    )
    gather_begin, gather_middle, gather_end = gather_steps(line, full_ref, width, chunks, sems[6:])
    begin(produce)
    for c in range(chunks):
        here = pl.ds(c * (rows // chunks), rows // chunks)
        middle(c)
        finish(c, new_ref)
        new_ref[here, :] += hidden_ref[here, :]
        full_ref[here, mine] = new_ref[here, :].astype(BF16)
        gather_begin(c)
    gather_middle()
    gather_end()
    end()


def forward_boundary(gated, weights, layer, hidden):
    count = lax.axis_size("chan")
    rows, width = hidden.shape
    chunks = 2
    return pl.pallas_call(
        functools.partial(boundary_kernel, count, chunks, layer),
        in_specs=[whole(1)[0], pl.BlockSpec(memory_space=pl.ANY), whole(1)[0]],
        out_specs=whole(2),
        out_shape=[jax.ShapeDtypeStruct((rows, width), F32), jax.ShapeDtypeStruct((rows, count * width), BF16)],
        scratch_shapes=scatter_scratch(count, chunks, rows, width)[:4]
        + [
            pltpu.VMEM((rows, count * width), BF16),
            pltpu.VMEM(weights.shape[1:], BF16),
            pltpu.SemaphoreType.DMA,
        ]
        + scatter_scratch(count, chunks, rows, width)[4:]
        + gather_sems(count, chunks),
        compiler_params=remote_params(1),
        cost_estimate=estimate(50),
        name="forward_boundary",
    )(gated, weights, hidden)


def back_kernel(
    count, chunks, gathers, layer, gmixed_ref, weights_ref, grad_ref, hidden_ref, inverse_ref, gain_ref, inner_ref, new_ref, ggain_ref, *more
):
    full_ref, more = (more[0], more[1:]) if gathers else (None, more)
    pair_buf, right_buf, left_buf, stage, inner_buf, column_ref, inner_send, inner_recv = more[:8]
    part_ref, weight_ref, weight_sem = more[8:11]
    sems = more[11:]
    fetch = pltpu.make_async_copy(weights_ref.at[layer], weight_ref, weight_sem)
    fetch.start()
    line = Line(count)
    rows, width = grad_ref.shape
    model = width * count
    mine = pl.ds(pl.multiple_of(line.me * width, width), width)
    others = [lax.rem(line.me + k, count) for k in range(1, count)]
    barrier = pltpu.get_barrier_semaphore()
    for other in others:
        pl.semaphore_signal(barrier, inc=1, device_id={"chan": other}, device_id_type=MESH)
    pl.semaphore_wait(barrier, count - 1)
    begin, middle, finish, end = scatter_steps(
        line, part_ref, pair_buf, right_buf, left_buf, stage, width, chunks, sems[:6]
    )
    if gathers:
        gather_begin, gather_middle, gather_end = gather_steps(line, full_ref, width, chunks, sems[6:])
    sums = [
        remote(inner_ref, inner_buf.at[k], inner_send.at[k], inner_recv.at[k], others[k]) for k in range(count - 1)
    ]
    for copy in sums:
        copy.start()
    fetch.wait()

    def produce(owner):
        features = pl.ds(pl.multiple_of(owner * width, width), width)
        part_ref[:, features] = dot(gmixed_ref[...], weight_ref[features, :], ((1,), (1,))).astype(BF16)

    begin(produce)
    eye = lax.broadcasted_iota(jnp.int32, (LANES, LANES), 0) == lax.broadcasted_iota(jnp.int32, (LANES, LANES), 1)
    ggain_ref[...] = jnp.zeros_like(ggain_ref)
    for c in range(chunks):
        here = pl.ds(c * (rows // chunks), rows // chunks)
        middle(c)
        if c == 0:
            inner = inner_ref[...]
            for k in range(count - 1):
                sums[k].wait_recv()
                inner = inner + inner_buf[k]
            for b in range(rows // LANES):
                column_ref[pl.ds(b * LANES, LANES), :] = jnp.sum(
                    jnp.where(eye, jnp.broadcast_to(inner[b : b + 1, :], (LANES, LANES)), 0.0), axis=1, keepdims=True
                )
        finish(c, new_ref)
        gnormed = new_ref[here, :]
        inverse = inverse_ref[here, :]
        hidden = hidden_ref[here, :]
        factor = inverse * inverse * column_ref[here, :] * (1.0 / model)
        ggain_ref[0:1, :] += jnp.sum(gnormed * hidden * inverse, axis=0, keepdims=True)
        new = grad_ref[here, :] + inverse * (gain_ref[...] * gnormed) - hidden * factor
        new_ref[here, :] = new
        if gathers:
            full_ref[here, mine] = new.astype(BF16)
            gather_begin(c)
    if gathers:
        gather_middle()
        gather_end()
    end()
    for copy in sums:
        copy.wait_send()


def backward_boundary(gmixed, weights, layer, grad, hidden, inverse, gain, inner, gathers):
    count = lax.axis_size("chan")
    rows, width = hidden.shape
    chunks = 2
    out_shape = [jax.ShapeDtypeStruct((rows, width), F32), jax.ShapeDtypeStruct((8, width), F32)]
    scratch = scatter_scratch(count, chunks, rows, width)
    scratch += [
        pltpu.VMEM((count - 1, rows // LANES, LANES), F32),
        pltpu.VMEM((rows, 1), F32),
        pltpu.SemaphoreType.DMA((count - 1,)),
        pltpu.SemaphoreType.DMA((count - 1,)),
    ]
    product = [
        pltpu.VMEM((rows, count * width), BF16),
        pltpu.VMEM(weights.shape[1:], BF16),
        pltpu.SemaphoreType.DMA,
    ]
    order = scratch[:4] + scratch[10:] + product + scratch[4:10]
    if gathers:
        out_shape.append(jax.ShapeDtypeStruct((rows, count * width), BF16))
        order += gather_sems(count, chunks)
    return pl.pallas_call(
        functools.partial(back_kernel, count, chunks, gathers, layer),
        in_specs=[whole(1)[0], pl.BlockSpec(memory_space=pl.ANY)] + whole(5),
        out_specs=whole(len(out_shape)),
        out_shape=out_shape,
        scratch_shapes=order,
        compiler_params=remote_params(2 if gathers else 3),
        cost_estimate=estimate(50 if gathers else 27),
        name="backward_boundary" if gathers else "backward_last",
    )(gmixed, weights, grad, hidden, inverse, gain, inner.reshape(rows // LANES, LANES))


def sum_kernel(count, part_ref, out_ref, arrived, total_ref, send1, recv1, send2, recv2):
    me = lax.axis_index("chan")
    rows = part_ref.shape[0] // count
    others = [lax.rem(me + k, count) for k in range(1, count)]
    barrier = pltpu.get_barrier_semaphore()
    for other in others:
        pl.semaphore_signal(barrier, inc=1, device_id={"chan": other}, device_id_type=MESH)
    pl.semaphore_wait(barrier, count - 1)

    def piece(ref, owner):
        return ref.at[pl.ds(pl.multiple_of(owner * rows, rows), rows)]

    first, second = [], []
    for k, other in enumerate(others):
        first.append(remote(piece(part_ref, other), arrived.at[k], send1.at[k], recv1.at[k], other))
        first[k].start()
    acc = piece(part_ref, me)[...].astype(F32)
    for k in range(count - 1):
        first[k].wait_recv()
        acc = acc + arrived[k].astype(F32)
    total_ref[...] = acc.astype(BF16)
    for k, other in enumerate(others):
        second.append(remote(total_ref, piece(out_ref, me), send2.at[k], recv2.at[k], other))
        second[k].start()
    piece(out_ref, me)[...] = total_ref[...]
    for copy in second:
        copy.wait()
    for copy in first:
        copy.wait_send()


def sum_chan(part):
    count = lax.axis_size("chan")
    rows, width = part.shape
    return pl.pallas_call(
        functools.partial(sum_kernel, count),
        in_specs=whole(1),
        out_specs=whole(1)[0],
        out_shape=jax.ShapeDtypeStruct((rows, width), BF16),
        scratch_shapes=[pltpu.VMEM((count - 1, rows // count, width), BF16), pltpu.VMEM((rows // count, width), BF16)]
        + [pltpu.SemaphoreType.DMA((count - 1,))] * 4,
        compiler_params=remote_params(4),
        cost_estimate=estimate(14),
        name="sum_chan",
    )(part)


def exchanged(value, bit):
    return lax.ppermute(value, "seq", [(i, i ^ bit) for i in range(lax.axis_size("seq"))])


class Summed:
    def __init__(self, value, halves):
        self.halves = halves
        self.bit = 1
        self.keep = value
        give = value
        if halves:
            half = value.shape[0] // 2
            core = lax.axis_index("seq") % 2
            self.keep = lax.dynamic_slice_in_dim(value, core * half, half, 0)
            give = lax.dynamic_slice_in_dim(value, (1 - core) * half, half, 0)
        self.wire = exchanged(give, 1)

    def step(self):
        total = self.keep.astype(F32) + self.wire.astype(F32)
        self.bit *= 2
        if self.bit < lax.axis_size("seq"):
            self.keep = total.astype(BF16)
            self.wire = exchanged(self.keep, self.bit)
        elif self.halves:
            self.keep = total.astype(BF16)
            self.wire = exchanged(self.keep, 1)
        else:
            self.keep = total

    def across(self):
        while self.bit * 2 < lax.axis_size("seq"):
            self.step()

    def last(self):
        while self.bit * 2 < lax.axis_size("seq"):
            self.step()
        return self.keep, self.wire

    def total(self):
        while self.bit < lax.axis_size("seq"):
            self.step()
        return (self.keep, self.wire) if self.halves else self.keep


def after(value, *sums):
    value, wires = lax.optimization_barrier((value, [one.wire for one in sums]))
    for one, wire in zip(sums, wires):
        one.wire = wire
    return value


def place_pairs_kernel(core_ref, *refs):
    *ins, out_ref = refs[-5:]
    own = pl.program_id(0) == 0
    for j in range(2):
        out_ref[0, :, j, :] = jnp.where(own, ins[2 * j][...].astype(F32), ins[2 * j + 1][...].astype(F32))


def place_rows_kernel(core_ref, *refs):
    mine, other, out_ref = refs[-3:]
    own = pl.program_id(0) == 0
    out_ref[0] = jnp.where(own, mine[...].astype(F32), other[...].astype(F32))


def place(kernel, parts, base, layer, layers, block, middle):
    half, width = parts[0].shape
    core = (lax.axis_index("seq") % 2).reshape(1)
    steps = half // block

    def where(kept):
        if kept:
            return lambda k, b, core: (jnp.where(k == 0, b, steps - 1), 0)
        return lambda k, b, core: (jnp.where(k == 1, b, 0), 0)

    def out(k, b, core):
        return (layer, (core[0] + k - 2 * core[0] * k) * steps + b) + (0,) * (1 + len(middle))

    ins = [pl.BlockSpec((block, width), where(p % 2 == 0)) for p in range(len(parts))]
    shape = (layers, 2 * half) + middle + (width,)
    args = list(parts)
    aliases = {}
    if base is not None:
        ins.insert(0, pl.BlockSpec(memory_space=pl.ANY))
        args.insert(0, base)
        aliases = {1: 0}
    return pl.pallas_call(
        kernel,
        grid_spec=pltpu.PrefetchScalarGridSpec(
            num_scalar_prefetch=1,
            grid=(2, steps),
            in_specs=ins,
            out_specs=pl.BlockSpec((1, block) + middle + (width,), out),
        ),
        out_shape=jax.ShapeDtypeStruct(shape, F32),
        input_output_aliases=aliases,
        compiler_params=params("arbitrary", "arbitrary"),
        cost_estimate=estimate(5),
        name="place",
    )(core, *args)


def dot(a, b, dims):
    return lax.dot_general(a, b, (dims, ((), ())), preferred_element_type=F32)


def rows_of_packed(rank_columns, rank, states, seqs, taps):
    names = [("xproj", rank_columns), ("dtproj", rank), ("decay", states), ("init", seqs * states)]
    names += [("taps", taps), ("shift", 1), ("bias", 1), ("skip", 1), ("conv", (taps - 1) * seqs)]
    places, row = {}, 0
    for name, size in names:
        places[name] = (row, row + size)
        row += size
    return places, row + (-row) % 16


def mid_kernel(
    gproj_ref, xproj_ref, gact_ref, inner_ref, head_ref, low_ref, taps_ref, shift_ref, rank_ref, gpre_ref, ggate_ref,
    gdecay_ref, gskip_ref, ginit_ref,
    gmixed_ref, packed_ref,
    dotted_ref, pad_ref, gconv_ref, tail_ref, give_ref, got_ref, send_sem, recv_sem,
):
    seqs, length = gact_ref.shape[:2]
    tokens = length * G
    count = gmixed_ref.shape[1] // (2 * LANES)
    taps = taps_ref.shape[0]
    over = taps - 1
    j = pl.program_id(0)
    place, peers = lax.axis_index("seq"), lax.axis_size("seq")
    states = gdecay_ref.shape[1]
    places, _ = rows_of_packed(gproj_ref.shape[1], rank_ref.shape[1], states, seqs, taps)

    def to_previous(t):
        return pltpu.make_async_remote_copy(
            src_ref=give_ref.at[t], dst_ref=got_ref.at[t], send_sem=send_sem.at[t], recv_sem=recv_sem.at[t],
            device_id={"seq": jnp.maximum(place - 1, 0)}, device_id_type=MESH,
        )

    @pl.when(j == 0)
    def _():
        barrier = pltpu.get_barrier_semaphore()

        @pl.when(place < peers - 1)
        def _():
            pl.semaphore_signal(barrier, inc=1, device_id={"seq": place + 1}, device_id_type=MESH)

        pl.when(place > 0)(lambda: pl.semaphore_wait(barrier, 1))

    columns = pl.ds(pl.multiple_of(j * LANES, LANES), LANES)
    gate_columns = pl.ds(pl.multiple_of((count + j) * LANES, LANES), LANES)
    gmixed_ref[:, gate_columns] = ggate_ref[...]
    dotted_ref[...] = jnp.dot(gproj_ref[...], xproj_ref[...], preferred_element_type=F32)
    zero = jnp.zeros((G, LANES), F32)
    weights = [jnp.broadcast_to(taps_ref[k : k + 1, :], (G, LANES)) for k in range(taps)]
    shift = jnp.broadcast_to(shift_ref[...], (G, LANES))
    sums = (zero,) * (taps + 1)
    early = [[None] * seqs for _ in range(over)]
    for s in range(seqs):
        for k in range(over):
            pad_ref[k] = head_ref[s, k]

        def fill(l, carry):
            pad_ref[l + over] = inner_ref[s, l]
            return carry

        lax.fori_loop(0, length, fill, 0, unroll=math.gcd(length, 8))

        def one(l, sums):
            parts = [pad_ref[l + k] for k in range(taps)]
            pre = shift
            for k in range(taps):
                pre = pre + weights[k] * parts[k]
            sig = 1.0 / (1.0 + jnp.exp(-pre))
            here = dotted_ref[pl.ds(pl.multiple_of(s * tokens + l * G, G), G), :]
            gconv = (gact_ref[s, l] + here) * (sig + pre * sig * (1.0 - sig))
            gconv_ref[l] = gconv
            return tuple(sums[k] + gconv * parts[k] for k in range(taps)) + (sums[taps] + gconv,)

        sums = lax.fori_loop(0, length, one, sums, unroll=math.gcd(length, 8))
        for k in range(over):
            gconv_ref[length + k] = shifted(gconv_ref[k], -1, 0.0)
            total = weights[0] * gconv_ref[k]
            for i in range(1, k + 1):
                total = total + weights[i] * gconv_ref[k - i]
            early[k][s] = total[0:1, :]
            give_ref[j, s, k : k + 1, :] = total[0:1, :]

        def inner_of(l):
            total = weights[0] * gconv_ref[l + over]
            for k in range(1, taps):
                total = total + weights[k] * gconv_ref[l + over - k]
            return total

        def pair(p, carry):
            both = jnp.concatenate([inner_of(2 * p), inner_of(2 * p + 1)], axis=0)
            gmixed_ref[pl.ds(pl.multiple_of(s * tokens + 2 * p * G, 2 * G), 2 * G), columns] = both.astype(BF16)
            return carry

        lax.fori_loop(0, length // 2 - 2, pair, 0, unroll=math.gcd(length // 2 - 2, 4))
        for q in range(4):
            tail_ref[j, s, q] = inner_of(length - 4 + q)
    pl.when(place > 0)(lambda: to_previous(j).start())

    def put(name, value):
        first, last = places[name]
        packed_ref[first:last, :] = value.astype(BF16)

    put("xproj", dot(gproj_ref[...], low_ref[...], ((0,), (0,))))
    put("dtproj", dot(rank_ref[...], gpre_ref[...], ((0,), (0,))))
    bias = jnp.dot(jnp.ones((16, seqs * tokens), BF16), gpre_ref[...], preferred_element_type=F32)[0:1, :]
    decay, skip = gdecay_ref[0], gskip_ref[0, 0:1, :]
    for s in range(1, seqs):
        decay = decay + gdecay_ref[s]
        skip = skip + gskip_ref[s, 0:1, :]
    put("decay", decay)
    first = place == 0
    for s in range(seqs):
        row = places["init"][0] + s * states
        packed_ref[row : row + states, :] = jnp.where(first, ginit_ref[s], 0.0).astype(BF16)
    rest = [jnp.sum(value, axis=0, keepdims=True) for value in sums]
    rest += [bias, skip]
    rest += [jnp.where(first, early[k][s], 0.0) for k in range(over) for s in range(seqs)]
    row = places["taps"][0]
    rest += [jnp.zeros((1, LANES), F32)] * (packed_ref.shape[0] - row - len(rest))
    packed_ref[row:, :] = jnp.concatenate(rest, axis=0).astype(BF16)

    @pl.when(j == count - 1)
    def _():
        last_row = lax.broadcasted_iota(jnp.int32, (G, LANES), 0) == G - 1
        inside = place < peers - 1
        for t in range(count):
            pl.when(place < peers - 1)(lambda: to_previous(t).wait_recv())
            for s in range(seqs):
                values = []
                for q in range(4):
                    value = tail_ref[t, s, q]
                    k = q - 4 + over
                    if k >= 0:
                        given = jnp.broadcast_to(got_ref[t, s, k : k + 1, :], (G, LANES))
                        value = value + jnp.where(jnp.logical_and(last_row, inside), given, 0.0)
                    values.append(value)
                for q in (0, 2):
                    row = s * tokens + (length - 4 + q) * G
                    both = jnp.concatenate(values[q : q + 2], axis=0)
                    gmixed_ref[row : row + 2 * G, t * LANES : (t + 1) * LANES] = both.astype(BF16)
            pl.when(place > 0)(lambda: to_previous(t).wait_send())


def mid_backward(
    gproj, xproj, gact, mixed, head, low, taps, shift, rank_part, gpre, ggate, gdecay, gskip, ginit
):
    seqs, length, _, chans = gact.shape
    rows = seqs * length * G
    count = chans // LANES
    states = gdecay.shape[1]
    over = taps.shape[0] - 1
    _, packed_rows = rows_of_packed(gproj.shape[1], rank_part.shape[1], states, seqs, taps.shape[0])
    token = pl.BlockSpec((seqs, length, G, LANES), lambda j: (0, 0, 0, j))
    row = pl.BlockSpec((rows, LANES), lambda j: (0, j))

    def column(height):
        return pl.BlockSpec((height, LANES), lambda j: (0, j))

    def stack(height):
        return pl.BlockSpec((seqs, height, LANES), lambda j: (0, 0, j))

    return pl.pallas_call(
        mid_kernel,
        grid=(count,),
        in_specs=[
            pl.BlockSpec(gproj.shape, lambda j: (0, 0)),
            column(xproj.shape[0]),
            token,
            token,
            pl.BlockSpec((seqs, over, G, LANES), lambda j: (0, 0, 0, j)),
            row,
            column(over + 1),
            column(1),
            pl.BlockSpec(rank_part.shape, lambda j: (0, 0)),
            row,
            row,
            stack(states),
            stack(8),
            stack(states),
        ],
        out_specs=[pl.BlockSpec((rows, 2 * chans), lambda j: (0, 0)), column(packed_rows)],
        out_shape=[
            jax.ShapeDtypeStruct((rows, 2 * chans), BF16),
            jax.ShapeDtypeStruct((packed_rows, chans), BF16),
        ],
        scratch_shapes=[
            pltpu.VMEM((rows, LANES), F32),
            pltpu.VMEM((length + over, G, LANES), F32),
            pltpu.VMEM((length + over, G, LANES), F32),
            pltpu.VMEM((count, seqs, 4, G, LANES), F32),
            pltpu.VMEM((count, seqs, 8, LANES), F32),
            pltpu.VMEM((count, seqs, 8, LANES), F32),
            pltpu.SemaphoreType.DMA((count,)),
            pltpu.SemaphoreType.DMA((count,)),
        ],
        compiler_params=pltpu.CompilerParams(
            dimension_semantics=("arbitrary",), collective_id=5, has_side_effects=True, vmem_limit_bytes=VMEM_LIMIT
        ),
        cost_estimate=estimate(8),
        name="mid_backward",
    )(gproj, xproj, gact, mixed, head, low, taps, shift, rank_part, gpre, ggate, gdecay, gskip, ginit)


def unpack_kernel(layers, places, seqs, *refs):
    smalls, gains, outs = refs[: 2 * layers], refs[2 * layers : 4 * layers], refs[4 * layers :]
    gain, taps, shift, xproj, dtproj, bias, decay, skip, conv, init = outs
    for i in range(layers):
        def rows(name):
            first, last = places[name]
            return smalls[2 * i][first:last, :].astype(F32) + smalls[2 * i + 1][first:last, :].astype(F32)

        gain[i : i + 1, :] = gains[2 * i][0:1, :].astype(F32) + gains[2 * i + 1][0:1, :].astype(F32)
        xproj[i], dtproj[i], decay[i] = rows("xproj"), rows("dtproj"), rows("decay")
        init[i] = rows("init")
        low, high = places["taps"][0], smalls[0].shape[0]
        rest = smalls[2 * i][low:high, :].astype(F32) + smalls[2 * i + 1][low:high, :].astype(F32)

        def of(name):
            first, last = places[name]
            return rest[first - low : last - low, :]

        taps[i] = of("taps")
        shift[i : i + 1, :], bias[i : i + 1, :], skip[i : i + 1, :] = of("shift"), of("bias"), of("skip")
        for k in range(conv.shape[1]):
            conv[i, k] = of("conv")[k * seqs : (k + 1) * seqs, :]


def unpack(smalls, gains, places, seqs, width):
    layers = len(smalls)
    chans = smalls[0][0].shape[1]

    def size(name):
        return places[name][1] - places[name][0]

    shapes = [
        (layers, width), (layers, size("taps"), chans), (layers, chans), (layers, size("xproj"), chans),
        (layers, size("dtproj"), chans), (layers, chans), (layers, size("decay"), chans), (layers, chans),
        (layers, size("conv") // seqs, seqs, chans), (layers, size("init"), chans),
    ]
    args = [value for pair in smalls for value in pair] + [value for pair in gains for value in pair]
    return pl.pallas_call(
        functools.partial(unpack_kernel, layers, places, seqs),
        in_specs=whole(len(args)),
        out_specs=whole(len(shapes)),
        out_shape=[jax.ShapeDtypeStruct(shape, F32) for shape in shapes],
        compiler_params=params(),
        cost_estimate=estimate(3),
        name="unpack",
    )(*args)


def passed_along(value, axis, by):
    peers = lax.axis_size(axis)
    pairs = [(i, i + by) for i in range(peers) if 0 <= i + by < peers]
    return lax.ppermute(value, axis, pairs)


def to_segments(value):
    seqs, tokens, width = value.shape
    return value.reshape(seqs, G, tokens // G, width).transpose(0, 2, 1, 3)


def from_segments(value):
    seqs, length, _, width = value.shape
    return value.transpose(0, 2, 1, 3).reshape(seqs, length * G, width)


def local(
    hidden_in,
    norm_gain,
    in_weight,
    conv_weight,
    conv_bias,
    xproj_weight,
    dtproj_weight,
    dt_bias,
    decay_log,
    skip_gain,
    out_weight,
    conv_state,
    scan_state,
    out_cotangent,
):
    layers = in_weight.shape[0]
    rank = dtproj_weight.shape[1]
    states = decay_log.shape[1]
    seqs, tokens, _ = hidden_in.shape
    length = tokens // G
    rows = seqs * tokens
    chans = in_weight.shape[3]
    model = hidden_in.shape[2] * lax.axis_size("chan")
    taps = conv_weight.shape[1]
    is_first = lax.axis_index("seq") == 0

    flat_all = lax.optimization_barrier(in_weight.reshape(layers, model, -1))
    first = to_segments(hidden_in).reshape(rows, -1)
    hidden = first.astype(F32)
    full, gains = gather_first(first, norm_gain)
    grad = to_segments(out_cotangent).reshape(rows, -1)
    grad_rows = lax.all_gather(grad, "chan", axis=1, tiled=True)
    grad = grad.astype(F32)
    saved = []
    for i in range(layers):
        wide = full[:rows].astype(F32)
        inverse = lax.rsqrt(jnp.sum(wide * wide, axis=1, keepdims=True) / model + EPS)
        normed = (wide * inverse * gains[i]).astype(BF16)
        flat_in = flat_all[i]
        mixed = dot(normed, flat_in, ((1,), (0,)))
        inner = mixed[:, :chans].reshape(seqs, length, G, chans)
        gate = mixed[:, chans:].reshape(seqs, length, G, chans)
        tail = inner[:, length - taps + 1 :]
        received = passed_along(tail[:, :, G - 1], "seq", 1)
        before = jnp.where(is_first, conv_state[i], received)
        head = jnp.concatenate([before[:, :, None], tail[:, :, : G - 1]], axis=2)
        padded = jnp.concatenate([head, inner], axis=1)
        pre = conv_bias[i] + sum(conv_weight[i, k] * padded[:, k : k + length] for k in range(taps))
        act = jax.nn.silu(pre)
        act_low = act.astype(BF16).reshape(rows, chans)
        projected = sum_chan(dot(act_low, xproj_weight[i], ((1,), (0,))).astype(BF16))
        rank_part = projected[:, :rank]
        maps = projected[:, rank:].reshape(seqs, tokens, 2 * states)
        delta = dot(rank_part, dtproj_weight[i], ((1,), (0,))) + dt_bias[i]
        delta = delta.reshape(seqs, length, G, chans)
        step = jax.nn.softplus(delta)
        prefix, span, packs = scan_ends(act, step, maps, decay_log[i])
        y, gated, start = scan_forward(
            act, step, gate, maps, decay_log[i], prefix, span, packs, scan_state[i], skip_gain[i : i + 1]
        )
        gated = gated.reshape(rows, chans)
        saved.append(
            (hidden, inverse, normed, flat_in, mixed, gate, head, act, act_low, rank_part, maps, delta, step,
             span, packs, y, gated, start)
        )
        if i + 1 < layers:
            hidden, full = forward_boundary(gated, out_weight, i, hidden)
        else:
            branch = dot(gated, out_weight[i], ((1,), (0,))).astype(BF16)
            branch_sum = lax.psum_scatter(branch, "chan", scatter_dimension=1, tiled=True)

    def finish(i, sums):
        nonlocal in_grads, out_grads
        in_grads = place(
            place_pairs_kernel, [*sums["inner"].total(), *sums["gate"].total()], in_grads, i, layers, model // 16, (2,)
        )
        out_grads = place(place_rows_kernel, list(sums["out"].total()), out_grads, i, layers, chans // 16, ())

    smalls = [None] * layers
    in_grads = out_grads = None
    before_sums = None
    for i in reversed(range(layers)):
        (hidden_i, inverse, normed, flat_in, mixed, gate, head, act, act_low, rank_part, maps, delta, step,
         span, packs, y, gated, start) = saved[i]
        sums = {}
        sums["out"] = Summed(dot(gated, grad_rows, ((0,), (0,))).astype(BF16), True)
        grad_gated = dot(grad_rows, out_weight[i], ((1,), (1,)))
        grad_gated = grad_gated.reshape(seqs, length, G, chans)
        suffix, back_packs = scan_adjoint(step, gate, grad_gated, maps, decay_log[i], span)
        back_packs = after(back_packs, sums["out"])
        sums["out"].across()
        scanned = scan_backward(
            act, step, delta, gate, y, grad_gated, maps, decay_log[i], start, suffix, span, back_packs, packs,
            skip_gain[i : i + 1],
        )
        gact, gpre, ggate, gmaps, gdecay, gskip, ginit = after(scanned, sums["out"])
        sums["out"].step()
        gpre = gpre.reshape(rows, chans)
        ggate = ggate.reshape(rows, chans)
        grad_rank = dot(gpre, dtproj_weight[i], ((1,), (1,)))
        proj_part = jnp.concatenate([grad_rank, gmaps.reshape(rows, -1)[:, : 2 * states]], axis=1).astype(BF16)
        sums["gate"] = Summed(dot(normed, ggate, ((0,), (0,))).astype(BF16), True)
        if i == layers - 1:
            proj_part, branch_sum = lax.optimization_barrier((proj_part, branch_sum))
            hidden = hidden + branch_sum.astype(F32)
        proj_part = after(proj_part, sums["gate"])
        sums["gate"].across()
        grad_proj = after(sum_chan(proj_part), sums["out"])
        gmixed, packed = mid_backward(
            grad_proj, xproj_weight[i].T, gact, mixed.reshape(seqs, length, G, -1), head, act_low, conv_weight[i],
            conv_bias[i : i + 1], rank_part, gpre, ggate, gdecay, gskip, ginit,
        )
        gmixed, packed = after((gmixed, packed), sums["gate"])
        sums["gate"].step()
        sums["small"] = Summed(packed, False)
        sums["inner"] = Summed(dot(normed, gmixed[:, :chans], ((0,), (0,))).astype(BF16), True)
        inner_sums = jnp.sum(gmixed.astype(F32) * mixed, axis=1)
        gmixed = after(gmixed, sums["inner"], sums["small"])
        sums["inner"].across()
        sums["small"].across()
        outs = backward_boundary(
            gmixed, flat_all, i, grad, hidden_i, inverse, norm_gain[i : i + 1], inner_sums, i > 0
        )
        outs = after(outs, sums["inner"], sums["small"])
        grad = outs[0]
        if i > 0:
            grad_rows = outs[2]
        sums["inner"].step()
        sums["gain"] = Summed(outs[1].astype(BF16), False)
        smalls[i] = sums
        if before_sums is not None:
            finish(i + 1, before_sums)
        before_sums = sums
    finish(0, before_sums)
    places, _ = rows_of_packed(xproj_weight.shape[2], rank, states, seqs, taps)
    gain, taps_grad, shift, xproj, dtproj, bias, decay, skip, conv, init = unpack(
        [one["small"].last() for one in smalls], [one["gain"].last() for one in smalls], places, seqs,
        norm_gain.shape[1],
    )

    def back_out(value):
        return from_segments(value.reshape(seqs, length, G, -1))

    return (
        back_out(hidden),
        back_out(grad),
        gain,
        in_grads,
        taps_grad,
        shift,
        xproj.transpose(0, 2, 1),
        dtproj,
        bias,
        decay,
        skip,
        out_grads,
        conv.transpose(0, 2, 1, 3),
        init.reshape(scan_state.shape),
    )


def solution(mesh):
    return jax.shard_map(
        local,
        mesh=mesh,
        in_specs=(
            P(None, "seq", "chan"),
            P(None, "chan"),
            P(None, None, None, "chan"),
            P(None, None, "chan"),
            P(None, "chan"),
            P(None, "chan", None),
            P(None, None, "chan"),
            P(None, "chan"),
            P(None, None, "chan"),
            P(None, "chan"),
            P(None, "chan", None),
            P(None, None, None, "chan"),
            P(None, None, None, "chan"),
            P(None, "seq", "chan"),
        ),
        out_specs=(
            P(None, "seq", "chan"),
            P(None, "seq", "chan"),
            P(None, "chan"),
            P(None, None, None, "chan"),
            P(None, None, "chan"),
            P(None, "chan"),
            P(None, "chan", None),
            P(None, None, "chan"),
            P(None, "chan"),
            P(None, None, "chan"),
            P(None, "chan"),
            P(None, "chan", None),
            P(None, None, None, "chan"),
            P(None, None, None, "chan"),
        ),
        check_vma=False,
    )
```

```python
import functools
import math

import jax
import jax.numpy as jnp
from jax import lax
from jax.experimental import pallas as pl
from jax.experimental.pallas import tpu as pltpu
from jax.sharding import PartitionSpec as P

EPS = 1e-05
G = 8
LANES = 128
LOG2E = 1.4426950408889634
LN2 = 0.6931471805599453
F32 = jnp.float32
BF16 = jnp.bfloat16
VMEM_LIMIT = 48 * 1024 * 1024
MESH = pl.DeviceIdType.MESH


def params(*semantics):
    return pltpu.CompilerParams(dimension_semantics=semantics, vmem_limit_bytes=VMEM_LIMIT)


def spread_maps(maps_ref, first, count, out_ref):
    shape = (maps_ref.shape[2], count * LANES)
    row = lax.broadcasted_iota(jnp.int32, shape, 0)
    col = lax.broadcasted_iota(jnp.int32, shape, 1) // LANES
    choice = jnp.where(row == col + first, 1.0, 0.0).astype(BF16)
    out_ref[...] = jnp.dot(maps_ref[0], choice, preferred_element_type=F32)


def part(ref, l, n):
    return ref[pl.ds(pl.multiple_of(l * G, G), G), n * LANES : (n + 1) * LANES]


def spread_rate(decay_ref, rate_ref):
    rate = jnp.exp(decay_ref[...]) * (-LOG2E)
    for n in range(rate.shape[0]):
        rate_ref[n] = jnp.broadcast_to(rate[n : n + 1, :], (G, LANES))


def shifted(value, by, fill):
    row = lax.broadcasted_iota(jnp.int32, value.shape, 0)
    moved = pltpu.roll(value, by % G, 0)
    inside = row >= by if by > 0 else row < G + by
    return jnp.where(inside, moved, fill)


def segment_prefix(ends, span, rate_ref, direction):
    step = 1
    while step < G:
        moved_span = shifted(span, direction * step, 0.0)
        ends = [
            e + jnp.exp2(span * rate_ref[n]) * shifted(e, direction * step, 0.0)
            for n, e in enumerate(ends)
        ]
        span = span + moved_span
        step *= 2
    return ends, span


class SeqExchange:
    def __init__(self, give_ref, got_ref, send_sem, recv_sem):
        self.refs = give_ref, got_ref
        self.sems = send_sem, recv_sem
        self.me, self.peers = lax.axis_index("seq"), lax.axis_size("seq")
        self.others = [lax.rem(self.me + k, self.peers) for k in range(1, self.peers)]

    def signal(self):
        barrier = pltpu.get_barrier_semaphore()
        for other in self.others:
            pl.semaphore_signal(barrier, inc=1, device_id={"seq": other}, device_id_type=MESH)

    def meet(self):
        if self.others:
            pl.semaphore_wait(pltpu.get_barrier_semaphore(), len(self.others))

    def copy(self, step, k):
        give, got = self.refs
        send, recv = self.sems
        return pltpu.make_async_remote_copy(
            src_ref=give.at[step], dst_ref=got.at[self.me, step], send_sem=send.at[step, k], recv_sem=recv.at[step, k],
            device_id={"seq": self.others[k]}, device_id_type=MESH,
        )

    def start(self, step):
        for k in range(len(self.others)):
            self.copy(step, k).start()

    def finish(self, steps):
        for step in range(steps):
            for k in range(len(self.others)):
                self.copy(step, k).wait()


def exchange_scratch(steps, rows):
    peers = lax.axis_size("seq")
    sems = pltpu.SemaphoreType.DMA((steps, max(peers - 1, 1)))
    return [pltpu.VMEM((steps, rows, LANES), F32), pltpu.VMEM((peers, steps, rows, LANES), F32), sems, sems]


def exchange_params(ident):
    return pltpu.CompilerParams(
        dimension_semantics=("arbitrary", "arbitrary"), collective_id=ident, has_side_effects=True,
        vmem_limit_bytes=VMEM_LIMIT,
    )


def exchange_step(exchange, packs_ref, give_ref, got_ref, rows):
    seqs, tiles = pl.num_programs(0), pl.num_programs(1)
    step = pl.program_id(0) * tiles + pl.program_id(1)
    total = give_ref.shape[0]
    wide = packs_ref.shape[3] // LANES
    give_ref[step] = rows
    pl.when(step == 0)(exchange.meet)
    exchange.start(step)

    @pl.when(step == total - 1)
    def _():
        exchange.finish(total)
        for i in range(total):
            for d in range(got_ref.shape[0]):
                packs_ref[d, i // wide, :, (i % wide) * LANES : (i % wide + 1) * LANES] = jnp.where(
                    exchange.me == d, give_ref[i], got_ref[d, i]
                )


def ends_kernel(
    act_ref, step_ref, maps_ref, decay_ref, prefix_ref, span_ref, packs_ref, b_ref, rate_ref, give_ref, got_ref, *sems
):
    length, states = act_ref.shape[1], decay_ref.shape[0]
    exchange = SeqExchange(give_ref, got_ref, *sems)
    pl.when(pl.program_id(0) + pl.program_id(1) == 0)(exchange.signal)

    @pl.when(pl.program_id(1) == 0)
    def _():
        spread_maps(maps_ref, 0, states, b_ref)

    spread_rate(decay_ref, rate_ref)

    def one(l, carry):
        h, total = carry
        st = step_ref[0, l]
        u = st * act_ref[0, l]
        h = tuple(
            jnp.exp2(st * rate_ref[n]) * h[n] + u * part(b_ref, l, n) for n in range(states)
        )
        return h, total + st

    zero = jnp.zeros((G, LANES), F32)
    h, total = lax.fori_loop(0, length, one, ((zero,) * states, zero), unroll=math.gcd(length, 8))
    ends, span = segment_prefix(list(h), total, rate_ref, 1)
    for n in range(states):
        prefix_ref[0, n] = shifted(ends[n], 1, 0.0)
    span_ref[0, 0] = shifted(span, 1, 0.0)
    span_ref[0, 1] = jnp.broadcast_to(span[G - 1 : G, :], (G, LANES)) - span
    rows = [e[G - 1 : G, :] for e in ends] + [jnp.broadcast_to(span[G - 1 : G, :], (8, LANES))]
    exchange_step(exchange, packs_ref, give_ref, got_ref, jnp.concatenate(rows, axis=0))


def scan_ends(act, step, maps, decay):
    seqs, length, _, chans = act.shape
    states = decay.shape[0]
    peers = lax.axis_size("seq")
    token = pl.BlockSpec((1, length, G, LANES), lambda s, j: (s, 0, 0, j))
    return pl.pallas_call(
        ends_kernel,
        grid=(seqs, chans // LANES),
        in_specs=[
            token,
            token,
            pl.BlockSpec((1, length * G, maps.shape[2]), lambda s, j: (s, 0, 0)),
            pl.BlockSpec((states, LANES), lambda s, j: (0, j)),
        ],
        out_specs=[
            pl.BlockSpec((1, states, G, LANES), lambda s, j: (s, 0, 0, j)),
            pl.BlockSpec((1, 2, G, LANES), lambda s, j: (s, 0, 0, j)),
            pl.BlockSpec((peers, seqs, states + 8, chans), lambda s, j: (0, 0, 0, 0)),
        ],
        out_shape=[
            jax.ShapeDtypeStruct((seqs, states, G, chans), F32),
            jax.ShapeDtypeStruct((seqs, 2, G, chans), F32),
            jax.ShapeDtypeStruct((peers, seqs, states + 8, chans), F32),
        ],
        scratch_shapes=[
            pltpu.VMEM((length * G, states * LANES), F32),
            pltpu.VMEM((states, G, LANES), F32),
        ]
        + exchange_scratch(seqs * chans // LANES, states + 8),
        compiler_params=exchange_params(6),
        cost_estimate=estimate(12),
        name="scan_ends",
    )(act, step, maps, decay)


def forward_kernel(
    act_ref, step_ref, gate_ref, maps_ref, decay_ref, prefix_ref, span_ref, packs_ref, init_ref, skip_ref,
    y_ref, gated_ref, start_ref, b_ref, c_ref, rate_ref,
):
    length, states = act_ref.shape[1], decay_ref.shape[0]

    @pl.when(pl.program_id(1) == 0)
    def _():
        spread_maps(maps_ref, 0, states, b_ref)
        spread_maps(maps_ref, states, states, c_ref)

    spread_rate(decay_ref, rate_ref)
    rate = jnp.exp(decay_ref[...]) * (-LOG2E)
    me = lax.axis_index("seq")
    entry = init_ref[0]
    for d in range(packs_ref.shape[0]):
        joined = jnp.exp2(rate * packs_ref[d, 0, states : states + 1, :]) * entry + packs_ref[d, 0, :states, :]
        entry = jnp.where(d < me, joined, entry)
    span = span_ref[0, 0]
    h = []
    for n in range(states):
        first = prefix_ref[0, n] + jnp.exp2(rate_ref[n] * span) * entry[n : n + 1, :]
        start_ref[0, n] = first
        h.append(first)
    skip = jnp.broadcast_to(skip_ref[...], (G, LANES))

    def one(k, h):
        h = list(h)
        halves = []
        for i in range(2):
            l = 2 * k + i
            st = step_ref[0, l]
            act = act_ref[0, l]
            u = st * act
            y = skip * act
            for n in range(states):
                h[n] = jnp.exp2(st * rate_ref[n]) * h[n] + u * part(b_ref, l, n)
                y = y + part(c_ref, l, n) * h[n]
            y_ref[0, l] = y
            gate = gate_ref[0, l]
            halves.append(y * (gate / (1.0 + jnp.exp(-gate))))
        gated_ref[0, pl.ds(pl.multiple_of(k * 2 * G, 2 * G), 2 * G), :] = jnp.concatenate(halves, axis=0).astype(BF16)
        return tuple(h)

    lax.fori_loop(0, length // 2, one, tuple(h), unroll=math.gcd(length // 2, 4))


def scan_forward(act, step, gate, maps, decay, prefix, span, packs, init, skip):
    seqs, length, _, chans = act.shape
    states = decay.shape[0]
    token = pl.BlockSpec((1, length, G, LANES), lambda s, j: (s, 0, 0, j))
    per_state = pl.BlockSpec((1, states, G, LANES), lambda s, j: (s, 0, 0, j))
    return pl.pallas_call(
        forward_kernel,
        grid=(seqs, chans // LANES),
        in_specs=[
            token,
            token,
            token,
            pl.BlockSpec((1, length * G, maps.shape[2]), lambda s, j: (s, 0, 0)),
            pl.BlockSpec((states, LANES), lambda s, j: (0, j)),
            per_state,
            pl.BlockSpec((1, 2, G, LANES), lambda s, j: (s, 0, 0, j)),
            pl.BlockSpec((packs.shape[0], 1, states + 8, LANES), lambda s, j: (0, s, 0, j)),
            pl.BlockSpec((1, states, LANES), lambda s, j: (s, 0, j)),
            pl.BlockSpec((1, LANES), lambda s, j: (0, j)),
        ],
        out_specs=[
            token,
            pl.BlockSpec((1, length * G, LANES), lambda s, j: (s, 0, j)),
            per_state,
        ],
        out_shape=[
            jax.ShapeDtypeStruct(act.shape, F32),
            jax.ShapeDtypeStruct((seqs, length * G, chans), BF16),
            jax.ShapeDtypeStruct((seqs, states, G, chans), F32),
        ],
        scratch_shapes=[
            pltpu.VMEM((length * G, states * LANES), F32),
            pltpu.VMEM((length * G, states * LANES), F32),
            pltpu.VMEM((states, G, LANES), F32),
        ],
        compiler_params=params("arbitrary", "arbitrary"),
        cost_estimate=estimate(20),
        name="scan_forward",
    )(act, step, gate, maps, decay, prefix, span, packs, init, skip)


def adjoint_kernel(
    step_ref, gate_ref, grad_ref, maps_ref, decay_ref, span_ref, suffix_ref, packs_ref, c_ref, rate_ref, give_ref,
    got_ref, *sems,
):
    length, states = step_ref.shape[1], decay_ref.shape[0]
    exchange = SeqExchange(give_ref, got_ref, *sems)
    pl.when(pl.program_id(0) + pl.program_id(1) == 0)(exchange.signal)

    @pl.when(pl.program_id(1) == 0)
    def _():
        spread_maps(maps_ref, states, states, c_ref)

    spread_rate(decay_ref, rate_ref)

    def one(k, carry):
        l = length - 1 - k
        st = step_ref[0, l]
        gate = gate_ref[0, l]
        gy = grad_ref[0, l] * (gate / (1.0 + jnp.exp(-gate)))
        return tuple(
            jnp.exp2(st * rate_ref[n]) * (carry[n] + gy * part(c_ref, l, n)) for n in range(states)
        )

    zero = jnp.zeros((G, LANES), F32)
    carry = lax.fori_loop(0, length, one, (zero,) * states, unroll=math.gcd(length, 8))
    own = span_ref[0, 1, 0:1, :] + span_ref[0, 0, 1:2, :] - span_ref[0, 0] - span_ref[0, 1]
    ends, _ = segment_prefix(list(carry), own, rate_ref, -1)
    for n in range(states):
        suffix_ref[0, n] = shifted(ends[n], -1, 0.0)
    rows = jnp.concatenate([e[0:1, :] for e in ends], axis=0)
    exchange_step(exchange, packs_ref, give_ref, got_ref, rows)


def scan_adjoint(step, gate, grad, maps, decay, span):
    seqs, length, _, chans = step.shape
    states = decay.shape[0]
    peers = lax.axis_size("seq")
    token = pl.BlockSpec((1, length, G, LANES), lambda s, j: (s, 0, 0, j))
    return pl.pallas_call(
        adjoint_kernel,
        grid=(seqs, chans // LANES),
        in_specs=[
            token,
            token,
            token,
            pl.BlockSpec((1, length * G, maps.shape[2]), lambda s, j: (s, 0, 0)),
            pl.BlockSpec((states, LANES), lambda s, j: (0, j)),
            pl.BlockSpec((1, 2, G, LANES), lambda s, j: (s, 0, 0, j)),
        ],
        out_specs=[
            pl.BlockSpec((1, states, G, LANES), lambda s, j: (s, 0, 0, j)),
            pl.BlockSpec((peers, seqs, states, chans), lambda s, j: (0, 0, 0, 0)),
        ],
        out_shape=[
            jax.ShapeDtypeStruct((seqs, states, G, chans), F32),
            jax.ShapeDtypeStruct((peers, seqs, states, chans), F32),
        ],
        scratch_shapes=[
            pltpu.VMEM((length * G, states * LANES), F32),
            pltpu.VMEM((states, G, LANES), F32),
        ]
        + exchange_scratch(seqs * chans // LANES, states),
        compiler_params=exchange_params(7),
        cost_estimate=estimate(15),
        name="scan_adjoint",
    )(step, gate, grad, maps, decay, span)


def backward_kernel(
    act_ref, step_ref, delta_ref, gate_ref, y_ref, grad_ref, maps_ref, decay_ref, start_ref, suffix_ref, span_ref,
    packs_ref, forward_packs_ref, skip_ref, weight_ref,
    gact_ref, gpre_ref, ggate_ref, proj_ref, gdecay_ref, gskip_ref, ginit_ref,
    b_ref, c_ref, rate_ref, h_ref, product_ref, select_ref, rank_ref,
):
    length, states = act_ref.shape[1], decay_ref.shape[0]
    wide = states * LANES

    @pl.when(pl.program_id(1) == 0)
    def _():
        spread_maps(maps_ref, 0, states, b_ref)
        spread_maps(maps_ref, states, states, c_ref)
        row = lax.broadcasted_iota(jnp.int32, select_ref.shape, 0) // LANES
        col = lax.broadcasted_iota(jnp.int32, select_ref.shape, 1)
        product_ref[...] = jnp.zeros_like(product_ref)
        rank_ref[...] = jnp.zeros_like(rank_ref)
        select_ref[...] = jnp.where(row == col, 1.0, 0.0).astype(BF16)

    spread_rate(decay_ref, rate_ref)
    rate = jnp.exp(decay_ref[...]) * (-LOG2E)
    me = lax.axis_index("seq")
    count = packs_ref.shape[0]
    entry = jnp.zeros((states, LANES), F32)
    for d in reversed(range(count)):
        joined = jnp.exp2(rate * forward_packs_ref[d, 0, states : states + 1, :]) * entry + packs_ref[d, 0]
        entry = jnp.where(d > me, joined, entry)
    after = span_ref[0, 1]
    skip = jnp.broadcast_to(skip_ref[...], (G, LANES))

    def forward(l, h):
        st = step_ref[0, l]
        u = st * act_ref[0, l]
        for n in range(states):
            h_ref[l, n] = h[n]
        return tuple(
            jnp.exp2(st * rate_ref[n]) * h[n] + u * part(b_ref, l, n) for n in range(states)
        )

    h = lax.fori_loop(
        0, length, forward, tuple(start_ref[0, n] for n in range(states)), unroll=math.gcd(length, 4)
    )
    for n in range(states):
        h_ref[length, n] = h[n]

    def back(k, state):
        carry, gdecay, gskip = list(state[0]), list(state[1]), state[2]
        lines = [length - 1 - 2 * k, length - 2 - 2 * k]
        st, act, u, gy, q, r = [], [], [], [], [], []
        ggate = []
        for l in lines:
            st.append(step_ref[0, l])
            act.append(act_ref[0, l])
            u.append(st[-1] * act[-1])
            gate = gate_ref[0, l]
            grad = grad_ref[0, l]
            sig = 1.0 / (1.0 + jnp.exp(-gate))
            silu = gate * sig
            gy.append(grad * silu)
            ggate.append(grad * y_ref[0, l] * (sig + silu * (1.0 - sig)))
            gskip = gskip + gy[-1] * act[-1]
            q.append(jnp.zeros((G, LANES), F32))
            r.append(jnp.zeros((G, LANES), F32))
        row = pl.multiple_of((length - 2 - 2 * k) * G, 2 * G)
        for n in range(states):
            late, early = [], []
            for i, l in enumerate(lines):
                lam = part(c_ref, l, n) * gy[i] + carry[n]
                early.append(lam * u[i])
                late.append(gy[i] * h_ref[l + 1, n])
                q[i] = q[i] + lam * part(b_ref, l, n)
                carry[n] = jnp.exp2(st[i] * rate_ref[n]) * lam
                w = carry[n] * h_ref[l, n]
                r[i] = r[i] + rate_ref[n] * w
                gdecay[n] = gdecay[n] + st[i] * w
            product_ref[pl.ds(row, 2 * G), n * LANES : (n + 1) * LANES] += jnp.concatenate(early[::-1], axis=0)
            product_ref[pl.ds(row, 2 * G), wide + n * LANES : wide + (n + 1) * LANES] += jnp.concatenate(late[::-1], axis=0)
        gpre = []
        for i, l in enumerate(lines):
            gact_ref[0, l] = skip * gy[i] + st[i] * q[i]
            gstep = LN2 * r[i] + act[i] * q[i]
            gpre.append(gstep / (1.0 + jnp.exp(-delta_ref[0, l])))
        gpre_ref[0, pl.ds(row, 2 * G), :] = jnp.concatenate(gpre[::-1], axis=0).astype(BF16)
        ggate_ref[0, pl.ds(row, 2 * G), :] = jnp.concatenate(ggate[::-1], axis=0).astype(BF16)
        return tuple(carry), tuple(gdecay), gskip

    zero = jnp.zeros((G, LANES), F32)
    first = tuple(
        suffix_ref[0, n] + jnp.exp2(rate_ref[n] * after) * entry[n : n + 1, :] for n in range(states)
    )
    carry, gdecay, gskip = lax.fori_loop(
        0, length // 2, back, (first, (zero,) * states, zero), unroll=math.gcd(length // 2, 2)
    )
    for n in range(states):
        ginit_ref[0, n : n + 1, :] = carry[n][0:1, :]
        total = jnp.sum(gdecay[n] * rate_ref[n], axis=0, keepdims=True)
        gdecay_ref[0, n : n + 1, :] = total * LN2
    gskip_ref[0] = jnp.broadcast_to(jnp.sum(gskip, axis=0, keepdims=True), (8, LANES))

    rank_ref[...] += dot(gpre_ref[0], weight_ref[...], ((1,), (1,)))

    @pl.when(pl.program_id(1) == pl.num_programs(1) - 1)
    def _():
        sums = jnp.dot(product_ref[...].astype(BF16), select_ref[...], preferred_element_type=F32)
        rank = rank_ref.shape[1]
        proj_ref[0, :, :rank] = rank_ref[...].astype(BF16)
        proj_ref[0, :, rank:] = sums[:, : 2 * states].astype(BF16)


def scan_backward(
    act, step, delta, gate, y, grad, maps, decay, start, suffix, span, packs, forward_packs, skip, weight
):
    seqs, length, _, chans = act.shape
    states = decay.shape[0]
    token = pl.BlockSpec((1, length, G, LANES), lambda s, j: (s, 0, 0, j))
    rows = pl.BlockSpec((1, length * G, LANES), lambda s, j: (s, 0, j))
    per_state = pl.BlockSpec((1, states, G, LANES), lambda s, j: (s, 0, 0, j))
    total = pl.BlockSpec((1, states, LANES), lambda s, j: (s, 0, j))
    return pl.pallas_call(
        backward_kernel,
        grid=(seqs, chans // LANES),
        in_specs=[
            token,
            token,
            token,
            token,
            token,
            token,
            pl.BlockSpec((1, length * G, maps.shape[2]), lambda s, j: (s, 0, 0)),
            pl.BlockSpec((states, LANES), lambda s, j: (0, j)),
            per_state,
            per_state,
            pl.BlockSpec((1, 2, G, LANES), lambda s, j: (s, 0, 0, j)),
            pl.BlockSpec((packs.shape[0], 1, states, LANES), lambda s, j: (0, s, 0, j)),
            pl.BlockSpec((packs.shape[0], 1, states + 8, LANES), lambda s, j: (0, s, 0, j)),
            pl.BlockSpec((1, LANES), lambda s, j: (0, j)),
            pl.BlockSpec((weight.shape[0], LANES), lambda s, j: (0, j)),
        ],
        out_specs=[
            token,
            rows,
            rows,
            pl.BlockSpec((1, length * G, weight.shape[0] + 2 * states), lambda s, j: (s, 0, 0)),
            total,
            pl.BlockSpec((1, 8, LANES), lambda s, j: (s, 0, j)),
            total,
        ],
        out_shape=[
            jax.ShapeDtypeStruct(act.shape, F32),
            jax.ShapeDtypeStruct((seqs, length * G, chans), BF16),
            jax.ShapeDtypeStruct((seqs, length * G, chans), BF16),
            jax.ShapeDtypeStruct((seqs, length * G, weight.shape[0] + 2 * states), BF16),
            jax.ShapeDtypeStruct((seqs, states, chans), F32),
            jax.ShapeDtypeStruct((seqs, 8, chans), F32),
            jax.ShapeDtypeStruct((seqs, states, chans), F32),
        ],
        scratch_shapes=[
            pltpu.VMEM((length * G, states * LANES), F32),
            pltpu.VMEM((length * G, states * LANES), F32),
            pltpu.VMEM((states, G, LANES), F32),
            pltpu.VMEM((length + 1, states, G, LANES), F32),
            pltpu.VMEM((length * G, 2 * states * LANES), F32),
            pltpu.VMEM((2 * states * LANES, LANES), BF16),
            pltpu.VMEM((length * G, weight.shape[0]), F32),
        ],
        compiler_params=params("arbitrary", "arbitrary"),
        cost_estimate=estimate(39),
        name="scan_backward",
    )(act, step, delta, gate, y, grad, maps, decay, start, suffix, span, packs, forward_packs, skip, weight)


def remote(src, dst, send, recv, to):
    return pltpu.make_async_remote_copy(
        src_ref=src, dst_ref=dst, send_sem=send, recv_sem=recv, device_id={"chan": to}, device_id_type=MESH
    )


class Line:
    def __init__(self, count):
        self.me = lax.axis_index("chan")
        self.half = count // 2
        self.at = self.me // 2
        self.low = self.me % 2
        self.pair = self.at * 2 + 1 - self.low
        self.right = jnp.minimum(self.at + 1, self.half - 1) * 2 + self.low
        self.left = jnp.maximum(self.at - 1, 0) * 2 + self.low
        self.has_right = self.at < self.half - 1
        self.has_left = self.at > 0

    def greet(self):
        barrier = pltpu.get_barrier_semaphore()

        def signal(to):
            pl.semaphore_signal(barrier, inc=1, device_id={"chan": to}, device_id_type=MESH)

        signal(self.pair)
        pl.when(self.has_right)(lambda: signal(self.right))
        pl.when(self.has_left)(lambda: signal(self.left))
        pl.semaphore_wait(barrier, 1 + jnp.minimum(self.at, 1) + jnp.minimum(self.half - 1 - self.at, 1))


def gather_steps(line, out_ref, width, chunks, sems):
    pair_send, pair_recv, right_send, right_recv, left_send, left_recv = sems
    half = line.half
    rows = out_ref.shape[0] // chunks

    def place(owner, c):
        return out_ref.at[pl.ds(c * rows, rows), pl.ds(pl.multiple_of(owner * width, width), width)]

    def to_pair(owner, slot, c):
        return remote(place(owner, c), place(owner, c), pair_send.at[slot, c], pair_recv.at[slot, c], line.pair)

    def to_right(owner, j, c):
        return remote(place(owner, c), place(owner, c), right_send.at[j, c], right_recv.at[j, c], line.right)

    def to_left(owner, j, c):
        return remote(place(owner, c), place(owner, c), left_send.at[j, c], left_recv.at[j, c], line.left)

    def begin(c):
        pl.when(line.has_right)(lambda: to_right(line.me, 0, c).start())
        pl.when(line.has_left)(lambda: to_left(line.me, 0, c).start())
        to_pair(line.me, 0, c).start()

    def middle(fill=lambda: None):
        for j in range(1, half):
            for c in range(chunks):
                fill()
                @pl.when(line.at >= j)
                def _():
                    owner = line.me - 2 * j
                    to_right(owner, j - 1, c).wait_recv()
                    pl.when(line.has_right)(lambda: to_right(owner, j, c).start())
                    to_pair(owner, j, c).start()

                @pl.when(line.at + j < half)
                def _():
                    owner = line.me + 2 * j
                    to_left(owner, j - 1, c).wait_recv()
                    pl.when(line.has_left)(lambda: to_left(owner, j, c).start())
                    to_pair(owner, half + j, c).start()

    def end():
        for c in range(chunks):
            to_pair(line.me, 0, c).wait()
            pl.when(line.has_right)(lambda: to_right(line.me, 0, c).wait_send())
            pl.when(line.has_left)(lambda: to_left(line.me, 0, c).wait_send())
            for j in range(1, half):
                @pl.when(line.at >= j)
                def _():
                    owner = line.me - 2 * j
                    to_pair(owner, j, c).wait()
                    pl.when(line.has_right)(lambda: to_right(owner, j, c).wait_send())

                @pl.when(line.at + j < half)
                def _():
                    owner = line.me + 2 * j
                    to_pair(owner, half + j, c).wait()
                    pl.when(line.has_left)(lambda: to_left(owner, j, c).wait_send())

    return begin, middle, end


def gather_sems(count, chunks):
    half = count // 2
    return [pltpu.SemaphoreType.DMA((2 * half, chunks))] * 2 + [pltpu.SemaphoreType.DMA((half, chunks))] * 4


def estimate(us):
    return pl.CostEstimate(flops=int(us * 1e8), bytes_accessed=1 << 20, transcendentals=0)


def remote_params(ident):
    return pltpu.CompilerParams(collective_id=ident, has_side_effects=True, vmem_limit_bytes=VMEM_LIMIT)


def whole(count):
    return [pl.BlockSpec(memory_space=pltpu.VMEM)] * count


def chunks_of(rows):
    return next(c for c in (3, 2, 1) if rows % (16 * c) == 0)


def gather_kernel(count, chunks, layers, part_ref, gain_ref, weights_ref, out_ref, *rest):
    flats, rest = rest[:layers], rest[layers:]
    fetched, flat_buf, fetch_sem, store_sem, *sems = rest
    line = Line(count)
    rows, width = part_ref.shape
    mine = pl.ds(pl.multiple_of(line.me * width, width), width)
    height = fetched.shape[1]
    steps = weights_ref.shape[1] // height
    total = layers * steps

    def fetch(i):
        here = weights_ref.at[i // steps, pl.ds(i % steps * height, height)]
        return pltpu.make_async_copy(here, fetched.at[i % 2], fetch_sem.at[i % 2])

    def store(i):
        here = flats[i // steps].at[pl.ds(i % steps * height, height)]
        return pltpu.make_async_copy(flat_buf.at[i % 2], here, store_sem.at[i % 2])

    fetch(0).start()
    fetch(1).start()
    out_ref[:rows, mine] = part_ref[...]
    gain = gain_ref[...]
    terms = []
    for _ in range(3):
        term = gain.astype(BF16).astype(F32)
        terms.append(term)
        gain = gain - term
    terms.append(jnp.zeros((16 - 3 * layers, width), F32))
    out_ref[rows:, mine] = jnp.concatenate(terms, axis=0).astype(BF16)
    line.greet()
    begin, middle, end = gather_steps(line, out_ref, width, chunks, sems)
    for c in range(chunks):
        begin(c)
    done = []

    def flatten():
        i = len(done)
        if i == total:
            return
        done.append(i)
        fetch(i).wait()
        if i >= steps + 2:
            store(i - 2).wait()

        def piece(r, carry):
            here = pl.ds(pl.multiple_of(r * 32, 32), 32)
            value = fetched[i % 2, here].astype(F32)
            value = value.reshape(32, 2 * value.shape[2]).astype(BF16)
            if i < steps:
                flats[0][pl.ds(pl.multiple_of(i * height + r * 32, 32), 32), :] = value
            else:
                flat_buf[i % 2, here, :] = value
            return carry

        lax.fori_loop(0, height // 32, piece, 0)
        if i >= steps:
            store(i).start()
        if i + 2 < total:
            fetch(i + 2).start()

    def fill():
        flatten()
        flatten()

    middle(fill)
    while len(done) < total:
        flatten()
    end()
    for i in range(max(total - 2, steps), total):
        store(i).wait()


def gather_first(part, gain, weights):
    count = lax.axis_size("chan")
    rows, width = part.shape
    layers, model = weights.shape[:2]
    chunks = chunks_of(rows + 16)
    height = 256
    flat = (model, 2 * weights.shape[3])
    full, *flats = pl.pallas_call(
        functools.partial(gather_kernel, count, chunks, layers),
        in_specs=whole(2) + [pl.BlockSpec(memory_space=pl.ANY)],
        out_specs=whole(2) + [pl.BlockSpec(memory_space=pl.ANY)] * (layers - 1),
        out_shape=[jax.ShapeDtypeStruct((rows + 16, count * width), BF16)] + [jax.ShapeDtypeStruct(flat, BF16)] * layers,
        scratch_shapes=[
            pltpu.VMEM((2, height) + weights.shape[2:], BF16),
            pltpu.VMEM((2, height, flat[1]), BF16),
            pltpu.SemaphoreType.DMA((2,)),
            pltpu.SemaphoreType.DMA((2,)),
        ]
        + gather_sems(count, chunks),
        compiler_params=remote_params(0),
        cost_estimate=estimate(25),
        name="gather_first",
    )(part, gain, weights)
    terms = full[rows : rows + 3 * layers].astype(F32)
    return full, terms[:layers] + terms[layers : 2 * layers] + terms[2 * layers :], flats


def scatter_steps(line, part_ref, pair_buf, right_buf, left_buf, stage, width, chunks, sems):
    pair_send, pair_recv, right_send, right_recv, left_send, left_recv = sems
    half = line.half
    rows = part_ref.shape[0] // chunks

    def block(owner, c):
        return part_ref.at[pl.ds(c * rows, rows), pl.ds(pl.multiple_of(owner * width, width), width)]

    def piece(ref, slot, c):
        return ref.at[slot, pl.ds(c * rows, rows)]

    def to_pair(at, c):
        return remote(block(at * 2 + 1 - line.low, c), pair_buf.at[at, pl.ds(c * rows, rows)], pair_send.at[at, c], pair_recv.at[at, c], line.pair)

    def to_right(j, c):
        return remote(piece(stage, j, c), piece(right_buf, j - 1, c), right_send.at[j - 1, c], right_recv.at[j - 1, c], line.right)

    def to_left(j, c):
        return remote(piece(stage, half + j, c), piece(left_buf, j - 1, c), left_send.at[j - 1, c], left_recv.at[j - 1, c], line.left)

    def begin(produce):
        for c in range(chunks):

            def send(at):
                if c == 0:
                    produce(at * 2 + 1 - line.low)
                to_pair(at, c).start()

            for j in range(half - 1, 0, -1):
                pl.when(line.at + j < half)(lambda: send(line.at + j))
                pl.when(line.at >= j)(lambda: send(line.at - j))
            send(line.at)
        for at in range(half):
            produce(at * 2 + line.low)

    def own_and_pair(at, c):
        to_pair(at, c).wait_recv()
        return block(at * 2 + line.low, c)[...].astype(F32) + pair_buf[at, pl.ds(c * rows, rows)].astype(F32)

    def middle(c):
        for j in range(half - 1, 0, -1):
            @pl.when(line.at + j < half)
            def _():
                stage[j, pl.ds(c * rows, rows)] = own_and_pair(line.at + j, c).astype(BF16)

                @pl.when(line.has_left)
                def _():
                    arrived = remote(piece(stage, j, c), piece(right_buf, j, c), right_send.at[j, c], right_recv.at[j, c], line.right)
                    arrived.wait_recv()
                    total = stage[j, pl.ds(c * rows, rows)].astype(F32) + right_buf[j, pl.ds(c * rows, rows)].astype(F32)
                    stage[j, pl.ds(c * rows, rows)] = total.astype(BF16)

                to_right(j, c).start()

            @pl.when(line.at >= j)
            def _():
                stage[half + j, pl.ds(c * rows, rows)] = own_and_pair(line.at - j, c).astype(BF16)

                @pl.when(line.has_right)
                def _():
                    arrived = remote(piece(stage, half + j, c), piece(left_buf, j, c), left_send.at[j, c], left_recv.at[j, c], line.left)
                    arrived.wait_recv()
                    total = stage[half + j, pl.ds(c * rows, rows)].astype(F32) + left_buf[j, pl.ds(c * rows, rows)].astype(F32)
                    stage[half + j, pl.ds(c * rows, rows)] = total.astype(BF16)

                to_left(j, c).start()

    def finish(c, out_ref):
        here = pl.ds(c * rows, rows)
        out_ref[here, :] = own_and_pair(line.at, c)

        @pl.when(line.has_left)
        def _():
            remote(piece(stage, 0, c), piece(right_buf, 0, c), right_send.at[0, c], right_recv.at[0, c], line.right).wait_recv()
            out_ref[here, :] += right_buf[0, here].astype(F32)

        @pl.when(line.has_right)
        def _():
            remote(piece(stage, 0, c), piece(left_buf, 0, c), left_send.at[0, c], left_recv.at[0, c], line.left).wait_recv()
            out_ref[here, :] += left_buf[0, here].astype(F32)

    def end():
        for c in range(chunks):
            for at in range(half):
                to_pair(at, c).wait_send()
            for j in range(1, half):
                pl.when(line.at + j < half)(lambda: to_right(j, c).wait_send())
                pl.when(line.at >= j)(lambda: to_left(j, c).wait_send())

    return begin, middle, finish, end


def scatter_scratch(count, chunks, rows, width):
    half = count // 2
    return (
        [pltpu.VMEM((half, rows, width), BF16)] * 3
        + [pltpu.VMEM((2 * half, rows, width), BF16)]
        + [pltpu.SemaphoreType.DMA((half, chunks))] * 6
    )


def boundary_kernel(
    count, chunks, layer, gated_ref, weights_ref, hidden_ref, new_ref, full_ref, pair_buf, right_buf, left_buf, stage,
    part_ref, weight_ref, weight_sem, *sems,
):
    line = Line(count)
    rows, width = hidden_ref.shape
    mine = pl.ds(pl.multiple_of(line.me * width, width), width)
    fetch = pltpu.make_async_copy(weights_ref.at[layer], weight_ref, weight_sem)
    fetch.start()
    line.greet()
    fetch.wait()

    def produce(owner):
        columns = pl.ds(pl.multiple_of(owner * width, width), width)
        block = jnp.dot(gated_ref[...], weight_ref[:, columns], preferred_element_type=F32)
        part_ref[:, columns] = block.astype(BF16)

    begin, middle, finish, end = scatter_steps(
        line, part_ref, pair_buf, right_buf, left_buf, stage, width, chunks, sems[:6]
    )
    gather_begin, gather_middle, gather_end = gather_steps(line, full_ref, width, chunks, sems[6:])
    begin(produce)
    for c in range(chunks):
        here = pl.ds(c * (rows // chunks), rows // chunks)
        middle(c)
        finish(c, new_ref)
        new_ref[here, :] += hidden_ref[here, :]
        full_ref[here, mine] = new_ref[here, :].astype(BF16)
        gather_begin(c)
    gather_middle()
    gather_end()
    end()


def forward_boundary(gated, weights, layer, hidden):
    count = lax.axis_size("chan")
    rows, width = hidden.shape
    chunks = 2
    return pl.pallas_call(
        functools.partial(boundary_kernel, count, chunks, layer),
        in_specs=[whole(1)[0], pl.BlockSpec(memory_space=pl.ANY), whole(1)[0]],
        out_specs=whole(2),
        out_shape=[jax.ShapeDtypeStruct((rows, width), F32), jax.ShapeDtypeStruct((rows, count * width), BF16)],
        scratch_shapes=scatter_scratch(count, chunks, rows, width)[:4]
        + [
            pltpu.VMEM((rows, count * width), BF16),
            pltpu.VMEM(weights.shape[1:], BF16),
            pltpu.SemaphoreType.DMA,
        ]
        + scatter_scratch(count, chunks, rows, width)[4:]
        + gather_sems(count, chunks),
        compiler_params=remote_params(1),
        cost_estimate=estimate(50),
        name="forward_boundary",
    )(gated, weights, hidden)


def back_kernel(
    count, chunks, gathers, gmixed_ref, weights_ref, grad_ref, hidden_ref, inverse_ref, gain_ref, inner_ref, new_ref, ggain_ref, *more
):
    full_ref, more = (more[0], more[1:]) if gathers else (None, more)
    pair_buf, right_buf, left_buf, stage, inner_buf, column_ref, inner_send, inner_recv = more[:8]
    part_ref, weight_ref, weight_sem = more[8:11]
    sems = more[11:]
    fetch = pltpu.make_async_copy(weights_ref, weight_ref, weight_sem)
    fetch.start()
    line = Line(count)
    rows, width = grad_ref.shape
    model = width * count
    mine = pl.ds(pl.multiple_of(line.me * width, width), width)
    others = [lax.rem(line.me + k, count) for k in range(1, count)]
    barrier = pltpu.get_barrier_semaphore()
    for other in others:
        pl.semaphore_signal(barrier, inc=1, device_id={"chan": other}, device_id_type=MESH)
    pl.semaphore_wait(barrier, count - 1)
    begin, middle, finish, end = scatter_steps(
        line, part_ref, pair_buf, right_buf, left_buf, stage, width, chunks, sems[:6]
    )
    if gathers:
        gather_begin, gather_middle, gather_end = gather_steps(line, full_ref, width, chunks, sems[6:])
    sums = [
        remote(inner_ref, inner_buf.at[k], inner_send.at[k], inner_recv.at[k], others[k]) for k in range(count - 1)
    ]
    for copy in sums:
        copy.start()
    fetch.wait()

    def produce(owner):
        features = pl.ds(pl.multiple_of(owner * width, width), width)
        part_ref[:, features] = dot(gmixed_ref[...], weight_ref[features, :], ((1,), (1,))).astype(BF16)

    begin(produce)
    eye = lax.broadcasted_iota(jnp.int32, (LANES, LANES), 0) == lax.broadcasted_iota(jnp.int32, (LANES, LANES), 1)
    ggain_ref[...] = jnp.zeros_like(ggain_ref)
    for c in range(chunks):
        here = pl.ds(c * (rows // chunks), rows // chunks)
        middle(c)
        if c == 0:
            inner = inner_ref[...]
            for k in range(count - 1):
                sums[k].wait_recv()
                inner = inner + inner_buf[k]
            for b in range(rows // LANES):
                column_ref[pl.ds(b * LANES, LANES), :] = jnp.sum(
                    jnp.where(eye, jnp.broadcast_to(inner[b : b + 1, :], (LANES, LANES)), 0.0), axis=1, keepdims=True
                )
        finish(c, new_ref)
        gnormed = new_ref[here, :]
        inverse = inverse_ref[here, :]
        hidden = hidden_ref[here, :]
        factor = inverse * inverse * column_ref[here, :] * (1.0 / model)
        ggain_ref[0:1, :] += jnp.sum(gnormed * hidden * inverse, axis=0, keepdims=True)
        new = grad_ref[here, :] + inverse * (gain_ref[...] * gnormed) - hidden * factor
        new_ref[here, :] = new
        if gathers:
            full_ref[here, mine] = new.astype(BF16)
            gather_begin(c)
    if gathers:
        gather_middle()
        gather_end()
    end()
    for copy in sums:
        copy.wait_send()


def backward_boundary(gmixed, weights, grad, hidden, inverse, gain, inner, gathers):
    count = lax.axis_size("chan")
    rows, width = hidden.shape
    chunks = 2
    out_shape = [jax.ShapeDtypeStruct((rows, width), F32), jax.ShapeDtypeStruct((8, width), F32)]
    scratch = scatter_scratch(count, chunks, rows, width)
    scratch += [
        pltpu.VMEM((count - 1, rows // LANES, LANES), F32),
        pltpu.VMEM((rows, 1), F32),
        pltpu.SemaphoreType.DMA((count - 1,)),
        pltpu.SemaphoreType.DMA((count - 1,)),
    ]
    product = [
        pltpu.VMEM((rows, count * width), BF16),
        pltpu.VMEM(weights.shape, BF16),
        pltpu.SemaphoreType.DMA,
    ]
    order = scratch[:4] + scratch[10:] + product + scratch[4:10]
    if gathers:
        out_shape.append(jax.ShapeDtypeStruct((rows, count * width), BF16))
        order += gather_sems(count, chunks)
    return pl.pallas_call(
        functools.partial(back_kernel, count, chunks, gathers),
        in_specs=[whole(1)[0], pl.BlockSpec(memory_space=pl.ANY)] + whole(5),
        out_specs=whole(len(out_shape)),
        out_shape=out_shape,
        scratch_shapes=order,
        compiler_params=remote_params(2 if gathers else 3),
        cost_estimate=estimate(50 if gathers else 27),
        name="backward_boundary" if gathers else "backward_last",
    )(gmixed, weights, grad, hidden, inverse, gain, inner.reshape(rows // LANES, LANES))


def sum_kernel(count, part_ref, out_ref, give, arrived, total_ref, result, send1, recv1, send2, recv2):
    me = lax.axis_index("chan")
    rows, width = part_ref.shape
    own, extra = rows // count, width - LANES
    sides = LANES // extra
    block = rows // sides
    more = block // count
    others = [lax.rem(me + k, count) for k in range(1, count)]
    barrier = pltpu.get_barrier_semaphore()
    for other in others:
        pl.semaphore_signal(barrier, inc=1, device_id={"chan": other}, device_id_type=MESH)

    def place_at(k):
        row = lax.broadcasted_iota(jnp.int32, (extra, LANES), 0)
        col = lax.broadcasted_iota(jnp.int32, (extra, LANES), 1)
        return jnp.where(col == row + k * extra, 1.0, 0.0).astype(BF16)

    side = jnp.zeros((block, LANES), F32)
    for k in range(sides):
        side = side + jnp.dot(part_ref[k * block : (k + 1) * block, LANES:], place_at(k), preferred_element_type=F32)
    side = side.astype(BF16)
    for o in range(count):
        give[o, :own, :] = part_ref[o * own : (o + 1) * own, :LANES]
        give[o, own:, :] = side[o * more : (o + 1) * more, :]
    pl.semaphore_wait(barrier, count - 1)
    first, second = [], []
    for k, other in enumerate(others):
        first.append(remote(give.at[other], arrived.at[k], send1.at[k], recv1.at[k], other))
        first[k].start()
    acc = give[me].astype(F32)
    for k in range(count - 1):
        first[k].wait_recv()
        acc = acc + arrived[k].astype(F32)
    total_ref[...] = acc.astype(BF16)
    for k, other in enumerate(others):
        second.append(remote(total_ref, result.at[me], send2.at[k], recv2.at[k], other))
        second[k].start()
    result[me] = total_ref[...]
    for copy in second:
        copy.wait()
    sums = [result[o] for o in range(count)]
    for o in range(count):
        out_ref[o * own : (o + 1) * own, :LANES] = sums[o][:own, :]
    side = jnp.concatenate([value[own:, :].astype(F32) for value in sums], axis=0).astype(BF16)
    for k in range(sides):
        columns = dot(side, place_at(k), ((1,), (1,)))
        out_ref[k * block : (k + 1) * block, LANES:] = columns.astype(BF16)
    for copy in first:
        copy.wait_send()


def sum_chan(part):
    count = lax.axis_size("chan")
    rows, width = part.shape
    piece = rows // count + rows // (LANES // (width - LANES)) // count
    return pl.pallas_call(
        functools.partial(sum_kernel, count),
        in_specs=whole(1),
        out_specs=whole(1)[0],
        out_shape=jax.ShapeDtypeStruct((rows, width), BF16),
        scratch_shapes=[
            pltpu.VMEM((count, piece, LANES), BF16),
            pltpu.VMEM((count - 1, piece, LANES), BF16),
            pltpu.VMEM((piece, LANES), BF16),
            pltpu.VMEM((count, piece, LANES), BF16),
        ]
        + [pltpu.SemaphoreType.DMA((count - 1,))] * 4,
        compiler_params=remote_params(4),
        cost_estimate=estimate(14),
        name="sum_chan",
    )(part)


def exchanged(value, bit):
    return lax.ppermute(value, "seq", [(i, i ^ bit) for i in range(lax.axis_size("seq"))])


class Summed:
    def __init__(self, value, halves):
        self.halves = halves
        self.bit = 1
        self.keep = value
        give = value
        if halves:
            half = value.shape[0] // 2
            core = lax.axis_index("seq") % 2
            self.keep = lax.dynamic_slice_in_dim(value, core * half, half, 0)
            give = lax.dynamic_slice_in_dim(value, (1 - core) * half, half, 0)
        self.wire = exchanged(give, 1)

    def step(self):
        total = self.keep.astype(F32) + self.wire.astype(F32)
        self.bit *= 2
        if self.bit < lax.axis_size("seq"):
            self.keep = total.astype(BF16)
            self.wire = exchanged(self.keep, self.bit)
        elif self.halves:
            self.keep = total.astype(BF16)
            self.wire = exchanged(self.keep, 1)
        else:
            self.keep = total

    def across(self):
        while self.bit * 2 < lax.axis_size("seq"):
            self.step()

    def last(self):
        while self.bit * 2 < lax.axis_size("seq"):
            self.step()
        return self.keep, self.wire

    def total(self):
        while self.bit < lax.axis_size("seq"):
            self.step()
        return (self.keep, self.wire) if self.halves else self.keep


def after(value, *sums):
    value, wires = lax.optimization_barrier((value, [one.wire for one in sums]))
    for one, wire in zip(sums, wires):
        one.wire = wire
    return value


def place_pairs_kernel(core_ref, *refs):
    *ins, out_ref = refs[-5:]
    own = pl.program_id(0) == 0
    for j in range(2):
        out_ref[0, :, j, :] = jnp.where(own, ins[2 * j][...].astype(F32), ins[2 * j + 1][...].astype(F32))


def place_rows_kernel(core_ref, *refs):
    mine, other, out_ref = refs[-3:]
    own = pl.program_id(0) == 0
    out_ref[0] = jnp.where(own, mine[...].astype(F32), other[...].astype(F32))


def place(kernel, parts, base, layer, layers, block, middle):
    half, width = parts[0].shape
    core = (lax.axis_index("seq") % 2).reshape(1)
    steps = half // block

    def where(kept):
        if kept:
            return lambda k, b, core: (jnp.where(k == 0, b, steps - 1), 0)
        return lambda k, b, core: (jnp.where(k == 1, b, 0), 0)

    def out(k, b, core):
        return (layer, (core[0] + k - 2 * core[0] * k) * steps + b) + (0,) * (1 + len(middle))

    ins = [pl.BlockSpec((block, width), where(p % 2 == 0)) for p in range(len(parts))]
    shape = (layers, 2 * half) + middle + (width,)
    args = list(parts)
    aliases = {}
    if base is not None:
        ins.insert(0, pl.BlockSpec(memory_space=pl.ANY))
        args.insert(0, base)
        aliases = {1: 0}
    return pl.pallas_call(
        kernel,
        grid_spec=pltpu.PrefetchScalarGridSpec(
            num_scalar_prefetch=1,
            grid=(2, steps),
            in_specs=ins,
            out_specs=pl.BlockSpec((1, block) + middle + (width,), out),
        ),
        out_shape=jax.ShapeDtypeStruct(shape, F32),
        input_output_aliases=aliases,
        compiler_params=params("arbitrary", "arbitrary"),
        cost_estimate=estimate(5),
        name="place",
    )(core, *args)


def dot(a, b, dims):
    return lax.dot_general(a, b, (dims, ((), ())), preferred_element_type=F32)


def rows_of_packed(rank_columns, rank, states, seqs, taps):
    names = [("xproj", rank_columns), ("dtproj", rank), ("decay", states), ("init", seqs * states)]
    names += [("taps", taps), ("shift", 1), ("bias", 1), ("skip", 1), ("conv", (taps - 1) * seqs)]
    places, row = {}, 0
    for name, size in names:
        places[name] = (row, row + size)
        row += size
    return places, row + (-row) % 16


def mid_kernel(
    gproj_ref, xproj_ref, gact_ref, inner_ref, head_ref, low_ref, taps_ref, shift_ref, rank_ref, gpre_ref, ggate_ref,
    gdecay_ref, gskip_ref, ginit_ref,
    gmixed_ref, packed_ref,
    dotted_ref, pad_ref, gconv_ref, tail_ref, give_ref, got_ref, send_sem, recv_sem,
):
    seqs, length = gact_ref.shape[:2]
    tokens = length * G
    count = gmixed_ref.shape[1] // (2 * LANES)
    taps = taps_ref.shape[0]
    over = taps - 1
    j = pl.program_id(0)
    place, peers = lax.axis_index("seq"), lax.axis_size("seq")
    states = gdecay_ref.shape[1]
    places, _ = rows_of_packed(gproj_ref.shape[1], rank_ref.shape[1], states, seqs, taps)

    def to_previous(t):
        return pltpu.make_async_remote_copy(
            src_ref=give_ref.at[t], dst_ref=got_ref.at[t], send_sem=send_sem.at[t], recv_sem=recv_sem.at[t],
            device_id={"seq": jnp.maximum(place - 1, 0)}, device_id_type=MESH,
        )

    @pl.when(j == 0)
    def _():
        barrier = pltpu.get_barrier_semaphore()

        @pl.when(place < peers - 1)
        def _():
            pl.semaphore_signal(barrier, inc=1, device_id={"seq": place + 1}, device_id_type=MESH)

        pl.when(place > 0)(lambda: pl.semaphore_wait(barrier, 1))

    columns = pl.ds(pl.multiple_of(j * LANES, LANES), LANES)
    gate_columns = pl.ds(pl.multiple_of((count + j) * LANES, LANES), LANES)
    gmixed_ref[:, gate_columns] = ggate_ref[...]
    dotted_ref[...] = jnp.dot(gproj_ref[...], xproj_ref[...], preferred_element_type=F32)
    zero = jnp.zeros((G, LANES), F32)
    weights = [jnp.broadcast_to(taps_ref[k : k + 1, :], (G, LANES)) for k in range(taps)]
    shift = jnp.broadcast_to(shift_ref[...], (G, LANES))
    sums = (zero,) * (taps + 1)
    early = [[None] * seqs for _ in range(over)]
    for s in range(seqs):
        for k in range(over):
            pad_ref[k] = head_ref[s, k]

        def fill(l, carry):
            pad_ref[l + over] = inner_ref[s, l]
            return carry

        lax.fori_loop(0, length, fill, 0, unroll=math.gcd(length, 8))

        def one(l, sums):
            parts = [pad_ref[l + k] for k in range(taps)]
            pre = shift
            for k in range(taps):
                pre = pre + weights[k] * parts[k]
            sig = 1.0 / (1.0 + jnp.exp(-pre))
            here = dotted_ref[pl.ds(pl.multiple_of(s * tokens + l * G, G), G), :]
            gconv = (gact_ref[s, l] + here) * (sig + pre * sig * (1.0 - sig))
            gconv_ref[l] = gconv
            return tuple(sums[k] + gconv * parts[k] for k in range(taps)) + (sums[taps] + gconv,)

        sums = lax.fori_loop(0, length, one, sums, unroll=math.gcd(length, 8))
        for k in range(over):
            gconv_ref[length + k] = shifted(gconv_ref[k], -1, 0.0)
            total = weights[0] * gconv_ref[k]
            for i in range(1, k + 1):
                total = total + weights[i] * gconv_ref[k - i]
            early[k][s] = total[0:1, :]
            give_ref[j, s, k : k + 1, :] = total[0:1, :]

        def inner_of(l):
            total = weights[0] * gconv_ref[l + over]
            for k in range(1, taps):
                total = total + weights[k] * gconv_ref[l + over - k]
            return total

        def pair(p, carry):
            both = jnp.concatenate([inner_of(2 * p), inner_of(2 * p + 1)], axis=0)
            gmixed_ref[pl.ds(pl.multiple_of(s * tokens + 2 * p * G, 2 * G), 2 * G), columns] = both.astype(BF16)
            return carry

        lax.fori_loop(0, length // 2 - 2, pair, 0, unroll=math.gcd(length // 2 - 2, 4))
        for q in range(4):
            tail_ref[j, s, q] = inner_of(length - 4 + q)
    pl.when(place > 0)(lambda: to_previous(j).start())

    def put(name, value):
        first, last = places[name]
        packed_ref[first:last, :] = value.astype(BF16)

    put("xproj", dot(gproj_ref[...], low_ref[...], ((0,), (0,))))
    put("dtproj", dot(rank_ref[...], gpre_ref[...], ((0,), (0,))))
    bias = jnp.dot(jnp.ones((16, seqs * tokens), BF16), gpre_ref[...], preferred_element_type=F32)[0:1, :]
    decay, skip = gdecay_ref[0], gskip_ref[0, 0:1, :]
    for s in range(1, seqs):
        decay = decay + gdecay_ref[s]
        skip = skip + gskip_ref[s, 0:1, :]
    put("decay", decay)
    first = place == 0
    for s in range(seqs):
        row = places["init"][0] + s * states
        packed_ref[row : row + states, :] = jnp.where(first, ginit_ref[s], 0.0).astype(BF16)
    rest = [jnp.sum(value, axis=0, keepdims=True) for value in sums]
    rest += [bias, skip]
    rest += [jnp.where(first, early[k][s], 0.0) for k in range(over) for s in range(seqs)]
    row = places["taps"][0]
    rest += [jnp.zeros((1, LANES), F32)] * (packed_ref.shape[0] - row - len(rest))
    packed_ref[row:, :] = jnp.concatenate(rest, axis=0).astype(BF16)

    @pl.when(j == count - 1)
    def _():
        last_row = lax.broadcasted_iota(jnp.int32, (G, LANES), 0) == G - 1
        inside = place < peers - 1
        for t in range(count):
            pl.when(place < peers - 1)(lambda: to_previous(t).wait_recv())
            for s in range(seqs):
                values = []
                for q in range(4):
                    value = tail_ref[t, s, q]
                    k = q - 4 + over
                    if k >= 0:
                        given = jnp.broadcast_to(got_ref[t, s, k : k + 1, :], (G, LANES))
                        value = value + jnp.where(jnp.logical_and(last_row, inside), given, 0.0)
                    values.append(value)
                for q in (0, 2):
                    row = s * tokens + (length - 4 + q) * G
                    both = jnp.concatenate(values[q : q + 2], axis=0)
                    gmixed_ref[row : row + 2 * G, t * LANES : (t + 1) * LANES] = both.astype(BF16)
            pl.when(place > 0)(lambda: to_previous(t).wait_send())


def mid_backward(
    gproj, xproj, gact, mixed, head, low, taps, shift, rank_part, gpre, ggate, gdecay, gskip, ginit
):
    seqs, length, _, chans = gact.shape
    rows = seqs * length * G
    count = chans // LANES
    states = gdecay.shape[1]
    over = taps.shape[0] - 1
    _, packed_rows = rows_of_packed(gproj.shape[1], rank_part.shape[1], states, seqs, taps.shape[0])
    token = pl.BlockSpec((seqs, length, G, LANES), lambda j: (0, 0, 0, j))
    row = pl.BlockSpec((rows, LANES), lambda j: (0, j))

    def column(height):
        return pl.BlockSpec((height, LANES), lambda j: (0, j))

    def stack(height):
        return pl.BlockSpec((seqs, height, LANES), lambda j: (0, 0, j))

    return pl.pallas_call(
        mid_kernel,
        grid=(count,),
        in_specs=[
            pl.BlockSpec(gproj.shape, lambda j: (0, 0)),
            column(xproj.shape[0]),
            token,
            token,
            pl.BlockSpec((seqs, over, G, LANES), lambda j: (0, 0, 0, j)),
            row,
            column(over + 1),
            column(1),
            pl.BlockSpec(rank_part.shape, lambda j: (0, 0)),
            row,
            row,
            stack(states),
            stack(8),
            stack(states),
        ],
        out_specs=[pl.BlockSpec((rows, 2 * chans), lambda j: (0, 0)), column(packed_rows)],
        out_shape=[
            jax.ShapeDtypeStruct((rows, 2 * chans), BF16),
            jax.ShapeDtypeStruct((packed_rows, chans), BF16),
        ],
        scratch_shapes=[
            pltpu.VMEM((rows, LANES), F32),
            pltpu.VMEM((length + over, G, LANES), F32),
            pltpu.VMEM((length + over, G, LANES), F32),
            pltpu.VMEM((count, seqs, 4, G, LANES), F32),
            pltpu.VMEM((count, seqs, 8, LANES), F32),
            pltpu.VMEM((count, seqs, 8, LANES), F32),
            pltpu.SemaphoreType.DMA((count,)),
            pltpu.SemaphoreType.DMA((count,)),
        ],
        compiler_params=pltpu.CompilerParams(
            dimension_semantics=("arbitrary",), collective_id=5, has_side_effects=True, vmem_limit_bytes=VMEM_LIMIT
        ),
        cost_estimate=estimate(8),
        name="mid_backward",
    )(gproj, xproj, gact, mixed, head, low, taps, shift, rank_part, gpre, ggate, gdecay, gskip, ginit)


def unpack_kernel(layers, places, seqs, *refs):
    smalls, gains, outs = refs[: 2 * layers], refs[2 * layers : 4 * layers], refs[4 * layers :]
    gain, taps, shift, xproj, dtproj, bias, decay, skip, conv, init = outs
    for i in range(layers):
        def rows(name):
            first, last = places[name]
            return smalls[2 * i][first:last, :].astype(F32) + smalls[2 * i + 1][first:last, :].astype(F32)

        gain[i : i + 1, :] = gains[2 * i][0:1, :].astype(F32) + gains[2 * i + 1][0:1, :].astype(F32)
        xproj[i], dtproj[i], decay[i] = rows("xproj"), rows("dtproj"), rows("decay")
        init[i] = rows("init")
        low, high = places["taps"][0], smalls[0].shape[0]
        rest = smalls[2 * i][low:high, :].astype(F32) + smalls[2 * i + 1][low:high, :].astype(F32)

        def of(name):
            first, last = places[name]
            return rest[first - low : last - low, :]

        taps[i] = of("taps")
        shift[i : i + 1, :], bias[i : i + 1, :], skip[i : i + 1, :] = of("shift"), of("bias"), of("skip")
        for k in range(conv.shape[1]):
            conv[i, k] = of("conv")[k * seqs : (k + 1) * seqs, :]


def unpack(smalls, gains, places, seqs, width):
    layers = len(smalls)
    chans = smalls[0][0].shape[1]

    def size(name):
        return places[name][1] - places[name][0]

    shapes = [
        (layers, width), (layers, size("taps"), chans), (layers, chans), (layers, size("xproj"), chans),
        (layers, size("dtproj"), chans), (layers, chans), (layers, size("decay"), chans), (layers, chans),
        (layers, size("conv") // seqs, seqs, chans), (layers, size("init"), chans),
    ]
    args = [value for pair in smalls for value in pair] + [value for pair in gains for value in pair]
    return pl.pallas_call(
        functools.partial(unpack_kernel, layers, places, seqs),
        in_specs=whole(len(args)),
        out_specs=whole(len(shapes)),
        out_shape=[jax.ShapeDtypeStruct(shape, F32) for shape in shapes],
        compiler_params=params(),
        cost_estimate=estimate(3),
        name="unpack",
    )(*args)


def passed_along(value, axis, by):
    peers = lax.axis_size(axis)
    pairs = [(i, i + by) for i in range(peers) if 0 <= i + by < peers]
    return lax.ppermute(value, axis, pairs)


def to_segments(value):
    seqs, tokens, width = value.shape
    return value.reshape(seqs, G, tokens // G, width).transpose(0, 2, 1, 3)


def from_segments(value):
    seqs, length, _, width = value.shape
    return value.transpose(0, 2, 1, 3).reshape(seqs, length * G, width)


def local(
    hidden_in,
    norm_gain,
    in_weight,
    conv_weight,
    conv_bias,
    xproj_weight,
    dtproj_weight,
    dt_bias,
    decay_log,
    skip_gain,
    out_weight,
    conv_state,
    scan_state,
    out_cotangent,
):
    layers = in_weight.shape[0]
    rank = dtproj_weight.shape[1]
    states = decay_log.shape[1]
    seqs, tokens, _ = hidden_in.shape
    length = tokens // G
    rows = seqs * tokens
    chans = in_weight.shape[3]
    model = hidden_in.shape[2] * lax.axis_size("chan")
    taps = conv_weight.shape[1]
    is_first = lax.axis_index("seq") == 0

    first = to_segments(hidden_in).reshape(rows, -1)
    hidden = first.astype(F32)
    full, gains, flats = gather_first(first, norm_gain, in_weight)
    grad = to_segments(out_cotangent).reshape(rows, -1)
    grad_rows = lax.all_gather(grad, "chan", axis=1, tiled=True)
    grad = grad.astype(F32)
    saved = []
    for i in range(layers):
        wide = full[:rows].astype(F32)
        inverse = lax.rsqrt(jnp.sum(wide * wide, axis=1, keepdims=True) / model + EPS)
        normed = (wide * inverse * gains[i]).astype(BF16)
        flat_in = flats[i]
        mixed = dot(normed, flat_in, ((1,), (0,)))
        inner = mixed[:, :chans].reshape(seqs, length, G, chans)
        gate = mixed[:, chans:].reshape(seqs, length, G, chans)
        tail = inner[:, length - taps + 1 :]
        received = passed_along(tail[:, :, G - 1], "seq", 1)
        before = jnp.where(is_first, conv_state[i], received)
        head = jnp.concatenate([before[:, :, None], tail[:, :, : G - 1]], axis=2)
        padded = jnp.concatenate([head, inner], axis=1)
        pre = conv_bias[i] + sum(conv_weight[i, k] * padded[:, k : k + length] for k in range(taps))
        act = jax.nn.silu(pre)
        act_low = act.astype(BF16).reshape(rows, chans)
        projected = sum_chan(dot(act_low, xproj_weight[i], ((1,), (0,))).astype(BF16))
        rank_part = projected[:, :rank]
        maps = projected[:, rank:].reshape(seqs, tokens, 2 * states)
        delta = dot(rank_part, dtproj_weight[i], ((1,), (0,))) + dt_bias[i]
        delta = delta.reshape(seqs, length, G, chans)
        step = jax.nn.softplus(delta)
        prefix, span, packs = scan_ends(act, step, maps, decay_log[i])
        y, gated, start = scan_forward(
            act, step, gate, maps, decay_log[i], prefix, span, packs, scan_state[i], skip_gain[i : i + 1]
        )
        gated = gated.reshape(rows, chans)
        saved.append(
            (hidden, inverse, normed, flat_in, mixed, gate, head, act, act_low, rank_part, maps, delta, step,
             span, packs, y, gated, start)
        )
        if i + 1 < layers:
            hidden, full = forward_boundary(gated, out_weight, i, hidden)
        else:
            branch = dot(gated, out_weight[i], ((1,), (0,))).astype(BF16)
            branch_sum = lax.psum_scatter(branch, "chan", scatter_dimension=1, tiled=True)

    def finish(i, sums):
        nonlocal in_grads, out_grads
        in_grads = place(
            place_pairs_kernel, [*sums["inner"].total(), *sums["gate"].total()], in_grads, i, layers, model // 4, (2,)
        )
        out_grads = place(place_rows_kernel, list(sums["out"].total()), out_grads, i, layers, chans // 2, ())

    smalls = [None] * layers
    in_grads = out_grads = None
    before_sums = None
    for i in reversed(range(layers)):
        (hidden_i, inverse, normed, flat_in, mixed, gate, head, act, act_low, rank_part, maps, delta, step,
         span, packs, y, gated, start) = saved[i]
        sums = {}
        sums["out"] = Summed(dot(gated, grad_rows, ((0,), (0,))).astype(BF16), True)
        grad_gated = dot(grad_rows, out_weight[i], ((1,), (1,)))
        grad_gated = grad_gated.reshape(seqs, length, G, chans)
        suffix, back_packs = scan_adjoint(step, gate, grad_gated, maps, decay_log[i], span)
        back_packs = after(back_packs, sums["out"])
        sums["out"].across()
        scanned = scan_backward(
            act, step, delta, gate, y, grad_gated, maps, decay_log[i], start, suffix, span, back_packs, packs,
            skip_gain[i : i + 1], dtproj_weight[i],
        )
        gact, gpre, ggate, proj_part, gdecay, gskip, ginit = after(scanned, sums["out"])
        sums["out"].step()
        gpre = gpre.reshape(rows, chans)
        ggate = ggate.reshape(rows, chans)
        proj_part = proj_part.reshape(rows, -1)
        sums["gate"] = Summed(dot(normed, ggate, ((0,), (0,))).astype(BF16), True)
        if i == layers - 1:
            proj_part, branch_sum = lax.optimization_barrier((proj_part, branch_sum))
            hidden = hidden + branch_sum.astype(F32)
        proj_part = after(proj_part, sums["gate"])
        sums["gate"].across()
        grad_proj = after(sum_chan(proj_part), sums["out"])
        gmixed, packed = mid_backward(
            grad_proj, xproj_weight[i].T, gact, mixed.reshape(seqs, length, G, -1), head, act_low, conv_weight[i],
            conv_bias[i : i + 1], rank_part, gpre, ggate, gdecay, gskip, ginit,
        )
        gmixed, packed = after((gmixed, packed), sums["gate"])
        sums["gate"].step()
        sums["small"] = Summed(packed, False)
        sums["inner"] = Summed(dot(normed, gmixed[:, :chans], ((0,), (0,))).astype(BF16), True)
        inner_sums = jnp.sum(gmixed.astype(F32) * mixed, axis=1)
        gmixed = after(gmixed, sums["inner"], sums["small"])
        sums["inner"].across()
        sums["small"].across()
        outs = backward_boundary(
            gmixed, flat_in, grad, hidden_i, inverse, norm_gain[i : i + 1], inner_sums, i > 0
        )
        outs = after(outs, sums["inner"], sums["small"])
        grad = outs[0]
        if i > 0:
            grad_rows = outs[2]
        sums["inner"].step()
        sums["gain"] = Summed(outs[1].astype(BF16), False)
        smalls[i] = sums
        if before_sums is not None:
            finish(i + 1, before_sums)
        before_sums = sums
    finish(0, before_sums)
    places, _ = rows_of_packed(xproj_weight.shape[2], rank, states, seqs, taps)
    gain, taps_grad, shift, xproj, dtproj, bias, decay, skip, conv, init = unpack(
        [one["small"].last() for one in smalls], [one["gain"].last() for one in smalls], places, seqs,
        norm_gain.shape[1],
    )

    def back_out(value):
        return from_segments(value.reshape(seqs, length, G, -1))

    return (
        back_out(hidden),
        back_out(grad),
        gain,
        in_grads,
        taps_grad,
        shift,
        xproj.transpose(0, 2, 1),
        dtproj,
        bias,
        decay,
        skip,
        out_grads,
        conv.transpose(0, 2, 1, 3),
        init.reshape(scan_state.shape),
    )


def solution(mesh):
    return jax.shard_map(
        local,
        mesh=mesh,
        in_specs=(
            P(None, "seq", "chan"),
            P(None, "chan"),
            P(None, None, None, "chan"),
            P(None, None, "chan"),
            P(None, "chan"),
            P(None, "chan", None),
            P(None, None, "chan"),
            P(None, "chan"),
            P(None, None, "chan"),
            P(None, "chan"),
            P(None, "chan", None),
            P(None, None, None, "chan"),
            P(None, None, None, "chan"),
            P(None, "seq", "chan"),
        ),
        out_specs=(
            P(None, "seq", "chan"),
            P(None, "seq", "chan"),
            P(None, "chan"),
            P(None, None, None, "chan"),
            P(None, None, "chan"),
            P(None, "chan"),
            P(None, "chan", None),
            P(None, None, "chan"),
            P(None, "chan"),
            P(None, None, "chan"),
            P(None, "chan"),
            P(None, "chan", None),
            P(None, None, None, "chan"),
            P(None, None, None, "chan"),
        ),
        check_vma=False,
    )
```

```python
import functools
import math

import jax
import jax.numpy as jnp
from jax import lax
from jax.experimental import pallas as pl
from jax.experimental.pallas import tpu as pltpu
from jax.sharding import PartitionSpec as P

EPS = 1e-05
G = 8
LANES = 128
LOG2E = 1.4426950408889634
LN2 = 0.6931471805599453
F32 = jnp.float32
BF16 = jnp.bfloat16
VMEM_LIMIT = 48 * 1024 * 1024
MESH = pl.DeviceIdType.MESH


def params(*semantics):
    return pltpu.CompilerParams(dimension_semantics=semantics, vmem_limit_bytes=VMEM_LIMIT)


def spread_maps(maps_ref, first, count, out_ref):
    shape = (maps_ref.shape[2], count * LANES)
    row = lax.broadcasted_iota(jnp.int32, shape, 0)
    col = lax.broadcasted_iota(jnp.int32, shape, 1) // LANES
    choice = jnp.where(row == col + first, 1.0, 0.0).astype(BF16)
    out_ref[...] = jnp.dot(maps_ref[0], choice, preferred_element_type=F32)


def part(ref, l, n):
    return ref[pl.ds(pl.multiple_of(l * G, G), G), n * LANES : (n + 1) * LANES]


def spread_rate(decay_ref, rate_ref):
    rate = jnp.exp(decay_ref[...]) * (-LOG2E)
    for n in range(rate.shape[0]):
        rate_ref[n] = jnp.broadcast_to(rate[n : n + 1, :], (G, LANES))


def shifted(value, by, fill):
    row = lax.broadcasted_iota(jnp.int32, value.shape, 0)
    moved = pltpu.roll(value, by % G, 0)
    inside = row >= by if by > 0 else row < G + by
    return jnp.where(inside, moved, fill)


def segment_prefix(ends, span, rate_ref, direction):
    step = 1
    while step < G:
        moved_span = shifted(span, direction * step, 0.0)
        ends = [
            e + jnp.exp2(span * rate_ref[n]) * shifted(e, direction * step, 0.0)
            for n, e in enumerate(ends)
        ]
        span = span + moved_span
        step *= 2
    return ends, span


class SeqExchange:
    def __init__(self, give_ref, got_ref, send_sem, recv_sem):
        self.refs = give_ref, got_ref
        self.sems = send_sem, recv_sem
        self.me, self.peers = lax.axis_index("seq"), lax.axis_size("seq")
        self.others = [lax.rem(self.me + k, self.peers) for k in range(1, self.peers)]

    def signal(self):
        barrier = pltpu.get_barrier_semaphore()
        for other in self.others:
            pl.semaphore_signal(barrier, inc=1, device_id={"seq": other}, device_id_type=MESH)

    def meet(self):
        if self.others:
            pl.semaphore_wait(pltpu.get_barrier_semaphore(), len(self.others))

    def copy(self, step, k):
        give, got = self.refs
        send, recv = self.sems
        return pltpu.make_async_remote_copy(
            src_ref=give.at[step], dst_ref=got.at[self.me, step], send_sem=send.at[step, k], recv_sem=recv.at[step, k],
            device_id={"seq": self.others[k]}, device_id_type=MESH,
        )

    def start(self, step):
        for k in range(len(self.others)):
            self.copy(step, k).start()

    def wait(self, step):
        for k in range(len(self.others)):
            self.copy(step, k).wait()

    def finish(self, steps):
        for step in range(steps):
            self.wait(step)


def exchange_scratch(steps, rows):
    peers = lax.axis_size("seq")
    sems = pltpu.SemaphoreType.DMA((steps, max(peers - 1, 1)))
    return [pltpu.VMEM((steps, rows, LANES), F32), pltpu.VMEM((peers, steps, rows, LANES), F32), sems, sems]


def exchange_params(ident):
    return pltpu.CompilerParams(
        dimension_semantics=("arbitrary", "arbitrary"), collective_id=ident, has_side_effects=True,
        vmem_limit_bytes=VMEM_LIMIT,
    )


def exchange_step(exchange, packs_ref, give_ref, got_ref, rows):
    seqs, tiles = pl.num_programs(0), pl.num_programs(1)
    step = pl.program_id(0) * tiles + pl.program_id(1)
    total = give_ref.shape[0]
    wide = packs_ref.shape[3] // LANES
    give_ref[step] = rows
    pl.when(step == 0)(exchange.meet)
    exchange.start(step)

    @pl.when(step == total - 1)
    def _():
        exchange.finish(total)
        for i in range(total):
            for d in range(got_ref.shape[0]):
                packs_ref[d, i // wide, :, (i % wide) * LANES : (i % wide + 1) * LANES] = jnp.where(
                    exchange.me == d, give_ref[i], got_ref[d, i]
                )


def forward_kernel(
    act_ref, step_ref, gate_ref, maps_ref, decay_ref, init_ref, skip_ref,
    y_ref, gated_ref, start_ref, span_ref, packs_ref,
    b_ref, c_ref, rate_ref, prefix_ref, spans_ref, give_ref, got_ref, *sems,
):
    length, states = act_ref.shape[1], decay_ref.shape[0]
    phase, s, j = pl.program_id(0), pl.program_id(1), pl.program_id(2)
    step = s * pl.num_programs(2) + j
    exchange = SeqExchange(give_ref, got_ref, *sems)
    pl.when(phase + step == 0)(exchange.signal)
    spread_rate(decay_ref, rate_ref)
    zero = jnp.zeros((G, LANES), F32)

    @pl.when(phase == 0)
    def _():
        pl.when(j == 0)(lambda: spread_maps(maps_ref, 0, states, b_ref.at[s]))

        def one(l, carry):
            h, total = carry
            st = step_ref[0, l]
            u = st * act_ref[0, l]
            h = tuple(
                jnp.exp2(st * rate_ref[n]) * h[n] + u * part(b_ref.at[s], l, n) for n in range(states)
            )
            return h, total + st

        h, total = lax.fori_loop(0, length, one, ((zero,) * states, zero), unroll=math.gcd(length, 8))
        ends, span = segment_prefix(list(h), total, rate_ref, 1)
        for n in range(states):
            prefix_ref[step, n] = shifted(ends[n], 1, 0.0)
        spans_ref[step, 0] = shifted(span, 1, 0.0)
        spans_ref[step, 1] = jnp.broadcast_to(span[G - 1 : G, :], (G, LANES)) - span
        rows = [e[G - 1 : G, :] for e in ends] + [jnp.broadcast_to(span[G - 1 : G, :], (8, LANES))]
        give_ref[step] = jnp.concatenate(rows, axis=0)
        pl.when(step == 0)(exchange.meet)
        exchange.start(step)

    @pl.when(phase == 1)
    def _():
        pl.when(j == 0)(lambda: spread_maps(maps_ref, states, states, c_ref))
        exchange.wait(step)
        rate = jnp.exp(decay_ref[...]) * (-LOG2E)
        entry = init_ref[0]
        for d in range(packs_ref.shape[0]):
            pack = jnp.where(exchange.me == d, give_ref[step], got_ref[d, step])
            packs_ref[d, 0] = pack
            joined = jnp.exp2(rate * pack[states : states + 1, :]) * entry + pack[:states, :]
            entry = jnp.where(d < exchange.me, joined, entry)
        span_ref[0] = spans_ref[step]
        span = spans_ref[step, 0]
        h = []
        for n in range(states):
            first = prefix_ref[step, n] + jnp.exp2(rate_ref[n] * span) * entry[n : n + 1, :]
            start_ref[0, n] = first
            h.append(first)
        skip = jnp.broadcast_to(skip_ref[...], (G, LANES))

        def one(k, h):
            h = list(h)
            halves = []
            for i in range(2):
                l = 2 * k + i
                st = step_ref[0, l]
                act = act_ref[0, l]
                u = st * act
                y = skip * act
                for n in range(states):
                    h[n] = jnp.exp2(st * rate_ref[n]) * h[n] + u * part(b_ref.at[s], l, n)
                    y = y + part(c_ref, l, n) * h[n]
                y_ref[0, l] = y
                gate = gate_ref[0, l]
                halves.append(y * (gate / (1.0 + jnp.exp(-gate))))
            row = pl.multiple_of(k * 2 * G, 2 * G)
            gated_ref[0, pl.ds(row, 2 * G), :] = jnp.concatenate(halves, axis=0).astype(BF16)
            return tuple(h)

        lax.fori_loop(0, length // 2, one, tuple(h), unroll=math.gcd(length // 2, 4))


def scan_forward(act, step, gate, maps, decay, init, skip):
    seqs, length, _, chans = act.shape
    states = decay.shape[0]
    peers = lax.axis_size("seq")
    tiles = chans // LANES
    token = pl.BlockSpec((1, length, G, LANES), lambda p, s, j: (s, 0, 0, j))

    def late(shape, index):
        return pl.BlockSpec(shape, lambda p, s, j: index(p * s, p * j))

    return pl.pallas_call(
        forward_kernel,
        grid=(2, seqs, tiles),
        in_specs=[
            token,
            token,
            late((1, length, G, LANES), lambda s, j: (s, 0, 0, j)),
            pl.BlockSpec((1, length * G, maps.shape[2]), lambda p, s, j: (s, 0, 0)),
            pl.BlockSpec((states, LANES), lambda p, s, j: (0, j)),
            late((1, states, LANES), lambda s, j: (s, 0, j)),
            late((1, LANES), lambda s, j: (0, j)),
        ],
        out_specs=[
            late((1, length, G, LANES), lambda s, j: (s, 0, 0, j)),
            late((1, length * G, LANES), lambda s, j: (s, 0, j)),
            late((1, states, G, LANES), lambda s, j: (s, 0, 0, j)),
            late((1, 2, G, LANES), lambda s, j: (s, 0, 0, j)),
            late((peers, 1, states + 8, LANES), lambda s, j: (0, s, 0, j)),
        ],
        out_shape=[
            jax.ShapeDtypeStruct(act.shape, F32),
            jax.ShapeDtypeStruct((seqs, length * G, chans), BF16),
            pltpu.HBM((seqs, states, G, chans), F32),
            pltpu.HBM((seqs, 2, G, chans), F32),
            pltpu.HBM((peers, seqs, states + 8, chans), F32),
        ],
        scratch_shapes=[
            pltpu.VMEM((seqs, length * G, states * LANES), F32),
            pltpu.VMEM((length * G, states * LANES), F32),
            pltpu.VMEM((states, G, LANES), F32),
            pltpu.VMEM((seqs * tiles, states, G, LANES), F32),
            pltpu.VMEM((seqs * tiles, 2, G, LANES), F32),
        ]
        + exchange_scratch(seqs * tiles, states + 8),
        compiler_params=pltpu.CompilerParams(
            dimension_semantics=("arbitrary",) * 3, collective_id=6, has_side_effects=True,
            vmem_limit_bytes=VMEM_LIMIT,
        ),
        cost_estimate=estimate(20),
        name="scan_forward",
    )(act, step, gate, maps, decay, init, skip)


def adjoint_kernel(
    step_ref, gate_ref, grad_ref, maps_ref, decay_ref, span_ref, suffix_ref, packs_ref, c_ref, rate_ref, give_ref,
    got_ref, *sems,
):
    length, states = step_ref.shape[1], decay_ref.shape[0]
    exchange = SeqExchange(give_ref, got_ref, *sems)
    pl.when(pl.program_id(0) + pl.program_id(1) == 0)(exchange.signal)

    @pl.when(pl.program_id(1) == 0)
    def _():
        spread_maps(maps_ref, states, states, c_ref)

    spread_rate(decay_ref, rate_ref)

    def one(k, carry):
        l = length - 1 - k
        st = step_ref[0, l]
        gate = gate_ref[0, l]
        gy = grad_ref[0, l] * (gate / (1.0 + jnp.exp(-gate)))
        return tuple(
            jnp.exp2(st * rate_ref[n]) * (carry[n] + gy * part(c_ref, l, n)) for n in range(states)
        )

    zero = jnp.zeros((G, LANES), F32)
    carry = lax.fori_loop(0, length, one, (zero,) * states, unroll=math.gcd(length, 8))
    own = span_ref[0, 1, 0:1, :] + span_ref[0, 0, 1:2, :] - span_ref[0, 0] - span_ref[0, 1]
    ends, _ = segment_prefix(list(carry), own, rate_ref, -1)
    for n in range(states):
        suffix_ref[0, n] = shifted(ends[n], -1, 0.0)
    rows = jnp.concatenate([e[0:1, :] for e in ends], axis=0)
    exchange_step(exchange, packs_ref, give_ref, got_ref, rows)


def scan_adjoint(step, gate, grad, maps, decay, span):
    seqs, length, _, chans = step.shape
    states = decay.shape[0]
    peers = lax.axis_size("seq")
    token = pl.BlockSpec((1, length, G, LANES), lambda s, j: (s, 0, 0, j))
    return pl.pallas_call(
        adjoint_kernel,
        grid=(seqs, chans // LANES),
        in_specs=[
            token,
            token,
            token,
            pl.BlockSpec((1, length * G, maps.shape[2]), lambda s, j: (s, 0, 0)),
            pl.BlockSpec((states, LANES), lambda s, j: (0, j)),
            pl.BlockSpec((1, 2, G, LANES), lambda s, j: (s, 0, 0, j)),
        ],
        out_specs=[
            pl.BlockSpec((1, states, G, LANES), lambda s, j: (s, 0, 0, j)),
            pl.BlockSpec((peers, seqs, states, chans), lambda s, j: (0, 0, 0, 0)),
        ],
        out_shape=[
            pltpu.HBM((seqs, states, G, chans), F32),
            pltpu.HBM((peers, seqs, states, chans), F32),
        ],
        scratch_shapes=[
            pltpu.VMEM((length * G, states * LANES), F32),
            pltpu.VMEM((states, G, LANES), F32),
        ]
        + exchange_scratch(seqs * chans // LANES, states),
        compiler_params=exchange_params(7),
        cost_estimate=estimate(15),
        name="scan_adjoint",
    )(step, gate, grad, maps, decay, span)


def backward_kernel(
    act_ref, step_ref, delta_ref, gate_ref, y_ref, grad_ref, maps_ref, decay_ref, start_ref, suffix_ref, span_ref,
    packs_ref, forward_packs_ref, skip_ref, weight_ref,
    gact_ref, gpre_ref, ggate_ref, proj_ref, gdecay_ref, gskip_ref, ginit_ref,
    b_ref, c_ref, rate_ref, h_ref, product_ref, select_ref, rank_ref,
):
    length, states = act_ref.shape[1], decay_ref.shape[0]
    wide = states * LANES

    @pl.when(pl.program_id(1) == 0)
    def _():
        spread_maps(maps_ref, 0, states, b_ref)
        spread_maps(maps_ref, states, states, c_ref)
        row = lax.broadcasted_iota(jnp.int32, select_ref.shape, 0) // LANES
        col = lax.broadcasted_iota(jnp.int32, select_ref.shape, 1)
        product_ref[...] = jnp.zeros_like(product_ref)
        rank_ref[...] = jnp.zeros_like(rank_ref)
        select_ref[...] = jnp.where(row == col, 1.0, 0.0).astype(BF16)

    spread_rate(decay_ref, rate_ref)
    rate = jnp.exp(decay_ref[...]) * (-LOG2E)
    me = lax.axis_index("seq")
    count = packs_ref.shape[0]
    entry = jnp.zeros((states, LANES), F32)
    for d in reversed(range(count)):
        joined = jnp.exp2(rate * forward_packs_ref[d, 0, states : states + 1, :]) * entry + packs_ref[d, 0]
        entry = jnp.where(d > me, joined, entry)
    after = span_ref[0, 1]
    skip = jnp.broadcast_to(skip_ref[...], (G, LANES))

    def forward(l, h):
        st = step_ref[0, l]
        u = st * act_ref[0, l]
        for n in range(states):
            h_ref[l, n] = h[n]
        return tuple(
            jnp.exp2(st * rate_ref[n]) * h[n] + u * part(b_ref, l, n) for n in range(states)
        )

    h = lax.fori_loop(
        0, length, forward, tuple(start_ref[0, n] for n in range(states)), unroll=math.gcd(length, 4)
    )
    for n in range(states):
        h_ref[length, n] = h[n]

    def back(k, state):
        carry, gdecay, gskip = list(state[0]), list(state[1]), state[2]
        lines = [length - 1 - 2 * k, length - 2 - 2 * k]
        st, act, u, gy, q, r = [], [], [], [], [], []
        ggate = []
        for l in lines:
            st.append(step_ref[0, l])
            act.append(act_ref[0, l])
            u.append(st[-1] * act[-1])
            gate = gate_ref[0, l]
            grad = grad_ref[0, l]
            sig = 1.0 / (1.0 + jnp.exp(-gate))
            silu = gate * sig
            gy.append(grad * silu)
            ggate.append(grad * y_ref[0, l] * (sig + silu * (1.0 - sig)))
            gskip = gskip + gy[-1] * act[-1]
            q.append(jnp.zeros((G, LANES), F32))
            r.append(jnp.zeros((G, LANES), F32))
        row = pl.multiple_of((length - 2 - 2 * k) * G, 2 * G)
        for n in range(states):
            late, early = [], []
            for i, l in enumerate(lines):
                lam = part(c_ref, l, n) * gy[i] + carry[n]
                early.append(lam * u[i])
                late.append(gy[i] * h_ref[l + 1, n])
                q[i] = q[i] + lam * part(b_ref, l, n)
                carry[n] = jnp.exp2(st[i] * rate_ref[n]) * lam
                w = carry[n] * h_ref[l, n]
                r[i] = r[i] + rate_ref[n] * w
                gdecay[n] = gdecay[n] + st[i] * w
            product_ref[pl.ds(row, 2 * G), n * LANES : (n + 1) * LANES] += jnp.concatenate(early[::-1], axis=0)
            product_ref[pl.ds(row, 2 * G), wide + n * LANES : wide + (n + 1) * LANES] += jnp.concatenate(late[::-1], axis=0)
        gpre = []
        for i, l in enumerate(lines):
            gact_ref[0, l] = skip * gy[i] + st[i] * q[i]
            gstep = LN2 * r[i] + act[i] * q[i]
            gpre.append(gstep / (1.0 + jnp.exp(-delta_ref[0, l])))
        gpre_ref[0, pl.ds(row, 2 * G), :] = jnp.concatenate(gpre[::-1], axis=0).astype(BF16)
        ggate_ref[0, pl.ds(row, 2 * G), :] = jnp.concatenate(ggate[::-1], axis=0).astype(BF16)
        return tuple(carry), tuple(gdecay), gskip

    zero = jnp.zeros((G, LANES), F32)
    first = tuple(
        suffix_ref[0, n] + jnp.exp2(rate_ref[n] * after) * entry[n : n + 1, :] for n in range(states)
    )
    carry, gdecay, gskip = lax.fori_loop(
        0, length // 2, back, (first, (zero,) * states, zero), unroll=math.gcd(length // 2, 2)
    )
    for n in range(states):
        ginit_ref[0, n : n + 1, :] = carry[n][0:1, :]
        total = jnp.sum(gdecay[n] * rate_ref[n], axis=0, keepdims=True)
        gdecay_ref[0, n : n + 1, :] = total * LN2
    gskip_ref[0] = jnp.broadcast_to(jnp.sum(gskip, axis=0, keepdims=True), (8, LANES))

    rank_ref[...] += dot(gpre_ref[0], weight_ref[...], ((1,), (1,)))

    @pl.when(pl.program_id(1) == pl.num_programs(1) - 1)
    def _():
        sums = jnp.dot(product_ref[...].astype(BF16), select_ref[...], preferred_element_type=F32)
        rank = rank_ref.shape[1]
        proj_ref[0, :, :rank] = rank_ref[...].astype(BF16)
        proj_ref[0, :, rank:] = sums[:, : 2 * states].astype(BF16)


def scan_backward(
    act, step, delta, gate, y, grad, maps, decay, start, suffix, span, packs, forward_packs, skip, weight
):
    seqs, length, _, chans = act.shape
    start, suffix, span, packs, forward_packs = (
        pltpu.with_memory_space_constraint(value, pltpu.HBM) for value in (start, suffix, span, packs, forward_packs)
    )
    states = decay.shape[0]
    token = pl.BlockSpec((1, length, G, LANES), lambda s, j: (s, 0, 0, j))
    rows = pl.BlockSpec((1, length * G, LANES), lambda s, j: (s, 0, j))
    per_state = pl.BlockSpec((1, states, G, LANES), lambda s, j: (s, 0, 0, j))
    total = pl.BlockSpec((1, states, LANES), lambda s, j: (s, 0, j))
    return pl.pallas_call(
        backward_kernel,
        grid=(seqs, chans // LANES),
        in_specs=[
            token,
            token,
            token,
            token,
            token,
            token,
            pl.BlockSpec((1, length * G, maps.shape[2]), lambda s, j: (s, 0, 0)),
            pl.BlockSpec((states, LANES), lambda s, j: (0, j)),
            per_state,
            per_state,
            pl.BlockSpec((1, 2, G, LANES), lambda s, j: (s, 0, 0, j)),
            pl.BlockSpec((packs.shape[0], 1, states, LANES), lambda s, j: (0, s, 0, j)),
            pl.BlockSpec((packs.shape[0], 1, states + 8, LANES), lambda s, j: (0, s, 0, j)),
            pl.BlockSpec((1, LANES), lambda s, j: (0, j)),
            pl.BlockSpec((weight.shape[0], LANES), lambda s, j: (0, j)),
        ],
        out_specs=[
            token,
            rows,
            rows,
            pl.BlockSpec((1, length * G, weight.shape[0] + 2 * states), lambda s, j: (s, 0, 0)),
            total,
            pl.BlockSpec((1, 8, LANES), lambda s, j: (s, 0, j)),
            total,
        ],
        out_shape=[
            jax.ShapeDtypeStruct(act.shape, F32),
            jax.ShapeDtypeStruct((seqs, length * G, chans), BF16),
            jax.ShapeDtypeStruct((seqs, length * G, chans), BF16),
            jax.ShapeDtypeStruct((seqs, length * G, weight.shape[0] + 2 * states), BF16),
            jax.ShapeDtypeStruct((seqs, states, chans), F32),
            jax.ShapeDtypeStruct((seqs, 8, chans), F32),
            jax.ShapeDtypeStruct((seqs, states, chans), F32),
        ],
        scratch_shapes=[
            pltpu.VMEM((length * G, states * LANES), F32),
            pltpu.VMEM((length * G, states * LANES), F32),
            pltpu.VMEM((states, G, LANES), F32),
            pltpu.VMEM((length + 1, states, G, LANES), F32),
            pltpu.VMEM((length * G, 2 * states * LANES), F32),
            pltpu.VMEM((2 * states * LANES, LANES), BF16),
            pltpu.VMEM((length * G, weight.shape[0]), F32),
        ],
        compiler_params=params("arbitrary", "arbitrary"),
        cost_estimate=estimate(39),
        name="scan_backward",
    )(act, step, delta, gate, y, grad, maps, decay, start, suffix, span, packs, forward_packs, skip, weight)


def remote(src, dst, send, recv, to):
    return pltpu.make_async_remote_copy(
        src_ref=src, dst_ref=dst, send_sem=send, recv_sem=recv, device_id={"chan": to}, device_id_type=MESH
    )


class Line:
    def __init__(self, count):
        self.me = lax.axis_index("chan")
        self.half = count // 2
        self.at = self.me // 2
        self.low = self.me % 2
        self.pair = self.at * 2 + 1 - self.low
        self.right = jnp.minimum(self.at + 1, self.half - 1) * 2 + self.low
        self.left = jnp.maximum(self.at - 1, 0) * 2 + self.low
        self.has_right = self.at < self.half - 1
        self.has_left = self.at > 0

    def greet(self):
        barrier = pltpu.get_barrier_semaphore()

        def signal(to):
            pl.semaphore_signal(barrier, inc=1, device_id={"chan": to}, device_id_type=MESH)

        signal(self.pair)
        pl.when(self.has_right)(lambda: signal(self.right))
        pl.when(self.has_left)(lambda: signal(self.left))
        pl.semaphore_wait(barrier, 1 + jnp.minimum(self.at, 1) + jnp.minimum(self.half - 1 - self.at, 1))


def gather_steps(line, out_ref, width, chunks, sems):
    pair_send, pair_recv, right_send, right_recv, left_send, left_recv = sems
    half = line.half
    rows = out_ref.shape[0] // chunks

    def place(owner, c):
        return out_ref.at[pl.ds(c * rows, rows), pl.ds(pl.multiple_of(owner * width, width), width)]

    def to_pair(owner, slot, c):
        return remote(place(owner, c), place(owner, c), pair_send.at[slot, c], pair_recv.at[slot, c], line.pair)

    def to_right(owner, j, c):
        return remote(place(owner, c), place(owner, c), right_send.at[j, c], right_recv.at[j, c], line.right)

    def to_left(owner, j, c):
        return remote(place(owner, c), place(owner, c), left_send.at[j, c], left_recv.at[j, c], line.left)

    def begin(c):
        pl.when(line.has_right)(lambda: to_right(line.me, 0, c).start())
        pl.when(line.has_left)(lambda: to_left(line.me, 0, c).start())
        to_pair(line.me, 0, c).start()

    def middle(fill=lambda: None):
        for j in range(1, half):
            for c in range(chunks):
                fill()
                @pl.when(line.at >= j)
                def _():
                    owner = line.me - 2 * j
                    to_right(owner, j - 1, c).wait_recv()
                    pl.when(line.has_right)(lambda: to_right(owner, j, c).start())
                    to_pair(owner, j, c).start()

                @pl.when(line.at + j < half)
                def _():
                    owner = line.me + 2 * j
                    to_left(owner, j - 1, c).wait_recv()
                    pl.when(line.has_left)(lambda: to_left(owner, j, c).start())
                    to_pair(owner, half + j, c).start()

    def end():
        for c in range(chunks):
            to_pair(line.me, 0, c).wait()
            pl.when(line.has_right)(lambda: to_right(line.me, 0, c).wait_send())
            pl.when(line.has_left)(lambda: to_left(line.me, 0, c).wait_send())
            for j in range(1, half):
                @pl.when(line.at >= j)
                def _():
                    owner = line.me - 2 * j
                    to_pair(owner, j, c).wait()
                    pl.when(line.has_right)(lambda: to_right(owner, j, c).wait_send())

                @pl.when(line.at + j < half)
                def _():
                    owner = line.me + 2 * j
                    to_pair(owner, half + j, c).wait()
                    pl.when(line.has_left)(lambda: to_left(owner, j, c).wait_send())

    return begin, middle, end


def gather_sems(count, chunks):
    half = count // 2
    return [pltpu.SemaphoreType.DMA((2 * half, chunks))] * 2 + [pltpu.SemaphoreType.DMA((half, chunks))] * 4


def estimate(us):
    return pl.CostEstimate(flops=int(us * 1e8), bytes_accessed=1 << 20, transcendentals=0)


def remote_params(ident):
    return pltpu.CompilerParams(collective_id=ident, has_side_effects=True, vmem_limit_bytes=VMEM_LIMIT)


def whole(count):
    return [pl.BlockSpec(memory_space=pltpu.VMEM)] * count


def chunks_of(rows):
    return next(c for c in (3, 2, 1) if rows % (16 * c) == 0)


def gather_kernel(count, chunks, layers, part_ref, gain_ref, weights_ref, out_ref, *rest):
    flats, rest = rest[:layers], rest[layers:]
    fetched, flat_buf, fetch_sem, store_sem, *sems = rest
    line = Line(count)
    rows, width = part_ref.shape
    mine = pl.ds(pl.multiple_of(line.me * width, width), width)
    height = fetched.shape[1]
    steps = weights_ref.shape[1] // height
    total = layers * steps

    def fetch(i):
        here = weights_ref.at[i // steps, pl.ds(i % steps * height, height)]
        return pltpu.make_async_copy(here, fetched.at[i % 2], fetch_sem.at[i % 2])

    def store(i):
        here = flats[i // steps].at[pl.ds(i % steps * height, height)]
        return pltpu.make_async_copy(flat_buf.at[i % 2], here, store_sem.at[i % 2])

    fetch(0).start()
    fetch(1).start()
    out_ref[:rows, mine] = part_ref[...]
    gain = gain_ref[...]
    terms = []
    for _ in range(3):
        term = gain.astype(BF16).astype(F32)
        terms.append(term)
        gain = gain - term
    terms.append(jnp.zeros((16 - 3 * layers, width), F32))
    out_ref[rows:, mine] = jnp.concatenate(terms, axis=0).astype(BF16)
    line.greet()
    begin, middle, end = gather_steps(line, out_ref, width, chunks, sems)
    for c in range(chunks):
        begin(c)
    done = []

    def flatten():
        i = len(done)
        if i == total:
            return
        done.append(i)
        fetch(i).wait()
        if i >= steps + 2:
            store(i - 2).wait()

        def piece(r, carry):
            here = pl.ds(pl.multiple_of(r * 32, 32), 32)
            value = fetched[i % 2, here].astype(F32)
            value = value.reshape(32, 2 * value.shape[2]).astype(BF16)
            if i < steps:
                flats[0][pl.ds(pl.multiple_of(i * height + r * 32, 32), 32), :] = value
            else:
                flat_buf[i % 2, here, :] = value
            return carry

        lax.fori_loop(0, height // 32, piece, 0)
        if i >= steps:
            store(i).start()
        if i + 2 < total:
            fetch(i + 2).start()

    def fill():
        flatten()
        flatten()

    middle(fill)
    while len(done) < total:
        flatten()
    end()
    for i in range(max(total - 2, steps), total):
        store(i).wait()


def gather_first(part, gain, weights):
    count = lax.axis_size("chan")
    rows, width = part.shape
    layers, model = weights.shape[:2]
    chunks = chunks_of(rows + 16)
    height = 256
    flat = (model, 2 * weights.shape[3])
    full, *flats = pl.pallas_call(
        functools.partial(gather_kernel, count, chunks, layers),
        in_specs=whole(2) + [pl.BlockSpec(memory_space=pl.ANY)],
        out_specs=whole(2) + [pl.BlockSpec(memory_space=pl.ANY)] * (layers - 1),
        out_shape=[jax.ShapeDtypeStruct((rows + 16, count * width), BF16)] + [jax.ShapeDtypeStruct(flat, BF16)] * layers,
        scratch_shapes=[
            pltpu.VMEM((2, height) + weights.shape[2:], BF16),
            pltpu.VMEM((2, height, flat[1]), BF16),
            pltpu.SemaphoreType.DMA((2,)),
            pltpu.SemaphoreType.DMA((2,)),
        ]
        + gather_sems(count, chunks),
        compiler_params=remote_params(0),
        cost_estimate=estimate(25),
        name="gather_first",
    )(part, gain, weights)
    terms = full[rows : rows + 3 * layers].astype(F32)
    return full, terms[:layers] + terms[layers : 2 * layers] + terms[2 * layers :], flats


def scatter_steps(line, part_ref, pair_buf, right_buf, left_buf, stage, width, chunks, sems):
    pair_send, pair_recv, right_send, right_recv, left_send, left_recv = sems
    half = line.half
    rows = part_ref.shape[0] // chunks

    def block(owner, c):
        return part_ref.at[pl.ds(c * rows, rows), pl.ds(pl.multiple_of(owner * width, width), width)]

    def piece(ref, slot, c):
        return ref.at[slot, pl.ds(c * rows, rows)]

    def to_pair(at, c):
        return remote(block(at * 2 + 1 - line.low, c), pair_buf.at[at, pl.ds(c * rows, rows)], pair_send.at[at, c], pair_recv.at[at, c], line.pair)

    def to_right(j, c):
        return remote(piece(stage, j, c), piece(right_buf, j - 1, c), right_send.at[j - 1, c], right_recv.at[j - 1, c], line.right)

    def to_left(j, c):
        return remote(piece(stage, half + j, c), piece(left_buf, j - 1, c), left_send.at[j - 1, c], left_recv.at[j - 1, c], line.left)

    def begin(produce):
        for c in range(chunks):

            def send(at):
                if c == 0:
                    produce(at * 2 + 1 - line.low)
                to_pair(at, c).start()

            for j in range(half - 1, 0, -1):
                pl.when(line.at + j < half)(lambda: send(line.at + j))
                pl.when(line.at >= j)(lambda: send(line.at - j))
            send(line.at)
        for at in range(half):
            produce(at * 2 + line.low)

    def own_and_pair(at, c):
        to_pair(at, c).wait_recv()
        return block(at * 2 + line.low, c)[...].astype(F32) + pair_buf[at, pl.ds(c * rows, rows)].astype(F32)

    def middle(c):
        for j in range(half - 1, 0, -1):
            @pl.when(line.at + j < half)
            def _():
                stage[j, pl.ds(c * rows, rows)] = own_and_pair(line.at + j, c).astype(BF16)

                @pl.when(line.has_left)
                def _():
                    arrived = remote(piece(stage, j, c), piece(right_buf, j, c), right_send.at[j, c], right_recv.at[j, c], line.right)
                    arrived.wait_recv()
                    total = stage[j, pl.ds(c * rows, rows)].astype(F32) + right_buf[j, pl.ds(c * rows, rows)].astype(F32)
                    stage[j, pl.ds(c * rows, rows)] = total.astype(BF16)

                to_right(j, c).start()

            @pl.when(line.at >= j)
            def _():
                stage[half + j, pl.ds(c * rows, rows)] = own_and_pair(line.at - j, c).astype(BF16)

                @pl.when(line.has_right)
                def _():
                    arrived = remote(piece(stage, half + j, c), piece(left_buf, j, c), left_send.at[j, c], left_recv.at[j, c], line.left)
                    arrived.wait_recv()
                    total = stage[half + j, pl.ds(c * rows, rows)].astype(F32) + left_buf[j, pl.ds(c * rows, rows)].astype(F32)
                    stage[half + j, pl.ds(c * rows, rows)] = total.astype(BF16)

                to_left(j, c).start()

    def finish(c, out_ref):
        here = pl.ds(c * rows, rows)
        out_ref[here, :] = own_and_pair(line.at, c)

        @pl.when(line.has_left)
        def _():
            remote(piece(stage, 0, c), piece(right_buf, 0, c), right_send.at[0, c], right_recv.at[0, c], line.right).wait_recv()
            out_ref[here, :] += right_buf[0, here].astype(F32)

        @pl.when(line.has_right)
        def _():
            remote(piece(stage, 0, c), piece(left_buf, 0, c), left_send.at[0, c], left_recv.at[0, c], line.left).wait_recv()
            out_ref[here, :] += left_buf[0, here].astype(F32)

    def end():
        for c in range(chunks):
            for at in range(half):
                to_pair(at, c).wait_send()
            for j in range(1, half):
                pl.when(line.at + j < half)(lambda: to_right(j, c).wait_send())
                pl.when(line.at >= j)(lambda: to_left(j, c).wait_send())

    return begin, middle, finish, end


def scatter_scratch(count, chunks, rows, width):
    half = count // 2
    return (
        [pltpu.VMEM((half, rows, width), BF16)] * 3
        + [pltpu.VMEM((2 * half, rows, width), BF16)]
        + [pltpu.SemaphoreType.DMA((half, chunks))] * 6
    )


def boundary_kernel(
    count, chunks, layer, gated_ref, weights_ref, hidden_ref, new_ref, full_ref, pair_buf, right_buf, left_buf, stage,
    part_ref, weight_ref, weight_sem, *sems,
):
    line = Line(count)
    rows, width = hidden_ref.shape
    mine = pl.ds(pl.multiple_of(line.me * width, width), width)
    fetch = pltpu.make_async_copy(weights_ref.at[layer], weight_ref, weight_sem)
    fetch.start()
    line.greet()
    fetch.wait()

    def produce(owner):
        columns = pl.ds(pl.multiple_of(owner * width, width), width)
        block = jnp.dot(gated_ref[...], weight_ref[:, columns], preferred_element_type=F32)
        part_ref[:, columns] = block.astype(BF16)

    begin, middle, finish, end = scatter_steps(
        line, part_ref, pair_buf, right_buf, left_buf, stage, width, chunks, sems[:6]
    )
    gather_begin, gather_middle, gather_end = gather_steps(line, full_ref, width, chunks, sems[6:])
    begin(produce)
    for c in range(chunks):
        here = pl.ds(c * (rows // chunks), rows // chunks)
        middle(c)
        finish(c, new_ref)
        new_ref[here, :] += hidden_ref[here, :]
        full_ref[here, mine] = new_ref[here, :].astype(BF16)
        gather_begin(c)
    gather_middle()
    gather_end()
    end()


def forward_boundary(gated, weights, layer, hidden):
    count = lax.axis_size("chan")
    rows, width = hidden.shape
    chunks = 2
    return pl.pallas_call(
        functools.partial(boundary_kernel, count, chunks, layer),
        in_specs=[whole(1)[0], pl.BlockSpec(memory_space=pl.ANY), whole(1)[0]],
        out_specs=whole(2),
        out_shape=[jax.ShapeDtypeStruct((rows, width), F32), jax.ShapeDtypeStruct((rows, count * width), BF16)],
        scratch_shapes=scatter_scratch(count, chunks, rows, width)[:4]
        + [
            pltpu.VMEM((rows, count * width), BF16),
            pltpu.VMEM(weights.shape[1:], BF16),
            pltpu.SemaphoreType.DMA,
        ]
        + scatter_scratch(count, chunks, rows, width)[4:]
        + gather_sems(count, chunks),
        compiler_params=remote_params(1),
        cost_estimate=estimate(50),
        name="forward_boundary",
    )(gated, weights, hidden)


def back_kernel(
    count, chunks, gathers, gmixed_ref, weights_ref, grad_ref, hidden_ref, inverse_ref, gain_ref, inner_ref, new_ref, ggain_ref, *more
):
    full_ref, more = (more[0], more[1:]) if gathers else (None, more)
    pair_buf, right_buf, left_buf, stage, inner_buf, column_ref, inner_send, inner_recv = more[:8]
    part_ref, weight_ref, weight_sem = more[8:11]
    sems = more[11:]
    fetch = pltpu.make_async_copy(weights_ref, weight_ref, weight_sem)
    fetch.start()
    line = Line(count)
    rows, width = grad_ref.shape
    model = width * count
    mine = pl.ds(pl.multiple_of(line.me * width, width), width)
    others = [lax.rem(line.me + k, count) for k in range(1, count)]
    barrier = pltpu.get_barrier_semaphore()
    for other in others:
        pl.semaphore_signal(barrier, inc=1, device_id={"chan": other}, device_id_type=MESH)
    pl.semaphore_wait(barrier, count - 1)
    begin, middle, finish, end = scatter_steps(
        line, part_ref, pair_buf, right_buf, left_buf, stage, width, chunks, sems[:6]
    )
    if gathers:
        gather_begin, gather_middle, gather_end = gather_steps(line, full_ref, width, chunks, sems[6:])
    sums = [
        remote(inner_ref, inner_buf.at[k], inner_send.at[k], inner_recv.at[k], others[k]) for k in range(count - 1)
    ]
    for copy in sums:
        copy.start()
    fetch.wait()

    def produce(owner):
        features = pl.ds(pl.multiple_of(owner * width, width), width)
        part_ref[:, features] = dot(gmixed_ref[...], weight_ref[features, :], ((1,), (1,))).astype(BF16)

    begin(produce)
    eye = lax.broadcasted_iota(jnp.int32, (LANES, LANES), 0) == lax.broadcasted_iota(jnp.int32, (LANES, LANES), 1)
    ggain_ref[...] = jnp.zeros_like(ggain_ref)
    for c in range(chunks):
        here = pl.ds(c * (rows // chunks), rows // chunks)
        middle(c)
        if c == 0:
            inner = inner_ref[...]
            for k in range(count - 1):
                sums[k].wait_recv()
                inner = inner + inner_buf[k]
            for b in range(rows // LANES):
                column_ref[pl.ds(b * LANES, LANES), :] = jnp.sum(
                    jnp.where(eye, jnp.broadcast_to(inner[b : b + 1, :], (LANES, LANES)), 0.0), axis=1, keepdims=True
                )
        finish(c, new_ref)
        gnormed = new_ref[here, :]
        inverse = inverse_ref[here, :]
        hidden = hidden_ref[here, :]
        factor = inverse * inverse * column_ref[here, :] * (1.0 / model)
        ggain_ref[0:1, :] += jnp.sum(gnormed * hidden * inverse, axis=0, keepdims=True)
        new = grad_ref[here, :] + inverse * (gain_ref[...] * gnormed) - hidden * factor
        new_ref[here, :] = new
        if gathers:
            full_ref[here, mine] = new.astype(BF16)
            gather_begin(c)
    if gathers:
        gather_middle()
        gather_end()
    end()
    for copy in sums:
        copy.wait_send()


def backward_boundary(gmixed, weights, grad, hidden, inverse, gain, inner, gathers):
    count = lax.axis_size("chan")
    rows, width = hidden.shape
    chunks = 2
    out_shape = [jax.ShapeDtypeStruct((rows, width), F32), jax.ShapeDtypeStruct((8, width), F32)]
    scratch = scatter_scratch(count, chunks, rows, width)
    scratch += [
        pltpu.VMEM((count - 1, rows // LANES, LANES), F32),
        pltpu.VMEM((rows, 1), F32),
        pltpu.SemaphoreType.DMA((count - 1,)),
        pltpu.SemaphoreType.DMA((count - 1,)),
    ]
    product = [
        pltpu.VMEM((rows, count * width), BF16),
        pltpu.VMEM(weights.shape, BF16),
        pltpu.SemaphoreType.DMA,
    ]
    order = scratch[:4] + scratch[10:] + product + scratch[4:10]
    if gathers:
        out_shape.append(jax.ShapeDtypeStruct((rows, count * width), BF16))
        order += gather_sems(count, chunks)
    return pl.pallas_call(
        functools.partial(back_kernel, count, chunks, gathers),
        in_specs=[whole(1)[0], pl.BlockSpec(memory_space=pl.ANY)] + whole(5),
        out_specs=whole(len(out_shape)),
        out_shape=out_shape,
        scratch_shapes=order,
        compiler_params=remote_params(2 if gathers else 3),
        cost_estimate=estimate(50 if gathers else 27),
        name="backward_boundary" if gathers else "backward_last",
    )(gmixed, weights, grad, hidden, inverse, gain, inner.reshape(rows // LANES, LANES))


def sum_kernel(count, part_ref, out_ref, give, arrived, total_ref, result, send1, recv1, send2, recv2):
    me = lax.axis_index("chan")
    rows, width = part_ref.shape
    own, extra = rows // count, width - LANES
    sides = LANES // extra
    block = rows // sides
    more = block // count
    others = [lax.rem(me + k, count) for k in range(1, count)]
    barrier = pltpu.get_barrier_semaphore()
    for other in others:
        pl.semaphore_signal(barrier, inc=1, device_id={"chan": other}, device_id_type=MESH)

    def place_at(k):
        row = lax.broadcasted_iota(jnp.int32, (extra, LANES), 0)
        col = lax.broadcasted_iota(jnp.int32, (extra, LANES), 1)
        return jnp.where(col == row + k * extra, 1.0, 0.0).astype(BF16)

    side = jnp.zeros((block, LANES), F32)
    for k in range(sides):
        side = side + jnp.dot(part_ref[k * block : (k + 1) * block, LANES:], place_at(k), preferred_element_type=F32)
    side = side.astype(BF16)
    for o in range(count):
        give[o, :own, :] = part_ref[o * own : (o + 1) * own, :LANES]
        give[o, own:, :] = side[o * more : (o + 1) * more, :]
    pl.semaphore_wait(barrier, count - 1)
    first, second = [], []
    for k, other in enumerate(others):
        first.append(remote(give.at[other], arrived.at[k], send1.at[k], recv1.at[k], other))
        first[k].start()
    acc = give[me].astype(F32)
    for k in range(count - 1):
        first[k].wait_recv()
        acc = acc + arrived[k].astype(F32)
    total_ref[...] = acc.astype(BF16)
    for k, other in enumerate(others):
        second.append(remote(total_ref, result.at[me], send2.at[k], recv2.at[k], other))
        second[k].start()
    result[me] = total_ref[...]
    for copy in second:
        copy.wait()
    sums = [result[o] for o in range(count)]
    for o in range(count):
        out_ref[o * own : (o + 1) * own, :LANES] = sums[o][:own, :]
    side = jnp.concatenate([value[own:, :].astype(F32) for value in sums], axis=0).astype(BF16)
    for k in range(sides):
        columns = dot(side, place_at(k), ((1,), (1,)))
        out_ref[k * block : (k + 1) * block, LANES:] = columns.astype(BF16)
    for copy in first:
        copy.wait_send()


def sum_chan(part):
    count = lax.axis_size("chan")
    rows, width = part.shape
    piece = rows // count + rows // (LANES // (width - LANES)) // count
    return pl.pallas_call(
        functools.partial(sum_kernel, count),
        in_specs=whole(1),
        out_specs=whole(1)[0],
        out_shape=jax.ShapeDtypeStruct((rows, width), BF16),
        scratch_shapes=[
            pltpu.VMEM((count, piece, LANES), BF16),
            pltpu.VMEM((count - 1, piece, LANES), BF16),
            pltpu.VMEM((piece, LANES), BF16),
            pltpu.VMEM((count, piece, LANES), BF16),
        ]
        + [pltpu.SemaphoreType.DMA((count - 1,))] * 4,
        compiler_params=remote_params(4),
        cost_estimate=estimate(14),
        name="sum_chan",
    )(part)


def exchanged(value, bit):
    return lax.ppermute(value, "seq", [(i, i ^ bit) for i in range(lax.axis_size("seq"))])


class Summed:
    def __init__(self, value, halves):
        self.halves = halves
        self.bit = 1
        self.keep = value
        give = value
        if halves:
            half = value.shape[0] // 2
            core = lax.axis_index("seq") % 2
            self.keep = lax.dynamic_slice_in_dim(value, core * half, half, 0)
            give = lax.dynamic_slice_in_dim(value, (1 - core) * half, half, 0)
        self.wire = exchanged(give, 1)

    def step(self):
        total = self.keep.astype(F32) + self.wire.astype(F32)
        self.bit *= 2
        if self.bit < lax.axis_size("seq"):
            self.keep = total.astype(BF16)
            self.wire = exchanged(self.keep, self.bit)
        elif self.halves:
            self.keep = total.astype(BF16)
            self.wire = exchanged(self.keep, 1)
        else:
            self.keep = total

    def across(self):
        while self.bit * 2 < lax.axis_size("seq"):
            self.step()

    def last(self):
        while self.bit * 2 < lax.axis_size("seq"):
            self.step()
        return self.keep, self.wire

    def total(self):
        while self.bit < lax.axis_size("seq"):
            self.step()
        return (self.keep, self.wire) if self.halves else self.keep


def after(value, *sums):
    value, wires = lax.optimization_barrier((value, [one.wire for one in sums]))
    for one, wire in zip(sums, wires):
        one.wire = wire
    return value


def place_pairs_kernel(core_ref, *refs):
    *ins, out_ref = refs[-5:]
    own = pl.program_id(0) == 0
    for j in range(2):
        out_ref[0, :, j, :] = jnp.where(own, ins[2 * j][...].astype(F32), ins[2 * j + 1][...].astype(F32))


def place_rows_kernel(core_ref, *refs):
    mine, other, out_ref = refs[-3:]
    own = pl.program_id(0) == 0
    out_ref[0] = jnp.where(own, mine[...].astype(F32), other[...].astype(F32))


def place(kernel, parts, base, layer, layers, block, middle):
    half, width = parts[0].shape
    core = (lax.axis_index("seq") % 2).reshape(1)
    steps = half // block

    def where(kept):
        if kept:
            return lambda k, b, core: (jnp.where(k == 0, b, steps - 1), 0)
        return lambda k, b, core: (jnp.where(k == 1, b, 0), 0)

    def out(k, b, core):
        return (layer, (core[0] + k - 2 * core[0] * k) * steps + b) + (0,) * (1 + len(middle))

    ins = [pl.BlockSpec((block, width), where(p % 2 == 0)) for p in range(len(parts))]
    shape = (layers, 2 * half) + middle + (width,)
    args = list(parts)
    aliases = {}
    if base is not None:
        ins.insert(0, pl.BlockSpec(memory_space=pl.ANY))
        args.insert(0, base)
        aliases = {1: 0}
    return pl.pallas_call(
        kernel,
        grid_spec=pltpu.PrefetchScalarGridSpec(
            num_scalar_prefetch=1,
            grid=(2, steps),
            in_specs=ins,
            out_specs=pl.BlockSpec((1, block) + middle + (width,), out),
        ),
        out_shape=jax.ShapeDtypeStruct(shape, F32),
        input_output_aliases=aliases,
        compiler_params=params("arbitrary", "arbitrary"),
        cost_estimate=estimate(5),
        name="place",
    )(core, *args)


def dot(a, b, dims):
    return lax.dot_general(a, b, (dims, ((), ())), preferred_element_type=F32)


def rows_of_packed(rank_columns, rank, states, seqs, taps):
    names = [("xproj", rank_columns), ("dtproj", rank), ("decay", states), ("init", seqs * states)]
    names += [("taps", taps), ("shift", 1), ("bias", 1), ("skip", 1), ("conv", (taps - 1) * seqs)]
    places, row = {}, 0
    for name, size in names:
        places[name] = (row, row + size)
        row += size
    return places, row + (-row) % 16


def mid_kernel(
    gproj_ref, xproj_ref, gact_ref, inner_ref, head_ref, low_ref, taps_ref, shift_ref, rank_ref, gpre_ref, ggate_ref,
    gdecay_ref, gskip_ref, ginit_ref,
    gmixed_ref, packed_ref,
    dotted_ref, pad_ref, gconv_ref, tail_ref, give_ref, got_ref, send_sem, recv_sem,
):
    seqs, length = gact_ref.shape[:2]
    tokens = length * G
    count = gmixed_ref.shape[1] // (2 * LANES)
    taps = taps_ref.shape[0]
    over = taps - 1
    j = pl.program_id(0)
    place, peers = lax.axis_index("seq"), lax.axis_size("seq")
    states = gdecay_ref.shape[1]
    places, _ = rows_of_packed(gproj_ref.shape[1], rank_ref.shape[1], states, seqs, taps)

    def to_previous(t):
        return pltpu.make_async_remote_copy(
            src_ref=give_ref.at[t], dst_ref=got_ref.at[t], send_sem=send_sem.at[t], recv_sem=recv_sem.at[t],
            device_id={"seq": jnp.maximum(place - 1, 0)}, device_id_type=MESH,
        )

    @pl.when(j == 0)
    def _():
        barrier = pltpu.get_barrier_semaphore()

        @pl.when(place < peers - 1)
        def _():
            pl.semaphore_signal(barrier, inc=1, device_id={"seq": place + 1}, device_id_type=MESH)

        pl.when(place > 0)(lambda: pl.semaphore_wait(barrier, 1))

    columns = pl.ds(pl.multiple_of(j * LANES, LANES), LANES)
    gate_columns = pl.ds(pl.multiple_of((count + j) * LANES, LANES), LANES)
    gmixed_ref[:, gate_columns] = ggate_ref[...]
    dotted_ref[...] = jnp.dot(gproj_ref[...], xproj_ref[...], preferred_element_type=F32)
    zero = jnp.zeros((G, LANES), F32)
    weights = [jnp.broadcast_to(taps_ref[k : k + 1, :], (G, LANES)) for k in range(taps)]
    shift = jnp.broadcast_to(shift_ref[...], (G, LANES))
    sums = (zero,) * (taps + 1)
    early = [[None] * seqs for _ in range(over)]
    for s in range(seqs):
        for k in range(over):
            pad_ref[k] = head_ref[s, k]

        def fill(l, carry):
            pad_ref[l + over] = inner_ref[s, l]
            return carry

        lax.fori_loop(0, length, fill, 0, unroll=math.gcd(length, 8))

        def one(l, sums):
            parts = [pad_ref[l + k] for k in range(taps)]
            pre = shift
            for k in range(taps):
                pre = pre + weights[k] * parts[k]
            sig = 1.0 / (1.0 + jnp.exp(-pre))
            here = dotted_ref[pl.ds(pl.multiple_of(s * tokens + l * G, G), G), :]
            gconv = (gact_ref[s, l] + here) * (sig + pre * sig * (1.0 - sig))
            gconv_ref[l] = gconv
            return tuple(sums[k] + gconv * parts[k] for k in range(taps)) + (sums[taps] + gconv,)

        sums = lax.fori_loop(0, length, one, sums, unroll=math.gcd(length, 8))
        for k in range(over):
            gconv_ref[length + k] = shifted(gconv_ref[k], -1, 0.0)
            total = weights[0] * gconv_ref[k]
            for i in range(1, k + 1):
                total = total + weights[i] * gconv_ref[k - i]
            early[k][s] = total[0:1, :]
            give_ref[j, s, k : k + 1, :] = total[0:1, :]

        def inner_of(l):
            total = weights[0] * gconv_ref[l + over]
            for k in range(1, taps):
                total = total + weights[k] * gconv_ref[l + over - k]
            return total

        def pair(p, carry):
            both = jnp.concatenate([inner_of(2 * p), inner_of(2 * p + 1)], axis=0)
            gmixed_ref[pl.ds(pl.multiple_of(s * tokens + 2 * p * G, 2 * G), 2 * G), columns] = both.astype(BF16)
            return carry

        lax.fori_loop(0, length // 2 - 2, pair, 0, unroll=math.gcd(length // 2 - 2, 4))
        for q in range(4):
            tail_ref[j, s, q] = inner_of(length - 4 + q)
    pl.when(place > 0)(lambda: to_previous(j).start())

    def put(name, value):
        first, last = places[name]
        packed_ref[first:last, :] = value.astype(BF16)

    put("xproj", dot(gproj_ref[...], low_ref[...], ((0,), (0,))))
    put("dtproj", dot(rank_ref[...], gpre_ref[...], ((0,), (0,))))
    bias = jnp.dot(jnp.ones((16, seqs * tokens), BF16), gpre_ref[...], preferred_element_type=F32)[0:1, :]
    decay, skip = gdecay_ref[0], gskip_ref[0, 0:1, :]
    for s in range(1, seqs):
        decay = decay + gdecay_ref[s]
        skip = skip + gskip_ref[s, 0:1, :]
    put("decay", decay)
    first = place == 0
    for s in range(seqs):
        row = places["init"][0] + s * states
        packed_ref[row : row + states, :] = jnp.where(first, ginit_ref[s], 0.0).astype(BF16)
    rest = [jnp.sum(value, axis=0, keepdims=True) for value in sums]
    rest += [bias, skip]
    rest += [jnp.where(first, early[k][s], 0.0) for k in range(over) for s in range(seqs)]
    row = places["taps"][0]
    rest += [jnp.zeros((1, LANES), F32)] * (packed_ref.shape[0] - row - len(rest))
    packed_ref[row:, :] = jnp.concatenate(rest, axis=0).astype(BF16)

    @pl.when(j == count - 1)
    def _():
        last_row = lax.broadcasted_iota(jnp.int32, (G, LANES), 0) == G - 1
        inside = place < peers - 1
        for t in range(count):
            pl.when(place < peers - 1)(lambda: to_previous(t).wait_recv())
            for s in range(seqs):
                values = []
                for q in range(4):
                    value = tail_ref[t, s, q]
                    k = q - 4 + over
                    if k >= 0:
                        given = jnp.broadcast_to(got_ref[t, s, k : k + 1, :], (G, LANES))
                        value = value + jnp.where(jnp.logical_and(last_row, inside), given, 0.0)
                    values.append(value)
                for q in (0, 2):
                    row = s * tokens + (length - 4 + q) * G
                    both = jnp.concatenate(values[q : q + 2], axis=0)
                    gmixed_ref[row : row + 2 * G, t * LANES : (t + 1) * LANES] = both.astype(BF16)
            pl.when(place > 0)(lambda: to_previous(t).wait_send())


def mid_backward(
    gproj, xproj, gact, mixed, head, low, taps, shift, rank_part, gpre, ggate, gdecay, gskip, ginit
):
    seqs, length, _, chans = gact.shape
    rows = seqs * length * G
    count = chans // LANES
    states = gdecay.shape[1]
    over = taps.shape[0] - 1
    _, packed_rows = rows_of_packed(gproj.shape[1], rank_part.shape[1], states, seqs, taps.shape[0])
    token = pl.BlockSpec((seqs, length, G, LANES), lambda j: (0, 0, 0, j))
    row = pl.BlockSpec((rows, LANES), lambda j: (0, j))

    def column(height):
        return pl.BlockSpec((height, LANES), lambda j: (0, j))

    def stack(height):
        return pl.BlockSpec((seqs, height, LANES), lambda j: (0, 0, j))

    return pl.pallas_call(
        mid_kernel,
        grid=(count,),
        in_specs=[
            pl.BlockSpec(gproj.shape, lambda j: (0, 0)),
            column(xproj.shape[0]),
            token,
            token,
            pl.BlockSpec((seqs, over, G, LANES), lambda j: (0, 0, 0, j)),
            row,
            column(over + 1),
            column(1),
            pl.BlockSpec(rank_part.shape, lambda j: (0, 0)),
            row,
            row,
            stack(states),
            stack(8),
            stack(states),
        ],
        out_specs=[pl.BlockSpec((rows, 2 * chans), lambda j: (0, 0)), column(packed_rows)],
        out_shape=[
            jax.ShapeDtypeStruct((rows, 2 * chans), BF16),
            jax.ShapeDtypeStruct((packed_rows, chans), BF16),
        ],
        scratch_shapes=[
            pltpu.VMEM((rows, LANES), F32),
            pltpu.VMEM((length + over, G, LANES), F32),
            pltpu.VMEM((length + over, G, LANES), F32),
            pltpu.VMEM((count, seqs, 4, G, LANES), F32),
            pltpu.VMEM((count, seqs, 8, LANES), F32),
            pltpu.VMEM((count, seqs, 8, LANES), F32),
            pltpu.SemaphoreType.DMA((count,)),
            pltpu.SemaphoreType.DMA((count,)),
        ],
        compiler_params=pltpu.CompilerParams(
            dimension_semantics=("arbitrary",), collective_id=5, has_side_effects=True, vmem_limit_bytes=VMEM_LIMIT
        ),
        cost_estimate=estimate(8),
        name="mid_backward",
    )(gproj, xproj, gact, mixed, head, low, taps, shift, rank_part, gpre, ggate, gdecay, gskip, ginit)


def unpack_kernel(layers, places, seqs, *refs):
    smalls, gains, outs = refs[: 2 * layers], refs[2 * layers : 4 * layers], refs[4 * layers :]
    gain, taps, shift, xproj, dtproj, bias, decay, skip, conv, init = outs
    for i in range(layers):
        def rows(name):
            first, last = places[name]
            return smalls[2 * i][first:last, :].astype(F32) + smalls[2 * i + 1][first:last, :].astype(F32)

        gain[i : i + 1, :] = gains[2 * i][0:1, :].astype(F32) + gains[2 * i + 1][0:1, :].astype(F32)
        xproj[i], dtproj[i], decay[i] = rows("xproj"), rows("dtproj"), rows("decay")
        init[i] = rows("init")
        low, high = places["taps"][0], smalls[0].shape[0]
        rest = smalls[2 * i][low:high, :].astype(F32) + smalls[2 * i + 1][low:high, :].astype(F32)

        def of(name):
            first, last = places[name]
            return rest[first - low : last - low, :]

        taps[i] = of("taps")
        shift[i : i + 1, :], bias[i : i + 1, :], skip[i : i + 1, :] = of("shift"), of("bias"), of("skip")
        for k in range(conv.shape[1]):
            conv[i, k] = of("conv")[k * seqs : (k + 1) * seqs, :]


def unpack(smalls, gains, places, seqs, width):
    layers = len(smalls)
    chans = smalls[0][0].shape[1]

    def size(name):
        return places[name][1] - places[name][0]

    shapes = [
        (layers, width), (layers, size("taps"), chans), (layers, chans), (layers, size("xproj"), chans),
        (layers, size("dtproj"), chans), (layers, chans), (layers, size("decay"), chans), (layers, chans),
        (layers, size("conv") // seqs, seqs, chans), (layers, size("init"), chans),
    ]
    args = [value for pair in smalls for value in pair] + [value for pair in gains for value in pair]
    return pl.pallas_call(
        functools.partial(unpack_kernel, layers, places, seqs),
        in_specs=whole(len(args)),
        out_specs=whole(len(shapes)),
        out_shape=[jax.ShapeDtypeStruct(shape, F32) for shape in shapes],
        compiler_params=params(),
        cost_estimate=estimate(3),
        name="unpack",
    )(*args)


def passed_along(value, axis, by):
    peers = lax.axis_size(axis)
    pairs = [(i, i + by) for i in range(peers) if 0 <= i + by < peers]
    return lax.ppermute(value, axis, pairs)


def to_segments(value):
    seqs, tokens, width = value.shape
    return value.reshape(seqs, G, tokens // G, width).transpose(0, 2, 1, 3)


def from_segments(value):
    seqs, length, _, width = value.shape
    return value.transpose(0, 2, 1, 3).reshape(seqs, length * G, width)


def local(
    hidden_in,
    norm_gain,
    in_weight,
    conv_weight,
    conv_bias,
    xproj_weight,
    dtproj_weight,
    dt_bias,
    decay_log,
    skip_gain,
    out_weight,
    conv_state,
    scan_state,
    out_cotangent,
):
    layers = in_weight.shape[0]
    rank = dtproj_weight.shape[1]
    states = decay_log.shape[1]
    seqs, tokens, _ = hidden_in.shape
    length = tokens // G
    rows = seqs * tokens
    chans = in_weight.shape[3]
    model = hidden_in.shape[2] * lax.axis_size("chan")
    taps = conv_weight.shape[1]
    is_first = lax.axis_index("seq") == 0

    first = to_segments(hidden_in).reshape(rows, -1)
    hidden = first.astype(F32)
    full, gains, flats = gather_first(first, norm_gain, in_weight)
    grad = to_segments(out_cotangent).reshape(rows, -1)
    grad_rows = lax.all_gather(grad, "chan", axis=1, tiled=True)
    grad = grad.astype(F32)
    saved = []
    for i in range(layers):
        wide = full[:rows].astype(F32)
        inverse = lax.rsqrt(jnp.sum(wide * wide, axis=1, keepdims=True) / model + EPS)
        normed = (wide * inverse * gains[i]).astype(BF16)
        flat_in = flats[i]
        mixed = dot(normed, flat_in, ((1,), (0,)))
        inner = mixed[:, :chans].reshape(seqs, length, G, chans)
        gate = mixed[:, chans:].reshape(seqs, length, G, chans)
        tail = inner[:, length - taps + 1 :]
        received = passed_along(tail[:, :, G - 1], "seq", 1)
        before = jnp.where(is_first, conv_state[i], received)
        head = jnp.concatenate([before[:, :, None], tail[:, :, : G - 1]], axis=2)
        padded = jnp.concatenate([head, inner], axis=1)
        pre = conv_bias[i] + sum(conv_weight[i, k] * padded[:, k : k + length] for k in range(taps))
        act = jax.nn.silu(pre)
        act_low = act.astype(BF16).reshape(rows, chans)
        projected = sum_chan(dot(act_low, xproj_weight[i], ((1,), (0,))).astype(BF16))
        rank_part = projected[:, :rank]
        maps = projected[:, rank:].reshape(seqs, tokens, 2 * states)
        delta = dot(rank_part, dtproj_weight[i], ((1,), (0,))) + dt_bias[i]
        delta = delta.reshape(seqs, length, G, chans)
        step = jax.nn.softplus(delta)
        y, gated, start, span, packs = scan_forward(
            act, step, gate, maps, decay_log[i], scan_state[i], skip_gain[i : i + 1]
        )
        gated = gated.reshape(rows, chans)
        saved.append(
            (hidden, inverse, normed, flat_in, mixed, gate, head, act, act_low, rank_part, maps, delta, step,
             span, packs, y, gated, start)
        )
        if i + 1 < layers:
            hidden, full = forward_boundary(gated, out_weight, i, hidden)
        else:
            branch = dot(gated, out_weight[i], ((1,), (0,))).astype(BF16)
            branch_sum = lax.psum_scatter(branch, "chan", scatter_dimension=1, tiled=True)

    def finish(i, sums):
        nonlocal in_grads, out_grads
        in_grads = place(
            place_pairs_kernel, [*sums["inner"].total(), *sums["gate"].total()], in_grads, i, layers, model // 4, (2,)
        )
        out_grads = place(place_rows_kernel, list(sums["out"].total()), out_grads, i, layers, chans // 2, ())

    smalls = [None] * layers
    in_grads = out_grads = None
    before_sums = None
    for i in reversed(range(layers)):
        (hidden_i, inverse, normed, flat_in, mixed, gate, head, act, act_low, rank_part, maps, delta, step,
         span, packs, y, gated, start) = saved[i]
        sums = {}
        sums["out"] = Summed(dot(gated, grad_rows, ((0,), (0,))).astype(BF16), True)
        grad_gated = dot(grad_rows, out_weight[i], ((1,), (1,)))
        grad_gated = grad_gated.reshape(seqs, length, G, chans)
        suffix, back_packs = scan_adjoint(step, gate, grad_gated, maps, decay_log[i], span)
        back_packs = after(back_packs, sums["out"])
        sums["out"].across()
        scanned = scan_backward(
            act, step, delta, gate, y, grad_gated, maps, decay_log[i], start, suffix, span, back_packs, packs,
            skip_gain[i : i + 1], dtproj_weight[i],
        )
        gact, gpre, ggate, proj_part, gdecay, gskip, ginit = after(scanned, sums["out"])
        sums["out"].step()
        gpre = gpre.reshape(rows, chans)
        ggate = ggate.reshape(rows, chans)
        proj_part = proj_part.reshape(rows, -1)
        sums["gate"] = Summed(dot(normed, ggate, ((0,), (0,))).astype(BF16), True)
        if i == layers - 1:
            proj_part, branch_sum = lax.optimization_barrier((proj_part, branch_sum))
            hidden = hidden + branch_sum.astype(F32)
        proj_part = after(proj_part, sums["gate"])
        sums["gate"].across()
        grad_proj = after(sum_chan(proj_part), sums["out"])
        gmixed, packed = mid_backward(
            grad_proj, xproj_weight[i].T, gact, mixed.reshape(seqs, length, G, -1), head, act_low, conv_weight[i],
            conv_bias[i : i + 1], rank_part, gpre, ggate, gdecay, gskip, ginit,
        )
        gmixed, packed = after((gmixed, packed), sums["gate"])
        sums["gate"].step()
        sums["small"] = Summed(packed, False)
        sums["inner"] = Summed(dot(normed, gmixed[:, :chans], ((0,), (0,))).astype(BF16), True)
        inner_sums = jnp.sum(gmixed.astype(F32) * mixed, axis=1)
        gmixed = after(gmixed, sums["inner"], sums["small"])
        sums["inner"].across()
        sums["small"].across()
        outs = backward_boundary(
            gmixed, flat_in, grad, hidden_i, inverse, norm_gain[i : i + 1], inner_sums, i > 0
        )
        outs = after(outs, sums["inner"], sums["small"])
        grad = outs[0]
        if i > 0:
            grad_rows = outs[2]
        sums["inner"].step()
        sums["gain"] = Summed(outs[1].astype(BF16), False)
        smalls[i] = sums
        if before_sums is not None:
            finish(i + 1, before_sums)
        before_sums = sums
    finish(0, before_sums)
    places, _ = rows_of_packed(xproj_weight.shape[2], rank, states, seqs, taps)
    gain, taps_grad, shift, xproj, dtproj, bias, decay, skip, conv, init = unpack(
        [one["small"].last() for one in smalls], [one["gain"].last() for one in smalls], places, seqs,
        norm_gain.shape[1],
    )

    def back_out(value):
        return from_segments(value.reshape(seqs, length, G, -1))

    return (
        back_out(hidden),
        back_out(grad),
        gain,
        in_grads,
        taps_grad,
        shift,
        xproj.transpose(0, 2, 1),
        dtproj,
        bias,
        decay,
        skip,
        out_grads,
        conv.transpose(0, 2, 1, 3),
        init.reshape(scan_state.shape),
    )


def solution(mesh):
    return jax.shard_map(
        local,
        mesh=mesh,
        in_specs=(
            P(None, "seq", "chan"),
            P(None, "chan"),
            P(None, None, None, "chan"),
            P(None, None, "chan"),
            P(None, "chan"),
            P(None, "chan", None),
            P(None, None, "chan"),
            P(None, "chan"),
            P(None, None, "chan"),
            P(None, "chan"),
            P(None, "chan", None),
            P(None, None, None, "chan"),
            P(None, None, None, "chan"),
            P(None, "seq", "chan"),
        ),
        out_specs=(
            P(None, "seq", "chan"),
            P(None, "seq", "chan"),
            P(None, "chan"),
            P(None, None, None, "chan"),
            P(None, None, "chan"),
            P(None, "chan"),
            P(None, "chan", None),
            P(None, None, "chan"),
            P(None, "chan"),
            P(None, None, "chan"),
            P(None, "chan"),
            P(None, "chan", None),
            P(None, None, None, "chan"),
            P(None, None, None, "chan"),
        ),
        check_vma=False,
    )
```

```python
import functools
import math

import jax
import jax.numpy as jnp
from jax import lax
from jax.experimental import pallas as pl
from jax.experimental.pallas import tpu as pltpu
from jax.sharding import PartitionSpec as P

EPS = 1e-05
G = 8
LANES = 128
LOG2E = 1.4426950408889634
LN2 = 0.6931471805599453
F32 = jnp.float32
BF16 = jnp.bfloat16
VMEM_LIMIT = 48 * 1024 * 1024
MESH = pl.DeviceIdType.MESH


def params(*semantics):
    return pltpu.CompilerParams(dimension_semantics=semantics, vmem_limit_bytes=VMEM_LIMIT)


def spread_maps(maps_ref, first, count, out_ref):
    shape = (maps_ref.shape[2], count * LANES)
    row = lax.broadcasted_iota(jnp.int32, shape, 0)
    col = lax.broadcasted_iota(jnp.int32, shape, 1) // LANES
    choice = jnp.where(row == col + first, 1.0, 0.0).astype(BF16)
    out_ref[...] = jnp.dot(maps_ref[0], choice, preferred_element_type=F32)


def part(ref, l, n):
    return ref[pl.ds(pl.multiple_of(l * G, G), G), n * LANES : (n + 1) * LANES]


def spread_rate(decay_ref, rate_ref):
    rate = jnp.exp(decay_ref[...]) * (-LOG2E)
    for n in range(rate.shape[0]):
        rate_ref[n] = jnp.broadcast_to(rate[n : n + 1, :], (G, LANES))


def shifted(value, by, fill):
    row = lax.broadcasted_iota(jnp.int32, value.shape, 0)
    moved = pltpu.roll(value, by % G, 0)
    inside = row >= by if by > 0 else row < G + by
    return jnp.where(inside, moved, fill)


def segment_prefix(ends, span, rate_ref, direction):
    step = 1
    while step < G:
        moved_span = shifted(span, direction * step, 0.0)
        ends = [
            e + jnp.exp2(span * rate_ref[n]) * shifted(e, direction * step, 0.0)
            for n, e in enumerate(ends)
        ]
        span = span + moved_span
        step *= 2
    return ends, span


class SeqExchange:
    def __init__(self, give_ref, got_ref, send_sem, recv_sem):
        self.refs = give_ref, got_ref
        self.sems = send_sem, recv_sem
        self.me, self.peers = lax.axis_index("seq"), lax.axis_size("seq")
        self.others = [lax.rem(self.me + k, self.peers) for k in range(1, self.peers)]

    def signal(self):
        barrier = pltpu.get_barrier_semaphore()
        for other in self.others:
            pl.semaphore_signal(barrier, inc=1, device_id={"seq": other}, device_id_type=MESH)

    def meet(self):
        if self.others:
            pl.semaphore_wait(pltpu.get_barrier_semaphore(), len(self.others))

    def copy(self, step, k):
        give, got = self.refs
        send, recv = self.sems
        return pltpu.make_async_remote_copy(
            src_ref=give.at[step], dst_ref=got.at[self.me, step], send_sem=send.at[step, k], recv_sem=recv.at[step, k],
            device_id={"seq": self.others[k]}, device_id_type=MESH,
        )

    def start(self, step):
        for k in range(len(self.others)):
            self.copy(step, k).start()

    def wait(self, step):
        for k in range(len(self.others)):
            self.copy(step, k).wait()

    def finish(self, steps):
        for step in range(steps):
            self.wait(step)


def exchange_scratch(steps, rows):
    peers = lax.axis_size("seq")
    sems = pltpu.SemaphoreType.DMA((steps, max(peers - 1, 1)))
    return [pltpu.VMEM((steps, rows, LANES), F32), pltpu.VMEM((peers, steps, rows, LANES), F32), sems, sems]


def exchange_params(ident):
    return pltpu.CompilerParams(
        dimension_semantics=("arbitrary", "arbitrary"), collective_id=ident, has_side_effects=True,
        vmem_limit_bytes=VMEM_LIMIT,
    )


def exchange_step(exchange, packs_ref, give_ref, got_ref, rows):
    seqs, tiles = pl.num_programs(0), pl.num_programs(1)
    step = pl.program_id(0) * tiles + pl.program_id(1)
    total = give_ref.shape[0]
    wide = packs_ref.shape[3] // LANES
    give_ref[step] = rows
    pl.when(step == 0)(exchange.meet)
    exchange.start(step)

    @pl.when(step == total - 1)
    def _():
        exchange.finish(total)
        for i in range(total):
            for d in range(got_ref.shape[0]):
                packs_ref[d, i // wide, :, (i % wide) * LANES : (i % wide + 1) * LANES] = jnp.where(
                    exchange.me == d, give_ref[i], got_ref[d, i]
                )


def forward_kernel(
    act_ref, step_ref, gate_ref, maps_ref, decay_ref, init_ref, skip_ref,
    y_ref, gated_ref, start_ref, span_ref, packs_ref,
    b_ref, c_ref, rate_ref, prefix_ref, spans_ref, give_ref, got_ref, *sems,
):
    length, states = act_ref.shape[1], decay_ref.shape[0]
    phase, s, j = pl.program_id(0), pl.program_id(1), pl.program_id(2)
    step = s * pl.num_programs(2) + j
    exchange = SeqExchange(give_ref, got_ref, *sems)
    pl.when(phase + step == 0)(exchange.signal)
    spread_rate(decay_ref, rate_ref)
    zero = jnp.zeros((G, LANES), F32)

    @pl.when(phase == 0)
    def _():
        pl.when(j == 0)(lambda: spread_maps(maps_ref, 0, states, b_ref.at[s]))

        def one(l, carry):
            h, total = carry
            st = step_ref[0, l]
            u = st * act_ref[0, l]
            h = tuple(
                jnp.exp2(st * rate_ref[n]) * h[n] + u * part(b_ref.at[s], l, n) for n in range(states)
            )
            return h, total + st

        h, total = lax.fori_loop(0, length, one, ((zero,) * states, zero), unroll=math.gcd(length, 8))
        ends, span = segment_prefix(list(h), total, rate_ref, 1)
        for n in range(states):
            prefix_ref[step, n] = shifted(ends[n], 1, 0.0)
        spans_ref[step, 0] = shifted(span, 1, 0.0)
        spans_ref[step, 1] = jnp.broadcast_to(span[G - 1 : G, :], (G, LANES)) - span
        rows = [e[G - 1 : G, :] for e in ends] + [jnp.broadcast_to(span[G - 1 : G, :], (8, LANES))]
        give_ref[step] = jnp.concatenate(rows, axis=0)
        pl.when(step == 0)(exchange.meet)
        exchange.start(step)

    @pl.when(phase == 1)
    def _():
        pl.when(j == 0)(lambda: spread_maps(maps_ref, states, states, c_ref))
        exchange.wait(step)
        rate = jnp.exp(decay_ref[...]) * (-LOG2E)
        entry = init_ref[0]
        for d in range(packs_ref.shape[0]):
            pack = jnp.where(exchange.me == d, give_ref[step], got_ref[d, step])
            packs_ref[d, 0] = pack
            joined = jnp.exp2(rate * pack[states : states + 1, :]) * entry + pack[:states, :]
            entry = jnp.where(d < exchange.me, joined, entry)
        span_ref[0] = spans_ref[step]
        span = spans_ref[step, 0]
        h = []
        for n in range(states):
            first = prefix_ref[step, n] + jnp.exp2(rate_ref[n] * span) * entry[n : n + 1, :]
            start_ref[0, n] = first
            h.append(first)
        skip = jnp.broadcast_to(skip_ref[...], (G, LANES))

        def one(k, h):
            h = list(h)
            halves = []
            for i in range(2):
                l = 2 * k + i
                st = step_ref[0, l]
                act = act_ref[0, l]
                u = st * act
                y = skip * act
                for n in range(states):
                    h[n] = jnp.exp2(st * rate_ref[n]) * h[n] + u * part(b_ref.at[s], l, n)
                    y = y + part(c_ref, l, n) * h[n]
                y_ref[0, l] = y
                gate = gate_ref[0, l]
                halves.append(y * (gate / (1.0 + jnp.exp(-gate))))
            row = pl.multiple_of(k * 2 * G, 2 * G)
            gated_ref[0, pl.ds(row, 2 * G), :] = jnp.concatenate(halves, axis=0).astype(BF16)
            return tuple(h)

        lax.fori_loop(0, length // 2, one, tuple(h), unroll=math.gcd(length // 2, 4))


def scan_forward(act, step, gate, maps, decay, init, skip):
    seqs, length, _, chans = act.shape
    states = decay.shape[0]
    peers = lax.axis_size("seq")
    tiles = chans // LANES
    token = pl.BlockSpec((1, length, G, LANES), lambda p, s, j: (s, 0, 0, j))

    def late(shape, index):
        return pl.BlockSpec(shape, lambda p, s, j: index(p * s, p * j))

    return pl.pallas_call(
        forward_kernel,
        grid=(2, seqs, tiles),
        in_specs=[
            token,
            token,
            late((1, length, G, LANES), lambda s, j: (s, 0, 0, j)),
            pl.BlockSpec((1, length * G, maps.shape[2]), lambda p, s, j: (s, 0, 0)),
            pl.BlockSpec((states, LANES), lambda p, s, j: (0, j)),
            late((1, states, LANES), lambda s, j: (s, 0, j)),
            late((1, LANES), lambda s, j: (0, j)),
        ],
        out_specs=[
            late((1, length, G, LANES), lambda s, j: (s, 0, 0, j)),
            late((1, length * G, LANES), lambda s, j: (s, 0, j)),
            late((1, states, G, LANES), lambda s, j: (s, 0, 0, j)),
            late((1, 2, G, LANES), lambda s, j: (s, 0, 0, j)),
            late((peers, 1, states + 8, LANES), lambda s, j: (0, s, 0, j)),
        ],
        out_shape=[
            jax.ShapeDtypeStruct(act.shape, F32),
            jax.ShapeDtypeStruct((seqs, length * G, chans), BF16),
            pltpu.HBM((seqs, states, G, chans), F32),
            pltpu.HBM((seqs, 2, G, chans), F32),
            pltpu.HBM((peers, seqs, states + 8, chans), F32),
        ],
        scratch_shapes=[
            pltpu.VMEM((seqs, length * G, states * LANES), F32),
            pltpu.VMEM((length * G, states * LANES), F32),
            pltpu.VMEM((states, G, LANES), F32),
            pltpu.VMEM((seqs * tiles, states, G, LANES), F32),
            pltpu.VMEM((seqs * tiles, 2, G, LANES), F32),
        ]
        + exchange_scratch(seqs * tiles, states + 8),
        compiler_params=pltpu.CompilerParams(
            dimension_semantics=("arbitrary",) * 3, collective_id=6, has_side_effects=True,
            vmem_limit_bytes=VMEM_LIMIT,
        ),
        cost_estimate=estimate(20),
        name="scan_forward",
    )(act, step, gate, maps, decay, init, skip)


def adjoint_kernel(
    step_ref, gate_ref, grad_ref, maps_ref, decay_ref, span_ref, suffix_ref, packs_ref, c_ref, rate_ref, give_ref,
    got_ref, *sems,
):
    length, states = step_ref.shape[1], decay_ref.shape[0]
    columns = pl.ds(pl.multiple_of(pl.program_id(1) * LANES, LANES), LANES)
    step_ref, gate_ref, grad_ref = (ref.at[:, :, :, columns] for ref in (step_ref, gate_ref, grad_ref))
    exchange = SeqExchange(give_ref, got_ref, *sems)
    pl.when(pl.program_id(0) + pl.program_id(1) == 0)(exchange.signal)

    @pl.when(pl.program_id(1) == 0)
    def _():
        spread_maps(maps_ref, states, states, c_ref)

    spread_rate(decay_ref, rate_ref)

    def one(k, carry):
        l = length - 1 - k
        st = step_ref[0, l]
        gate = gate_ref[0, l]
        gy = grad_ref[0, l] * (gate / (1.0 + jnp.exp(-gate)))
        return tuple(
            jnp.exp2(st * rate_ref[n]) * (carry[n] + gy * part(c_ref, l, n)) for n in range(states)
        )

    zero = jnp.zeros((G, LANES), F32)
    carry = lax.fori_loop(0, length, one, (zero,) * states, unroll=math.gcd(length, 8))
    own = span_ref[0, 1, 0:1, :] + span_ref[0, 0, 1:2, :] - span_ref[0, 0] - span_ref[0, 1]
    ends, _ = segment_prefix(list(carry), own, rate_ref, -1)
    for n in range(states):
        suffix_ref[0, n] = shifted(ends[n], -1, 0.0)
    rows = jnp.concatenate([e[0:1, :] for e in ends], axis=0)
    exchange_step(exchange, packs_ref, give_ref, got_ref, rows)


def scan_adjoint(step, gate, grad, maps, decay, span):
    seqs, length, _, chans = step.shape
    states = decay.shape[0]
    peers = lax.axis_size("seq")
    broad = pl.BlockSpec((1, length, G, chans), lambda s, j: (s, 0, 0, 0))
    return pl.pallas_call(
        adjoint_kernel,
        grid=(seqs, chans // LANES),
        in_specs=[
            broad,
            broad,
            broad,
            pl.BlockSpec((1, length * G, maps.shape[2]), lambda s, j: (s, 0, 0)),
            pl.BlockSpec((states, LANES), lambda s, j: (0, j)),
            pl.BlockSpec((1, 2, G, LANES), lambda s, j: (s, 0, 0, j)),
        ],
        out_specs=[
            pl.BlockSpec((1, states, G, LANES), lambda s, j: (s, 0, 0, j)),
            pl.BlockSpec((peers, seqs, states, chans), lambda s, j: (0, 0, 0, 0)),
        ],
        out_shape=[
            pltpu.HBM((seqs, states, G, chans), F32),
            pltpu.HBM((peers, seqs, states, chans), F32),
        ],
        scratch_shapes=[
            pltpu.VMEM((length * G, states * LANES), F32),
            pltpu.VMEM((states, G, LANES), F32),
        ]
        + exchange_scratch(seqs * chans // LANES, states),
        compiler_params=exchange_params(7),
        cost_estimate=estimate(15),
        name="scan_adjoint",
    )(step, gate, grad, maps, decay, span)


def backward_kernel(
    act_ref, step_ref, delta_ref, gate_ref, y_ref, grad_ref, maps_ref, decay_ref, start_ref, suffix_ref, span_ref,
    packs_ref, forward_packs_ref, skip_ref, weight_ref,
    gact_ref, gpre_ref, ggate_ref, proj_ref, gdecay_ref, gskip_ref, ginit_ref,
    b_ref, c_ref, rate_ref, h_ref, product_ref, select_ref, rank_ref,
):
    length, states = act_ref.shape[1], decay_ref.shape[0]
    columns = pl.ds(pl.multiple_of(pl.program_id(1) * LANES, LANES), LANES)
    act_ref, step_ref, delta_ref, gate_ref, y_ref, grad_ref = (
        ref.at[:, :, :, columns] for ref in (act_ref, step_ref, delta_ref, gate_ref, y_ref, grad_ref)
    )
    wide = states * LANES

    @pl.when(pl.program_id(1) == 0)
    def _():
        spread_maps(maps_ref, 0, states, b_ref)
        spread_maps(maps_ref, states, states, c_ref)
        row = lax.broadcasted_iota(jnp.int32, select_ref.shape, 0) // LANES
        col = lax.broadcasted_iota(jnp.int32, select_ref.shape, 1)
        product_ref[...] = jnp.zeros_like(product_ref)
        rank_ref[...] = jnp.zeros_like(rank_ref)
        select_ref[...] = jnp.where(row == col, 1.0, 0.0).astype(BF16)

    spread_rate(decay_ref, rate_ref)
    rate = jnp.exp(decay_ref[...]) * (-LOG2E)
    me = lax.axis_index("seq")
    count = packs_ref.shape[0]
    entry = jnp.zeros((states, LANES), F32)
    for d in reversed(range(count)):
        joined = jnp.exp2(rate * forward_packs_ref[d, 0, states : states + 1, :]) * entry + packs_ref[d, 0]
        entry = jnp.where(d > me, joined, entry)
    after = span_ref[0, 1]
    skip = jnp.broadcast_to(skip_ref[...], (G, LANES))

    def forward(l, h):
        st = step_ref[0, l]
        u = st * act_ref[0, l]
        for n in range(states):
            h_ref[l, n] = h[n]
        return tuple(
            jnp.exp2(st * rate_ref[n]) * h[n] + u * part(b_ref, l, n) for n in range(states)
        )

    h = lax.fori_loop(
        0, length, forward, tuple(start_ref[0, n] for n in range(states)), unroll=math.gcd(length, 4)
    )
    for n in range(states):
        h_ref[length, n] = h[n]

    def back(k, state):
        carry, gdecay, gskip = list(state[0]), list(state[1]), state[2]
        lines = [length - 1 - 2 * k, length - 2 - 2 * k]
        st, act, u, gy, q, r = [], [], [], [], [], []
        ggate = []
        for l in lines:
            st.append(step_ref[0, l])
            act.append(act_ref[0, l])
            u.append(st[-1] * act[-1])
            gate = gate_ref[0, l]
            grad = grad_ref[0, l]
            sig = 1.0 / (1.0 + jnp.exp(-gate))
            silu = gate * sig
            gy.append(grad * silu)
            ggate.append(grad * y_ref[0, l] * (sig + silu * (1.0 - sig)))
            gskip = gskip + gy[-1] * act[-1]
            q.append(jnp.zeros((G, LANES), F32))
            r.append(jnp.zeros((G, LANES), F32))
        row = pl.multiple_of((length - 2 - 2 * k) * G, 2 * G)
        for n in range(states):
            late, early = [], []
            for i, l in enumerate(lines):
                lam = part(c_ref, l, n) * gy[i] + carry[n]
                early.append(lam * u[i])
                late.append(gy[i] * h_ref[l + 1, n])
                q[i] = q[i] + lam * part(b_ref, l, n)
                carry[n] = jnp.exp2(st[i] * rate_ref[n]) * lam
                w = carry[n] * h_ref[l, n]
                r[i] = r[i] + rate_ref[n] * w
                gdecay[n] = gdecay[n] + st[i] * w
            product_ref[pl.ds(row, 2 * G), n * LANES : (n + 1) * LANES] += jnp.concatenate(early[::-1], axis=0)
            product_ref[pl.ds(row, 2 * G), wide + n * LANES : wide + (n + 1) * LANES] += jnp.concatenate(late[::-1], axis=0)
        gpre = []
        for i, l in enumerate(lines):
            gact_ref[0, l] = skip * gy[i] + st[i] * q[i]
            gstep = LN2 * r[i] + act[i] * q[i]
            gpre.append(gstep / (1.0 + jnp.exp(-delta_ref[0, l])))
        gpre_ref[0, pl.ds(row, 2 * G), :] = jnp.concatenate(gpre[::-1], axis=0).astype(BF16)
        ggate_ref[0, pl.ds(row, 2 * G), :] = jnp.concatenate(ggate[::-1], axis=0).astype(BF16)
        return tuple(carry), tuple(gdecay), gskip

    zero = jnp.zeros((G, LANES), F32)
    first = tuple(
        suffix_ref[0, n] + jnp.exp2(rate_ref[n] * after) * entry[n : n + 1, :] for n in range(states)
    )
    carry, gdecay, gskip = lax.fori_loop(
        0, length // 2, back, (first, (zero,) * states, zero), unroll=math.gcd(length // 2, 2)
    )
    for n in range(states):
        ginit_ref[0, n : n + 1, :] = carry[n][0:1, :]
        total = jnp.sum(gdecay[n] * rate_ref[n], axis=0, keepdims=True)
        gdecay_ref[0, n : n + 1, :] = total * LN2
    gskip_ref[0] = jnp.broadcast_to(jnp.sum(gskip, axis=0, keepdims=True), (8, LANES))

    rank_ref[...] += dot(gpre_ref[0], weight_ref[...], ((1,), (1,)))

    @pl.when(pl.program_id(1) == pl.num_programs(1) - 1)
    def _():
        sums = jnp.dot(product_ref[...].astype(BF16), select_ref[...], preferred_element_type=F32)
        rank = rank_ref.shape[1]
        proj_ref[0, :, :rank] = rank_ref[...].astype(BF16)
        proj_ref[0, :, rank:] = sums[:, : 2 * states].astype(BF16)


def scan_backward(
    act, step, delta, gate, y, grad, maps, decay, start, suffix, span, packs, forward_packs, skip, weight
):
    seqs, length, _, chans = act.shape
    start, suffix, span, packs, forward_packs = (
        pltpu.with_memory_space_constraint(value, pltpu.HBM) for value in (start, suffix, span, packs, forward_packs)
    )
    states = decay.shape[0]
    token = pl.BlockSpec((1, length, G, LANES), lambda s, j: (s, 0, 0, j))
    broad = pl.BlockSpec((1, length, G, chans), lambda s, j: (s, 0, 0, 0))
    rows = pl.BlockSpec((1, length * G, LANES), lambda s, j: (s, 0, j))
    per_state = pl.BlockSpec((1, states, G, LANES), lambda s, j: (s, 0, 0, j))
    total = pl.BlockSpec((1, states, LANES), lambda s, j: (s, 0, j))
    return pl.pallas_call(
        backward_kernel,
        grid=(seqs, chans // LANES),
        in_specs=[
            broad,
            broad,
            broad,
            broad,
            broad,
            broad,
            pl.BlockSpec((1, length * G, maps.shape[2]), lambda s, j: (s, 0, 0)),
            pl.BlockSpec((states, LANES), lambda s, j: (0, j)),
            per_state,
            per_state,
            pl.BlockSpec((1, 2, G, LANES), lambda s, j: (s, 0, 0, j)),
            pl.BlockSpec((packs.shape[0], 1, states, LANES), lambda s, j: (0, s, 0, j)),
            pl.BlockSpec((packs.shape[0], 1, states + 8, LANES), lambda s, j: (0, s, 0, j)),
            pl.BlockSpec((1, LANES), lambda s, j: (0, j)),
            pl.BlockSpec((weight.shape[0], LANES), lambda s, j: (0, j)),
        ],
        out_specs=[
            token,
            rows,
            rows,
            pl.BlockSpec((1, length * G, weight.shape[0] + 2 * states), lambda s, j: (s, 0, 0)),
            total,
            pl.BlockSpec((1, 8, LANES), lambda s, j: (s, 0, j)),
            total,
        ],
        out_shape=[
            jax.ShapeDtypeStruct(act.shape, F32),
            jax.ShapeDtypeStruct((seqs, length * G, chans), BF16),
            jax.ShapeDtypeStruct((seqs, length * G, chans), BF16),
            jax.ShapeDtypeStruct((seqs, length * G, weight.shape[0] + 2 * states), BF16),
            jax.ShapeDtypeStruct((seqs, states, chans), F32),
            jax.ShapeDtypeStruct((seqs, 8, chans), F32),
            jax.ShapeDtypeStruct((seqs, states, chans), F32),
        ],
        scratch_shapes=[
            pltpu.VMEM((length * G, states * LANES), F32),
            pltpu.VMEM((length * G, states * LANES), F32),
            pltpu.VMEM((states, G, LANES), F32),
            pltpu.VMEM((length + 1, states, G, LANES), F32),
            pltpu.VMEM((length * G, 2 * states * LANES), F32),
            pltpu.VMEM((2 * states * LANES, LANES), BF16),
            pltpu.VMEM((length * G, weight.shape[0]), F32),
        ],
        compiler_params=params("arbitrary", "arbitrary"),
        cost_estimate=estimate(39),
        name="scan_backward",
    )(act, step, delta, gate, y, grad, maps, decay, start, suffix, span, packs, forward_packs, skip, weight)


def adjoint_and_backward_kernel(
    act_ref, step_ref, delta_ref, gate_ref, y_ref, grad_ref, maps_ref, decay_ref, start_ref, span_ref,
    forward_packs_ref, skip_ref, weight_ref,
    gact_ref, gpre_ref, ggate_ref, proj_ref, gdecay_ref, gskip_ref, ginit_ref,
    b_ref, c_ref, rate_ref, h_ref, product_ref, select_ref, rank_ref, suffix_ref, give_ref, got_ref, *sems,
):
    length, states = act_ref.shape[1], decay_ref.shape[0]
    phase, s, j = pl.program_id(0), pl.program_id(1), pl.program_id(2)
    block = s * pl.num_programs(2) + j
    columns = pl.ds(pl.multiple_of(j * LANES, LANES), LANES)
    act_ref, step_ref, delta_ref, gate_ref, y_ref, grad_ref = (
        ref.at[:, :, :, columns] for ref in (act_ref, step_ref, delta_ref, gate_ref, y_ref, grad_ref)
    )
    c_ref = c_ref.at[s]
    exchange = SeqExchange(give_ref, got_ref, *sems)
    pl.when(phase + block == 0)(exchange.signal)
    spread_rate(decay_ref, rate_ref)
    zero = jnp.zeros((G, LANES), F32)

    @pl.when(phase == 0)
    def _():
        pl.when(j == 0)(lambda: spread_maps(maps_ref, states, states, c_ref))

        def one(k, carry):
            l = length - 1 - k
            st = step_ref[0, l]
            gate = gate_ref[0, l]
            gy = grad_ref[0, l] * (gate / (1.0 + jnp.exp(-gate)))
            return tuple(
                jnp.exp2(st * rate_ref[n]) * (carry[n] + gy * part(c_ref, l, n)) for n in range(states)
            )

        carry = lax.fori_loop(0, length, one, (zero,) * states, unroll=math.gcd(length, 8))
        own = span_ref[0, 1, 0:1, :] + span_ref[0, 0, 1:2, :] - span_ref[0, 0] - span_ref[0, 1]
        ends, _ = segment_prefix(list(carry), own, rate_ref, -1)
        for n in range(states):
            suffix_ref[block, n] = shifted(ends[n], -1, 0.0)
        give_ref[block] = jnp.concatenate([e[0:1, :] for e in ends], axis=0)
        pl.when(block == 0)(exchange.meet)
        exchange.start(block)

    pl.when(phase == 1)(lambda: gradients(
        exchange, block, j, columns,
        act_ref, step_ref, delta_ref, gate_ref, y_ref, grad_ref, maps_ref, decay_ref, start_ref, span_ref,
        forward_packs_ref, skip_ref, weight_ref,
        gact_ref, gpre_ref, ggate_ref, proj_ref, gdecay_ref, gskip_ref, ginit_ref,
        b_ref, c_ref, rate_ref, h_ref, product_ref, select_ref, rank_ref, suffix_ref, give_ref, got_ref,
    ))


def gradients(
    exchange, block, tile, columns,
    act_ref, step_ref, delta_ref, gate_ref, y_ref, grad_ref, maps_ref, decay_ref, start_ref, span_ref,
    forward_packs_ref, skip_ref, weight_ref,
    gact_ref, gpre_ref, ggate_ref, proj_ref, gdecay_ref, gskip_ref, ginit_ref,
    b_ref, c_ref, rate_ref, h_ref, product_ref, select_ref, rank_ref, suffix_ref, give_ref, got_ref,
):
    length, states = act_ref.shape[1], decay_ref.shape[0]
    wide = states * LANES

    @pl.when(tile == 0)
    def _():
        spread_maps(maps_ref, 0, states, b_ref)
        row = lax.broadcasted_iota(jnp.int32, select_ref.shape, 0) // LANES
        col = lax.broadcasted_iota(jnp.int32, select_ref.shape, 1)
        product_ref[...] = jnp.zeros_like(product_ref)
        rank_ref[...] = jnp.zeros_like(rank_ref)
        select_ref[...] = jnp.where(row == col, 1.0, 0.0).astype(BF16)

    exchange.wait(block)
    rate = jnp.exp(decay_ref[...]) * (-LOG2E)
    entry = jnp.zeros((states, LANES), F32)
    for d in reversed(range(got_ref.shape[0])):
        pack = jnp.where(exchange.me == d, give_ref[block], got_ref[d, block])
        joined = jnp.exp2(rate * forward_packs_ref[d, 0, states : states + 1, :]) * entry + pack
        entry = jnp.where(d > exchange.me, joined, entry)
    after = span_ref[0, 1]
    skip = jnp.broadcast_to(skip_ref[...], (G, LANES))

    def forward(l, h):
        st = step_ref[0, l]
        u = st * act_ref[0, l]
        for n in range(states):
            h_ref[l, n] = h[n]
        return tuple(
            jnp.exp2(st * rate_ref[n]) * h[n] + u * part(b_ref, l, n) for n in range(states)
        )

    h = lax.fori_loop(
        0, length, forward, tuple(start_ref[0, n] for n in range(states)), unroll=math.gcd(length, 4)
    )
    for n in range(states):
        h_ref[length, n] = h[n]

    def back(k, state):
        carry, gdecay, gskip = list(state[0]), list(state[1]), state[2]
        lines = [length - 1 - 2 * k, length - 2 - 2 * k]
        st, act, u, gy, q, r = [], [], [], [], [], []
        ggate = []
        for l in lines:
            st.append(step_ref[0, l])
            act.append(act_ref[0, l])
            u.append(st[-1] * act[-1])
            gate = gate_ref[0, l]
            grad = grad_ref[0, l]
            sig = 1.0 / (1.0 + jnp.exp(-gate))
            silu = gate * sig
            gy.append(grad * silu)
            ggate.append(grad * y_ref[0, l] * (sig + silu * (1.0 - sig)))
            gskip = gskip + gy[-1] * act[-1]
            q.append(jnp.zeros((G, LANES), F32))
            r.append(jnp.zeros((G, LANES), F32))
        row = pl.multiple_of((length - 2 - 2 * k) * G, 2 * G)
        for n in range(states):
            late, early = [], []
            for i, l in enumerate(lines):
                lam = part(c_ref, l, n) * gy[i] + carry[n]
                early.append(lam * u[i])
                late.append(gy[i] * h_ref[l + 1, n])
                q[i] = q[i] + lam * part(b_ref, l, n)
                carry[n] = jnp.exp2(st[i] * rate_ref[n]) * lam
                w = carry[n] * h_ref[l, n]
                r[i] = r[i] + rate_ref[n] * w
                gdecay[n] = gdecay[n] + st[i] * w
            product_ref[pl.ds(row, 2 * G), n * LANES : (n + 1) * LANES] += jnp.concatenate(early[::-1], axis=0)
            product_ref[pl.ds(row, 2 * G), wide + n * LANES : wide + (n + 1) * LANES] += jnp.concatenate(late[::-1], axis=0)
        gpre = []
        for i, l in enumerate(lines):
            gact_ref[0, l] = skip * gy[i] + st[i] * q[i]
            gstep = LN2 * r[i] + act[i] * q[i]
            gpre.append(gstep / (1.0 + jnp.exp(-delta_ref[0, l])))
        gpre_ref[0, pl.ds(row, 2 * G), :] = jnp.concatenate(gpre[::-1], axis=0).astype(BF16)
        ggate_ref[0, pl.ds(row, 2 * G), :] = jnp.concatenate(ggate[::-1], axis=0).astype(BF16)
        return tuple(carry), tuple(gdecay), gskip

    zero = jnp.zeros((G, LANES), F32)
    first = tuple(
        suffix_ref[block, n] + jnp.exp2(rate_ref[n] * after) * entry[n : n + 1, :] for n in range(states)
    )
    carry, gdecay, gskip = lax.fori_loop(
        0, length // 2, back, (first, (zero,) * states, zero), unroll=math.gcd(length // 2, 2)
    )
    for n in range(states):
        ginit_ref[0, n : n + 1, :] = carry[n][0:1, :]
        total = jnp.sum(gdecay[n] * rate_ref[n], axis=0, keepdims=True)
        gdecay_ref[0, n : n + 1, :] = total * LN2
    gskip_ref[0] = jnp.broadcast_to(jnp.sum(gskip, axis=0, keepdims=True), (8, LANES))

    rank_ref[...] += dot(gpre_ref[0], weight_ref[...], ((1,), (1,)))

    @pl.when(tile == pl.num_programs(2) - 1)
    def _():
        sums = jnp.dot(product_ref[...].astype(BF16), select_ref[...], preferred_element_type=F32)
        rank = rank_ref.shape[1]
        proj_ref[0, :, :rank] = rank_ref[...].astype(BF16)
        proj_ref[0, :, rank:] = sums[:, : 2 * states].astype(BF16)


def scan_adjoint_and_backward(act, step, delta, gate, y, grad, maps, decay, start, span, forward_packs, skip, weight):
    seqs, length, _, chans = act.shape
    start, span, forward_packs = (
        pltpu.with_memory_space_constraint(value, pltpu.HBM) for value in (start, span, forward_packs)
    )
    states = decay.shape[0]
    peers = lax.axis_size("seq")
    tiles = chans // LANES

    def late(shape, index):
        return pl.BlockSpec(shape, lambda p, s, j: index(p * s, p * j))

    broad = pl.BlockSpec((1, length, G, chans), lambda p, s, j: (s, 0, 0, 0))
    late_broad = late((1, length, G, chans), lambda s, j: (s, 0, 0, 0))
    rows = late((1, length * G, LANES), lambda s, j: (s, 0, j))
    total = late((1, states, LANES), lambda s, j: (s, 0, j))
    return pl.pallas_call(
        adjoint_and_backward_kernel,
        grid=(2, seqs, tiles),
        in_specs=[
            late_broad,
            broad,
            late_broad,
            broad,
            late_broad,
            broad,
            pl.BlockSpec((1, length * G, maps.shape[2]), lambda p, s, j: (s, 0, 0)),
            pl.BlockSpec((states, LANES), lambda p, s, j: (0, j)),
            late((1, states, G, LANES), lambda s, j: (s, 0, 0, j)),
            pl.BlockSpec((1, 2, G, LANES), lambda p, s, j: (s, 0, 0, j)),
            late((peers, 1, states + 8, LANES), lambda s, j: (0, s, 0, j)),
            late((1, LANES), lambda s, j: (0, j)),
            late((weight.shape[0], LANES), lambda s, j: (0, j)),
        ],
        out_specs=[
            late((1, length, G, LANES), lambda s, j: (s, 0, 0, j)),
            rows,
            rows,
            late((1, length * G, weight.shape[0] + 2 * states), lambda s, j: (s, 0, 0)),
            total,
            late((1, 8, LANES), lambda s, j: (s, 0, j)),
            total,
        ],
        out_shape=[
            jax.ShapeDtypeStruct(act.shape, F32),
            jax.ShapeDtypeStruct((seqs, length * G, chans), BF16),
            jax.ShapeDtypeStruct((seqs, length * G, chans), BF16),
            jax.ShapeDtypeStruct((seqs, length * G, weight.shape[0] + 2 * states), BF16),
            jax.ShapeDtypeStruct((seqs, states, chans), F32),
            jax.ShapeDtypeStruct((seqs, 8, chans), F32),
            jax.ShapeDtypeStruct((seqs, states, chans), F32),
        ],
        scratch_shapes=[
            pltpu.VMEM((length * G, states * LANES), F32),
            pltpu.VMEM((seqs, length * G, states * LANES), F32),
            pltpu.VMEM((states, G, LANES), F32),
            pltpu.VMEM((length + 1, states, G, LANES), F32),
            pltpu.VMEM((length * G, 2 * states * LANES), F32),
            pltpu.VMEM((2 * states * LANES, LANES), BF16),
            pltpu.VMEM((length * G, weight.shape[0]), F32),
            pltpu.VMEM((seqs * tiles, states, G, LANES), F32),
        ]
        + exchange_scratch(seqs * tiles, states),
        compiler_params=pltpu.CompilerParams(
            dimension_semantics=("arbitrary",) * 3, collective_id=9, has_side_effects=True,
            vmem_limit_bytes=VMEM_LIMIT,
        ),
        cost_estimate=estimate(39),
        name="scan_adjoint_and_backward",
    )(act, step, delta, gate, y, grad, maps, decay, start, span, forward_packs, skip, weight)


def remote(src, dst, send, recv, to):
    return pltpu.make_async_remote_copy(
        src_ref=src, dst_ref=dst, send_sem=send, recv_sem=recv, device_id={"chan": to}, device_id_type=MESH
    )


class Line:
    def __init__(self, count):
        self.me = lax.axis_index("chan")
        self.half = count // 2
        self.at = self.me // 2
        self.low = self.me % 2
        self.pair = self.at * 2 + 1 - self.low
        self.right = jnp.minimum(self.at + 1, self.half - 1) * 2 + self.low
        self.left = jnp.maximum(self.at - 1, 0) * 2 + self.low
        self.has_right = self.at < self.half - 1
        self.has_left = self.at > 0

    def greet(self):
        barrier = pltpu.get_barrier_semaphore()

        def signal(to):
            pl.semaphore_signal(barrier, inc=1, device_id={"chan": to}, device_id_type=MESH)

        signal(self.pair)
        pl.when(self.has_right)(lambda: signal(self.right))
        pl.when(self.has_left)(lambda: signal(self.left))
        pl.semaphore_wait(barrier, 1 + jnp.minimum(self.at, 1) + jnp.minimum(self.half - 1 - self.at, 1))


def gather_steps(line, out_ref, width, chunks, sems):
    pair_send, pair_recv, right_send, right_recv, left_send, left_recv = sems
    half = line.half
    rows = out_ref.shape[0] // chunks

    def place(owner, c):
        return out_ref.at[pl.ds(c * rows, rows), pl.ds(pl.multiple_of(owner * width, width), width)]

    def to_pair(owner, slot, c):
        return remote(place(owner, c), place(owner, c), pair_send.at[slot, c], pair_recv.at[slot, c], line.pair)

    def to_right(owner, j, c):
        return remote(place(owner, c), place(owner, c), right_send.at[j, c], right_recv.at[j, c], line.right)

    def to_left(owner, j, c):
        return remote(place(owner, c), place(owner, c), left_send.at[j, c], left_recv.at[j, c], line.left)

    def begin(c):
        pl.when(line.has_right)(lambda: to_right(line.me, 0, c).start())
        pl.when(line.has_left)(lambda: to_left(line.me, 0, c).start())
        to_pair(line.me, 0, c).start()

    def middle(fill=lambda: None):
        for j in range(1, half):
            for c in range(chunks):
                fill()
                @pl.when(line.at >= j)
                def _():
                    owner = line.me - 2 * j
                    to_right(owner, j - 1, c).wait_recv()
                    pl.when(line.has_right)(lambda: to_right(owner, j, c).start())
                    to_pair(owner, j, c).start()

                @pl.when(line.at + j < half)
                def _():
                    owner = line.me + 2 * j
                    to_left(owner, j - 1, c).wait_recv()
                    pl.when(line.has_left)(lambda: to_left(owner, j, c).start())
                    to_pair(owner, half + j, c).start()

    def end():
        for c in range(chunks):
            to_pair(line.me, 0, c).wait()
            pl.when(line.has_right)(lambda: to_right(line.me, 0, c).wait_send())
            pl.when(line.has_left)(lambda: to_left(line.me, 0, c).wait_send())
            for j in range(1, half):
                @pl.when(line.at >= j)
                def _():
                    owner = line.me - 2 * j
                    to_pair(owner, j, c).wait()
                    pl.when(line.has_right)(lambda: to_right(owner, j, c).wait_send())

                @pl.when(line.at + j < half)
                def _():
                    owner = line.me + 2 * j
                    to_pair(owner, half + j, c).wait()
                    pl.when(line.has_left)(lambda: to_left(owner, j, c).wait_send())

    return begin, middle, end


def gather_sems(count, chunks):
    half = count // 2
    return [pltpu.SemaphoreType.DMA((2 * half, chunks))] * 2 + [pltpu.SemaphoreType.DMA((half, chunks))] * 4


def estimate(us):
    return pl.CostEstimate(flops=int(us * 1e8), bytes_accessed=1 << 20, transcendentals=0)


def remote_params(ident):
    return pltpu.CompilerParams(collective_id=ident, has_side_effects=True, vmem_limit_bytes=VMEM_LIMIT)


def whole(count):
    return [pl.BlockSpec(memory_space=pltpu.VMEM)] * count


def chunks_of(rows):
    return next(c for c in (3, 2, 1) if rows % (16 * c) == 0)


def gather_kernel(count, chunks, layers, part_ref, gain_ref, weights_ref, out_ref, *rest):
    flats, rest = rest[:layers], rest[layers:]
    fetched, flat_buf, fetch_sem, store_sem, *sems = rest
    line = Line(count)
    rows, width = part_ref.shape
    mine = pl.ds(pl.multiple_of(line.me * width, width), width)
    height = fetched.shape[1]
    steps = weights_ref.shape[1] // height
    total = layers * steps

    def fetch(i):
        here = weights_ref.at[i // steps, pl.ds(i % steps * height, height)]
        return pltpu.make_async_copy(here, fetched.at[i % 2], fetch_sem.at[i % 2])

    def store(i):
        here = flats[i // steps].at[pl.ds(i % steps * height, height)]
        return pltpu.make_async_copy(flat_buf.at[i % 2], here, store_sem.at[i % 2])

    fetch(0).start()
    fetch(1).start()
    out_ref[:rows, mine] = part_ref[...]
    gain = gain_ref[...]
    terms = []
    for _ in range(3):
        term = gain.astype(BF16).astype(F32)
        terms.append(term)
        gain = gain - term
    terms.append(jnp.zeros((16 - 3 * layers, width), F32))
    out_ref[rows:, mine] = jnp.concatenate(terms, axis=0).astype(BF16)
    line.greet()
    begin, middle, end = gather_steps(line, out_ref, width, chunks, sems)
    for c in range(chunks):
        begin(c)
    done = []

    def flatten():
        i = len(done)
        if i == total:
            return
        done.append(i)
        fetch(i).wait()
        if i >= steps + 2:
            store(i - 2).wait()

        def piece(r, carry):
            here = pl.ds(pl.multiple_of(r * 32, 32), 32)
            value = fetched[i % 2, here].astype(F32)
            value = value.reshape(32, 2 * value.shape[2]).astype(BF16)
            if i < steps:
                flats[0][pl.ds(pl.multiple_of(i * height + r * 32, 32), 32), :] = value
            else:
                flat_buf[i % 2, here, :] = value
            return carry

        lax.fori_loop(0, height // 32, piece, 0)
        if i >= steps:
            store(i).start()
        if i + 2 < total:
            fetch(i + 2).start()

    def fill():
        flatten()
        flatten()

    middle(fill)
    while len(done) < total:
        flatten()
    end()
    for i in range(max(total - 2, steps), total):
        store(i).wait()


def gather_first(part, gain, weights):
    count = lax.axis_size("chan")
    rows, width = part.shape
    layers, model = weights.shape[:2]
    chunks = chunks_of(rows + 16)
    height = 256
    flat = (model, 2 * weights.shape[3])
    full, *flats = pl.pallas_call(
        functools.partial(gather_kernel, count, chunks, layers),
        in_specs=whole(2) + [pl.BlockSpec(memory_space=pl.ANY)],
        out_specs=whole(2) + [pl.BlockSpec(memory_space=pl.ANY)] * (layers - 1),
        out_shape=[jax.ShapeDtypeStruct((rows + 16, count * width), BF16)] + [jax.ShapeDtypeStruct(flat, BF16)] * layers,
        scratch_shapes=[
            pltpu.VMEM((2, height) + weights.shape[2:], BF16),
            pltpu.VMEM((2, height, flat[1]), BF16),
            pltpu.SemaphoreType.DMA((2,)),
            pltpu.SemaphoreType.DMA((2,)),
        ]
        + gather_sems(count, chunks),
        compiler_params=remote_params(0),
        cost_estimate=estimate(25),
        name="gather_first",
    )(part, gain, weights)
    terms = full[rows : rows + 3 * layers].astype(F32)
    return full, terms[:layers] + terms[layers : 2 * layers] + terms[2 * layers :], flats


def scatter_steps(line, part_ref, pair_buf, right_buf, left_buf, stage, width, chunks, sems):
    pair_send, pair_recv, right_send, right_recv, left_send, left_recv = sems
    half = line.half
    rows = part_ref.shape[0] // chunks

    def block(owner, c):
        return part_ref.at[pl.ds(c * rows, rows), pl.ds(pl.multiple_of(owner * width, width), width)]

    def piece(ref, slot, c):
        return ref.at[slot, pl.ds(c * rows, rows)]

    def to_pair(at, c):
        return remote(block(at * 2 + 1 - line.low, c), pair_buf.at[at, pl.ds(c * rows, rows)], pair_send.at[at, c], pair_recv.at[at, c], line.pair)

    def to_right(j, c):
        return remote(piece(stage, j, c), piece(right_buf, j - 1, c), right_send.at[j - 1, c], right_recv.at[j - 1, c], line.right)

    def to_left(j, c):
        return remote(piece(stage, half + j, c), piece(left_buf, j - 1, c), left_send.at[j - 1, c], left_recv.at[j - 1, c], line.left)

    def begin(produce):
        for c in range(chunks):

            def send(at):
                if c == 0:
                    produce(at * 2 + 1 - line.low)
                to_pair(at, c).start()

            for j in range(half - 1, 0, -1):
                pl.when(line.at + j < half)(lambda: send(line.at + j))
                pl.when(line.at >= j)(lambda: send(line.at - j))
            send(line.at)
        for at in range(half):
            produce(at * 2 + line.low)

    def own_and_pair(at, c):
        to_pair(at, c).wait_recv()
        return block(at * 2 + line.low, c)[...].astype(F32) + pair_buf[at, pl.ds(c * rows, rows)].astype(F32)

    def middle(c):
        for j in range(half - 1, 0, -1):
            @pl.when(line.at + j < half)
            def _():
                stage[j, pl.ds(c * rows, rows)] = own_and_pair(line.at + j, c).astype(BF16)

                @pl.when(line.has_left)
                def _():
                    arrived = remote(piece(stage, j, c), piece(right_buf, j, c), right_send.at[j, c], right_recv.at[j, c], line.right)
                    arrived.wait_recv()
                    total = stage[j, pl.ds(c * rows, rows)].astype(F32) + right_buf[j, pl.ds(c * rows, rows)].astype(F32)
                    stage[j, pl.ds(c * rows, rows)] = total.astype(BF16)

                to_right(j, c).start()

            @pl.when(line.at >= j)
            def _():
                stage[half + j, pl.ds(c * rows, rows)] = own_and_pair(line.at - j, c).astype(BF16)

                @pl.when(line.has_right)
                def _():
                    arrived = remote(piece(stage, half + j, c), piece(left_buf, j, c), left_send.at[j, c], left_recv.at[j, c], line.left)
                    arrived.wait_recv()
                    total = stage[half + j, pl.ds(c * rows, rows)].astype(F32) + left_buf[j, pl.ds(c * rows, rows)].astype(F32)
                    stage[half + j, pl.ds(c * rows, rows)] = total.astype(BF16)

                to_left(j, c).start()

    def finish(c, out_ref):
        here = pl.ds(c * rows, rows)
        out_ref[here, :] = own_and_pair(line.at, c)

        @pl.when(line.has_left)
        def _():
            remote(piece(stage, 0, c), piece(right_buf, 0, c), right_send.at[0, c], right_recv.at[0, c], line.right).wait_recv()
            out_ref[here, :] += right_buf[0, here].astype(F32)

        @pl.when(line.has_right)
        def _():
            remote(piece(stage, 0, c), piece(left_buf, 0, c), left_send.at[0, c], left_recv.at[0, c], line.left).wait_recv()
            out_ref[here, :] += left_buf[0, here].astype(F32)

    def end():
        for c in range(chunks):
            for at in range(half):
                to_pair(at, c).wait_send()
            for j in range(1, half):
                pl.when(line.at + j < half)(lambda: to_right(j, c).wait_send())
                pl.when(line.at >= j)(lambda: to_left(j, c).wait_send())

    return begin, middle, finish, end


def scatter_scratch(count, chunks, rows, width):
    half = count // 2
    return (
        [pltpu.VMEM((half, rows, width), BF16)] * 3
        + [pltpu.VMEM((2 * half, rows, width), BF16)]
        + [pltpu.SemaphoreType.DMA((half, chunks))] * 6
    )


def boundary_kernel(
    count, chunks, layer, gated_ref, weights_ref, hidden_ref, new_ref, full_ref, pair_buf, right_buf, left_buf, stage,
    part_ref, weight_ref, weight_sem, *sems,
):
    line = Line(count)
    rows, width = hidden_ref.shape
    mine = pl.ds(pl.multiple_of(line.me * width, width), width)
    fetch = pltpu.make_async_copy(weights_ref.at[layer], weight_ref, weight_sem)
    fetch.start()
    line.greet()
    fetch.wait()

    def produce(owner):
        columns = pl.ds(pl.multiple_of(owner * width, width), width)
        block = jnp.dot(gated_ref[...], weight_ref[:, columns], preferred_element_type=F32)
        part_ref[:, columns] = block.astype(BF16)

    begin, middle, finish, end = scatter_steps(
        line, part_ref, pair_buf, right_buf, left_buf, stage, width, chunks, sems[:6]
    )
    gather_begin, gather_middle, gather_end = gather_steps(line, full_ref, width, chunks, sems[6:])
    begin(produce)
    for c in range(chunks):
        here = pl.ds(c * (rows // chunks), rows // chunks)
        middle(c)
        finish(c, new_ref)
        new_ref[here, :] += hidden_ref[here, :]
        full_ref[here, mine] = new_ref[here, :].astype(BF16)
        gather_begin(c)
    gather_middle()
    gather_end()
    end()


def forward_boundary(gated, weights, layer, hidden):
    count = lax.axis_size("chan")
    rows, width = hidden.shape
    chunks = 2
    return pl.pallas_call(
        functools.partial(boundary_kernel, count, chunks, layer),
        in_specs=[whole(1)[0], pl.BlockSpec(memory_space=pl.ANY), whole(1)[0]],
        out_specs=whole(2),
        out_shape=[jax.ShapeDtypeStruct((rows, width), F32), jax.ShapeDtypeStruct((rows, count * width), BF16)],
        scratch_shapes=scatter_scratch(count, chunks, rows, width)[:4]
        + [
            pltpu.VMEM((rows, count * width), BF16),
            pltpu.VMEM(weights.shape[1:], BF16),
            pltpu.SemaphoreType.DMA,
        ]
        + scatter_scratch(count, chunks, rows, width)[4:]
        + gather_sems(count, chunks),
        compiler_params=remote_params(1),
        cost_estimate=estimate(50),
        name="forward_boundary",
    )(gated, weights, hidden)


def back_kernel(
    count, chunks, gathers, gmixed_ref, weights_ref, grad_ref, hidden_ref, inverse_ref, gain_ref, inner_ref, new_ref, ggain_ref, *more
):
    full_ref, more = (more[0], more[1:]) if gathers else (None, more)
    pair_buf, right_buf, left_buf, stage, inner_buf, column_ref, inner_send, inner_recv = more[:8]
    part_ref, weight_ref, weight_sem = more[8:11]
    sems = more[11:]
    fetch = pltpu.make_async_copy(weights_ref, weight_ref, weight_sem)
    fetch.start()
    line = Line(count)
    rows, width = grad_ref.shape
    model = width * count
    mine = pl.ds(pl.multiple_of(line.me * width, width), width)
    others = [lax.rem(line.me + k, count) for k in range(1, count)]
    barrier = pltpu.get_barrier_semaphore()
    for other in others:
        pl.semaphore_signal(barrier, inc=1, device_id={"chan": other}, device_id_type=MESH)
    pl.semaphore_wait(barrier, count - 1)
    begin, middle, finish, end = scatter_steps(
        line, part_ref, pair_buf, right_buf, left_buf, stage, width, chunks, sems[:6]
    )
    if gathers:
        gather_begin, gather_middle, gather_end = gather_steps(line, full_ref, width, chunks, sems[6:])
    sums = [
        remote(inner_ref, inner_buf.at[k], inner_send.at[k], inner_recv.at[k], others[k]) for k in range(count - 1)
    ]
    for copy in sums:
        copy.start()
    fetch.wait()

    def produce(owner):
        features = pl.ds(pl.multiple_of(owner * width, width), width)
        part_ref[:, features] = dot(gmixed_ref[...], weight_ref[features, :], ((1,), (1,))).astype(BF16)

    begin(produce)
    eye = lax.broadcasted_iota(jnp.int32, (LANES, LANES), 0) == lax.broadcasted_iota(jnp.int32, (LANES, LANES), 1)
    ggain_ref[...] = jnp.zeros_like(ggain_ref)
    for c in range(chunks):
        here = pl.ds(c * (rows // chunks), rows // chunks)
        middle(c)
        if c == 0:
            inner = inner_ref[...]
            for k in range(count - 1):
                sums[k].wait_recv()
                inner = inner + inner_buf[k]
            for b in range(rows // LANES):
                column_ref[pl.ds(b * LANES, LANES), :] = jnp.sum(
                    jnp.where(eye, jnp.broadcast_to(inner[b : b + 1, :], (LANES, LANES)), 0.0), axis=1, keepdims=True
                )
        finish(c, new_ref)
        gnormed = new_ref[here, :]
        inverse = inverse_ref[here, :]
        hidden = hidden_ref[here, :]
        factor = inverse * inverse * column_ref[here, :] * (1.0 / model)
        ggain_ref[0:1, :] += jnp.sum(gnormed * hidden * inverse, axis=0, keepdims=True)
        new = grad_ref[here, :] + inverse * (gain_ref[...] * gnormed) - hidden * factor
        new_ref[here, :] = new
        if gathers:
            full_ref[here, mine] = new.astype(BF16)
            gather_begin(c)
    if gathers:
        gather_middle()
        gather_end()
    end()
    for copy in sums:
        copy.wait_send()


def backward_boundary(gmixed, weights, grad, hidden, inverse, gain, inner, gathers):
    count = lax.axis_size("chan")
    rows, width = hidden.shape
    chunks = 2
    out_shape = [jax.ShapeDtypeStruct((rows, width), F32), jax.ShapeDtypeStruct((8, width), F32)]
    scratch = scatter_scratch(count, chunks, rows, width)
    scratch += [
        pltpu.VMEM((count - 1, rows // LANES, LANES), F32),
        pltpu.VMEM((rows, 1), F32),
        pltpu.SemaphoreType.DMA((count - 1,)),
        pltpu.SemaphoreType.DMA((count - 1,)),
    ]
    product = [
        pltpu.VMEM((rows, count * width), BF16),
        pltpu.VMEM(weights.shape, BF16),
        pltpu.SemaphoreType.DMA,
    ]
    order = scratch[:4] + scratch[10:] + product + scratch[4:10]
    if gathers:
        out_shape.append(jax.ShapeDtypeStruct((rows, count * width), BF16))
        order += gather_sems(count, chunks)
    return pl.pallas_call(
        functools.partial(back_kernel, count, chunks, gathers),
        in_specs=[whole(1)[0], pl.BlockSpec(memory_space=pl.ANY)] + whole(5),
        out_specs=whole(len(out_shape)),
        out_shape=out_shape,
        scratch_shapes=order,
        compiler_params=remote_params(2 if gathers else 3),
        cost_estimate=estimate(50 if gathers else 27),
        name="backward_boundary" if gathers else "backward_last",
    )(gmixed, weights, grad, hidden, inverse, gain, inner.reshape(rows // LANES, LANES))


def sum_kernel(count, part_ref, out_ref, give, arrived, total_ref, result, send1, recv1, send2, recv2):
    me = lax.axis_index("chan")
    rows, width = part_ref.shape
    own, extra = rows // count, width - LANES
    sides = LANES // extra
    block = rows // sides
    more = block // count
    others = [lax.rem(me + k, count) for k in range(1, count)]
    barrier = pltpu.get_barrier_semaphore()
    for other in others:
        pl.semaphore_signal(barrier, inc=1, device_id={"chan": other}, device_id_type=MESH)

    def place_at(k):
        row = lax.broadcasted_iota(jnp.int32, (extra, LANES), 0)
        col = lax.broadcasted_iota(jnp.int32, (extra, LANES), 1)
        return jnp.where(col == row + k * extra, 1.0, 0.0).astype(BF16)

    side = jnp.zeros((block, LANES), F32)
    for k in range(sides):
        side = side + jnp.dot(part_ref[k * block : (k + 1) * block, LANES:], place_at(k), preferred_element_type=F32)
    side = side.astype(BF16)
    for o in range(count):
        give[o, :own, :] = part_ref[o * own : (o + 1) * own, :LANES]
        give[o, own:, :] = side[o * more : (o + 1) * more, :]
    pl.semaphore_wait(barrier, count - 1)
    first, second = [], []
    for k, other in enumerate(others):
        first.append(remote(give.at[other], arrived.at[k], send1.at[k], recv1.at[k], other))
        first[k].start()
    acc = give[me].astype(F32)
    for k in range(count - 1):
        first[k].wait_recv()
        acc = acc + arrived[k].astype(F32)
    total_ref[...] = acc.astype(BF16)
    for k, other in enumerate(others):
        second.append(remote(total_ref, result.at[me], send2.at[k], recv2.at[k], other))
        second[k].start()
    result[me] = total_ref[...]
    for copy in second:
        copy.wait()
    sums = [result[o] for o in range(count)]
    for o in range(count):
        out_ref[o * own : (o + 1) * own, :LANES] = sums[o][:own, :]
    side = jnp.concatenate([value[own:, :].astype(F32) for value in sums], axis=0).astype(BF16)
    for k in range(sides):
        columns = dot(side, place_at(k), ((1,), (1,)))
        out_ref[k * block : (k + 1) * block, LANES:] = columns.astype(BF16)
    for copy in first:
        copy.wait_send()


def sum_chan(part):
    count = lax.axis_size("chan")
    rows, width = part.shape
    piece = rows // count + rows // (LANES // (width - LANES)) // count
    return pl.pallas_call(
        functools.partial(sum_kernel, count),
        in_specs=whole(1),
        out_specs=whole(1)[0],
        out_shape=jax.ShapeDtypeStruct((rows, width), BF16),
        scratch_shapes=[
            pltpu.VMEM((count, piece, LANES), BF16),
            pltpu.VMEM((count - 1, piece, LANES), BF16),
            pltpu.VMEM((piece, LANES), BF16),
            pltpu.VMEM((count, piece, LANES), BF16),
        ]
        + [pltpu.SemaphoreType.DMA((count - 1,))] * 4,
        compiler_params=remote_params(4),
        cost_estimate=estimate(14),
        name="sum_chan",
    )(part)


def exchanged(value, bit):
    return lax.ppermute(value, "seq", [(i, i ^ bit) for i in range(lax.axis_size("seq"))])


class Summed:
    def __init__(self, value, halves):
        self.halves = halves
        self.bit = 1
        self.keep = value
        give = value
        if halves:
            half = value.shape[0] // 2
            core = lax.axis_index("seq") % 2
            self.keep = lax.dynamic_slice_in_dim(value, core * half, half, 0)
            give = lax.dynamic_slice_in_dim(value, (1 - core) * half, half, 0)
        self.wire = exchanged(give, 1)

    def step(self):
        total = self.keep.astype(F32) + self.wire.astype(F32)
        self.bit *= 2
        if self.bit < lax.axis_size("seq"):
            self.keep = total.astype(BF16)
            self.wire = exchanged(self.keep, self.bit)
        elif self.halves:
            self.keep = total.astype(BF16)
            self.wire = exchanged(self.keep, 1)
        else:
            self.keep = total

    def across(self):
        while self.bit * 2 < lax.axis_size("seq"):
            self.step()

    def last(self):
        while self.bit * 2 < lax.axis_size("seq"):
            self.step()
        return self.keep, self.wire

    def total(self):
        while self.bit < lax.axis_size("seq"):
            self.step()
        return (self.keep, self.wire) if self.halves else self.keep


def after(value, *sums):
    value, wires = lax.optimization_barrier((value, [one.wire for one in sums]))
    for one, wire in zip(sums, wires):
        one.wire = wire
    return value


def place_pairs_kernel(core_ref, *refs):
    *ins, out_ref = refs[-5:]
    own = pl.program_id(0) == 0
    for j in range(2):
        out_ref[0, :, j, :] = jnp.where(own, ins[2 * j][...].astype(F32), ins[2 * j + 1][...].astype(F32))


def place_rows_kernel(core_ref, *refs):
    mine, other, out_ref = refs[-3:]
    own = pl.program_id(0) == 0
    out_ref[0] = jnp.where(own, mine[...].astype(F32), other[...].astype(F32))


def place(kernel, parts, base, layer, layers, block, middle):
    half, width = parts[0].shape
    core = (lax.axis_index("seq") % 2).reshape(1)
    steps = half // block

    def where(kept):
        if kept:
            return lambda k, b, core: (jnp.where(k == 0, b, steps - 1), 0)
        return lambda k, b, core: (jnp.where(k == 1, b, 0), 0)

    def out(k, b, core):
        return (layer, (core[0] + k - 2 * core[0] * k) * steps + b) + (0,) * (1 + len(middle))

    ins = [pl.BlockSpec((block, width), where(p % 2 == 0)) for p in range(len(parts))]
    shape = (layers, 2 * half) + middle + (width,)
    args = list(parts)
    aliases = {}
    if base is not None:
        ins.insert(0, pl.BlockSpec(memory_space=pl.ANY))
        args.insert(0, base)
        aliases = {1: 0}
    return pl.pallas_call(
        kernel,
        grid_spec=pltpu.PrefetchScalarGridSpec(
            num_scalar_prefetch=1,
            grid=(2, steps),
            in_specs=ins,
            out_specs=pl.BlockSpec((1, block) + middle + (width,), out),
        ),
        out_shape=jax.ShapeDtypeStruct(shape, F32),
        input_output_aliases=aliases,
        compiler_params=params("arbitrary", "arbitrary"),
        cost_estimate=estimate(5),
        name="place",
    )(core, *args)


def dot(a, b, dims):
    return lax.dot_general(a, b, (dims, ((), ())), preferred_element_type=F32)


def rows_of_packed(rank_columns, rank, states, seqs, taps):
    names = [("xproj", rank_columns), ("dtproj", rank), ("decay", states), ("init", seqs * states)]
    names += [("taps", taps), ("shift", 1), ("bias", 1), ("skip", 1), ("conv", (taps - 1) * seqs)]
    places, row = {}, 0
    for name, size in names:
        places[name] = (row, row + size)
        row += size
    return places, row + (-row) % 16


def mid_kernel(
    gproj_ref, xproj_ref, gact_ref, inner_ref, head_ref, low_ref, taps_ref, shift_ref, rank_ref, gpre_ref, ggate_ref,
    gdecay_ref, gskip_ref, ginit_ref,
    gmixed_ref, packed_ref,
    dotted_ref, pad_ref, gconv_ref, tail_ref, give_ref, got_ref, send_sem, recv_sem,
):
    seqs, length = gact_ref.shape[:2]
    tokens = length * G
    count = gmixed_ref.shape[1] // (2 * LANES)
    taps = taps_ref.shape[0]
    over = taps - 1
    j = pl.program_id(0)
    place, peers = lax.axis_index("seq"), lax.axis_size("seq")
    states = gdecay_ref.shape[1]
    places, _ = rows_of_packed(gproj_ref.shape[1], rank_ref.shape[1], states, seqs, taps)

    def to_previous(t):
        return pltpu.make_async_remote_copy(
            src_ref=give_ref.at[t], dst_ref=got_ref.at[t], send_sem=send_sem.at[t], recv_sem=recv_sem.at[t],
            device_id={"seq": jnp.maximum(place - 1, 0)}, device_id_type=MESH,
        )

    @pl.when(j == 0)
    def _():
        barrier = pltpu.get_barrier_semaphore()

        @pl.when(place < peers - 1)
        def _():
            pl.semaphore_signal(barrier, inc=1, device_id={"seq": place + 1}, device_id_type=MESH)

        pl.when(place > 0)(lambda: pl.semaphore_wait(barrier, 1))

    columns = pl.ds(pl.multiple_of(j * LANES, LANES), LANES)
    gate_columns = pl.ds(pl.multiple_of((count + j) * LANES, LANES), LANES)
    gmixed_ref[:, gate_columns] = ggate_ref[...]
    dotted_ref[...] = jnp.dot(gproj_ref[...], xproj_ref[...], preferred_element_type=F32)
    zero = jnp.zeros((G, LANES), F32)
    weights = [jnp.broadcast_to(taps_ref[k : k + 1, :], (G, LANES)) for k in range(taps)]
    shift = jnp.broadcast_to(shift_ref[...], (G, LANES))
    sums = (zero,) * (taps + 1)
    early = [[None] * seqs for _ in range(over)]
    for s in range(seqs):
        for k in range(over):
            pad_ref[k] = head_ref[s, k]

        def fill(l, carry):
            pad_ref[l + over] = inner_ref[s, l]
            return carry

        lax.fori_loop(0, length, fill, 0, unroll=math.gcd(length, 8))

        def one(l, sums):
            parts = [pad_ref[l + k] for k in range(taps)]
            pre = shift
            for k in range(taps):
                pre = pre + weights[k] * parts[k]
            sig = 1.0 / (1.0 + jnp.exp(-pre))
            here = dotted_ref[pl.ds(pl.multiple_of(s * tokens + l * G, G), G), :]
            gconv = (gact_ref[s, l] + here) * (sig + pre * sig * (1.0 - sig))
            gconv_ref[l] = gconv
            return tuple(sums[k] + gconv * parts[k] for k in range(taps)) + (sums[taps] + gconv,)

        sums = lax.fori_loop(0, length, one, sums, unroll=math.gcd(length, 8))
        for k in range(over):
            gconv_ref[length + k] = shifted(gconv_ref[k], -1, 0.0)
            total = weights[0] * gconv_ref[k]
            for i in range(1, k + 1):
                total = total + weights[i] * gconv_ref[k - i]
            early[k][s] = total[0:1, :]
            give_ref[j, s, k : k + 1, :] = total[0:1, :]

        def inner_of(l):
            total = weights[0] * gconv_ref[l + over]
            for k in range(1, taps):
                total = total + weights[k] * gconv_ref[l + over - k]
            return total

        def pair(p, carry):
            both = jnp.concatenate([inner_of(2 * p), inner_of(2 * p + 1)], axis=0)
            gmixed_ref[pl.ds(pl.multiple_of(s * tokens + 2 * p * G, 2 * G), 2 * G), columns] = both.astype(BF16)
            return carry

        lax.fori_loop(0, length // 2 - 2, pair, 0, unroll=math.gcd(length // 2 - 2, 4))
        for q in range(4):
            tail_ref[j, s, q] = inner_of(length - 4 + q)
    pl.when(place > 0)(lambda: to_previous(j).start())

    def put(name, value):
        first, last = places[name]
        packed_ref[first:last, :] = value.astype(BF16)

    put("xproj", dot(gproj_ref[...], low_ref[...], ((0,), (0,))))
    put("dtproj", dot(rank_ref[...], gpre_ref[...], ((0,), (0,))))
    bias = jnp.dot(jnp.ones((16, seqs * tokens), BF16), gpre_ref[...], preferred_element_type=F32)[0:1, :]
    decay, skip = gdecay_ref[0], gskip_ref[0, 0:1, :]
    for s in range(1, seqs):
        decay = decay + gdecay_ref[s]
        skip = skip + gskip_ref[s, 0:1, :]
    put("decay", decay)
    first = place == 0
    for s in range(seqs):
        row = places["init"][0] + s * states
        packed_ref[row : row + states, :] = jnp.where(first, ginit_ref[s], 0.0).astype(BF16)
    rest = [jnp.sum(value, axis=0, keepdims=True) for value in sums]
    rest += [bias, skip]
    rest += [jnp.where(first, early[k][s], 0.0) for k in range(over) for s in range(seqs)]
    row = places["taps"][0]
    rest += [jnp.zeros((1, LANES), F32)] * (packed_ref.shape[0] - row - len(rest))
    packed_ref[row:, :] = jnp.concatenate(rest, axis=0).astype(BF16)

    @pl.when(j == count - 1)
    def _():
        last_row = lax.broadcasted_iota(jnp.int32, (G, LANES), 0) == G - 1
        inside = place < peers - 1
        for t in range(count):
            pl.when(place < peers - 1)(lambda: to_previous(t).wait_recv())
            for s in range(seqs):
                values = []
                for q in range(4):
                    value = tail_ref[t, s, q]
                    k = q - 4 + over
                    if k >= 0:
                        given = jnp.broadcast_to(got_ref[t, s, k : k + 1, :], (G, LANES))
                        value = value + jnp.where(jnp.logical_and(last_row, inside), given, 0.0)
                    values.append(value)
                for q in (0, 2):
                    row = s * tokens + (length - 4 + q) * G
                    both = jnp.concatenate(values[q : q + 2], axis=0)
                    gmixed_ref[row : row + 2 * G, t * LANES : (t + 1) * LANES] = both.astype(BF16)
            pl.when(place > 0)(lambda: to_previous(t).wait_send())


def mid_backward(
    gproj, xproj, gact, mixed, head, low, taps, shift, rank_part, gpre, ggate, gdecay, gskip, ginit
):
    seqs, length, _, chans = gact.shape
    rows = seqs * length * G
    count = chans // LANES
    states = gdecay.shape[1]
    over = taps.shape[0] - 1
    _, packed_rows = rows_of_packed(gproj.shape[1], rank_part.shape[1], states, seqs, taps.shape[0])
    token = pl.BlockSpec((seqs, length, G, LANES), lambda j: (0, 0, 0, j))
    row = pl.BlockSpec((rows, LANES), lambda j: (0, j))

    def column(height):
        return pl.BlockSpec((height, LANES), lambda j: (0, j))

    def stack(height):
        return pl.BlockSpec((seqs, height, LANES), lambda j: (0, 0, j))

    return pl.pallas_call(
        mid_kernel,
        grid=(count,),
        in_specs=[
            pl.BlockSpec(gproj.shape, lambda j: (0, 0)),
            column(xproj.shape[0]),
            token,
            token,
            pl.BlockSpec((seqs, over, G, LANES), lambda j: (0, 0, 0, j)),
            row,
            column(over + 1),
            column(1),
            pl.BlockSpec(rank_part.shape, lambda j: (0, 0)),
            row,
            row,
            stack(states),
            stack(8),
            stack(states),
        ],
        out_specs=[pl.BlockSpec((rows, 2 * chans), lambda j: (0, 0)), column(packed_rows)],
        out_shape=[
            jax.ShapeDtypeStruct((rows, 2 * chans), BF16),
            jax.ShapeDtypeStruct((packed_rows, chans), BF16),
        ],
        scratch_shapes=[
            pltpu.VMEM((rows, LANES), F32),
            pltpu.VMEM((length + over, G, LANES), F32),
            pltpu.VMEM((length + over, G, LANES), F32),
            pltpu.VMEM((count, seqs, 4, G, LANES), F32),
            pltpu.VMEM((count, seqs, 8, LANES), F32),
            pltpu.VMEM((count, seqs, 8, LANES), F32),
            pltpu.SemaphoreType.DMA((count,)),
            pltpu.SemaphoreType.DMA((count,)),
        ],
        compiler_params=pltpu.CompilerParams(
            dimension_semantics=("arbitrary",), collective_id=5, has_side_effects=True, vmem_limit_bytes=VMEM_LIMIT
        ),
        cost_estimate=estimate(8),
        name="mid_backward",
    )(gproj, xproj, gact, mixed, head, low, taps, shift, rank_part, gpre, ggate, gdecay, gskip, ginit)


def unpack_kernel(layers, places, seqs, *refs):
    smalls, gains, outs = refs[: 2 * layers], refs[2 * layers : 4 * layers], refs[4 * layers :]
    gain, taps, shift, xproj, dtproj, bias, decay, skip, conv, init = outs
    for i in range(layers):
        def rows(name):
            first, last = places[name]
            return smalls[2 * i][first:last, :].astype(F32) + smalls[2 * i + 1][first:last, :].astype(F32)

        gain[i : i + 1, :] = gains[2 * i][0:1, :].astype(F32) + gains[2 * i + 1][0:1, :].astype(F32)
        xproj[i], dtproj[i], decay[i] = rows("xproj"), rows("dtproj"), rows("decay")
        init[i] = rows("init")
        low, high = places["taps"][0], smalls[0].shape[0]
        rest = smalls[2 * i][low:high, :].astype(F32) + smalls[2 * i + 1][low:high, :].astype(F32)

        def of(name):
            first, last = places[name]
            return rest[first - low : last - low, :]

        taps[i] = of("taps")
        shift[i : i + 1, :], bias[i : i + 1, :], skip[i : i + 1, :] = of("shift"), of("bias"), of("skip")
        for k in range(conv.shape[1]):
            conv[i, k] = of("conv")[k * seqs : (k + 1) * seqs, :]


def unpack(smalls, gains, places, seqs, width):
    layers = len(smalls)
    chans = smalls[0][0].shape[1]

    def size(name):
        return places[name][1] - places[name][0]

    shapes = [
        (layers, width), (layers, size("taps"), chans), (layers, chans), (layers, size("xproj"), chans),
        (layers, size("dtproj"), chans), (layers, chans), (layers, size("decay"), chans), (layers, chans),
        (layers, size("conv") // seqs, seqs, chans), (layers, size("init"), chans),
    ]
    args = [value for pair in smalls for value in pair] + [value for pair in gains for value in pair]
    return pl.pallas_call(
        functools.partial(unpack_kernel, layers, places, seqs),
        in_specs=whole(len(args)),
        out_specs=whole(len(shapes)),
        out_shape=[jax.ShapeDtypeStruct(shape, F32) for shape in shapes],
        compiler_params=params(),
        cost_estimate=estimate(3),
        name="unpack",
    )(*args)


def passed_along(value, axis, by):
    peers = lax.axis_size(axis)
    pairs = [(i, i + by) for i in range(peers) if 0 <= i + by < peers]
    return lax.ppermute(value, axis, pairs)


def to_segments(value):
    seqs, tokens, width = value.shape
    return value.reshape(seqs, G, tokens // G, width).transpose(0, 2, 1, 3)


def from_segments(value):
    seqs, length, _, width = value.shape
    return value.transpose(0, 2, 1, 3).reshape(seqs, length * G, width)


def local(
    hidden_in,
    norm_gain,
    in_weight,
    conv_weight,
    conv_bias,
    xproj_weight,
    dtproj_weight,
    dt_bias,
    decay_log,
    skip_gain,
    out_weight,
    conv_state,
    scan_state,
    out_cotangent,
):
    layers = in_weight.shape[0]
    rank = dtproj_weight.shape[1]
    states = decay_log.shape[1]
    seqs, tokens, _ = hidden_in.shape
    length = tokens // G
    rows = seqs * tokens
    chans = in_weight.shape[3]
    model = hidden_in.shape[2] * lax.axis_size("chan")
    taps = conv_weight.shape[1]
    is_first = lax.axis_index("seq") == 0

    first = to_segments(hidden_in).reshape(rows, -1)
    hidden = first.astype(F32)
    full, gains, flats = gather_first(first, norm_gain, in_weight)
    grad = to_segments(out_cotangent).reshape(rows, -1)
    grad_rows = lax.all_gather(grad, "chan", axis=1, tiled=True)
    grad = grad.astype(F32)
    saved = []
    for i in range(layers):
        wide = full[:rows].astype(F32)
        inverse = lax.rsqrt(jnp.sum(wide * wide, axis=1, keepdims=True) / model + EPS)
        normed = (wide * inverse * gains[i]).astype(BF16)
        flat_in = flats[i]
        mixed = dot(normed, flat_in, ((1,), (0,)))
        inner = mixed[:, :chans].reshape(seqs, length, G, chans)
        gate = mixed[:, chans:].reshape(seqs, length, G, chans)
        tail = inner[:, length - taps + 1 :]
        received = passed_along(tail[:, :, G - 1], "seq", 1)
        before = jnp.where(is_first, conv_state[i], received)
        head = jnp.concatenate([before[:, :, None], tail[:, :, : G - 1]], axis=2)
        padded = jnp.concatenate([head, inner], axis=1)
        pre = conv_bias[i] + sum(conv_weight[i, k] * padded[:, k : k + length] for k in range(taps))
        act = jax.nn.silu(pre)
        act_low = act.astype(BF16).reshape(rows, chans)
        projected = sum_chan(dot(act_low, xproj_weight[i], ((1,), (0,))).astype(BF16))
        rank_part = projected[:, :rank]
        maps = projected[:, rank:].reshape(seqs, tokens, 2 * states)
        delta = dot(rank_part, dtproj_weight[i], ((1,), (0,))) + dt_bias[i]
        delta = delta.reshape(seqs, length, G, chans)
        step = jax.nn.softplus(delta)
        y, gated, start, span, packs = scan_forward(
            act, step, gate, maps, decay_log[i], scan_state[i], skip_gain[i : i + 1]
        )
        gated = gated.reshape(rows, chans)
        saved.append(
            (hidden, inverse, normed, flat_in, mixed, gate, head, act, act_low, rank_part, maps, delta, step,
             span, packs, y, gated, start)
        )
        if i + 1 < layers:
            hidden, full = forward_boundary(gated, out_weight, i, hidden)
        else:
            branch = dot(gated, out_weight[i], ((1,), (0,))).astype(BF16)
            branch_sum = lax.psum_scatter(branch, "chan", scatter_dimension=1, tiled=True)

    def finish(i, sums):
        nonlocal in_grads, out_grads
        in_grads = place(
            place_pairs_kernel, [*sums["inner"].total(), *sums["gate"].total()], in_grads, i, layers, model // 4, (2,)
        )
        out_grads = place(place_rows_kernel, list(sums["out"].total()), out_grads, i, layers, chans // 2, ())

    smalls = [None] * layers
    in_grads = out_grads = None
    before_sums = None
    for i in reversed(range(layers)):
        (hidden_i, inverse, normed, flat_in, mixed, gate, head, act, act_low, rank_part, maps, delta, step,
         span, packs, y, gated, start) = saved[i]
        sums = {}
        sums["out"] = Summed(dot(gated, grad_rows, ((0,), (0,))).astype(BF16), True)
        grad_gated = dot(grad_rows, out_weight[i], ((1,), (1,)))
        grad_gated = grad_gated.reshape(seqs, length, G, chans)
        last = i == layers - 1
        if last:
            scanned = scan_adjoint_and_backward(
                act, step, delta, gate, y, grad_gated, maps, decay_log[i], start, span, packs, skip_gain[i : i + 1],
                dtproj_weight[i],
            )
        else:
            suffix, back_packs = scan_adjoint(step, gate, grad_gated, maps, decay_log[i], span)
            back_packs = after(back_packs, sums["out"])
            sums["out"].across()
            scanned = scan_backward(
                act, step, delta, gate, y, grad_gated, maps, decay_log[i], start, suffix, span, back_packs, packs,
                skip_gain[i : i + 1], dtproj_weight[i],
            )
        gact, gpre, ggate, proj_part, gdecay, gskip, ginit = after(scanned, sums["out"])
        sums["out"].across() if last else sums["out"].step()
        gpre = gpre.reshape(rows, chans)
        ggate = ggate.reshape(rows, chans)
        proj_part = proj_part.reshape(rows, -1)
        sums["gate"] = Summed(dot(normed, ggate, ((0,), (0,))).astype(BF16), True)
        proj_part = after(proj_part, sums["gate"])
        sums["gate"].across()
        grad_proj = sum_chan(proj_part)
        if not last:
            grad_proj = after(grad_proj, sums["out"])
        gmixed, packed = mid_backward(
            grad_proj, xproj_weight[i].T, gact, mixed.reshape(seqs, length, G, -1), head, act_low, conv_weight[i],
            conv_bias[i : i + 1], rank_part, gpre, ggate, gdecay, gskip, ginit,
        )
        gmixed, packed = after((gmixed, packed), sums["out" if last else "gate"])
        if last:
            gmixed, branch_sum = lax.optimization_barrier((gmixed, branch_sum))
            hidden = hidden + branch_sum.astype(F32)
        sums["out" if last else "gate"].step()
        sums["small"] = Summed(packed, False)
        sums["inner"] = Summed(dot(normed, gmixed[:, :chans], ((0,), (0,))).astype(BF16), True)
        inner_sums = jnp.sum(gmixed.astype(F32) * mixed, axis=1)
        gmixed = after(gmixed, sums["inner"], sums["small"])
        sums["inner"].across()
        sums["small"].across()
        outs = backward_boundary(
            gmixed, flat_in, grad, hidden_i, inverse, norm_gain[i : i + 1], inner_sums, i > 0
        )
        if last:
            outs = after(outs, sums["gate"], sums["inner"], sums["small"])
            sums["gate"].step()
        else:
            outs = after(outs, sums["inner"], sums["small"])
        grad = outs[0]
        if i > 0:
            grad_rows = outs[2]
        sums["inner"].step()
        sums["gain"] = Summed(outs[1].astype(BF16), False)
        smalls[i] = sums
        if before_sums is not None:
            finish(i + 1, before_sums)
        before_sums = sums
    finish(0, before_sums)
    places, _ = rows_of_packed(xproj_weight.shape[2], rank, states, seqs, taps)
    gain, taps_grad, shift, xproj, dtproj, bias, decay, skip, conv, init = unpack(
        [one["small"].last() for one in smalls], [one["gain"].last() for one in smalls], places, seqs,
        norm_gain.shape[1],
    )

    def back_out(value):
        return from_segments(value.reshape(seqs, length, G, -1))

    return (
        back_out(hidden),
        back_out(grad),
        gain,
        in_grads,
        taps_grad,
        shift,
        xproj.transpose(0, 2, 1),
        dtproj,
        bias,
        decay,
        skip,
        out_grads,
        conv.transpose(0, 2, 1, 3),
        init.reshape(scan_state.shape),
    )


def solution(mesh):
    return jax.shard_map(
        local,
        mesh=mesh,
        in_specs=(
            P(None, "seq", "chan"),
            P(None, "chan"),
            P(None, None, None, "chan"),
            P(None, None, "chan"),
            P(None, "chan"),
            P(None, "chan", None),
            P(None, None, "chan"),
            P(None, "chan"),
            P(None, None, "chan"),
            P(None, "chan"),
            P(None, "chan", None),
            P(None, None, None, "chan"),
            P(None, None, None, "chan"),
            P(None, "seq", "chan"),
        ),
        out_specs=(
            P(None, "seq", "chan"),
            P(None, "seq", "chan"),
            P(None, "chan"),
            P(None, None, None, "chan"),
            P(None, None, "chan"),
            P(None, "chan"),
            P(None, "chan", None),
            P(None, None, "chan"),
            P(None, "chan"),
            P(None, None, "chan"),
            P(None, "chan"),
            P(None, "chan", None),
            P(None, None, None, "chan"),
            P(None, None, None, "chan"),
        ),
        check_vma=False,
    )
```

```python
import functools
import math

import jax
import jax.numpy as jnp
from jax import lax
from jax.experimental import pallas as pl
from jax.experimental.pallas import tpu as pltpu
from jax.sharding import PartitionSpec as P

EPS = 1e-05
G = 8
LANES = 128
LOG2E = 1.4426950408889634
LN2 = 0.6931471805599453
F32 = jnp.float32
BF16 = jnp.bfloat16
VMEM_LIMIT = 42 * 1024 * 1024
MESH = pl.DeviceIdType.MESH


def params(*semantics):
    return pltpu.CompilerParams(dimension_semantics=semantics, vmem_limit_bytes=VMEM_LIMIT)


def spread_maps(maps_ref, first, count, out_ref):
    shape = (maps_ref.shape[2], count * LANES)
    row = lax.broadcasted_iota(jnp.int32, shape, 0)
    col = lax.broadcasted_iota(jnp.int32, shape, 1) // LANES
    choice = jnp.where(row == col + first, 1.0, 0.0).astype(BF16)
    out_ref[...] = jnp.dot(maps_ref[0], choice, preferred_element_type=F32)


def part(ref, l, n):
    return ref[pl.ds(pl.multiple_of(l * G, G), G), n * LANES : (n + 1) * LANES]


def spread_rate(decay_ref, rate_ref):
    rate = jnp.exp(decay_ref[...]) * (-LOG2E)
    for n in range(rate.shape[0]):
        rate_ref[n] = jnp.broadcast_to(rate[n : n + 1, :], (G, LANES))


def shifted(value, by, fill):
    row = lax.broadcasted_iota(jnp.int32, value.shape, 0)
    moved = pltpu.roll(value, by % G, 0)
    inside = row >= by if by > 0 else row < G + by
    return jnp.where(inside, moved, fill)


def segment_prefix(ends, span, rate_ref, direction):
    step = 1
    while step < G:
        moved_span = shifted(span, direction * step, 0.0)
        ends = [
            e + jnp.exp2(span * rate_ref[n]) * shifted(e, direction * step, 0.0)
            for n, e in enumerate(ends)
        ]
        span = span + moved_span
        step *= 2
    return ends, span


class SeqExchange:
    def __init__(self, give_ref, got_ref, send_sem, recv_sem):
        self.refs = give_ref, got_ref
        self.sems = send_sem, recv_sem
        self.me, self.peers = lax.axis_index("seq"), lax.axis_size("seq")
        self.others = [lax.rem(self.me + k, self.peers) for k in range(1, self.peers)]

    def signal(self):
        barrier = pltpu.get_barrier_semaphore()
        for other in self.others:
            pl.semaphore_signal(barrier, inc=1, device_id={"seq": other}, device_id_type=MESH)

    def meet(self):
        if self.others:
            pl.semaphore_wait(pltpu.get_barrier_semaphore(), len(self.others))

    def copy(self, step, k):
        give, got = self.refs
        send, recv = self.sems
        return pltpu.make_async_remote_copy(
            src_ref=give.at[step], dst_ref=got.at[self.me, step], send_sem=send.at[step, k], recv_sem=recv.at[step, k],
            device_id={"seq": self.others[k]}, device_id_type=MESH,
        )

    def start(self, step):
        for k in range(len(self.others)):
            self.copy(step, k).start()

    def wait(self, step):
        for k in range(len(self.others)):
            self.copy(step, k).wait()

    def finish(self, steps):
        for step in range(steps):
            self.wait(step)


def exchange_scratch(steps, rows):
    peers = lax.axis_size("seq")
    sems = pltpu.SemaphoreType.DMA((steps, max(peers - 1, 1)))
    return [pltpu.VMEM((steps, rows, LANES), F32), pltpu.VMEM((peers, steps, rows, LANES), F32), sems, sems]


def exchange_params(ident):
    return pltpu.CompilerParams(
        dimension_semantics=("arbitrary", "arbitrary"), collective_id=ident, has_side_effects=True,
        vmem_limit_bytes=VMEM_LIMIT,
    )


def exchange_step(exchange, packs_ref, give_ref, got_ref, rows):
    seqs, tiles = pl.num_programs(0), pl.num_programs(1)
    step = pl.program_id(0) * tiles + pl.program_id(1)
    total = give_ref.shape[0]
    wide = packs_ref.shape[3] // LANES
    give_ref[step] = rows
    pl.when(step == 0)(exchange.meet)
    exchange.start(step)

    @pl.when(step == total - 1)
    def _():
        exchange.finish(total)
        for i in range(total):
            for d in range(got_ref.shape[0]):
                packs_ref[d, i // wide, :, (i % wide) * LANES : (i % wide + 1) * LANES] = jnp.where(
                    exchange.me == d, give_ref[i], got_ref[d, i]
                )


def forward_kernel(
    act_ref, step_ref, gate_ref, maps_ref, decay_ref, init_ref, skip_ref,
    y_ref, gated_ref, start_ref, span_ref, packs_ref,
    b_ref, c_ref, rate_ref, prefix_ref, spans_ref, give_ref, got_ref, *sems,
):
    length, states = act_ref.shape[1], decay_ref.shape[0]
    phase, s, j = pl.program_id(0), pl.program_id(1), pl.program_id(2)
    step = s * pl.num_programs(2) + j
    exchange = SeqExchange(give_ref, got_ref, *sems)
    pl.when(phase + step == 0)(exchange.signal)
    spread_rate(decay_ref, rate_ref)
    zero = jnp.zeros((G, LANES), F32)

    @pl.when(phase == 0)
    def _():
        pl.when(j == 0)(lambda: spread_maps(maps_ref, 0, states, b_ref.at[s]))

        def one(l, carry):
            h, total = carry
            st = step_ref[0, l]
            u = st * act_ref[0, l]
            h = tuple(
                jnp.exp2(st * rate_ref[n]) * h[n] + u * part(b_ref.at[s], l, n) for n in range(states)
            )
            return h, total + st

        h, total = lax.fori_loop(0, length, one, ((zero,) * states, zero), unroll=math.gcd(length, 8))
        ends, span = segment_prefix(list(h), total, rate_ref, 1)
        for n in range(states):
            prefix_ref[step, n] = shifted(ends[n], 1, 0.0)
        spans_ref[step, 0] = shifted(span, 1, 0.0)
        spans_ref[step, 1] = jnp.broadcast_to(span[G - 1 : G, :], (G, LANES)) - span
        rows = [e[G - 1 : G, :] for e in ends] + [jnp.broadcast_to(span[G - 1 : G, :], (8, LANES))]
        give_ref[step] = jnp.concatenate(rows, axis=0)
        pl.when(step == 0)(exchange.meet)
        exchange.start(step)

    @pl.when(phase == 1)
    def _():
        pl.when(j == 0)(lambda: spread_maps(maps_ref, states, states, c_ref))
        exchange.wait(step)
        rate = jnp.exp(decay_ref[...]) * (-LOG2E)
        entry = init_ref[0]
        for d in range(packs_ref.shape[0]):
            pack = jnp.where(exchange.me == d, give_ref[step], got_ref[d, step])
            packs_ref[d, 0] = pack
            joined = jnp.exp2(rate * pack[states : states + 1, :]) * entry + pack[:states, :]
            entry = jnp.where(d < exchange.me, joined, entry)
        span_ref[0] = spans_ref[step]
        span = spans_ref[step, 0]
        h = []
        for n in range(states):
            first = prefix_ref[step, n] + jnp.exp2(rate_ref[n] * span) * entry[n : n + 1, :]
            start_ref[0, n] = first
            h.append(first)
        skip = jnp.broadcast_to(skip_ref[...], (G, LANES))

        def one(k, h):
            h = list(h)
            halves = []
            for i in range(2):
                l = 2 * k + i
                st = step_ref[0, l]
                act = act_ref[0, l]
                u = st * act
                y = skip * act
                for n in range(states):
                    h[n] = jnp.exp2(st * rate_ref[n]) * h[n] + u * part(b_ref.at[s], l, n)
                    y = y + part(c_ref, l, n) * h[n]
                y_ref[0, l] = y
                gate = gate_ref[0, l]
                halves.append(y * (gate / (1.0 + jnp.exp(-gate))))
            row = pl.multiple_of(k * 2 * G, 2 * G)
            gated_ref[0, pl.ds(row, 2 * G), :] = jnp.concatenate(halves, axis=0).astype(BF16)
            return tuple(h)

        lax.fori_loop(0, length // 2, one, tuple(h), unroll=math.gcd(length // 2, 4))


def scan_forward(act, step, gate, maps, decay, init, skip):
    seqs, length, _, chans = act.shape
    states = decay.shape[0]
    peers = lax.axis_size("seq")
    tiles = chans // LANES
    token = pl.BlockSpec((1, length, G, LANES), lambda p, s, j: (s, 0, 0, j))

    def late(shape, index):
        return pl.BlockSpec(shape, lambda p, s, j: index(p * s, p * j))

    return pl.pallas_call(
        forward_kernel,
        grid=(2, seqs, tiles),
        in_specs=[
            token,
            token,
            late((1, length, G, LANES), lambda s, j: (s, 0, 0, j)),
            pl.BlockSpec((1, length * G, maps.shape[2]), lambda p, s, j: (s, 0, 0)),
            pl.BlockSpec((states, LANES), lambda p, s, j: (0, j)),
            late((1, states, LANES), lambda s, j: (s, 0, j)),
            late((1, LANES), lambda s, j: (0, j)),
        ],
        out_specs=[
            late((1, length, G, LANES), lambda s, j: (s, 0, 0, j)),
            late((1, length * G, LANES), lambda s, j: (s, 0, j)),
            late((1, states, G, LANES), lambda s, j: (s, 0, 0, j)),
            late((1, 2, G, LANES), lambda s, j: (s, 0, 0, j)),
            late((peers, 1, states + 8, LANES), lambda s, j: (0, s, 0, j)),
        ],
        out_shape=[
            jax.ShapeDtypeStruct(act.shape, F32),
            jax.ShapeDtypeStruct((seqs, length * G, chans), BF16),
            pltpu.HBM((seqs, states, G, chans), F32),
            pltpu.HBM((seqs, 2, G, chans), F32),
            pltpu.HBM((peers, seqs, states + 8, chans), F32),
        ],
        scratch_shapes=[
            pltpu.VMEM((seqs, length * G, states * LANES), F32),
            pltpu.VMEM((length * G, states * LANES), F32),
            pltpu.VMEM((states, G, LANES), F32),
            pltpu.VMEM((seqs * tiles, states, G, LANES), F32),
            pltpu.VMEM((seqs * tiles, 2, G, LANES), F32),
        ]
        + exchange_scratch(seqs * tiles, states + 8),
        compiler_params=pltpu.CompilerParams(
            dimension_semantics=("arbitrary",) * 3, collective_id=6, has_side_effects=True,
            vmem_limit_bytes=VMEM_LIMIT,
        ),
        cost_estimate=estimate(20),
        name="scan_forward",
    )(act, step, gate, maps, decay, init, skip)


def adjoint_kernel(
    step_ref, gate_ref, grad_ref, maps_ref, decay_ref, span_ref, suffix_ref, packs_ref, c_ref, rate_ref, give_ref,
    got_ref, *sems,
):
    length, states = step_ref.shape[1], decay_ref.shape[0]
    columns = pl.ds(pl.multiple_of(pl.program_id(1) * LANES, LANES), LANES)
    step_ref, gate_ref, grad_ref = (ref.at[:, :, :, columns] for ref in (step_ref, gate_ref, grad_ref))
    exchange = SeqExchange(give_ref, got_ref, *sems)
    pl.when(pl.program_id(0) + pl.program_id(1) == 0)(exchange.signal)

    @pl.when(pl.program_id(1) == 0)
    def _():
        spread_maps(maps_ref, states, states, c_ref)

    spread_rate(decay_ref, rate_ref)

    def one(k, carry):
        l = length - 1 - k
        st = step_ref[0, l]
        gate = gate_ref[0, l]
        gy = grad_ref[0, l] * (gate / (1.0 + jnp.exp(-gate)))
        return tuple(
            jnp.exp2(st * rate_ref[n]) * (carry[n] + gy * part(c_ref, l, n)) for n in range(states)
        )

    zero = jnp.zeros((G, LANES), F32)
    carry = lax.fori_loop(0, length, one, (zero,) * states, unroll=math.gcd(length, 8))
    own = span_ref[0, 1, 0:1, :] + span_ref[0, 0, 1:2, :] - span_ref[0, 0] - span_ref[0, 1]
    ends, _ = segment_prefix(list(carry), own, rate_ref, -1)
    for n in range(states):
        suffix_ref[0, n] = shifted(ends[n], -1, 0.0)
    rows = jnp.concatenate([e[0:1, :] for e in ends], axis=0)
    exchange_step(exchange, packs_ref, give_ref, got_ref, rows)


def scan_adjoint(step, gate, grad, maps, decay, span):
    seqs, length, _, chans = step.shape
    states = decay.shape[0]
    peers = lax.axis_size("seq")
    broad = pl.BlockSpec((1, length, G, chans), lambda s, j: (s, 0, 0, 0))
    return pl.pallas_call(
        adjoint_kernel,
        grid=(seqs, chans // LANES),
        in_specs=[
            broad,
            broad,
            broad,
            pl.BlockSpec((1, length * G, maps.shape[2]), lambda s, j: (s, 0, 0)),
            pl.BlockSpec((states, LANES), lambda s, j: (0, j)),
            pl.BlockSpec((1, 2, G, LANES), lambda s, j: (s, 0, 0, j)),
        ],
        out_specs=[
            pl.BlockSpec((1, states, G, LANES), lambda s, j: (s, 0, 0, j)),
            pl.BlockSpec((peers, seqs, states, chans), lambda s, j: (0, 0, 0, 0)),
        ],
        out_shape=[
            pltpu.HBM((seqs, states, G, chans), F32),
            pltpu.HBM((peers, seqs, states, chans), F32),
        ],
        scratch_shapes=[
            pltpu.VMEM((length * G, states * LANES), F32),
            pltpu.VMEM((states, G, LANES), F32),
        ]
        + exchange_scratch(seqs * chans // LANES, states),
        compiler_params=exchange_params(7),
        cost_estimate=estimate(15),
        name="scan_adjoint",
    )(step, gate, grad, maps, decay, span)


def backward_kernel(
    act_ref, step_ref, delta_ref, gate_ref, y_ref, grad_ref, maps_ref, decay_ref, start_ref, suffix_ref, span_ref,
    packs_ref, forward_packs_ref, skip_ref, weight_ref,
    gact_ref, gpre_ref, ggate_ref, proj_ref, gdecay_ref, gskip_ref, ginit_ref,
    b_ref, c_ref, rate_ref, h_ref, product_ref, select_ref, rank_ref,
):
    length, states = act_ref.shape[1], decay_ref.shape[0]
    columns = pl.ds(pl.multiple_of(pl.program_id(1) * LANES, LANES), LANES)
    act_ref, step_ref, delta_ref, gate_ref, y_ref, grad_ref = (
        ref.at[:, :, :, columns] for ref in (act_ref, step_ref, delta_ref, gate_ref, y_ref, grad_ref)
    )
    wide = states * LANES

    @pl.when(pl.program_id(1) == 0)
    def _():
        spread_maps(maps_ref, 0, states, b_ref)
        spread_maps(maps_ref, states, states, c_ref)
        row = lax.broadcasted_iota(jnp.int32, select_ref.shape, 0) // LANES
        col = lax.broadcasted_iota(jnp.int32, select_ref.shape, 1)
        product_ref[...] = jnp.zeros_like(product_ref)
        rank_ref[...] = jnp.zeros_like(rank_ref)
        select_ref[...] = jnp.where(row == col, 1.0, 0.0).astype(BF16)

    spread_rate(decay_ref, rate_ref)
    rate = jnp.exp(decay_ref[...]) * (-LOG2E)
    me = lax.axis_index("seq")
    count = packs_ref.shape[0]
    entry = jnp.zeros((states, LANES), F32)
    for d in reversed(range(count)):
        joined = jnp.exp2(rate * forward_packs_ref[d, 0, states : states + 1, :]) * entry + packs_ref[d, 0]
        entry = jnp.where(d > me, joined, entry)
    after = span_ref[0, 1]
    skip = jnp.broadcast_to(skip_ref[...], (G, LANES))

    def forward(l, h):
        st = step_ref[0, l]
        u = st * act_ref[0, l]
        for n in range(states):
            h_ref[l, n] = h[n]
        return tuple(
            jnp.exp2(st * rate_ref[n]) * h[n] + u * part(b_ref, l, n) for n in range(states)
        )

    h = lax.fori_loop(
        0, length, forward, tuple(start_ref[0, n] for n in range(states)), unroll=math.gcd(length, 4)
    )
    for n in range(states):
        h_ref[length, n] = h[n]

    def back(k, state):
        carry, gdecay, gskip = list(state[0]), list(state[1]), state[2]
        lines = [length - 1 - 2 * k, length - 2 - 2 * k]
        st, act, u, gy, q, r = [], [], [], [], [], []
        ggate = []
        for l in lines:
            st.append(step_ref[0, l])
            act.append(act_ref[0, l])
            u.append(st[-1] * act[-1])
            gate = gate_ref[0, l]
            grad = grad_ref[0, l]
            sig = 1.0 / (1.0 + jnp.exp(-gate))
            silu = gate * sig
            gy.append(grad * silu)
            ggate.append(grad * y_ref[0, l] * (sig + silu * (1.0 - sig)))
            gskip = gskip + gy[-1] * act[-1]
            q.append(jnp.zeros((G, LANES), F32))
            r.append(jnp.zeros((G, LANES), F32))
        row = pl.multiple_of((length - 2 - 2 * k) * G, 2 * G)
        for n in range(states):
            late, early = [], []
            for i, l in enumerate(lines):
                lam = part(c_ref, l, n) * gy[i] + carry[n]
                early.append(lam * u[i])
                late.append(gy[i] * h_ref[l + 1, n])
                q[i] = q[i] + lam * part(b_ref, l, n)
                carry[n] = jnp.exp2(st[i] * rate_ref[n]) * lam
                w = carry[n] * h_ref[l, n]
                r[i] = r[i] + rate_ref[n] * w
                gdecay[n] = gdecay[n] + st[i] * w
            product_ref[pl.ds(row, 2 * G), n * LANES : (n + 1) * LANES] += jnp.concatenate(early[::-1], axis=0)
            product_ref[pl.ds(row, 2 * G), wide + n * LANES : wide + (n + 1) * LANES] += jnp.concatenate(late[::-1], axis=0)
        gpre = []
        for i, l in enumerate(lines):
            gact_ref[0, l] = skip * gy[i] + st[i] * q[i]
            gstep = LN2 * r[i] + act[i] * q[i]
            gpre.append(gstep / (1.0 + jnp.exp(-delta_ref[0, l])))
        gpre_ref[0, pl.ds(row, 2 * G), :] = jnp.concatenate(gpre[::-1], axis=0).astype(BF16)
        ggate_ref[0, pl.ds(row, 2 * G), :] = jnp.concatenate(ggate[::-1], axis=0).astype(BF16)
        return tuple(carry), tuple(gdecay), gskip

    zero = jnp.zeros((G, LANES), F32)
    first = tuple(
        suffix_ref[0, n] + jnp.exp2(rate_ref[n] * after) * entry[n : n + 1, :] for n in range(states)
    )
    carry, gdecay, gskip = lax.fori_loop(
        0, length // 2, back, (first, (zero,) * states, zero), unroll=math.gcd(length // 2, 2)
    )
    for n in range(states):
        ginit_ref[0, n : n + 1, :] = carry[n][0:1, :]
        total = jnp.sum(gdecay[n] * rate_ref[n], axis=0, keepdims=True)
        gdecay_ref[0, n : n + 1, :] = total * LN2
    gskip_ref[0] = jnp.broadcast_to(jnp.sum(gskip, axis=0, keepdims=True), (8, LANES))

    rank_ref[...] += dot(gpre_ref[0], weight_ref[...], ((1,), (1,)))

    @pl.when(pl.program_id(1) == pl.num_programs(1) - 1)
    def _():
        sums = jnp.dot(product_ref[...].astype(BF16), select_ref[...], preferred_element_type=F32)
        rank = rank_ref.shape[1]
        proj_ref[0, :, :rank] = rank_ref[...].astype(BF16)
        proj_ref[0, :, rank:] = sums[:, : 2 * states].astype(BF16)


def scan_backward(
    act, step, delta, gate, y, grad, maps, decay, start, suffix, span, packs, forward_packs, skip, weight
):
    seqs, length, _, chans = act.shape
    start, suffix, span, packs, forward_packs = (
        pltpu.with_memory_space_constraint(value, pltpu.HBM) for value in (start, suffix, span, packs, forward_packs)
    )
    states = decay.shape[0]
    token = pl.BlockSpec((1, length, G, LANES), lambda s, j: (s, 0, 0, j))
    broad = pl.BlockSpec((1, length, G, chans), lambda s, j: (s, 0, 0, 0))
    rows = pl.BlockSpec((1, length * G, LANES), lambda s, j: (s, 0, j))
    per_state = pl.BlockSpec((1, states, G, LANES), lambda s, j: (s, 0, 0, j))
    total = pl.BlockSpec((1, states, LANES), lambda s, j: (s, 0, j))
    return pl.pallas_call(
        backward_kernel,
        grid=(seqs, chans // LANES),
        in_specs=[
            broad,
            broad,
            broad,
            broad,
            broad,
            broad,
            pl.BlockSpec((1, length * G, maps.shape[2]), lambda s, j: (s, 0, 0)),
            pl.BlockSpec((states, LANES), lambda s, j: (0, j)),
            per_state,
            per_state,
            pl.BlockSpec((1, 2, G, LANES), lambda s, j: (s, 0, 0, j)),
            pl.BlockSpec((packs.shape[0], 1, states, LANES), lambda s, j: (0, s, 0, j)),
            pl.BlockSpec((packs.shape[0], 1, states + 8, LANES), lambda s, j: (0, s, 0, j)),
            pl.BlockSpec((1, LANES), lambda s, j: (0, j)),
            pl.BlockSpec((weight.shape[0], LANES), lambda s, j: (0, j)),
        ],
        out_specs=[
            token,
            rows,
            rows,
            pl.BlockSpec((1, length * G, weight.shape[0] + 2 * states), lambda s, j: (s, 0, 0)),
            total,
            pl.BlockSpec((1, 8, LANES), lambda s, j: (s, 0, j)),
            total,
        ],
        out_shape=[
            jax.ShapeDtypeStruct(act.shape, F32),
            jax.ShapeDtypeStruct((seqs, length * G, chans), BF16),
            jax.ShapeDtypeStruct((seqs, length * G, chans), BF16),
            jax.ShapeDtypeStruct((seqs, length * G, weight.shape[0] + 2 * states), BF16),
            jax.ShapeDtypeStruct((seqs, states, chans), F32),
            jax.ShapeDtypeStruct((seqs, 8, chans), F32),
            jax.ShapeDtypeStruct((seqs, states, chans), F32),
        ],
        scratch_shapes=[
            pltpu.VMEM((length * G, states * LANES), F32),
            pltpu.VMEM((length * G, states * LANES), F32),
            pltpu.VMEM((states, G, LANES), F32),
            pltpu.VMEM((length + 1, states, G, LANES), F32),
            pltpu.VMEM((length * G, 2 * states * LANES), F32),
            pltpu.VMEM((2 * states * LANES, LANES), BF16),
            pltpu.VMEM((length * G, weight.shape[0]), F32),
        ],
        compiler_params=params("arbitrary", "arbitrary"),
        cost_estimate=estimate(39),
        name="scan_backward",
    )(act, step, delta, gate, y, grad, maps, decay, start, suffix, span, packs, forward_packs, skip, weight)


def adjoint_and_backward_kernel(
    act_ref, step_ref, delta_ref, gate_ref, y_ref, grad_ref, maps_ref, decay_ref, start_ref, span_ref,
    forward_packs_ref, skip_ref, weight_ref,
    gact_ref, gpre_ref, ggate_ref, proj_ref, gdecay_ref, gskip_ref, ginit_ref,
    b_ref, c_ref, rate_ref, h_ref, product_ref, select_ref, rank_ref, suffix_ref, give_ref, got_ref, *sems,
):
    length, states = act_ref.shape[1], decay_ref.shape[0]
    phase, s, j = pl.program_id(0), pl.program_id(1), pl.program_id(2)
    block = s * pl.num_programs(2) + j
    columns = pl.ds(pl.multiple_of(j * LANES, LANES), LANES)
    act_ref, step_ref, delta_ref, gate_ref, y_ref, grad_ref = (
        ref.at[:, :, :, columns] for ref in (act_ref, step_ref, delta_ref, gate_ref, y_ref, grad_ref)
    )
    c_ref = c_ref.at[s]
    exchange = SeqExchange(give_ref, got_ref, *sems)
    pl.when(phase + block == 0)(exchange.signal)
    spread_rate(decay_ref, rate_ref)
    zero = jnp.zeros((G, LANES), F32)

    @pl.when(phase == 0)
    def _():
        pl.when(j == 0)(lambda: spread_maps(maps_ref, states, states, c_ref))

        def one(k, carry):
            l = length - 1 - k
            st = step_ref[0, l]
            gate = gate_ref[0, l]
            gy = grad_ref[0, l] * (gate / (1.0 + jnp.exp(-gate)))
            return tuple(
                jnp.exp2(st * rate_ref[n]) * (carry[n] + gy * part(c_ref, l, n)) for n in range(states)
            )

        carry = lax.fori_loop(0, length, one, (zero,) * states, unroll=math.gcd(length, 8))
        own = span_ref[0, 1, 0:1, :] + span_ref[0, 0, 1:2, :] - span_ref[0, 0] - span_ref[0, 1]
        ends, _ = segment_prefix(list(carry), own, rate_ref, -1)
        for n in range(states):
            suffix_ref[block, n] = shifted(ends[n], -1, 0.0)
        give_ref[block] = jnp.concatenate([e[0:1, :] for e in ends], axis=0)
        pl.when(block == 0)(exchange.meet)
        exchange.start(block)

    pl.when(phase == 1)(lambda: gradients(
        exchange, block, j, columns,
        act_ref, step_ref, delta_ref, gate_ref, y_ref, grad_ref, maps_ref, decay_ref, start_ref, span_ref,
        forward_packs_ref, skip_ref, weight_ref,
        gact_ref, gpre_ref, ggate_ref, proj_ref, gdecay_ref, gskip_ref, ginit_ref,
        b_ref, c_ref, rate_ref, h_ref, product_ref, select_ref, rank_ref, suffix_ref, give_ref, got_ref,
    ))


def gradients(
    exchange, block, tile, columns,
    act_ref, step_ref, delta_ref, gate_ref, y_ref, grad_ref, maps_ref, decay_ref, start_ref, span_ref,
    forward_packs_ref, skip_ref, weight_ref,
    gact_ref, gpre_ref, ggate_ref, proj_ref, gdecay_ref, gskip_ref, ginit_ref,
    b_ref, c_ref, rate_ref, h_ref, product_ref, select_ref, rank_ref, suffix_ref, give_ref, got_ref,
):
    length, states = act_ref.shape[1], decay_ref.shape[0]
    wide = states * LANES

    @pl.when(tile == 0)
    def _():
        spread_maps(maps_ref, 0, states, b_ref)
        row = lax.broadcasted_iota(jnp.int32, select_ref.shape, 0) // LANES
        col = lax.broadcasted_iota(jnp.int32, select_ref.shape, 1)
        product_ref[...] = jnp.zeros_like(product_ref)
        rank_ref[...] = jnp.zeros_like(rank_ref)
        select_ref[...] = jnp.where(row == col, 1.0, 0.0).astype(BF16)

    exchange.wait(block)
    rate = jnp.exp(decay_ref[...]) * (-LOG2E)
    entry = jnp.zeros((states, LANES), F32)
    for d in reversed(range(got_ref.shape[0])):
        pack = jnp.where(exchange.me == d, give_ref[block], got_ref[d, block])
        joined = jnp.exp2(rate * forward_packs_ref[d, 0, states : states + 1, :]) * entry + pack
        entry = jnp.where(d > exchange.me, joined, entry)
    after = span_ref[0, 1]
    skip = jnp.broadcast_to(skip_ref[...], (G, LANES))

    def forward(l, h):
        st = step_ref[0, l]
        u = st * act_ref[0, l]
        for n in range(states):
            h_ref[l, n] = h[n]
        return tuple(
            jnp.exp2(st * rate_ref[n]) * h[n] + u * part(b_ref, l, n) for n in range(states)
        )

    h = lax.fori_loop(
        0, length, forward, tuple(start_ref[0, n] for n in range(states)), unroll=math.gcd(length, 4)
    )
    for n in range(states):
        h_ref[length, n] = h[n]

    def back(k, state):
        carry, gdecay, gskip = list(state[0]), list(state[1]), state[2]
        lines = [length - 1 - 2 * k, length - 2 - 2 * k]
        st, act, u, gy, q, r = [], [], [], [], [], []
        ggate = []
        for l in lines:
            st.append(step_ref[0, l])
            act.append(act_ref[0, l])
            u.append(st[-1] * act[-1])
            gate = gate_ref[0, l]
            grad = grad_ref[0, l]
            sig = 1.0 / (1.0 + jnp.exp(-gate))
            silu = gate * sig
            gy.append(grad * silu)
            ggate.append(grad * y_ref[0, l] * (sig + silu * (1.0 - sig)))
            gskip = gskip + gy[-1] * act[-1]
            q.append(jnp.zeros((G, LANES), F32))
            r.append(jnp.zeros((G, LANES), F32))
        row = pl.multiple_of((length - 2 - 2 * k) * G, 2 * G)
        for n in range(states):
            late, early = [], []
            for i, l in enumerate(lines):
                lam = part(c_ref, l, n) * gy[i] + carry[n]
                early.append(lam * u[i])
                late.append(gy[i] * h_ref[l + 1, n])
                q[i] = q[i] + lam * part(b_ref, l, n)
                carry[n] = jnp.exp2(st[i] * rate_ref[n]) * lam
                w = carry[n] * h_ref[l, n]
                r[i] = r[i] + rate_ref[n] * w
                gdecay[n] = gdecay[n] + st[i] * w
            product_ref[pl.ds(row, 2 * G), n * LANES : (n + 1) * LANES] += jnp.concatenate(early[::-1], axis=0)
            product_ref[pl.ds(row, 2 * G), wide + n * LANES : wide + (n + 1) * LANES] += jnp.concatenate(late[::-1], axis=0)
        gpre = []
        for i, l in enumerate(lines):
            gact_ref[0, l] = skip * gy[i] + st[i] * q[i]
            gstep = LN2 * r[i] + act[i] * q[i]
            gpre.append(gstep / (1.0 + jnp.exp(-delta_ref[0, l])))
        gpre_ref[0, pl.ds(row, 2 * G), :] = jnp.concatenate(gpre[::-1], axis=0).astype(BF16)
        ggate_ref[0, pl.ds(row, 2 * G), :] = jnp.concatenate(ggate[::-1], axis=0).astype(BF16)
        return tuple(carry), tuple(gdecay), gskip

    zero = jnp.zeros((G, LANES), F32)
    first = tuple(
        suffix_ref[block, n] + jnp.exp2(rate_ref[n] * after) * entry[n : n + 1, :] for n in range(states)
    )
    carry, gdecay, gskip = lax.fori_loop(
        0, length // 2, back, (first, (zero,) * states, zero), unroll=math.gcd(length // 2, 2)
    )
    for n in range(states):
        ginit_ref[0, n : n + 1, :] = carry[n][0:1, :]
        total = jnp.sum(gdecay[n] * rate_ref[n], axis=0, keepdims=True)
        gdecay_ref[0, n : n + 1, :] = total * LN2
    gskip_ref[0] = jnp.broadcast_to(jnp.sum(gskip, axis=0, keepdims=True), (8, LANES))

    rank_ref[...] += dot(gpre_ref[0], weight_ref[...], ((1,), (1,)))

    @pl.when(tile == pl.num_programs(2) - 1)
    def _():
        sums = jnp.dot(product_ref[...].astype(BF16), select_ref[...], preferred_element_type=F32)
        rank = rank_ref.shape[1]
        proj_ref[0, :, :rank] = rank_ref[...].astype(BF16)
        proj_ref[0, :, rank:] = sums[:, : 2 * states].astype(BF16)


def scan_adjoint_and_backward(act, step, delta, gate, y, grad, maps, decay, start, span, forward_packs, skip, weight):
    seqs, length, _, chans = act.shape
    start, span, forward_packs = (
        pltpu.with_memory_space_constraint(value, pltpu.HBM) for value in (start, span, forward_packs)
    )
    states = decay.shape[0]
    peers = lax.axis_size("seq")
    tiles = chans // LANES

    def late(shape, index):
        return pl.BlockSpec(shape, lambda p, s, j: index(p * s, p * j))

    broad = pl.BlockSpec((1, length, G, chans), lambda p, s, j: (s, 0, 0, 0))
    late_broad = late((1, length, G, chans), lambda s, j: (s, 0, 0, 0))
    rows = late((1, length * G, LANES), lambda s, j: (s, 0, j))
    total = late((1, states, LANES), lambda s, j: (s, 0, j))
    return pl.pallas_call(
        adjoint_and_backward_kernel,
        grid=(2, seqs, tiles),
        in_specs=[
            late_broad,
            broad,
            late_broad,
            broad,
            late_broad,
            broad,
            pl.BlockSpec((1, length * G, maps.shape[2]), lambda p, s, j: (s, 0, 0)),
            pl.BlockSpec((states, LANES), lambda p, s, j: (0, j)),
            late((1, states, G, LANES), lambda s, j: (s, 0, 0, j)),
            pl.BlockSpec((1, 2, G, LANES), lambda p, s, j: (s, 0, 0, j)),
            late((peers, 1, states + 8, LANES), lambda s, j: (0, s, 0, j)),
            late((1, LANES), lambda s, j: (0, j)),
            late((weight.shape[0], LANES), lambda s, j: (0, j)),
        ],
        out_specs=[
            late((1, length, G, LANES), lambda s, j: (s, 0, 0, j)),
            rows,
            rows,
            late((1, length * G, weight.shape[0] + 2 * states), lambda s, j: (s, 0, 0)),
            total,
            late((1, 8, LANES), lambda s, j: (s, 0, j)),
            total,
        ],
        out_shape=[
            jax.ShapeDtypeStruct(act.shape, F32),
            jax.ShapeDtypeStruct((seqs, length * G, chans), BF16),
            jax.ShapeDtypeStruct((seqs, length * G, chans), BF16),
            jax.ShapeDtypeStruct((seqs, length * G, weight.shape[0] + 2 * states), BF16),
            jax.ShapeDtypeStruct((seqs, states, chans), F32),
            jax.ShapeDtypeStruct((seqs, 8, chans), F32),
            jax.ShapeDtypeStruct((seqs, states, chans), F32),
        ],
        scratch_shapes=[
            pltpu.VMEM((length * G, states * LANES), F32),
            pltpu.VMEM((seqs, length * G, states * LANES), F32),
            pltpu.VMEM((states, G, LANES), F32),
            pltpu.VMEM((length + 1, states, G, LANES), F32),
            pltpu.VMEM((length * G, 2 * states * LANES), F32),
            pltpu.VMEM((2 * states * LANES, LANES), BF16),
            pltpu.VMEM((length * G, weight.shape[0]), F32),
            pltpu.VMEM((seqs * tiles, states, G, LANES), F32),
        ]
        + exchange_scratch(seqs * tiles, states),
        compiler_params=pltpu.CompilerParams(
            dimension_semantics=("arbitrary",) * 3, collective_id=9, has_side_effects=True,
            vmem_limit_bytes=VMEM_LIMIT,
        ),
        cost_estimate=estimate(39),
        name="scan_adjoint_and_backward",
    )(act, step, delta, gate, y, grad, maps, decay, start, span, forward_packs, skip, weight)


def remote(src, dst, send, recv, to):
    return pltpu.make_async_remote_copy(
        src_ref=src, dst_ref=dst, send_sem=send, recv_sem=recv, device_id={"chan": to}, device_id_type=MESH
    )


class Line:
    def __init__(self, count):
        self.me = lax.axis_index("chan")
        self.half = count // 2
        self.at = self.me // 2
        self.low = self.me % 2
        self.pair = self.at * 2 + 1 - self.low
        self.right = jnp.minimum(self.at + 1, self.half - 1) * 2 + self.low
        self.left = jnp.maximum(self.at - 1, 0) * 2 + self.low
        self.has_right = self.at < self.half - 1
        self.has_left = self.at > 0

    def greet(self):
        barrier = pltpu.get_barrier_semaphore()

        def signal(to):
            pl.semaphore_signal(barrier, inc=1, device_id={"chan": to}, device_id_type=MESH)

        signal(self.pair)
        pl.when(self.has_right)(lambda: signal(self.right))
        pl.when(self.has_left)(lambda: signal(self.left))
        pl.semaphore_wait(barrier, 1 + jnp.minimum(self.at, 1) + jnp.minimum(self.half - 1 - self.at, 1))


def gather_steps(line, out_ref, width, chunks, sems):
    pair_send, pair_recv, right_send, right_recv, left_send, left_recv = sems
    half = line.half
    rows = out_ref.shape[0] // chunks

    def place(owner, c):
        return out_ref.at[pl.ds(c * rows, rows), pl.ds(pl.multiple_of(owner * width, width), width)]

    def to_pair(owner, slot, c):
        return remote(place(owner, c), place(owner, c), pair_send.at[slot, c], pair_recv.at[slot, c], line.pair)

    def to_right(owner, j, c):
        return remote(place(owner, c), place(owner, c), right_send.at[j, c], right_recv.at[j, c], line.right)

    def to_left(owner, j, c):
        return remote(place(owner, c), place(owner, c), left_send.at[j, c], left_recv.at[j, c], line.left)

    def begin(c):
        pl.when(line.has_right)(lambda: to_right(line.me, 0, c).start())
        pl.when(line.has_left)(lambda: to_left(line.me, 0, c).start())
        to_pair(line.me, 0, c).start()

    def middle(fill=lambda: None):
        for j in range(1, half):
            for c in range(chunks):
                fill()
                @pl.when(line.at >= j)
                def _():
                    owner = line.me - 2 * j
                    to_right(owner, j - 1, c).wait_recv()
                    pl.when(line.has_right)(lambda: to_right(owner, j, c).start())
                    to_pair(owner, j, c).start()

                @pl.when(line.at + j < half)
                def _():
                    owner = line.me + 2 * j
                    to_left(owner, j - 1, c).wait_recv()
                    pl.when(line.has_left)(lambda: to_left(owner, j, c).start())
                    to_pair(owner, half + j, c).start()

    def end():
        for c in range(chunks):
            to_pair(line.me, 0, c).wait()
            pl.when(line.has_right)(lambda: to_right(line.me, 0, c).wait_send())
            pl.when(line.has_left)(lambda: to_left(line.me, 0, c).wait_send())
            for j in range(1, half):
                @pl.when(line.at >= j)
                def _():
                    owner = line.me - 2 * j
                    to_pair(owner, j, c).wait()
                    pl.when(line.has_right)(lambda: to_right(owner, j, c).wait_send())

                @pl.when(line.at + j < half)
                def _():
                    owner = line.me + 2 * j
                    to_pair(owner, half + j, c).wait()
                    pl.when(line.has_left)(lambda: to_left(owner, j, c).wait_send())

    return begin, middle, end


def gather_sems(count, chunks):
    half = count // 2
    return [pltpu.SemaphoreType.DMA((2 * half, chunks))] * 2 + [pltpu.SemaphoreType.DMA((half, chunks))] * 4


def estimate(us):
    return pl.CostEstimate(flops=int(us * 1e8), bytes_accessed=1 << 20, transcendentals=0)


def remote_params(ident):
    return pltpu.CompilerParams(collective_id=ident, has_side_effects=True, vmem_limit_bytes=VMEM_LIMIT)


def whole(count):
    return [pl.BlockSpec(memory_space=pltpu.VMEM)] * count


def chunks_of(rows):
    return next(c for c in (3, 2, 1) if rows % (16 * c) == 0)


def gather_kernel(count, chunks, layers, part_ref, gain_ref, weights_ref, out_ref, *rest):
    flats, rest = rest[:layers], rest[layers:]
    fetched, flat_buf, fetch_sem, store_sem, *sems = rest
    line = Line(count)
    rows, width = part_ref.shape
    mine = pl.ds(pl.multiple_of(line.me * width, width), width)
    height = fetched.shape[1]
    steps = weights_ref.shape[1] // height
    total = layers * steps

    def fetch(i):
        here = weights_ref.at[i // steps, pl.ds(i % steps * height, height)]
        return pltpu.make_async_copy(here, fetched.at[i % 2], fetch_sem.at[i % 2])

    def store(i):
        here = flats[i // steps].at[pl.ds(i % steps * height, height)]
        return pltpu.make_async_copy(flat_buf.at[i % 2], here, store_sem.at[i % 2])

    fetch(0).start()
    fetch(1).start()
    out_ref[:rows, mine] = part_ref[...]
    gain = gain_ref[...]
    terms = []
    for _ in range(3):
        term = gain.astype(BF16).astype(F32)
        terms.append(term)
        gain = gain - term
    terms.append(jnp.zeros((16 - 3 * layers, width), F32))
    out_ref[rows:, mine] = jnp.concatenate(terms, axis=0).astype(BF16)
    line.greet()
    begin, middle, end = gather_steps(line, out_ref, width, chunks, sems)
    for c in range(chunks):
        begin(c)
    done = []

    def flatten():
        i = len(done)
        if i == total:
            return
        done.append(i)
        fetch(i).wait()
        if i >= steps + 2:
            store(i - 2).wait()

        def piece(r, carry):
            here = pl.ds(pl.multiple_of(r * 32, 32), 32)
            value = fetched[i % 2, here].astype(F32)
            value = value.reshape(32, 2 * value.shape[2]).astype(BF16)
            if i < steps:
                flats[0][pl.ds(pl.multiple_of(i * height + r * 32, 32), 32), :] = value
            else:
                flat_buf[i % 2, here, :] = value
            return carry

        lax.fori_loop(0, height // 32, piece, 0)
        if i >= steps:
            store(i).start()
        if i + 2 < total:
            fetch(i + 2).start()

    def fill():
        flatten()
        flatten()

    middle(fill)
    while len(done) < total:
        flatten()
    end()
    for i in range(max(total - 2, steps), total):
        store(i).wait()


def gather_first(part, gain, weights):
    count = lax.axis_size("chan")
    rows, width = part.shape
    layers, model = weights.shape[:2]
    chunks = chunks_of(rows + 16)
    height = 256
    flat = (model, 2 * weights.shape[3])
    full, *flats = pl.pallas_call(
        functools.partial(gather_kernel, count, chunks, layers),
        in_specs=whole(2) + [pl.BlockSpec(memory_space=pl.ANY)],
        out_specs=whole(2) + [pl.BlockSpec(memory_space=pl.ANY)] * (layers - 1),
        out_shape=[jax.ShapeDtypeStruct((rows + 16, count * width), BF16)] + [jax.ShapeDtypeStruct(flat, BF16)] * layers,
        scratch_shapes=[
            pltpu.VMEM((2, height) + weights.shape[2:], BF16),
            pltpu.VMEM((2, height, flat[1]), BF16),
            pltpu.SemaphoreType.DMA((2,)),
            pltpu.SemaphoreType.DMA((2,)),
        ]
        + gather_sems(count, chunks),
        compiler_params=remote_params(0),
        cost_estimate=estimate(25),
        name="gather_first",
    )(part, gain, weights)
    terms = full[rows : rows + 3 * layers].astype(F32)
    return full, terms[:layers] + terms[layers : 2 * layers] + terms[2 * layers :], flats


def scatter_steps(line, part_ref, pair_buf, right_buf, left_buf, stage, width, chunks, sems):
    pair_send, pair_recv, right_send, right_recv, left_send, left_recv = sems
    half = line.half
    rows = part_ref.shape[0] // chunks

    def block(owner, c):
        return part_ref.at[pl.ds(c * rows, rows), pl.ds(pl.multiple_of(owner * width, width), width)]

    def piece(ref, slot, c):
        return ref.at[slot, pl.ds(c * rows, rows)]

    def to_pair(at, c):
        return remote(block(at * 2 + 1 - line.low, c), pair_buf.at[at, pl.ds(c * rows, rows)], pair_send.at[at, c], pair_recv.at[at, c], line.pair)

    def to_right(j, c):
        return remote(piece(stage, j, c), piece(right_buf, j - 1, c), right_send.at[j - 1, c], right_recv.at[j - 1, c], line.right)

    def to_left(j, c):
        return remote(piece(stage, half + j, c), piece(left_buf, j - 1, c), left_send.at[j - 1, c], left_recv.at[j - 1, c], line.left)

    def begin(produce):
        for c in range(chunks):

            def send(at):
                if c == 0:
                    produce(at * 2 + 1 - line.low)
                to_pair(at, c).start()

            for j in range(half - 1, 0, -1):
                pl.when(line.at + j < half)(lambda: send(line.at + j))
                pl.when(line.at >= j)(lambda: send(line.at - j))
            send(line.at)
        for at in range(half):
            produce(at * 2 + line.low)

    def own_and_pair(at, c):
        to_pair(at, c).wait_recv()
        return block(at * 2 + line.low, c)[...].astype(F32) + pair_buf[at, pl.ds(c * rows, rows)].astype(F32)

    def middle(c):
        for j in range(half - 1, 0, -1):
            @pl.when(line.at + j < half)
            def _():
                stage[j, pl.ds(c * rows, rows)] = own_and_pair(line.at + j, c).astype(BF16)

                @pl.when(line.has_left)
                def _():
                    arrived = remote(piece(stage, j, c), piece(right_buf, j, c), right_send.at[j, c], right_recv.at[j, c], line.right)
                    arrived.wait_recv()
                    total = stage[j, pl.ds(c * rows, rows)].astype(F32) + right_buf[j, pl.ds(c * rows, rows)].astype(F32)
                    stage[j, pl.ds(c * rows, rows)] = total.astype(BF16)

                to_right(j, c).start()

            @pl.when(line.at >= j)
            def _():
                stage[half + j, pl.ds(c * rows, rows)] = own_and_pair(line.at - j, c).astype(BF16)

                @pl.when(line.has_right)
                def _():
                    arrived = remote(piece(stage, half + j, c), piece(left_buf, j, c), left_send.at[j, c], left_recv.at[j, c], line.left)
                    arrived.wait_recv()
                    total = stage[half + j, pl.ds(c * rows, rows)].astype(F32) + left_buf[j, pl.ds(c * rows, rows)].astype(F32)
                    stage[half + j, pl.ds(c * rows, rows)] = total.astype(BF16)

                to_left(j, c).start()

    def finish(c, out_ref):
        here = pl.ds(c * rows, rows)
        out_ref[here, :] = own_and_pair(line.at, c)

        @pl.when(line.has_left)
        def _():
            remote(piece(stage, 0, c), piece(right_buf, 0, c), right_send.at[0, c], right_recv.at[0, c], line.right).wait_recv()
            out_ref[here, :] += right_buf[0, here].astype(F32)

        @pl.when(line.has_right)
        def _():
            remote(piece(stage, 0, c), piece(left_buf, 0, c), left_send.at[0, c], left_recv.at[0, c], line.left).wait_recv()
            out_ref[here, :] += left_buf[0, here].astype(F32)

    def end():
        for c in range(chunks):
            for at in range(half):
                to_pair(at, c).wait_send()
            for j in range(1, half):
                pl.when(line.at + j < half)(lambda: to_right(j, c).wait_send())
                pl.when(line.at >= j)(lambda: to_left(j, c).wait_send())

    return begin, middle, finish, end


def scatter_scratch(count, chunks, rows, width):
    half = count // 2
    return (
        [pltpu.VMEM((half, rows, width), BF16)] * 3
        + [pltpu.VMEM((2 * half, rows, width), BF16)]
        + [pltpu.SemaphoreType.DMA((half, chunks))] * 6
    )


def boundary_kernel(
    count, chunks, layer, gated_ref, weights_ref, hidden_ref, new_ref, full_ref, pair_buf, right_buf, left_buf, stage,
    part_ref, weight_ref, weight_sem, *sems,
):
    line = Line(count)
    rows, width = hidden_ref.shape
    mine = pl.ds(pl.multiple_of(line.me * width, width), width)
    fetch = pltpu.make_async_copy(weights_ref.at[layer], weight_ref, weight_sem)
    fetch.start()
    line.greet()
    fetch.wait()

    def produce(owner):
        columns = pl.ds(pl.multiple_of(owner * width, width), width)
        block = jnp.dot(gated_ref[...], weight_ref[:, columns], preferred_element_type=F32)
        part_ref[:, columns] = block.astype(BF16)

    begin, middle, finish, end = scatter_steps(
        line, part_ref, pair_buf, right_buf, left_buf, stage, width, chunks, sems[:6]
    )
    gather_begin, gather_middle, gather_end = gather_steps(line, full_ref, width, chunks, sems[6:])
    begin(produce)
    for c in range(chunks):
        here = pl.ds(c * (rows // chunks), rows // chunks)
        middle(c)
        finish(c, new_ref)
        new_ref[here, :] += hidden_ref[here, :]
        full_ref[here, mine] = new_ref[here, :].astype(BF16)
        gather_begin(c)
    gather_middle()
    gather_end()
    end()


def forward_boundary(gated, weights, layer, hidden):
    count = lax.axis_size("chan")
    rows, width = hidden.shape
    chunks = 2
    return pl.pallas_call(
        functools.partial(boundary_kernel, count, chunks, layer),
        in_specs=[whole(1)[0], pl.BlockSpec(memory_space=pl.ANY), whole(1)[0]],
        out_specs=whole(2),
        out_shape=[jax.ShapeDtypeStruct((rows, width), F32), jax.ShapeDtypeStruct((rows, count * width), BF16)],
        scratch_shapes=scatter_scratch(count, chunks, rows, width)[:4]
        + [
            pltpu.VMEM((rows, count * width), BF16),
            pltpu.VMEM(weights.shape[1:], BF16),
            pltpu.SemaphoreType.DMA,
        ]
        + scatter_scratch(count, chunks, rows, width)[4:]
        + gather_sems(count, chunks),
        compiler_params=remote_params(1),
        cost_estimate=estimate(50),
        name="forward_boundary",
    )(gated, weights, hidden)


def back_kernel(
    count, chunks, gathers, gmixed_ref, weights_ref, grad_ref, hidden_ref, inverse_ref, gain_ref, inner_ref, new_ref, ggain_ref, *more
):
    full_ref, more = (more[0], more[1:]) if gathers else (None, more)
    pair_buf, right_buf, left_buf, stage, inner_buf, column_ref, inner_send, inner_recv = more[:8]
    part_ref, weight_ref, weight_sem = more[8:11]
    sems = more[11:]
    fetch = pltpu.make_async_copy(weights_ref, weight_ref, weight_sem)
    fetch.start()
    line = Line(count)
    rows, width = grad_ref.shape
    model = width * count
    mine = pl.ds(pl.multiple_of(line.me * width, width), width)
    others = [lax.rem(line.me + k, count) for k in range(1, count)]
    barrier = pltpu.get_barrier_semaphore()
    for other in others:
        pl.semaphore_signal(barrier, inc=1, device_id={"chan": other}, device_id_type=MESH)
    pl.semaphore_wait(barrier, count - 1)
    begin, middle, finish, end = scatter_steps(
        line, part_ref, pair_buf, right_buf, left_buf, stage, width, chunks, sems[:6]
    )
    if gathers:
        gather_begin, gather_middle, gather_end = gather_steps(line, full_ref, width, chunks, sems[6:])
    sums = [
        remote(inner_ref, inner_buf.at[k], inner_send.at[k], inner_recv.at[k], others[k]) for k in range(count - 1)
    ]
    for copy in sums:
        copy.start()
    fetch.wait()

    def produce(owner):
        features = pl.ds(pl.multiple_of(owner * width, width), width)
        part_ref[:, features] = dot(gmixed_ref[...], weight_ref[features, :], ((1,), (1,))).astype(BF16)

    begin(produce)
    eye = lax.broadcasted_iota(jnp.int32, (LANES, LANES), 0) == lax.broadcasted_iota(jnp.int32, (LANES, LANES), 1)
    ggain_ref[...] = jnp.zeros_like(ggain_ref)
    for c in range(chunks):
        here = pl.ds(c * (rows // chunks), rows // chunks)
        middle(c)
        if c == 0:
            inner = inner_ref[...]
            for k in range(count - 1):
                sums[k].wait_recv()
                inner = inner + inner_buf[k]
            for b in range(rows // LANES):
                column_ref[pl.ds(b * LANES, LANES), :] = jnp.sum(
                    jnp.where(eye, jnp.broadcast_to(inner[b : b + 1, :], (LANES, LANES)), 0.0), axis=1, keepdims=True
                )
        finish(c, new_ref)
        gnormed = new_ref[here, :]
        inverse = inverse_ref[here, :]
        hidden = hidden_ref[here, :]
        factor = inverse * inverse * column_ref[here, :] * (1.0 / model)
        ggain_ref[0:1, :] += jnp.sum(gnormed * hidden * inverse, axis=0, keepdims=True)
        new = grad_ref[here, :] + inverse * (gain_ref[...] * gnormed) - hidden * factor
        new_ref[here, :] = new
        if gathers:
            full_ref[here, mine] = new.astype(BF16)
            gather_begin(c)
    if gathers:
        gather_middle()
        gather_end()
    end()
    for copy in sums:
        copy.wait_send()


def backward_boundary(gmixed, weights, grad, hidden, inverse, gain, inner, gathers):
    count = lax.axis_size("chan")
    rows, width = hidden.shape
    chunks = 2
    out_shape = [jax.ShapeDtypeStruct((rows, width), F32), jax.ShapeDtypeStruct((8, width), F32)]
    scratch = scatter_scratch(count, chunks, rows, width)
    scratch += [
        pltpu.VMEM((count - 1, rows // LANES, LANES), F32),
        pltpu.VMEM((rows, 1), F32),
        pltpu.SemaphoreType.DMA((count - 1,)),
        pltpu.SemaphoreType.DMA((count - 1,)),
    ]
    product = [
        pltpu.VMEM((rows, count * width), BF16),
        pltpu.VMEM(weights.shape, BF16),
        pltpu.SemaphoreType.DMA,
    ]
    order = scratch[:4] + scratch[10:] + product + scratch[4:10]
    if gathers:
        out_shape.append(jax.ShapeDtypeStruct((rows, count * width), BF16))
        order += gather_sems(count, chunks)
    return pl.pallas_call(
        functools.partial(back_kernel, count, chunks, gathers),
        in_specs=[whole(1)[0], pl.BlockSpec(memory_space=pl.ANY)] + whole(5),
        out_specs=whole(len(out_shape)),
        out_shape=out_shape,
        scratch_shapes=order,
        compiler_params=remote_params(2 if gathers else 3),
        cost_estimate=estimate(50 if gathers else 27),
        name="backward_boundary" if gathers else "backward_last",
    )(gmixed, weights, grad, hidden, inverse, gain, inner.reshape(rows // LANES, LANES))


def sum_kernel(count, part_ref, out_ref, give, arrived, total_ref, result, send1, recv1, send2, recv2):
    me = lax.axis_index("chan")
    rows, width = part_ref.shape
    own, extra = rows // count, width - LANES
    sides = LANES // extra
    block = rows // sides
    more = block // count
    others = [lax.rem(me + k, count) for k in range(1, count)]
    barrier = pltpu.get_barrier_semaphore()
    for other in others:
        pl.semaphore_signal(barrier, inc=1, device_id={"chan": other}, device_id_type=MESH)

    def place_at(k):
        row = lax.broadcasted_iota(jnp.int32, (extra, LANES), 0)
        col = lax.broadcasted_iota(jnp.int32, (extra, LANES), 1)
        return jnp.where(col == row + k * extra, 1.0, 0.0).astype(BF16)

    side = jnp.zeros((block, LANES), F32)
    for k in range(sides):
        side = side + jnp.dot(part_ref[k * block : (k + 1) * block, LANES:], place_at(k), preferred_element_type=F32)
    side = side.astype(BF16)
    for o in range(count):
        give[o, :own, :] = part_ref[o * own : (o + 1) * own, :LANES]
        give[o, own:, :] = side[o * more : (o + 1) * more, :]
    pl.semaphore_wait(barrier, count - 1)
    first, second = [], []
    for k, other in enumerate(others):
        first.append(remote(give.at[other], arrived.at[k], send1.at[k], recv1.at[k], other))
        first[k].start()
    acc = give[me].astype(F32)
    for k in range(count - 1):
        first[k].wait_recv()
        acc = acc + arrived[k].astype(F32)
    total_ref[...] = acc.astype(BF16)
    for k, other in enumerate(others):
        second.append(remote(total_ref, result.at[me], send2.at[k], recv2.at[k], other))
        second[k].start()
    result[me] = total_ref[...]
    for copy in second:
        copy.wait()
    sums = [result[o] for o in range(count)]
    for o in range(count):
        out_ref[o * own : (o + 1) * own, :LANES] = sums[o][:own, :]
    side = jnp.concatenate([value[own:, :].astype(F32) for value in sums], axis=0).astype(BF16)
    for k in range(sides):
        columns = dot(side, place_at(k), ((1,), (1,)))
        out_ref[k * block : (k + 1) * block, LANES:] = columns.astype(BF16)
    for copy in first:
        copy.wait_send()


def sum_chan(part):
    count = lax.axis_size("chan")
    rows, width = part.shape
    piece = rows // count + rows // (LANES // (width - LANES)) // count
    return pl.pallas_call(
        functools.partial(sum_kernel, count),
        in_specs=whole(1),
        out_specs=whole(1)[0],
        out_shape=jax.ShapeDtypeStruct((rows, width), BF16),
        scratch_shapes=[
            pltpu.VMEM((count, piece, LANES), BF16),
            pltpu.VMEM((count - 1, piece, LANES), BF16),
            pltpu.VMEM((piece, LANES), BF16),
            pltpu.VMEM((count, piece, LANES), BF16),
        ]
        + [pltpu.SemaphoreType.DMA((count - 1,))] * 4,
        compiler_params=remote_params(4),
        cost_estimate=estimate(14),
        name="sum_chan",
    )(part)


def exchanged(value, bit):
    return lax.ppermute(value, "seq", [(i, i ^ bit) for i in range(lax.axis_size("seq"))])


class Summed:
    def __init__(self, value, halves):
        self.halves = halves
        self.bit = 1
        self.keep = value
        give = value
        if halves:
            half = value.shape[0] // 2
            core = lax.axis_index("seq") % 2
            self.keep = lax.dynamic_slice_in_dim(value, core * half, half, 0)
            give = lax.dynamic_slice_in_dim(value, (1 - core) * half, half, 0)
        self.wire = exchanged(give, 1)

    def step(self):
        total = self.keep.astype(F32) + self.wire.astype(F32)
        self.bit *= 2
        if self.bit < lax.axis_size("seq"):
            self.keep = total.astype(BF16)
            self.wire = exchanged(self.keep, self.bit)
        elif self.halves:
            self.keep = total.astype(BF16)
            self.wire = exchanged(self.keep, 1)
        else:
            self.keep = total

    def across(self):
        while self.bit * 2 < lax.axis_size("seq"):
            self.step()

    def last(self):
        while self.bit * 2 < lax.axis_size("seq"):
            self.step()
        return self.keep, self.wire

    def total(self):
        while self.bit < lax.axis_size("seq"):
            self.step()
        return (self.keep, self.wire) if self.halves else self.keep


def after(value, *sums):
    value, wires = lax.optimization_barrier((value, [one.wire for one in sums]))
    for one, wire in zip(sums, wires):
        one.wire = wire
    return value


def place_pairs_kernel(core_ref, *refs):
    *ins, out_ref = refs[-5:]
    own = pl.program_id(0) == 0
    for j in range(2):
        out_ref[0, :, j, :] = jnp.where(own, ins[2 * j][...].astype(F32), ins[2 * j + 1][...].astype(F32))


def place_rows_kernel(core_ref, *refs):
    mine, other, out_ref = refs[-3:]
    own = pl.program_id(0) == 0
    out_ref[0] = jnp.where(own, mine[...].astype(F32), other[...].astype(F32))


def place(kernel, parts, base, layer, layers, block, middle):
    half, width = parts[0].shape
    core = (lax.axis_index("seq") % 2).reshape(1)
    steps = half // block

    def where(kept):
        if kept:
            return lambda k, b, core: (jnp.where(k == 0, b, steps - 1), 0)
        return lambda k, b, core: (jnp.where(k == 1, b, 0), 0)

    def out(k, b, core):
        return (layer, (core[0] + k - 2 * core[0] * k) * steps + b) + (0,) * (1 + len(middle))

    ins = [pl.BlockSpec((block, width), where(p % 2 == 0)) for p in range(len(parts))]
    shape = (layers, 2 * half) + middle + (width,)
    args = list(parts)
    aliases = {}
    if base is not None:
        ins.insert(0, pl.BlockSpec(memory_space=pl.ANY))
        args.insert(0, base)
        aliases = {1: 0}
    return pl.pallas_call(
        kernel,
        grid_spec=pltpu.PrefetchScalarGridSpec(
            num_scalar_prefetch=1,
            grid=(2, steps),
            in_specs=ins,
            out_specs=pl.BlockSpec((1, block) + middle + (width,), out),
        ),
        out_shape=jax.ShapeDtypeStruct(shape, F32),
        input_output_aliases=aliases,
        compiler_params=params("arbitrary", "arbitrary"),
        cost_estimate=estimate(5),
        name="place",
    )(core, *args)


def dot(a, b, dims):
    return lax.dot_general(a, b, (dims, ((), ())), preferred_element_type=F32)


def rows_of_packed(rank_columns, rank, states, seqs, taps):
    names = [("xproj", rank_columns), ("dtproj", rank), ("decay", states), ("init", seqs * states)]
    names += [("taps", taps), ("shift", 1), ("bias", 1), ("skip", 1), ("conv", (taps - 1) * seqs)]
    places, row = {}, 0
    for name, size in names:
        places[name] = (row, row + size)
        row += size
    return places, row + (-row) % 16


def mid_kernel(
    gproj_ref, xproj_ref, gact_ref, inner_ref, head_ref, low_ref, taps_ref, shift_ref, rank_ref, gpre_ref, ggate_ref,
    gdecay_ref, gskip_ref, ginit_ref,
    gmixed_ref, packed_ref,
    dotted_ref, pad_ref, gconv_ref, tail_ref, give_ref, got_ref, send_sem, recv_sem,
):
    seqs, length = gact_ref.shape[:2]
    tokens = length * G
    count = gmixed_ref.shape[1] // (2 * LANES)
    taps = taps_ref.shape[0]
    over = taps - 1
    j = pl.program_id(0)
    place, peers = lax.axis_index("seq"), lax.axis_size("seq")
    states = gdecay_ref.shape[1]
    places, _ = rows_of_packed(gproj_ref.shape[1], rank_ref.shape[1], states, seqs, taps)

    def to_previous(t):
        return pltpu.make_async_remote_copy(
            src_ref=give_ref.at[t], dst_ref=got_ref.at[t], send_sem=send_sem.at[t], recv_sem=recv_sem.at[t],
            device_id={"seq": jnp.maximum(place - 1, 0)}, device_id_type=MESH,
        )

    @pl.when(j == 0)
    def _():
        barrier = pltpu.get_barrier_semaphore()

        @pl.when(place < peers - 1)
        def _():
            pl.semaphore_signal(barrier, inc=1, device_id={"seq": place + 1}, device_id_type=MESH)

        pl.when(place > 0)(lambda: pl.semaphore_wait(barrier, 1))

    columns = pl.ds(pl.multiple_of(j * LANES, LANES), LANES)
    gate_columns = pl.ds(pl.multiple_of((count + j) * LANES, LANES), LANES)
    gmixed_ref[:, gate_columns] = ggate_ref[...]
    dotted_ref[...] = jnp.dot(gproj_ref[...], xproj_ref[...], preferred_element_type=F32)
    zero = jnp.zeros((G, LANES), F32)
    weights = [jnp.broadcast_to(taps_ref[k : k + 1, :], (G, LANES)) for k in range(taps)]
    shift = jnp.broadcast_to(shift_ref[...], (G, LANES))
    sums = (zero,) * (taps + 1)
    early = [[None] * seqs for _ in range(over)]
    for s in range(seqs):
        for k in range(over):
            pad_ref[k] = head_ref[s, k]

        def fill(l, carry):
            pad_ref[l + over] = inner_ref[s, l]
            return carry

        lax.fori_loop(0, length, fill, 0, unroll=math.gcd(length, 8))

        def one(l, sums):
            parts = [pad_ref[l + k] for k in range(taps)]
            pre = shift
            for k in range(taps):
                pre = pre + weights[k] * parts[k]
            sig = 1.0 / (1.0 + jnp.exp(-pre))
            here = dotted_ref[pl.ds(pl.multiple_of(s * tokens + l * G, G), G), :]
            gconv = (gact_ref[s, l] + here) * (sig + pre * sig * (1.0 - sig))
            gconv_ref[l] = gconv
            return tuple(sums[k] + gconv * parts[k] for k in range(taps)) + (sums[taps] + gconv,)

        sums = lax.fori_loop(0, length, one, sums, unroll=math.gcd(length, 8))
        for k in range(over):
            gconv_ref[length + k] = shifted(gconv_ref[k], -1, 0.0)
            total = weights[0] * gconv_ref[k]
            for i in range(1, k + 1):
                total = total + weights[i] * gconv_ref[k - i]
            early[k][s] = total[0:1, :]
            give_ref[j, s, k : k + 1, :] = total[0:1, :]

        def inner_of(l):
            total = weights[0] * gconv_ref[l + over]
            for k in range(1, taps):
                total = total + weights[k] * gconv_ref[l + over - k]
            return total

        def pair(p, carry):
            both = jnp.concatenate([inner_of(2 * p), inner_of(2 * p + 1)], axis=0)
            gmixed_ref[pl.ds(pl.multiple_of(s * tokens + 2 * p * G, 2 * G), 2 * G), columns] = both.astype(BF16)
            return carry

        lax.fori_loop(0, length // 2 - 2, pair, 0, unroll=math.gcd(length // 2 - 2, 4))
        for q in range(4):
            tail_ref[j, s, q] = inner_of(length - 4 + q)
    pl.when(place > 0)(lambda: to_previous(j).start())

    def put(name, value):
        first, last = places[name]
        packed_ref[first:last, :] = value.astype(BF16)

    put("xproj", dot(gproj_ref[...], low_ref[...], ((0,), (0,))))
    put("dtproj", dot(rank_ref[...], gpre_ref[...], ((0,), (0,))))
    bias = jnp.dot(jnp.ones((16, seqs * tokens), BF16), gpre_ref[...], preferred_element_type=F32)[0:1, :]
    decay, skip = gdecay_ref[0], gskip_ref[0, 0:1, :]
    for s in range(1, seqs):
        decay = decay + gdecay_ref[s]
        skip = skip + gskip_ref[s, 0:1, :]
    put("decay", decay)
    first = place == 0
    for s in range(seqs):
        row = places["init"][0] + s * states
        packed_ref[row : row + states, :] = jnp.where(first, ginit_ref[s], 0.0).astype(BF16)
    rest = [jnp.sum(value, axis=0, keepdims=True) for value in sums]
    rest += [bias, skip]
    rest += [jnp.where(first, early[k][s], 0.0) for k in range(over) for s in range(seqs)]
    row = places["taps"][0]
    rest += [jnp.zeros((1, LANES), F32)] * (packed_ref.shape[0] - row - len(rest))
    packed_ref[row:, :] = jnp.concatenate(rest, axis=0).astype(BF16)

    @pl.when(j == count - 1)
    def _():
        last_row = lax.broadcasted_iota(jnp.int32, (G, LANES), 0) == G - 1
        inside = place < peers - 1
        for t in range(count):
            pl.when(place < peers - 1)(lambda: to_previous(t).wait_recv())
            for s in range(seqs):
                values = []
                for q in range(4):
                    value = tail_ref[t, s, q]
                    k = q - 4 + over
                    if k >= 0:
                        given = jnp.broadcast_to(got_ref[t, s, k : k + 1, :], (G, LANES))
                        value = value + jnp.where(jnp.logical_and(last_row, inside), given, 0.0)
                    values.append(value)
                for q in (0, 2):
                    row = s * tokens + (length - 4 + q) * G
                    both = jnp.concatenate(values[q : q + 2], axis=0)
                    gmixed_ref[row : row + 2 * G, t * LANES : (t + 1) * LANES] = both.astype(BF16)
            pl.when(place > 0)(lambda: to_previous(t).wait_send())


def mid_backward(
    gproj, xproj, gact, mixed, head, low, taps, shift, rank_part, gpre, ggate, gdecay, gskip, ginit
):
    seqs, length, _, chans = gact.shape
    rows = seqs * length * G
    count = chans // LANES
    states = gdecay.shape[1]
    over = taps.shape[0] - 1
    _, packed_rows = rows_of_packed(gproj.shape[1], rank_part.shape[1], states, seqs, taps.shape[0])
    token = pl.BlockSpec((seqs, length, G, LANES), lambda j: (0, 0, 0, j))
    row = pl.BlockSpec((rows, LANES), lambda j: (0, j))

    def column(height):
        return pl.BlockSpec((height, LANES), lambda j: (0, j))

    def stack(height):
        return pl.BlockSpec((seqs, height, LANES), lambda j: (0, 0, j))

    return pl.pallas_call(
        mid_kernel,
        grid=(count,),
        in_specs=[
            pl.BlockSpec(gproj.shape, lambda j: (0, 0)),
            column(xproj.shape[0]),
            token,
            token,
            pl.BlockSpec((seqs, over, G, LANES), lambda j: (0, 0, 0, j)),
            row,
            column(over + 1),
            column(1),
            pl.BlockSpec(rank_part.shape, lambda j: (0, 0)),
            row,
            row,
            stack(states),
            stack(8),
            stack(states),
        ],
        out_specs=[pl.BlockSpec((rows, 2 * chans), lambda j: (0, 0)), column(packed_rows)],
        out_shape=[
            jax.ShapeDtypeStruct((rows, 2 * chans), BF16),
            jax.ShapeDtypeStruct((packed_rows, chans), BF16),
        ],
        scratch_shapes=[
            pltpu.VMEM((rows, LANES), F32),
            pltpu.VMEM((length + over, G, LANES), F32),
            pltpu.VMEM((length + over, G, LANES), F32),
            pltpu.VMEM((count, seqs, 4, G, LANES), F32),
            pltpu.VMEM((count, seqs, 8, LANES), F32),
            pltpu.VMEM((count, seqs, 8, LANES), F32),
            pltpu.SemaphoreType.DMA((count,)),
            pltpu.SemaphoreType.DMA((count,)),
        ],
        compiler_params=pltpu.CompilerParams(
            dimension_semantics=("arbitrary",), collective_id=5, has_side_effects=True, vmem_limit_bytes=VMEM_LIMIT
        ),
        cost_estimate=estimate(8),
        name="mid_backward",
    )(gproj, xproj, gact, mixed, head, low, taps, shift, rank_part, gpre, ggate, gdecay, gskip, ginit)


def unpack_kernel(layers, places, seqs, *refs):
    smalls, gains, outs = refs[: 2 * layers], refs[2 * layers : 4 * layers], refs[4 * layers :]
    gain, taps, shift, xproj, dtproj, bias, decay, skip, conv, init = outs
    for i in range(layers):
        def rows(name):
            first, last = places[name]
            return smalls[2 * i][first:last, :].astype(F32) + smalls[2 * i + 1][first:last, :].astype(F32)

        gain[i : i + 1, :] = gains[2 * i][0:1, :].astype(F32) + gains[2 * i + 1][0:1, :].astype(F32)
        xproj[i], dtproj[i], decay[i] = rows("xproj"), rows("dtproj"), rows("decay")
        init[i] = rows("init")
        low, high = places["taps"][0], smalls[0].shape[0]
        rest = smalls[2 * i][low:high, :].astype(F32) + smalls[2 * i + 1][low:high, :].astype(F32)

        def of(name):
            first, last = places[name]
            return rest[first - low : last - low, :]

        taps[i] = of("taps")
        shift[i : i + 1, :], bias[i : i + 1, :], skip[i : i + 1, :] = of("shift"), of("bias"), of("skip")
        for k in range(conv.shape[1]):
            conv[i, k] = of("conv")[k * seqs : (k + 1) * seqs, :]


def unpack(smalls, gains, places, seqs, width):
    layers = len(smalls)
    chans = smalls[0][0].shape[1]

    def size(name):
        return places[name][1] - places[name][0]

    shapes = [
        (layers, width), (layers, size("taps"), chans), (layers, chans), (layers, size("xproj"), chans),
        (layers, size("dtproj"), chans), (layers, chans), (layers, size("decay"), chans), (layers, chans),
        (layers, size("conv") // seqs, seqs, chans), (layers, size("init"), chans),
    ]
    args = [value for pair in smalls for value in pair] + [value for pair in gains for value in pair]
    return pl.pallas_call(
        functools.partial(unpack_kernel, layers, places, seqs),
        in_specs=whole(len(args)),
        out_specs=whole(len(shapes)),
        out_shape=[jax.ShapeDtypeStruct(shape, F32) for shape in shapes],
        compiler_params=params(),
        cost_estimate=estimate(3),
        name="unpack",
    )(*args)


def passed_along(value, axis, by):
    peers = lax.axis_size(axis)
    pairs = [(i, i + by) for i in range(peers) if 0 <= i + by < peers]
    return lax.ppermute(value, axis, pairs)


def to_segments(value):
    seqs, tokens, width = value.shape
    return value.reshape(seqs, G, tokens // G, width).transpose(0, 2, 1, 3)


def from_segments(value):
    seqs, length, _, width = value.shape
    return value.transpose(0, 2, 1, 3).reshape(seqs, length * G, width)


def local(
    hidden_in,
    norm_gain,
    in_weight,
    conv_weight,
    conv_bias,
    xproj_weight,
    dtproj_weight,
    dt_bias,
    decay_log,
    skip_gain,
    out_weight,
    conv_state,
    scan_state,
    out_cotangent,
):
    layers = in_weight.shape[0]
    rank = dtproj_weight.shape[1]
    states = decay_log.shape[1]
    seqs, tokens, _ = hidden_in.shape
    length = tokens // G
    rows = seqs * tokens
    chans = in_weight.shape[3]
    model = hidden_in.shape[2] * lax.axis_size("chan")
    taps = conv_weight.shape[1]
    is_first = lax.axis_index("seq") == 0

    first = to_segments(hidden_in).reshape(rows, -1)
    hidden = first.astype(F32)
    full, gains, flats = gather_first(first, norm_gain, in_weight)
    grad = to_segments(out_cotangent).reshape(rows, -1)
    grad_rows = lax.all_gather(grad, "chan", axis=1, tiled=True)
    grad = grad.astype(F32)
    saved = []
    for i in range(layers):
        wide = full[:rows].astype(F32)
        inverse = lax.rsqrt(jnp.sum(wide * wide, axis=1, keepdims=True) / model + EPS)
        normed = (wide * inverse * gains[i]).astype(BF16)
        flat_in = flats[i]
        mixed = dot(normed, flat_in, ((1,), (0,)))
        inner = mixed[:, :chans].reshape(seqs, length, G, chans)
        gate = mixed[:, chans:].reshape(seqs, length, G, chans)
        tail = inner[:, length - taps + 1 :]
        received = passed_along(tail[:, :, G - 1], "seq", 1)
        before = jnp.where(is_first, conv_state[i], received)
        head = jnp.concatenate([before[:, :, None], tail[:, :, : G - 1]], axis=2)
        padded = jnp.concatenate([head, inner], axis=1)
        pre = conv_bias[i] + sum(conv_weight[i, k] * padded[:, k : k + length] for k in range(taps))
        act = jax.nn.silu(pre)
        act_low = act.astype(BF16).reshape(rows, chans)
        projected = sum_chan(dot(act_low, xproj_weight[i], ((1,), (0,))).astype(BF16))
        rank_part = projected[:, :rank]
        maps = projected[:, rank:].reshape(seqs, tokens, 2 * states)
        delta = dot(rank_part, dtproj_weight[i], ((1,), (0,))) + dt_bias[i]
        delta = delta.reshape(seqs, length, G, chans)
        step = jax.nn.softplus(delta)
        y, gated, start, span, packs = scan_forward(
            act, step, gate, maps, decay_log[i], scan_state[i], skip_gain[i : i + 1]
        )
        gated = gated.reshape(rows, chans)
        saved.append(
            (hidden, inverse, normed, flat_in, mixed, gate, head, act, act_low, rank_part, maps, delta, step,
             span, packs, y, gated, start)
        )
        if i + 1 < layers:
            hidden, full = forward_boundary(gated, out_weight, i, hidden)
        else:
            branch = dot(gated, out_weight[i], ((1,), (0,))).astype(BF16)
            branch_sum = lax.psum_scatter(branch, "chan", scatter_dimension=1, tiled=True)

    def finish(i, sums):
        nonlocal in_grads, out_grads
        in_grads = place(
            place_pairs_kernel, [*sums["inner"].total(), *sums["gate"].total()], in_grads, i, layers, model // 4, (2,)
        )
        out_grads = place(place_rows_kernel, list(sums["out"].total()), out_grads, i, layers, chans // 2, ())

    smalls = [None] * layers
    in_grads = out_grads = None
    before_sums = None
    for i in reversed(range(layers)):
        (hidden_i, inverse, normed, flat_in, mixed, gate, head, act, act_low, rank_part, maps, delta, step,
         span, packs, y, gated, start) = saved[i]
        sums = {}
        sums["out"] = Summed(dot(gated, grad_rows, ((0,), (0,))).astype(BF16), True)
        grad_gated = dot(grad_rows, out_weight[i], ((1,), (1,)))
        grad_gated = grad_gated.reshape(seqs, length, G, chans)
        last = i == layers - 1
        if last:
            scanned = scan_adjoint_and_backward(
                act, step, delta, gate, y, grad_gated, maps, decay_log[i], start, span, packs, skip_gain[i : i + 1],
                dtproj_weight[i],
            )
        else:
            suffix, back_packs = scan_adjoint(step, gate, grad_gated, maps, decay_log[i], span)
            back_packs = after(back_packs, sums["out"])
            sums["out"].across()
            scanned = scan_backward(
                act, step, delta, gate, y, grad_gated, maps, decay_log[i], start, suffix, span, back_packs, packs,
                skip_gain[i : i + 1], dtproj_weight[i],
            )
        gact, gpre, ggate, proj_part, gdecay, gskip, ginit = after(scanned, sums["out"])
        sums["out"].across() if last else sums["out"].step()
        gpre = gpre.reshape(rows, chans)
        ggate = ggate.reshape(rows, chans)
        proj_part = proj_part.reshape(rows, -1)
        sums["gate"] = Summed(dot(normed, ggate, ((0,), (0,))).astype(BF16), True)
        proj_part = after(proj_part, sums["gate"])
        sums["gate"].across()
        grad_proj = sum_chan(proj_part)
        if not last:
            grad_proj = after(grad_proj, sums["out"])
        gmixed, packed = mid_backward(
            grad_proj, xproj_weight[i].T, gact, mixed.reshape(seqs, length, G, -1), head, act_low, conv_weight[i],
            conv_bias[i : i + 1], rank_part, gpre, ggate, gdecay, gskip, ginit,
        )
        gmixed, packed = after((gmixed, packed), sums["out" if last else "gate"])
        if last:
            gmixed, branch_sum = lax.optimization_barrier((gmixed, branch_sum))
            hidden = hidden + branch_sum.astype(F32)
        sums["out" if last else "gate"].step()
        sums["small"] = Summed(packed, False)
        sums["inner"] = Summed(dot(normed, gmixed[:, :chans], ((0,), (0,))).astype(BF16), True)
        inner_sums = jnp.sum(gmixed.astype(F32) * mixed, axis=1)
        gmixed = after(gmixed, sums["inner"], sums["small"])
        sums["inner"].across()
        sums["small"].across()
        outs = backward_boundary(
            gmixed, flat_in, grad, hidden_i, inverse, norm_gain[i : i + 1], inner_sums, i > 0
        )
        if last:
            outs = after(outs, sums["gate"], sums["inner"], sums["small"])
            sums["gate"].step()
        else:
            outs = after(outs, sums["inner"], sums["small"])
        grad = outs[0]
        if i > 0:
            grad_rows = outs[2]
        sums["inner"].step()
        sums["gain"] = Summed(outs[1].astype(BF16), False)
        smalls[i] = sums
        if before_sums is not None:
            finish(i + 1, before_sums)
        before_sums = sums
    finish(0, before_sums)
    places, _ = rows_of_packed(xproj_weight.shape[2], rank, states, seqs, taps)
    gain, taps_grad, shift, xproj, dtproj, bias, decay, skip, conv, init = unpack(
        [one["small"].last() for one in smalls], [one["gain"].last() for one in smalls], places, seqs,
        norm_gain.shape[1],
    )

    def back_out(value):
        return from_segments(value.reshape(seqs, length, G, -1))

    return (
        back_out(hidden),
        back_out(grad),
        gain,
        in_grads,
        taps_grad,
        shift,
        xproj.transpose(0, 2, 1),
        dtproj,
        bias,
        decay,
        skip,
        out_grads,
        conv.transpose(0, 2, 1, 3),
        init.reshape(scan_state.shape),
    )


def solution(mesh):
    return jax.shard_map(
        local,
        mesh=mesh,
        in_specs=(
            P(None, "seq", "chan"),
            P(None, "chan"),
            P(None, None, None, "chan"),
            P(None, None, "chan"),
            P(None, "chan"),
            P(None, "chan", None),
            P(None, None, "chan"),
            P(None, "chan"),
            P(None, None, "chan"),
            P(None, "chan"),
            P(None, "chan", None),
            P(None, None, None, "chan"),
            P(None, None, None, "chan"),
            P(None, "seq", "chan"),
        ),
        out_specs=(
            P(None, "seq", "chan"),
            P(None, "seq", "chan"),
            P(None, "chan"),
            P(None, None, None, "chan"),
            P(None, None, "chan"),
            P(None, "chan"),
            P(None, "chan", None),
            P(None, None, "chan"),
            P(None, "chan"),
            P(None, None, "chan"),
            P(None, "chan"),
            P(None, "chan", None),
            P(None, None, None, "chan"),
            P(None, None, None, "chan"),
        ),
        check_vma=False,
    )
```

```python
import functools
import math

import jax
import jax.numpy as jnp
from jax import lax
from jax.experimental import pallas as pl
from jax.experimental.pallas import tpu as pltpu
from jax.sharding import PartitionSpec as P

EPS = 1e-05
G = 8
LANES = 128
LOG2E = 1.4426950408889634
LN2 = 0.6931471805599453
F32 = jnp.float32
BF16 = jnp.bfloat16
VMEM_LIMIT = 42 * 1024 * 1024
MESH = pl.DeviceIdType.MESH


def params(*semantics):
    return pltpu.CompilerParams(dimension_semantics=semantics, vmem_limit_bytes=VMEM_LIMIT)


def spread_maps(maps_ref, first, count, out_ref):
    shape = (maps_ref.shape[2], count * LANES)
    row = lax.broadcasted_iota(jnp.int32, shape, 0)
    col = lax.broadcasted_iota(jnp.int32, shape, 1) // LANES
    choice = jnp.where(row == col + first, 1.0, 0.0).astype(BF16)
    out_ref[...] = jnp.dot(maps_ref[0], choice, preferred_element_type=F32)


def part(ref, l, n):
    return ref[pl.ds(pl.multiple_of(l * G, G), G), n * LANES : (n + 1) * LANES]


def spread_rate(decay_ref, rate_ref):
    rate = jnp.exp(decay_ref[...]) * (-LOG2E)
    for n in range(rate.shape[0]):
        rate_ref[n] = jnp.broadcast_to(rate[n : n + 1, :], (G, LANES))


def shifted(value, by, fill):
    row = lax.broadcasted_iota(jnp.int32, value.shape, 0)
    moved = pltpu.roll(value, by % G, 0)
    inside = row >= by if by > 0 else row < G + by
    return jnp.where(inside, moved, fill)


def segment_prefix(ends, span, rate_ref, direction):
    step = 1
    while step < G:
        moved_span = shifted(span, direction * step, 0.0)
        ends = [
            e + jnp.exp2(span * rate_ref[n]) * shifted(e, direction * step, 0.0)
            for n, e in enumerate(ends)
        ]
        span = span + moved_span
        step *= 2
    return ends, span


class SeqExchange:
    def __init__(self, give_ref, got_ref, send_sem, recv_sem):
        self.refs = give_ref, got_ref
        self.sems = send_sem, recv_sem
        self.me, self.peers = lax.axis_index("seq"), lax.axis_size("seq")
        self.others = [lax.rem(self.me + k, self.peers) for k in range(1, self.peers)]

    def signal(self):
        barrier = pltpu.get_barrier_semaphore()
        for other in self.others:
            pl.semaphore_signal(barrier, inc=1, device_id={"seq": other}, device_id_type=MESH)

    def meet(self):
        if self.others:
            pl.semaphore_wait(pltpu.get_barrier_semaphore(), len(self.others))

    def copy(self, step, k):
        give, got = self.refs
        send, recv = self.sems
        return pltpu.make_async_remote_copy(
            src_ref=give.at[step], dst_ref=got.at[self.me, step], send_sem=send.at[step, k], recv_sem=recv.at[step, k],
            device_id={"seq": self.others[k]}, device_id_type=MESH,
        )

    def start(self, step):
        for k in range(len(self.others)):
            self.copy(step, k).start()

    def wait(self, step):
        for k in range(len(self.others)):
            self.copy(step, k).wait()

    def finish(self, steps):
        for step in range(steps):
            self.wait(step)


def exchange_scratch(steps, rows):
    peers = lax.axis_size("seq")
    sems = pltpu.SemaphoreType.DMA((steps, max(peers - 1, 1)))
    return [pltpu.VMEM((steps, rows, LANES), F32), pltpu.VMEM((peers, steps, rows, LANES), F32), sems, sems]


def exchange_params(ident):
    return pltpu.CompilerParams(
        dimension_semantics=("arbitrary", "arbitrary"), collective_id=ident, has_side_effects=True,
        vmem_limit_bytes=VMEM_LIMIT,
    )


def exchange_step(exchange, packs_ref, give_ref, got_ref, rows):
    seqs, tiles = pl.num_programs(0), pl.num_programs(1)
    step = pl.program_id(0) * tiles + pl.program_id(1)
    total = give_ref.shape[0]
    wide = packs_ref.shape[3] // LANES
    give_ref[step] = rows
    pl.when(step == 0)(exchange.meet)
    exchange.start(step)

    @pl.when(step == total - 1)
    def _():
        exchange.finish(total)
        for i in range(total):
            for d in range(got_ref.shape[0]):
                packs_ref[d, i // wide, :, (i % wide) * LANES : (i % wide + 1) * LANES] = jnp.where(
                    exchange.me == d, give_ref[i], got_ref[d, i]
                )


def forward_kernel(
    act_ref, step_ref, gate_ref, maps_ref, decay_ref, init_ref, skip_ref,
    y_ref, gated_ref, start_ref, span_ref, packs_ref,
    b_ref, c_ref, rate_ref, prefix_ref, spans_ref, give_ref, got_ref, *sems,
):
    length, states = act_ref.shape[1], decay_ref.shape[0]
    phase, s, j = pl.program_id(0), pl.program_id(1), pl.program_id(2)
    step = s * pl.num_programs(2) + j
    exchange = SeqExchange(give_ref, got_ref, *sems)
    pl.when(phase + step == 0)(exchange.signal)
    spread_rate(decay_ref, rate_ref)
    zero = jnp.zeros((G, LANES), F32)

    @pl.when(phase == 0)
    def _():
        pl.when(j == 0)(lambda: spread_maps(maps_ref, 0, states, b_ref.at[s]))

        def one(l, carry):
            h, total = carry
            st = step_ref[0, l]
            u = st * act_ref[0, l]
            h = tuple(
                jnp.exp2(st * rate_ref[n]) * h[n] + u * part(b_ref.at[s], l, n) for n in range(states)
            )
            return h, total + st

        h, total = lax.fori_loop(0, length, one, ((zero,) * states, zero), unroll=math.gcd(length, 8))
        ends, span = segment_prefix(list(h), total, rate_ref, 1)
        for n in range(states):
            prefix_ref[step, n] = shifted(ends[n], 1, 0.0)
        spans_ref[step, 0] = shifted(span, 1, 0.0)
        spans_ref[step, 1] = jnp.broadcast_to(span[G - 1 : G, :], (G, LANES)) - span
        rows = [e[G - 1 : G, :] for e in ends] + [jnp.broadcast_to(span[G - 1 : G, :], (8, LANES))]
        give_ref[step] = jnp.concatenate(rows, axis=0)
        pl.when(step == 0)(exchange.meet)
        exchange.start(step)

    @pl.when(phase == 1)
    def _():
        pl.when(j == 0)(lambda: spread_maps(maps_ref, states, states, c_ref))
        exchange.wait(step)
        rate = jnp.exp(decay_ref[...]) * (-LOG2E)
        entry = init_ref[0]
        for d in range(packs_ref.shape[0]):
            pack = jnp.where(exchange.me == d, give_ref[step], got_ref[d, step])
            packs_ref[d, 0] = pack
            joined = jnp.exp2(rate * pack[states : states + 1, :]) * entry + pack[:states, :]
            entry = jnp.where(d < exchange.me, joined, entry)
        span_ref[0] = spans_ref[step]
        span = spans_ref[step, 0]
        h = []
        for n in range(states):
            first = prefix_ref[step, n] + jnp.exp2(rate_ref[n] * span) * entry[n : n + 1, :]
            start_ref[0, n] = first
            h.append(first)
        skip = jnp.broadcast_to(skip_ref[...], (G, LANES))

        def one(k, h):
            h = list(h)
            halves = []
            for i in range(2):
                l = 2 * k + i
                st = step_ref[0, l]
                act = act_ref[0, l]
                u = st * act
                y = skip * act
                for n in range(states):
                    h[n] = jnp.exp2(st * rate_ref[n]) * h[n] + u * part(b_ref.at[s], l, n)
                    y = y + part(c_ref, l, n) * h[n]
                y_ref[0, l] = y
                gate = gate_ref[0, l]
                halves.append(y * (gate / (1.0 + jnp.exp(-gate))))
            row = pl.multiple_of(k * 2 * G, 2 * G)
            gated_ref[0, pl.ds(row, 2 * G), :] = jnp.concatenate(halves, axis=0).astype(BF16)
            return tuple(h)

        lax.fori_loop(0, length // 2, one, tuple(h), unroll=math.gcd(length // 2, 4))


def scan_forward(act, step, gate, maps, decay, init, skip):
    seqs, length, _, chans = act.shape
    states = decay.shape[0]
    peers = lax.axis_size("seq")
    tiles = chans // LANES
    token = pl.BlockSpec((1, length, G, LANES), lambda p, s, j: (s, 0, 0, j))

    def late(shape, index):
        return pl.BlockSpec(shape, lambda p, s, j: index(p * s, p * j))

    return pl.pallas_call(
        forward_kernel,
        grid=(2, seqs, tiles),
        in_specs=[
            token,
            token,
            late((1, length, G, LANES), lambda s, j: (s, 0, 0, j)),
            pl.BlockSpec((1, length * G, maps.shape[2]), lambda p, s, j: (s, 0, 0)),
            pl.BlockSpec((states, LANES), lambda p, s, j: (0, j)),
            late((1, states, LANES), lambda s, j: (s, 0, j)),
            late((1, LANES), lambda s, j: (0, j)),
        ],
        out_specs=[
            late((1, length, G, LANES), lambda s, j: (s, 0, 0, j)),
            late((1, length * G, LANES), lambda s, j: (s, 0, j)),
            late((1, states, G, LANES), lambda s, j: (s, 0, 0, j)),
            late((1, 2, G, LANES), lambda s, j: (s, 0, 0, j)),
            late((peers, 1, states + 8, LANES), lambda s, j: (0, s, 0, j)),
        ],
        out_shape=[
            jax.ShapeDtypeStruct(act.shape, F32),
            jax.ShapeDtypeStruct((seqs, length * G, chans), BF16),
            pltpu.HBM((seqs, states, G, chans), F32),
            pltpu.HBM((seqs, 2, G, chans), F32),
            pltpu.HBM((peers, seqs, states + 8, chans), F32),
        ],
        scratch_shapes=[
            pltpu.VMEM((seqs, length * G, states * LANES), F32),
            pltpu.VMEM((length * G, states * LANES), F32),
            pltpu.VMEM((states, G, LANES), F32),
            pltpu.VMEM((seqs * tiles, states, G, LANES), F32),
            pltpu.VMEM((seqs * tiles, 2, G, LANES), F32),
        ]
        + exchange_scratch(seqs * tiles, states + 8),
        compiler_params=pltpu.CompilerParams(
            dimension_semantics=("arbitrary",) * 3, collective_id=6, has_side_effects=True,
            vmem_limit_bytes=VMEM_LIMIT,
        ),
        cost_estimate=estimate(20),
        name="scan_forward",
    )(act, step, gate, maps, decay, init, skip)


def adjoint_kernel(
    step_ref, gate_ref, grad_ref, maps_ref, decay_ref, span_ref, suffix_ref, packs_ref, c_ref, rate_ref, give_ref,
    got_ref, *sems,
):
    length, states = step_ref.shape[1], decay_ref.shape[0]
    columns = pl.ds(pl.multiple_of(pl.program_id(1) * LANES, LANES), LANES)
    step_ref, gate_ref, grad_ref = (ref.at[:, :, :, columns] for ref in (step_ref, gate_ref, grad_ref))
    exchange = SeqExchange(give_ref, got_ref, *sems)
    pl.when(pl.program_id(0) + pl.program_id(1) == 0)(exchange.signal)

    @pl.when(pl.program_id(1) == 0)
    def _():
        spread_maps(maps_ref, states, states, c_ref)

    spread_rate(decay_ref, rate_ref)

    def one(k, carry):
        l = length - 1 - k
        st = step_ref[0, l]
        gate = gate_ref[0, l]
        gy = grad_ref[0, l] * (gate / (1.0 + jnp.exp(-gate)))
        return tuple(
            jnp.exp2(st * rate_ref[n]) * (carry[n] + gy * part(c_ref, l, n)) for n in range(states)
        )

    zero = jnp.zeros((G, LANES), F32)
    carry = lax.fori_loop(0, length, one, (zero,) * states, unroll=math.gcd(length, 8))
    own = span_ref[0, 1, 0:1, :] + span_ref[0, 0, 1:2, :] - span_ref[0, 0] - span_ref[0, 1]
    ends, _ = segment_prefix(list(carry), own, rate_ref, -1)
    for n in range(states):
        suffix_ref[0, n] = shifted(ends[n], -1, 0.0)
    rows = jnp.concatenate([e[0:1, :] for e in ends], axis=0)
    exchange_step(exchange, packs_ref, give_ref, got_ref, rows)


def scan_adjoint(step, gate, grad, maps, decay, span):
    seqs, length, _, chans = step.shape
    states = decay.shape[0]
    peers = lax.axis_size("seq")
    broad = pl.BlockSpec((1, length, G, chans), lambda s, j: (s, 0, 0, 0))
    return pl.pallas_call(
        adjoint_kernel,
        grid=(seqs, chans // LANES),
        in_specs=[
            broad,
            broad,
            broad,
            pl.BlockSpec((1, length * G, maps.shape[2]), lambda s, j: (s, 0, 0)),
            pl.BlockSpec((states, LANES), lambda s, j: (0, j)),
            pl.BlockSpec((1, 2, G, LANES), lambda s, j: (s, 0, 0, j)),
        ],
        out_specs=[
            pl.BlockSpec((1, states, G, LANES), lambda s, j: (s, 0, 0, j)),
            pl.BlockSpec((peers, seqs, states, chans), lambda s, j: (0, 0, 0, 0)),
        ],
        out_shape=[
            pltpu.HBM((seqs, states, G, chans), F32),
            pltpu.HBM((peers, seqs, states, chans), F32),
        ],
        scratch_shapes=[
            pltpu.VMEM((length * G, states * LANES), F32),
            pltpu.VMEM((states, G, LANES), F32),
        ]
        + exchange_scratch(seqs * chans // LANES, states),
        compiler_params=exchange_params(7),
        cost_estimate=estimate(15),
        name="scan_adjoint",
    )(step, gate, grad, maps, decay, span)


def backward_kernel(
    act_ref, step_ref, delta_ref, gate_ref, y_ref, grad_ref, maps_ref, decay_ref, start_ref, suffix_ref, span_ref,
    packs_ref, forward_packs_ref, skip_ref, weight_ref,
    gact_ref, gpre_ref, ggate_ref, proj_ref, gdecay_ref, gskip_ref, ginit_ref,
    b_ref, c_ref, rate_ref, h_ref, product_ref, select_ref, rank_ref,
):
    length, states = act_ref.shape[1], decay_ref.shape[0]
    columns = pl.ds(pl.multiple_of(pl.program_id(1) * LANES, LANES), LANES)
    act_ref, step_ref, delta_ref, gate_ref, y_ref, grad_ref = (
        ref.at[:, :, :, columns] for ref in (act_ref, step_ref, delta_ref, gate_ref, y_ref, grad_ref)
    )
    wide = states * LANES

    @pl.when(pl.program_id(1) == 0)
    def _():
        spread_maps(maps_ref, 0, states, b_ref)
        spread_maps(maps_ref, states, states, c_ref)
        row = lax.broadcasted_iota(jnp.int32, select_ref.shape, 0) // LANES
        col = lax.broadcasted_iota(jnp.int32, select_ref.shape, 1)
        product_ref[...] = jnp.zeros_like(product_ref)
        rank_ref[...] = jnp.zeros_like(rank_ref)
        select_ref[...] = jnp.where(row == col, 1.0, 0.0).astype(BF16)

    spread_rate(decay_ref, rate_ref)
    rate = jnp.exp(decay_ref[...]) * (-LOG2E)
    me = lax.axis_index("seq")
    count = packs_ref.shape[0]
    entry = jnp.zeros((states, LANES), F32)
    for d in reversed(range(count)):
        joined = jnp.exp2(rate * forward_packs_ref[d, 0, states : states + 1, :]) * entry + packs_ref[d, 0]
        entry = jnp.where(d > me, joined, entry)
    after = span_ref[0, 1]
    skip = jnp.broadcast_to(skip_ref[...], (G, LANES))

    def forward(l, h):
        st = step_ref[0, l]
        u = st * act_ref[0, l]
        for n in range(states):
            h_ref[l, n] = h[n]
        return tuple(
            jnp.exp2(st * rate_ref[n]) * h[n] + u * part(b_ref, l, n) for n in range(states)
        )

    h = lax.fori_loop(
        0, length, forward, tuple(start_ref[0, n] for n in range(states)), unroll=math.gcd(length, 4)
    )
    for n in range(states):
        h_ref[length, n] = h[n]

    def back(k, state):
        carry, gdecay, gskip = list(state[0]), list(state[1]), state[2]
        lines = [length - 1 - 2 * k, length - 2 - 2 * k]
        st, act, u, gy, q, r = [], [], [], [], [], []
        ggate = []
        for l in lines:
            st.append(step_ref[0, l])
            act.append(act_ref[0, l])
            u.append(st[-1] * act[-1])
            gate = gate_ref[0, l]
            grad = grad_ref[0, l]
            sig = 1.0 / (1.0 + jnp.exp(-gate))
            silu = gate * sig
            gy.append(grad * silu)
            ggate.append(grad * y_ref[0, l] * (sig + silu * (1.0 - sig)))
            gskip = gskip + gy[-1] * act[-1]
            q.append(jnp.zeros((G, LANES), F32))
            r.append(jnp.zeros((G, LANES), F32))
        row = pl.multiple_of((length - 2 - 2 * k) * G, 2 * G)
        for n in range(states):
            late, early = [], []
            for i, l in enumerate(lines):
                lam = part(c_ref, l, n) * gy[i] + carry[n]
                early.append(lam * u[i])
                late.append(gy[i] * h_ref[l + 1, n])
                q[i] = q[i] + lam * part(b_ref, l, n)
                carry[n] = jnp.exp2(st[i] * rate_ref[n]) * lam
                w = carry[n] * h_ref[l, n]
                r[i] = r[i] + rate_ref[n] * w
                gdecay[n] = gdecay[n] + st[i] * w
            product_ref[pl.ds(row, 2 * G), n * LANES : (n + 1) * LANES] += jnp.concatenate(early[::-1], axis=0)
            product_ref[pl.ds(row, 2 * G), wide + n * LANES : wide + (n + 1) * LANES] += jnp.concatenate(late[::-1], axis=0)
        gpre = []
        for i, l in enumerate(lines):
            gact_ref[0, l] = skip * gy[i] + st[i] * q[i]
            gstep = LN2 * r[i] + act[i] * q[i]
            gpre.append(gstep / (1.0 + jnp.exp(-delta_ref[0, l])))
        gpre_ref[0, pl.ds(row, 2 * G), :] = jnp.concatenate(gpre[::-1], axis=0).astype(BF16)
        ggate_ref[0, pl.ds(row, 2 * G), :] = jnp.concatenate(ggate[::-1], axis=0).astype(BF16)
        return tuple(carry), tuple(gdecay), gskip

    zero = jnp.zeros((G, LANES), F32)
    first = tuple(
        suffix_ref[0, n] + jnp.exp2(rate_ref[n] * after) * entry[n : n + 1, :] for n in range(states)
    )
    carry, gdecay, gskip = lax.fori_loop(
        0, length // 2, back, (first, (zero,) * states, zero), unroll=math.gcd(length // 2, 4)
    )
    for n in range(states):
        ginit_ref[0, n : n + 1, :] = carry[n][0:1, :]
        total = jnp.sum(gdecay[n] * rate_ref[n], axis=0, keepdims=True)
        gdecay_ref[0, n : n + 1, :] = total * LN2
    gskip_ref[0] = jnp.broadcast_to(jnp.sum(gskip, axis=0, keepdims=True), (8, LANES))

    rank_ref[...] += dot(gpre_ref[0], weight_ref[...], ((1,), (1,)))

    @pl.when(pl.program_id(1) == pl.num_programs(1) - 1)
    def _():
        sums = jnp.dot(product_ref[...].astype(BF16), select_ref[...], preferred_element_type=F32)
        rank = rank_ref.shape[1]
        proj_ref[0, :, :rank] = rank_ref[...].astype(BF16)
        proj_ref[0, :, rank:] = sums[:, : 2 * states].astype(BF16)


def scan_backward(
    act, step, delta, gate, y, grad, maps, decay, start, suffix, span, packs, forward_packs, skip, weight
):
    seqs, length, _, chans = act.shape
    start, suffix, span, packs, forward_packs = (
        pltpu.with_memory_space_constraint(value, pltpu.HBM) for value in (start, suffix, span, packs, forward_packs)
    )
    states = decay.shape[0]
    token = pl.BlockSpec((1, length, G, LANES), lambda s, j: (s, 0, 0, j))
    broad = pl.BlockSpec((1, length, G, chans), lambda s, j: (s, 0, 0, 0))
    rows = pl.BlockSpec((1, length * G, LANES), lambda s, j: (s, 0, j))
    per_state = pl.BlockSpec((1, states, G, LANES), lambda s, j: (s, 0, 0, j))
    total = pl.BlockSpec((1, states, LANES), lambda s, j: (s, 0, j))
    return pl.pallas_call(
        backward_kernel,
        grid=(seqs, chans // LANES),
        in_specs=[
            broad,
            broad,
            broad,
            broad,
            broad,
            broad,
            pl.BlockSpec((1, length * G, maps.shape[2]), lambda s, j: (s, 0, 0)),
            pl.BlockSpec((states, LANES), lambda s, j: (0, j)),
            per_state,
            per_state,
            pl.BlockSpec((1, 2, G, LANES), lambda s, j: (s, 0, 0, j)),
            pl.BlockSpec((packs.shape[0], 1, states, LANES), lambda s, j: (0, s, 0, j)),
            pl.BlockSpec((packs.shape[0], 1, states + 8, LANES), lambda s, j: (0, s, 0, j)),
            pl.BlockSpec((1, LANES), lambda s, j: (0, j)),
            pl.BlockSpec((weight.shape[0], LANES), lambda s, j: (0, j)),
        ],
        out_specs=[
            token,
            rows,
            rows,
            pl.BlockSpec((1, length * G, weight.shape[0] + 2 * states), lambda s, j: (s, 0, 0)),
            total,
            pl.BlockSpec((1, 8, LANES), lambda s, j: (s, 0, j)),
            total,
        ],
        out_shape=[
            jax.ShapeDtypeStruct(act.shape, F32),
            jax.ShapeDtypeStruct((seqs, length * G, chans), BF16),
            jax.ShapeDtypeStruct((seqs, length * G, chans), BF16),
            jax.ShapeDtypeStruct((seqs, length * G, weight.shape[0] + 2 * states), BF16),
            jax.ShapeDtypeStruct((seqs, states, chans), F32),
            jax.ShapeDtypeStruct((seqs, 8, chans), F32),
            jax.ShapeDtypeStruct((seqs, states, chans), F32),
        ],
        scratch_shapes=[
            pltpu.VMEM((length * G, states * LANES), F32),
            pltpu.VMEM((length * G, states * LANES), F32),
            pltpu.VMEM((states, G, LANES), F32),
            pltpu.VMEM((length + 1, states, G, LANES), F32),
            pltpu.VMEM((length * G, 2 * states * LANES), F32),
            pltpu.VMEM((2 * states * LANES, LANES), BF16),
            pltpu.VMEM((length * G, weight.shape[0]), F32),
        ],
        compiler_params=params("arbitrary", "arbitrary"),
        cost_estimate=estimate(39),
        name="scan_backward",
    )(act, step, delta, gate, y, grad, maps, decay, start, suffix, span, packs, forward_packs, skip, weight)


def adjoint_and_backward_kernel(
    act_ref, step_ref, delta_ref, gate_ref, y_ref, grad_ref, maps_ref, decay_ref, start_ref, span_ref,
    forward_packs_ref, skip_ref, weight_ref,
    gact_ref, gpre_ref, ggate_ref, proj_ref, gdecay_ref, gskip_ref, ginit_ref,
    b_ref, c_ref, rate_ref, h_ref, product_ref, select_ref, rank_ref, suffix_ref, give_ref, got_ref, *sems,
):
    length, states = act_ref.shape[1], decay_ref.shape[0]
    phase, s, j = pl.program_id(0), pl.program_id(1), pl.program_id(2)
    block = s * pl.num_programs(2) + j
    columns = pl.ds(pl.multiple_of(j * LANES, LANES), LANES)
    act_ref, step_ref, delta_ref, gate_ref, y_ref, grad_ref = (
        ref.at[:, :, :, columns] for ref in (act_ref, step_ref, delta_ref, gate_ref, y_ref, grad_ref)
    )
    c_ref = c_ref.at[s]
    exchange = SeqExchange(give_ref, got_ref, *sems)
    pl.when(phase + block == 0)(exchange.signal)
    spread_rate(decay_ref, rate_ref)
    zero = jnp.zeros((G, LANES), F32)

    @pl.when(phase == 0)
    def _():
        pl.when(j == 0)(lambda: spread_maps(maps_ref, states, states, c_ref))

        def one(k, carry):
            l = length - 1 - k
            st = step_ref[0, l]
            gate = gate_ref[0, l]
            gy = grad_ref[0, l] * (gate / (1.0 + jnp.exp(-gate)))
            return tuple(
                jnp.exp2(st * rate_ref[n]) * (carry[n] + gy * part(c_ref, l, n)) for n in range(states)
            )

        carry = lax.fori_loop(0, length, one, (zero,) * states, unroll=math.gcd(length, 8))
        own = span_ref[0, 1, 0:1, :] + span_ref[0, 0, 1:2, :] - span_ref[0, 0] - span_ref[0, 1]
        ends, _ = segment_prefix(list(carry), own, rate_ref, -1)
        for n in range(states):
            suffix_ref[block, n] = shifted(ends[n], -1, 0.0)
        give_ref[block] = jnp.concatenate([e[0:1, :] for e in ends], axis=0)
        pl.when(block == 0)(exchange.meet)
        exchange.start(block)

    pl.when(phase == 1)(lambda: gradients(
        exchange, block, j, columns,
        act_ref, step_ref, delta_ref, gate_ref, y_ref, grad_ref, maps_ref, decay_ref, start_ref, span_ref,
        forward_packs_ref, skip_ref, weight_ref,
        gact_ref, gpre_ref, ggate_ref, proj_ref, gdecay_ref, gskip_ref, ginit_ref,
        b_ref, c_ref, rate_ref, h_ref, product_ref, select_ref, rank_ref, suffix_ref, give_ref, got_ref,
    ))


def gradients(
    exchange, block, tile, columns,
    act_ref, step_ref, delta_ref, gate_ref, y_ref, grad_ref, maps_ref, decay_ref, start_ref, span_ref,
    forward_packs_ref, skip_ref, weight_ref,
    gact_ref, gpre_ref, ggate_ref, proj_ref, gdecay_ref, gskip_ref, ginit_ref,
    b_ref, c_ref, rate_ref, h_ref, product_ref, select_ref, rank_ref, suffix_ref, give_ref, got_ref,
):
    length, states = act_ref.shape[1], decay_ref.shape[0]
    wide = states * LANES

    @pl.when(tile == 0)
    def _():
        spread_maps(maps_ref, 0, states, b_ref)
        row = lax.broadcasted_iota(jnp.int32, select_ref.shape, 0) // LANES
        col = lax.broadcasted_iota(jnp.int32, select_ref.shape, 1)
        product_ref[...] = jnp.zeros_like(product_ref)
        rank_ref[...] = jnp.zeros_like(rank_ref)
        select_ref[...] = jnp.where(row == col, 1.0, 0.0).astype(BF16)

    exchange.wait(block)
    rate = jnp.exp(decay_ref[...]) * (-LOG2E)
    entry = jnp.zeros((states, LANES), F32)
    for d in reversed(range(got_ref.shape[0])):
        pack = jnp.where(exchange.me == d, give_ref[block], got_ref[d, block])
        joined = jnp.exp2(rate * forward_packs_ref[d, 0, states : states + 1, :]) * entry + pack
        entry = jnp.where(d > exchange.me, joined, entry)
    after = span_ref[0, 1]
    skip = jnp.broadcast_to(skip_ref[...], (G, LANES))

    def forward(l, h):
        st = step_ref[0, l]
        u = st * act_ref[0, l]
        for n in range(states):
            h_ref[l, n] = h[n]
        return tuple(
            jnp.exp2(st * rate_ref[n]) * h[n] + u * part(b_ref, l, n) for n in range(states)
        )

    h = lax.fori_loop(
        0, length, forward, tuple(start_ref[0, n] for n in range(states)), unroll=math.gcd(length, 4)
    )
    for n in range(states):
        h_ref[length, n] = h[n]

    def back(k, state):
        carry, gdecay, gskip = list(state[0]), list(state[1]), state[2]
        lines = [length - 1 - 2 * k, length - 2 - 2 * k]
        st, act, u, gy, q, r = [], [], [], [], [], []
        ggate = []
        for l in lines:
            st.append(step_ref[0, l])
            act.append(act_ref[0, l])
            u.append(st[-1] * act[-1])
            gate = gate_ref[0, l]
            grad = grad_ref[0, l]
            sig = 1.0 / (1.0 + jnp.exp(-gate))
            silu = gate * sig
            gy.append(grad * silu)
            ggate.append(grad * y_ref[0, l] * (sig + silu * (1.0 - sig)))
            gskip = gskip + gy[-1] * act[-1]
            q.append(jnp.zeros((G, LANES), F32))
            r.append(jnp.zeros((G, LANES), F32))
        row = pl.multiple_of((length - 2 - 2 * k) * G, 2 * G)
        for n in range(states):
            late, early = [], []
            for i, l in enumerate(lines):
                lam = part(c_ref, l, n) * gy[i] + carry[n]
                early.append(lam * u[i])
                late.append(gy[i] * h_ref[l + 1, n])
                q[i] = q[i] + lam * part(b_ref, l, n)
                carry[n] = jnp.exp2(st[i] * rate_ref[n]) * lam
                w = carry[n] * h_ref[l, n]
                r[i] = r[i] + rate_ref[n] * w
                gdecay[n] = gdecay[n] + st[i] * w
            product_ref[pl.ds(row, 2 * G), n * LANES : (n + 1) * LANES] += jnp.concatenate(early[::-1], axis=0)
            product_ref[pl.ds(row, 2 * G), wide + n * LANES : wide + (n + 1) * LANES] += jnp.concatenate(late[::-1], axis=0)
        gpre = []
        for i, l in enumerate(lines):
            gact_ref[0, l] = skip * gy[i] + st[i] * q[i]
            gstep = LN2 * r[i] + act[i] * q[i]
            gpre.append(gstep / (1.0 + jnp.exp(-delta_ref[0, l])))
        gpre_ref[0, pl.ds(row, 2 * G), :] = jnp.concatenate(gpre[::-1], axis=0).astype(BF16)
        ggate_ref[0, pl.ds(row, 2 * G), :] = jnp.concatenate(ggate[::-1], axis=0).astype(BF16)
        return tuple(carry), tuple(gdecay), gskip

    zero = jnp.zeros((G, LANES), F32)
    first = tuple(
        suffix_ref[block, n] + jnp.exp2(rate_ref[n] * after) * entry[n : n + 1, :] for n in range(states)
    )
    carry, gdecay, gskip = lax.fori_loop(
        0, length // 2, back, (first, (zero,) * states, zero), unroll=math.gcd(length // 2, 4)
    )
    for n in range(states):
        ginit_ref[0, n : n + 1, :] = carry[n][0:1, :]
        total = jnp.sum(gdecay[n] * rate_ref[n], axis=0, keepdims=True)
        gdecay_ref[0, n : n + 1, :] = total * LN2
    gskip_ref[0] = jnp.broadcast_to(jnp.sum(gskip, axis=0, keepdims=True), (8, LANES))

    rank_ref[...] += dot(gpre_ref[0], weight_ref[...], ((1,), (1,)))

    @pl.when(tile == pl.num_programs(2) - 1)
    def _():
        sums = jnp.dot(product_ref[...].astype(BF16), select_ref[...], preferred_element_type=F32)
        rank = rank_ref.shape[1]
        proj_ref[0, :, :rank] = rank_ref[...].astype(BF16)
        proj_ref[0, :, rank:] = sums[:, : 2 * states].astype(BF16)


def scan_adjoint_and_backward(act, step, delta, gate, y, grad, maps, decay, start, span, forward_packs, skip, weight):
    seqs, length, _, chans = act.shape
    start, span, forward_packs = (
        pltpu.with_memory_space_constraint(value, pltpu.HBM) for value in (start, span, forward_packs)
    )
    states = decay.shape[0]
    peers = lax.axis_size("seq")
    tiles = chans // LANES

    def late(shape, index):
        return pl.BlockSpec(shape, lambda p, s, j: index(p * s, p * j))

    broad = pl.BlockSpec((1, length, G, chans), lambda p, s, j: (s, 0, 0, 0))
    late_broad = late((1, length, G, chans), lambda s, j: (s, 0, 0, 0))
    rows = late((1, length * G, LANES), lambda s, j: (s, 0, j))
    total = late((1, states, LANES), lambda s, j: (s, 0, j))
    return pl.pallas_call(
        adjoint_and_backward_kernel,
        grid=(2, seqs, tiles),
        in_specs=[
            late_broad,
            broad,
            late_broad,
            broad,
            late_broad,
            broad,
            pl.BlockSpec((1, length * G, maps.shape[2]), lambda p, s, j: (s, 0, 0)),
            pl.BlockSpec((states, LANES), lambda p, s, j: (0, j)),
            late((1, states, G, LANES), lambda s, j: (s, 0, 0, j)),
            pl.BlockSpec((1, 2, G, LANES), lambda p, s, j: (s, 0, 0, j)),
            late((peers, 1, states + 8, LANES), lambda s, j: (0, s, 0, j)),
            late((1, LANES), lambda s, j: (0, j)),
            late((weight.shape[0], LANES), lambda s, j: (0, j)),
        ],
        out_specs=[
            late((1, length, G, LANES), lambda s, j: (s, 0, 0, j)),
            rows,
            rows,
            late((1, length * G, weight.shape[0] + 2 * states), lambda s, j: (s, 0, 0)),
            total,
            late((1, 8, LANES), lambda s, j: (s, 0, j)),
            total,
        ],
        out_shape=[
            jax.ShapeDtypeStruct(act.shape, F32),
            jax.ShapeDtypeStruct((seqs, length * G, chans), BF16),
            jax.ShapeDtypeStruct((seqs, length * G, chans), BF16),
            jax.ShapeDtypeStruct((seqs, length * G, weight.shape[0] + 2 * states), BF16),
            jax.ShapeDtypeStruct((seqs, states, chans), F32),
            jax.ShapeDtypeStruct((seqs, 8, chans), F32),
            jax.ShapeDtypeStruct((seqs, states, chans), F32),
        ],
        scratch_shapes=[
            pltpu.VMEM((length * G, states * LANES), F32),
            pltpu.VMEM((seqs, length * G, states * LANES), F32),
            pltpu.VMEM((states, G, LANES), F32),
            pltpu.VMEM((length + 1, states, G, LANES), F32),
            pltpu.VMEM((length * G, 2 * states * LANES), F32),
            pltpu.VMEM((2 * states * LANES, LANES), BF16),
            pltpu.VMEM((length * G, weight.shape[0]), F32),
            pltpu.VMEM((seqs * tiles, states, G, LANES), F32),
        ]
        + exchange_scratch(seqs * tiles, states),
        compiler_params=pltpu.CompilerParams(
            dimension_semantics=("arbitrary",) * 3, collective_id=9, has_side_effects=True,
            vmem_limit_bytes=VMEM_LIMIT,
        ),
        cost_estimate=estimate(39),
        name="scan_adjoint_and_backward",
    )(act, step, delta, gate, y, grad, maps, decay, start, span, forward_packs, skip, weight)


def remote(src, dst, send, recv, to):
    return pltpu.make_async_remote_copy(
        src_ref=src, dst_ref=dst, send_sem=send, recv_sem=recv, device_id={"chan": to}, device_id_type=MESH
    )


class Line:
    def __init__(self, count):
        self.me = lax.axis_index("chan")
        self.half = count // 2
        self.at = self.me // 2
        self.low = self.me % 2
        self.pair = self.at * 2 + 1 - self.low
        self.right = jnp.minimum(self.at + 1, self.half - 1) * 2 + self.low
        self.left = jnp.maximum(self.at - 1, 0) * 2 + self.low
        self.has_right = self.at < self.half - 1
        self.has_left = self.at > 0

    def greet(self):
        barrier = pltpu.get_barrier_semaphore()

        def signal(to):
            pl.semaphore_signal(barrier, inc=1, device_id={"chan": to}, device_id_type=MESH)

        signal(self.pair)
        pl.when(self.has_right)(lambda: signal(self.right))
        pl.when(self.has_left)(lambda: signal(self.left))
        pl.semaphore_wait(barrier, 1 + jnp.minimum(self.at, 1) + jnp.minimum(self.half - 1 - self.at, 1))


def gather_steps(line, out_ref, width, chunks, sems):
    pair_send, pair_recv, right_send, right_recv, left_send, left_recv = sems
    half = line.half
    rows = out_ref.shape[0] // chunks

    def place(owner, c):
        return out_ref.at[pl.ds(c * rows, rows), pl.ds(pl.multiple_of(owner * width, width), width)]

    def to_pair(owner, slot, c):
        return remote(place(owner, c), place(owner, c), pair_send.at[slot, c], pair_recv.at[slot, c], line.pair)

    def to_right(owner, j, c):
        return remote(place(owner, c), place(owner, c), right_send.at[j, c], right_recv.at[j, c], line.right)

    def to_left(owner, j, c):
        return remote(place(owner, c), place(owner, c), left_send.at[j, c], left_recv.at[j, c], line.left)

    def begin(c):
        pl.when(line.has_right)(lambda: to_right(line.me, 0, c).start())
        pl.when(line.has_left)(lambda: to_left(line.me, 0, c).start())
        to_pair(line.me, 0, c).start()

    def middle(fill=lambda: None):
        for j in range(1, half):
            for c in range(chunks):
                fill()
                @pl.when(line.at >= j)
                def _():
                    owner = line.me - 2 * j
                    to_right(owner, j - 1, c).wait_recv()
                    pl.when(line.has_right)(lambda: to_right(owner, j, c).start())
                    to_pair(owner, j, c).start()

                @pl.when(line.at + j < half)
                def _():
                    owner = line.me + 2 * j
                    to_left(owner, j - 1, c).wait_recv()
                    pl.when(line.has_left)(lambda: to_left(owner, j, c).start())
                    to_pair(owner, half + j, c).start()

    def end():
        for c in range(chunks):
            to_pair(line.me, 0, c).wait()
            pl.when(line.has_right)(lambda: to_right(line.me, 0, c).wait_send())
            pl.when(line.has_left)(lambda: to_left(line.me, 0, c).wait_send())
            for j in range(1, half):
                @pl.when(line.at >= j)
                def _():
                    owner = line.me - 2 * j
                    to_pair(owner, j, c).wait()
                    pl.when(line.has_right)(lambda: to_right(owner, j, c).wait_send())

                @pl.when(line.at + j < half)
                def _():
                    owner = line.me + 2 * j
                    to_pair(owner, half + j, c).wait()
                    pl.when(line.has_left)(lambda: to_left(owner, j, c).wait_send())

    return begin, middle, end


def gather_sems(count, chunks):
    half = count // 2
    return [pltpu.SemaphoreType.DMA((2 * half, chunks))] * 2 + [pltpu.SemaphoreType.DMA((half, chunks))] * 4


def estimate(us):
    return pl.CostEstimate(flops=int(us * 1e8), bytes_accessed=1 << 20, transcendentals=0)


def remote_params(ident):
    return pltpu.CompilerParams(collective_id=ident, has_side_effects=True, vmem_limit_bytes=VMEM_LIMIT)


def whole(count):
    return [pl.BlockSpec(memory_space=pltpu.VMEM)] * count


def chunks_of(rows):
    return next(c for c in (3, 2, 1) if rows % (16 * c) == 0)


def gather_kernel(count, chunks, layers, part_ref, gain_ref, weights_ref, out_ref, *rest):
    flats, rest = rest[:layers], rest[layers:]
    fetched, flat_buf, fetch_sem, store_sem, *sems = rest
    line = Line(count)
    rows, width = part_ref.shape
    mine = pl.ds(pl.multiple_of(line.me * width, width), width)
    height = fetched.shape[1]
    steps = weights_ref.shape[1] // height
    total = layers * steps

    def fetch(i):
        here = weights_ref.at[i // steps, pl.ds(i % steps * height, height)]
        return pltpu.make_async_copy(here, fetched.at[i % 2], fetch_sem.at[i % 2])

    def store(i):
        here = flats[i // steps].at[pl.ds(i % steps * height, height)]
        return pltpu.make_async_copy(flat_buf.at[i % 2], here, store_sem.at[i % 2])

    fetch(0).start()
    fetch(1).start()
    out_ref[:rows, mine] = part_ref[...]
    gain = gain_ref[...]
    terms = []
    for _ in range(3):
        term = gain.astype(BF16).astype(F32)
        terms.append(term)
        gain = gain - term
    terms.append(jnp.zeros((16 - 3 * layers, width), F32))
    out_ref[rows:, mine] = jnp.concatenate(terms, axis=0).astype(BF16)
    line.greet()
    begin, middle, end = gather_steps(line, out_ref, width, chunks, sems)
    for c in range(chunks):
        begin(c)
    done = []

    def flatten():
        i = len(done)
        if i == total:
            return
        done.append(i)
        fetch(i).wait()
        if i >= steps + 2:
            store(i - 2).wait()

        def piece(r, carry):
            here = pl.ds(pl.multiple_of(r * 32, 32), 32)
            value = fetched[i % 2, here].astype(F32)
            value = value.reshape(32, 2 * value.shape[2]).astype(BF16)
            if i < steps:
                flats[0][pl.ds(pl.multiple_of(i * height + r * 32, 32), 32), :] = value
            else:
                flat_buf[i % 2, here, :] = value
            return carry

        lax.fori_loop(0, height // 32, piece, 0)
        if i >= steps:
            store(i).start()
        if i + 2 < total:
            fetch(i + 2).start()

    def fill():
        flatten()
        flatten()

    middle(fill)
    while len(done) < total:
        flatten()
    end()
    for i in range(max(total - 2, steps), total):
        store(i).wait()


def gather_first(part, gain, weights):
    count = lax.axis_size("chan")
    rows, width = part.shape
    layers, model = weights.shape[:2]
    chunks = chunks_of(rows + 16)
    height = 256
    flat = (model, 2 * weights.shape[3])
    full, *flats = pl.pallas_call(
        functools.partial(gather_kernel, count, chunks, layers),
        in_specs=whole(2) + [pl.BlockSpec(memory_space=pl.ANY)],
        out_specs=whole(2) + [pl.BlockSpec(memory_space=pl.ANY)] * (layers - 1),
        out_shape=[jax.ShapeDtypeStruct((rows + 16, count * width), BF16)] + [jax.ShapeDtypeStruct(flat, BF16)] * layers,
        scratch_shapes=[
            pltpu.VMEM((2, height) + weights.shape[2:], BF16),
            pltpu.VMEM((2, height, flat[1]), BF16),
            pltpu.SemaphoreType.DMA((2,)),
            pltpu.SemaphoreType.DMA((2,)),
        ]
        + gather_sems(count, chunks),
        compiler_params=remote_params(0),
        cost_estimate=estimate(25),
        name="gather_first",
    )(part, gain, weights)
    terms = full[rows : rows + 3 * layers].astype(F32)
    return full, terms[:layers] + terms[layers : 2 * layers] + terms[2 * layers :], flats


def scatter_steps(line, part_ref, pair_buf, right_buf, left_buf, stage, width, chunks, sems):
    pair_send, pair_recv, right_send, right_recv, left_send, left_recv = sems
    half = line.half
    rows = part_ref.shape[0] // chunks

    def block(owner, c):
        return part_ref.at[pl.ds(c * rows, rows), pl.ds(pl.multiple_of(owner * width, width), width)]

    def piece(ref, slot, c):
        return ref.at[slot, pl.ds(c * rows, rows)]

    def to_pair(at, c):
        return remote(block(at * 2 + 1 - line.low, c), pair_buf.at[at, pl.ds(c * rows, rows)], pair_send.at[at, c], pair_recv.at[at, c], line.pair)

    def to_right(j, c):
        return remote(piece(stage, j, c), piece(right_buf, j - 1, c), right_send.at[j - 1, c], right_recv.at[j - 1, c], line.right)

    def to_left(j, c):
        return remote(piece(stage, half + j, c), piece(left_buf, j - 1, c), left_send.at[j - 1, c], left_recv.at[j - 1, c], line.left)

    def begin(produce):
        for c in range(chunks):

            def send(at):
                if c == 0:
                    produce(at * 2 + 1 - line.low)
                to_pair(at, c).start()

            for j in range(half - 1, 0, -1):
                pl.when(line.at + j < half)(lambda: send(line.at + j))
                pl.when(line.at >= j)(lambda: send(line.at - j))
            send(line.at)
        for at in range(half):
            produce(at * 2 + line.low)

    def own_and_pair(at, c):
        to_pair(at, c).wait_recv()
        return block(at * 2 + line.low, c)[...].astype(F32) + pair_buf[at, pl.ds(c * rows, rows)].astype(F32)

    def middle(c):
        for j in range(half - 1, 0, -1):
            @pl.when(line.at + j < half)
            def _():
                stage[j, pl.ds(c * rows, rows)] = own_and_pair(line.at + j, c).astype(BF16)

                @pl.when(line.has_left)
                def _():
                    arrived = remote(piece(stage, j, c), piece(right_buf, j, c), right_send.at[j, c], right_recv.at[j, c], line.right)
                    arrived.wait_recv()
                    total = stage[j, pl.ds(c * rows, rows)].astype(F32) + right_buf[j, pl.ds(c * rows, rows)].astype(F32)
                    stage[j, pl.ds(c * rows, rows)] = total.astype(BF16)

                to_right(j, c).start()

            @pl.when(line.at >= j)
            def _():
                stage[half + j, pl.ds(c * rows, rows)] = own_and_pair(line.at - j, c).astype(BF16)

                @pl.when(line.has_right)
                def _():
                    arrived = remote(piece(stage, half + j, c), piece(left_buf, j, c), left_send.at[j, c], left_recv.at[j, c], line.left)
                    arrived.wait_recv()
                    total = stage[half + j, pl.ds(c * rows, rows)].astype(F32) + left_buf[j, pl.ds(c * rows, rows)].astype(F32)
                    stage[half + j, pl.ds(c * rows, rows)] = total.astype(BF16)

                to_left(j, c).start()

    def finish(c, out_ref):
        here = pl.ds(c * rows, rows)
        out_ref[here, :] = own_and_pair(line.at, c)

        @pl.when(line.has_left)
        def _():
            remote(piece(stage, 0, c), piece(right_buf, 0, c), right_send.at[0, c], right_recv.at[0, c], line.right).wait_recv()
            out_ref[here, :] += right_buf[0, here].astype(F32)

        @pl.when(line.has_right)
        def _():
            remote(piece(stage, 0, c), piece(left_buf, 0, c), left_send.at[0, c], left_recv.at[0, c], line.left).wait_recv()
            out_ref[here, :] += left_buf[0, here].astype(F32)

    def end():
        for c in range(chunks):
            for at in range(half):
                to_pair(at, c).wait_send()
            for j in range(1, half):
                pl.when(line.at + j < half)(lambda: to_right(j, c).wait_send())
                pl.when(line.at >= j)(lambda: to_left(j, c).wait_send())

    return begin, middle, finish, end


def scatter_scratch(count, chunks, rows, width):
    half = count // 2
    return (
        [pltpu.VMEM((half, rows, width), BF16)] * 3
        + [pltpu.VMEM((2 * half, rows, width), BF16)]
        + [pltpu.SemaphoreType.DMA((half, chunks))] * 6
    )


def boundary_kernel(
    count, chunks, layer, gated_ref, weights_ref, hidden_ref, new_ref, full_ref, pair_buf, right_buf, left_buf, stage,
    part_ref, weight_ref, weight_sem, *sems,
):
    line = Line(count)
    rows, width = hidden_ref.shape
    mine = pl.ds(pl.multiple_of(line.me * width, width), width)
    fetch = pltpu.make_async_copy(weights_ref.at[layer], weight_ref, weight_sem)
    fetch.start()
    line.greet()
    fetch.wait()

    def produce(owner):
        columns = pl.ds(pl.multiple_of(owner * width, width), width)
        block = jnp.dot(gated_ref[...], weight_ref[:, columns], preferred_element_type=F32)
        part_ref[:, columns] = block.astype(BF16)

    begin, middle, finish, end = scatter_steps(
        line, part_ref, pair_buf, right_buf, left_buf, stage, width, chunks, sems[:6]
    )
    gather_begin, gather_middle, gather_end = gather_steps(line, full_ref, width, chunks, sems[6:])
    begin(produce)
    for c in range(chunks):
        here = pl.ds(c * (rows // chunks), rows // chunks)
        middle(c)
        finish(c, new_ref)
        new_ref[here, :] += hidden_ref[here, :]
        full_ref[here, mine] = new_ref[here, :].astype(BF16)
        gather_begin(c)
    gather_middle()
    gather_end()
    end()


def forward_boundary(gated, weights, layer, hidden):
    count = lax.axis_size("chan")
    rows, width = hidden.shape
    chunks = 2
    return pl.pallas_call(
        functools.partial(boundary_kernel, count, chunks, layer),
        in_specs=[whole(1)[0], pl.BlockSpec(memory_space=pl.ANY), whole(1)[0]],
        out_specs=whole(2),
        out_shape=[jax.ShapeDtypeStruct((rows, width), F32), jax.ShapeDtypeStruct((rows, count * width), BF16)],
        scratch_shapes=scatter_scratch(count, chunks, rows, width)[:4]
        + [
            pltpu.VMEM((rows, count * width), BF16),
            pltpu.VMEM(weights.shape[1:], BF16),
            pltpu.SemaphoreType.DMA,
        ]
        + scatter_scratch(count, chunks, rows, width)[4:]
        + gather_sems(count, chunks),
        compiler_params=remote_params(1),
        cost_estimate=estimate(50),
        name="forward_boundary",
    )(gated, weights, hidden)


def back_kernel(
    count, chunks, gathers, gmixed_ref, weights_ref, grad_ref, hidden_ref, inverse_ref, gain_ref, inner_ref, new_ref, ggain_ref, *more
):
    full_ref, more = (more[0], more[1:]) if gathers else (None, more)
    pair_buf, right_buf, left_buf, stage, inner_buf, column_ref, inner_send, inner_recv = more[:8]
    part_ref, weight_ref, weight_sem = more[8:11]
    sems = more[11:]
    fetch = pltpu.make_async_copy(weights_ref, weight_ref, weight_sem)
    fetch.start()
    line = Line(count)
    rows, width = grad_ref.shape
    model = width * count
    mine = pl.ds(pl.multiple_of(line.me * width, width), width)
    others = [lax.rem(line.me + k, count) for k in range(1, count)]
    barrier = pltpu.get_barrier_semaphore()
    for other in others:
        pl.semaphore_signal(barrier, inc=1, device_id={"chan": other}, device_id_type=MESH)
    pl.semaphore_wait(barrier, count - 1)
    begin, middle, finish, end = scatter_steps(
        line, part_ref, pair_buf, right_buf, left_buf, stage, width, chunks, sems[:6]
    )
    if gathers:
        gather_begin, gather_middle, gather_end = gather_steps(line, full_ref, width, chunks, sems[6:])
    sums = [
        remote(inner_ref, inner_buf.at[k], inner_send.at[k], inner_recv.at[k], others[k]) for k in range(count - 1)
    ]
    for copy in sums:
        copy.start()
    fetch.wait()

    def produce(owner):
        features = pl.ds(pl.multiple_of(owner * width, width), width)
        part_ref[:, features] = dot(gmixed_ref[...], weight_ref[features, :], ((1,), (1,))).astype(BF16)

    begin(produce)
    eye = lax.broadcasted_iota(jnp.int32, (LANES, LANES), 0) == lax.broadcasted_iota(jnp.int32, (LANES, LANES), 1)
    ggain_ref[...] = jnp.zeros_like(ggain_ref)
    for c in range(chunks):
        here = pl.ds(c * (rows // chunks), rows // chunks)
        middle(c)
        if c == 0:
            inner = inner_ref[...]
            for k in range(count - 1):
                sums[k].wait_recv()
                inner = inner + inner_buf[k]
            for b in range(rows // LANES):
                column_ref[pl.ds(b * LANES, LANES), :] = jnp.sum(
                    jnp.where(eye, jnp.broadcast_to(inner[b : b + 1, :], (LANES, LANES)), 0.0), axis=1, keepdims=True
                )
        finish(c, new_ref)
        gnormed = new_ref[here, :]
        inverse = inverse_ref[here, :]
        hidden = hidden_ref[here, :]
        factor = inverse * inverse * column_ref[here, :] * (1.0 / model)
        ggain_ref[0:1, :] += jnp.sum(gnormed * hidden * inverse, axis=0, keepdims=True)
        new = grad_ref[here, :] + inverse * (gain_ref[...] * gnormed) - hidden * factor
        new_ref[here, :] = new
        if gathers:
            full_ref[here, mine] = new.astype(BF16)
            gather_begin(c)
    if gathers:
        gather_middle()
        gather_end()
    end()
    for copy in sums:
        copy.wait_send()


def backward_boundary(gmixed, weights, grad, hidden, inverse, gain, inner, gathers):
    count = lax.axis_size("chan")
    rows, width = hidden.shape
    chunks = 2
    out_shape = [jax.ShapeDtypeStruct((rows, width), F32), jax.ShapeDtypeStruct((8, width), F32)]
    scratch = scatter_scratch(count, chunks, rows, width)
    scratch += [
        pltpu.VMEM((count - 1, rows // LANES, LANES), F32),
        pltpu.VMEM((rows, 1), F32),
        pltpu.SemaphoreType.DMA((count - 1,)),
        pltpu.SemaphoreType.DMA((count - 1,)),
    ]
    product = [
        pltpu.VMEM((rows, count * width), BF16),
        pltpu.VMEM(weights.shape, BF16),
        pltpu.SemaphoreType.DMA,
    ]
    order = scratch[:4] + scratch[10:] + product + scratch[4:10]
    if gathers:
        out_shape.append(jax.ShapeDtypeStruct((rows, count * width), BF16))
        order += gather_sems(count, chunks)
    return pl.pallas_call(
        functools.partial(back_kernel, count, chunks, gathers),
        in_specs=[whole(1)[0], pl.BlockSpec(memory_space=pl.ANY)] + whole(5),
        out_specs=whole(len(out_shape)),
        out_shape=out_shape,
        scratch_shapes=order,
        compiler_params=remote_params(2 if gathers else 3),
        cost_estimate=estimate(50 if gathers else 27),
        name="backward_boundary" if gathers else "backward_last",
    )(gmixed, weights, grad, hidden, inverse, gain, inner.reshape(rows // LANES, LANES))


def sum_kernel(count, part_ref, out_ref, give, arrived, total_ref, result, send1, recv1, send2, recv2):
    me = lax.axis_index("chan")
    rows, width = part_ref.shape
    own, extra = rows // count, width - LANES
    sides = LANES // extra
    block = rows // sides
    more = block // count
    others = [lax.rem(me + k, count) for k in range(1, count)]
    barrier = pltpu.get_barrier_semaphore()
    for other in others:
        pl.semaphore_signal(barrier, inc=1, device_id={"chan": other}, device_id_type=MESH)

    def place_at(k):
        row = lax.broadcasted_iota(jnp.int32, (extra, LANES), 0)
        col = lax.broadcasted_iota(jnp.int32, (extra, LANES), 1)
        return jnp.where(col == row + k * extra, 1.0, 0.0).astype(BF16)

    side = jnp.zeros((block, LANES), F32)
    for k in range(sides):
        side = side + jnp.dot(part_ref[k * block : (k + 1) * block, LANES:], place_at(k), preferred_element_type=F32)
    side = side.astype(BF16)
    for o in range(count):
        give[o, :own, :] = part_ref[o * own : (o + 1) * own, :LANES]
        give[o, own:, :] = side[o * more : (o + 1) * more, :]
    pl.semaphore_wait(barrier, count - 1)
    first, second = [], []
    for k, other in enumerate(others):
        first.append(remote(give.at[other], arrived.at[k], send1.at[k], recv1.at[k], other))
        first[k].start()
    acc = give[me].astype(F32)
    for k in range(count - 1):
        first[k].wait_recv()
        acc = acc + arrived[k].astype(F32)
    total_ref[...] = acc.astype(BF16)
    for k, other in enumerate(others):
        second.append(remote(total_ref, result.at[me], send2.at[k], recv2.at[k], other))
        second[k].start()
    result[me] = total_ref[...]
    for copy in second:
        copy.wait()
    sums = [result[o] for o in range(count)]
    for o in range(count):
        out_ref[o * own : (o + 1) * own, :LANES] = sums[o][:own, :]
    side = jnp.concatenate([value[own:, :].astype(F32) for value in sums], axis=0).astype(BF16)
    for k in range(sides):
        columns = dot(side, place_at(k), ((1,), (1,)))
        out_ref[k * block : (k + 1) * block, LANES:] = columns.astype(BF16)
    for copy in first:
        copy.wait_send()


def sum_chan(part):
    count = lax.axis_size("chan")
    rows, width = part.shape
    piece = rows // count + rows // (LANES // (width - LANES)) // count
    return pl.pallas_call(
        functools.partial(sum_kernel, count),
        in_specs=whole(1),
        out_specs=whole(1)[0],
        out_shape=jax.ShapeDtypeStruct((rows, width), BF16),
        scratch_shapes=[
            pltpu.VMEM((count, piece, LANES), BF16),
            pltpu.VMEM((count - 1, piece, LANES), BF16),
            pltpu.VMEM((piece, LANES), BF16),
            pltpu.VMEM((count, piece, LANES), BF16),
        ]
        + [pltpu.SemaphoreType.DMA((count - 1,))] * 4,
        compiler_params=remote_params(4),
        cost_estimate=estimate(14),
        name="sum_chan",
    )(part)


def exchanged(value, bit):
    return lax.ppermute(value, "seq", [(i, i ^ bit) for i in range(lax.axis_size("seq"))])


class Summed:
    def __init__(self, value, halves):
        self.halves = halves
        self.bit = 1
        self.keep = value
        give = value
        if halves:
            half = value.shape[0] // 2
            core = lax.axis_index("seq") % 2
            self.keep = lax.dynamic_slice_in_dim(value, core * half, half, 0)
            give = lax.dynamic_slice_in_dim(value, (1 - core) * half, half, 0)
        self.wire = exchanged(give, 1)

    def step(self):
        total = self.keep.astype(F32) + self.wire.astype(F32)
        self.bit *= 2
        if self.bit < lax.axis_size("seq"):
            self.keep = total.astype(BF16)
            self.wire = exchanged(self.keep, self.bit)
        elif self.halves:
            self.keep = total.astype(BF16)
            self.wire = exchanged(self.keep, 1)
        else:
            self.keep = total

    def across(self):
        while self.bit * 2 < lax.axis_size("seq"):
            self.step()

    def last(self):
        while self.bit * 2 < lax.axis_size("seq"):
            self.step()
        return self.keep, self.wire

    def total(self):
        while self.bit < lax.axis_size("seq"):
            self.step()
        return (self.keep, self.wire) if self.halves else self.keep


def after(value, *sums):
    value, wires = lax.optimization_barrier((value, [one.wire for one in sums]))
    for one, wire in zip(sums, wires):
        one.wire = wire
    return value


def place_pairs_kernel(core_ref, *refs):
    *ins, out_ref = refs[-5:]
    own = pl.program_id(0) == 0
    for j in range(2):
        out_ref[0, :, j, :] = jnp.where(own, ins[2 * j][...].astype(F32), ins[2 * j + 1][...].astype(F32))


def place_rows_kernel(core_ref, *refs):
    mine, other, out_ref = refs[-3:]
    own = pl.program_id(0) == 0
    out_ref[0] = jnp.where(own, mine[...].astype(F32), other[...].astype(F32))


def place(kernel, parts, base, layer, layers, block, middle):
    half, width = parts[0].shape
    core = (lax.axis_index("seq") % 2).reshape(1)
    steps = half // block

    def where(kept):
        if kept:
            return lambda k, b, core: (jnp.where(k == 0, b, steps - 1), 0)
        return lambda k, b, core: (jnp.where(k == 1, b, 0), 0)

    def out(k, b, core):
        return (layer, (core[0] + k - 2 * core[0] * k) * steps + b) + (0,) * (1 + len(middle))

    ins = [pl.BlockSpec((block, width), where(p % 2 == 0)) for p in range(len(parts))]
    shape = (layers, 2 * half) + middle + (width,)
    args = list(parts)
    aliases = {}
    if base is not None:
        ins.insert(0, pl.BlockSpec(memory_space=pl.ANY))
        args.insert(0, base)
        aliases = {1: 0}
    return pl.pallas_call(
        kernel,
        grid_spec=pltpu.PrefetchScalarGridSpec(
            num_scalar_prefetch=1,
            grid=(2, steps),
            in_specs=ins,
            out_specs=pl.BlockSpec((1, block) + middle + (width,), out),
        ),
        out_shape=jax.ShapeDtypeStruct(shape, F32),
        input_output_aliases=aliases,
        compiler_params=params("arbitrary", "arbitrary"),
        cost_estimate=estimate(5),
        name="place",
    )(core, *args)


def dot(a, b, dims):
    return lax.dot_general(a, b, (dims, ((), ())), preferred_element_type=F32)


def rows_of_packed(rank_columns, rank, states, seqs, taps):
    names = [("xproj", rank_columns), ("dtproj", rank), ("decay", states), ("init", seqs * states)]
    names += [("taps", taps), ("shift", 1), ("bias", 1), ("skip", 1), ("conv", (taps - 1) * seqs)]
    places, row = {}, 0
    for name, size in names:
        places[name] = (row, row + size)
        row += size
    return places, row + (-row) % 16


def mid_kernel(
    gproj_ref, xproj_ref, gact_ref, inner_ref, head_ref, low_ref, taps_ref, shift_ref, rank_ref, gpre_ref, ggate_ref,
    gdecay_ref, gskip_ref, ginit_ref,
    gmixed_ref, packed_ref,
    dotted_ref, pad_ref, gconv_ref, tail_ref, give_ref, got_ref, send_sem, recv_sem,
):
    seqs, length = gact_ref.shape[:2]
    tokens = length * G
    count = gmixed_ref.shape[1] // (2 * LANES)
    taps = taps_ref.shape[0]
    over = taps - 1
    j = pl.program_id(0)
    place, peers = lax.axis_index("seq"), lax.axis_size("seq")
    states = gdecay_ref.shape[1]
    places, _ = rows_of_packed(gproj_ref.shape[1], rank_ref.shape[1], states, seqs, taps)

    def to_previous(t):
        return pltpu.make_async_remote_copy(
            src_ref=give_ref.at[t], dst_ref=got_ref.at[t], send_sem=send_sem.at[t], recv_sem=recv_sem.at[t],
            device_id={"seq": jnp.maximum(place - 1, 0)}, device_id_type=MESH,
        )

    @pl.when(j == 0)
    def _():
        barrier = pltpu.get_barrier_semaphore()

        @pl.when(place < peers - 1)
        def _():
            pl.semaphore_signal(barrier, inc=1, device_id={"seq": place + 1}, device_id_type=MESH)

        pl.when(place > 0)(lambda: pl.semaphore_wait(barrier, 1))

    columns = pl.ds(pl.multiple_of(j * LANES, LANES), LANES)
    gate_columns = pl.ds(pl.multiple_of((count + j) * LANES, LANES), LANES)
    gmixed_ref[:, gate_columns] = ggate_ref[...]
    dotted_ref[...] = jnp.dot(gproj_ref[...], xproj_ref[...], preferred_element_type=F32)
    zero = jnp.zeros((G, LANES), F32)
    weights = [jnp.broadcast_to(taps_ref[k : k + 1, :], (G, LANES)) for k in range(taps)]
    shift = jnp.broadcast_to(shift_ref[...], (G, LANES))
    sums = (zero,) * (taps + 1)
    early = [[None] * seqs for _ in range(over)]
    for s in range(seqs):
        for k in range(over):
            pad_ref[k] = head_ref[s, k]

        def fill(l, carry):
            pad_ref[l + over] = inner_ref[s, l]
            return carry

        lax.fori_loop(0, length, fill, 0, unroll=math.gcd(length, 8))

        def one(l, sums):
            parts = [pad_ref[l + k] for k in range(taps)]
            pre = shift
            for k in range(taps):
                pre = pre + weights[k] * parts[k]
            sig = 1.0 / (1.0 + jnp.exp(-pre))
            here = dotted_ref[pl.ds(pl.multiple_of(s * tokens + l * G, G), G), :]
            gconv = (gact_ref[s, l] + here) * (sig + pre * sig * (1.0 - sig))
            gconv_ref[l] = gconv
            return tuple(sums[k] + gconv * parts[k] for k in range(taps)) + (sums[taps] + gconv,)

        sums = lax.fori_loop(0, length, one, sums, unroll=math.gcd(length, 8))
        for k in range(over):
            gconv_ref[length + k] = shifted(gconv_ref[k], -1, 0.0)
            total = weights[0] * gconv_ref[k]
            for i in range(1, k + 1):
                total = total + weights[i] * gconv_ref[k - i]
            early[k][s] = total[0:1, :]
            give_ref[j, s, k : k + 1, :] = total[0:1, :]

        def inner_of(l):
            total = weights[0] * gconv_ref[l + over]
            for k in range(1, taps):
                total = total + weights[k] * gconv_ref[l + over - k]
            return total

        def pair(p, carry):
            both = jnp.concatenate([inner_of(2 * p), inner_of(2 * p + 1)], axis=0)
            gmixed_ref[pl.ds(pl.multiple_of(s * tokens + 2 * p * G, 2 * G), 2 * G), columns] = both.astype(BF16)
            return carry

        lax.fori_loop(0, length // 2 - 2, pair, 0, unroll=math.gcd(length // 2 - 2, 4))
        for q in range(4):
            tail_ref[j, s, q] = inner_of(length - 4 + q)
    pl.when(place > 0)(lambda: to_previous(j).start())

    def put(name, value):
        first, last = places[name]
        packed_ref[first:last, :] = value.astype(BF16)

    put("xproj", dot(gproj_ref[...], low_ref[...], ((0,), (0,))))
    put("dtproj", dot(rank_ref[...], gpre_ref[...], ((0,), (0,))))
    bias = jnp.dot(jnp.ones((16, seqs * tokens), BF16), gpre_ref[...], preferred_element_type=F32)[0:1, :]
    decay, skip = gdecay_ref[0], gskip_ref[0, 0:1, :]
    for s in range(1, seqs):
        decay = decay + gdecay_ref[s]
        skip = skip + gskip_ref[s, 0:1, :]
    put("decay", decay)
    first = place == 0
    for s in range(seqs):
        row = places["init"][0] + s * states
        packed_ref[row : row + states, :] = jnp.where(first, ginit_ref[s], 0.0).astype(BF16)
    rest = [jnp.sum(value, axis=0, keepdims=True) for value in sums]
    rest += [bias, skip]
    rest += [jnp.where(first, early[k][s], 0.0) for k in range(over) for s in range(seqs)]
    row = places["taps"][0]
    rest += [jnp.zeros((1, LANES), F32)] * (packed_ref.shape[0] - row - len(rest))
    packed_ref[row:, :] = jnp.concatenate(rest, axis=0).astype(BF16)

    @pl.when(j == count - 1)
    def _():
        last_row = lax.broadcasted_iota(jnp.int32, (G, LANES), 0) == G - 1
        inside = place < peers - 1
        for t in range(count):
            pl.when(place < peers - 1)(lambda: to_previous(t).wait_recv())
            for s in range(seqs):
                values = []
                for q in range(4):
                    value = tail_ref[t, s, q]
                    k = q - 4 + over
                    if k >= 0:
                        given = jnp.broadcast_to(got_ref[t, s, k : k + 1, :], (G, LANES))
                        value = value + jnp.where(jnp.logical_and(last_row, inside), given, 0.0)
                    values.append(value)
                for q in (0, 2):
                    row = s * tokens + (length - 4 + q) * G
                    both = jnp.concatenate(values[q : q + 2], axis=0)
                    gmixed_ref[row : row + 2 * G, t * LANES : (t + 1) * LANES] = both.astype(BF16)
            pl.when(place > 0)(lambda: to_previous(t).wait_send())


def mid_backward(
    gproj, xproj, gact, mixed, head, low, taps, shift, rank_part, gpre, ggate, gdecay, gskip, ginit
):
    seqs, length, _, chans = gact.shape
    rows = seqs * length * G
    count = chans // LANES
    states = gdecay.shape[1]
    over = taps.shape[0] - 1
    _, packed_rows = rows_of_packed(gproj.shape[1], rank_part.shape[1], states, seqs, taps.shape[0])
    token = pl.BlockSpec((seqs, length, G, LANES), lambda j: (0, 0, 0, j))
    row = pl.BlockSpec((rows, LANES), lambda j: (0, j))

    def column(height):
        return pl.BlockSpec((height, LANES), lambda j: (0, j))

    def stack(height):
        return pl.BlockSpec((seqs, height, LANES), lambda j: (0, 0, j))

    return pl.pallas_call(
        mid_kernel,
        grid=(count,),
        in_specs=[
            pl.BlockSpec(gproj.shape, lambda j: (0, 0)),
            column(xproj.shape[0]),
            token,
            token,
            pl.BlockSpec((seqs, over, G, LANES), lambda j: (0, 0, 0, j)),
            row,
            column(over + 1),
            column(1),
            pl.BlockSpec(rank_part.shape, lambda j: (0, 0)),
            row,
            row,
            stack(states),
            stack(8),
            stack(states),
        ],
        out_specs=[pl.BlockSpec((rows, 2 * chans), lambda j: (0, 0)), column(packed_rows)],
        out_shape=[
            jax.ShapeDtypeStruct((rows, 2 * chans), BF16),
            jax.ShapeDtypeStruct((packed_rows, chans), BF16),
        ],
        scratch_shapes=[
            pltpu.VMEM((rows, LANES), F32),
            pltpu.VMEM((length + over, G, LANES), F32),
            pltpu.VMEM((length + over, G, LANES), F32),
            pltpu.VMEM((count, seqs, 4, G, LANES), F32),
            pltpu.VMEM((count, seqs, 8, LANES), F32),
            pltpu.VMEM((count, seqs, 8, LANES), F32),
            pltpu.SemaphoreType.DMA((count,)),
            pltpu.SemaphoreType.DMA((count,)),
        ],
        compiler_params=pltpu.CompilerParams(
            dimension_semantics=("arbitrary",), collective_id=5, has_side_effects=True, vmem_limit_bytes=VMEM_LIMIT
        ),
        cost_estimate=estimate(8),
        name="mid_backward",
    )(gproj, xproj, gact, mixed, head, low, taps, shift, rank_part, gpre, ggate, gdecay, gskip, ginit)


def unpack_kernel(layers, places, seqs, *refs):
    smalls, gains, outs = refs[: 2 * layers], refs[2 * layers : 4 * layers], refs[4 * layers :]
    gain, taps, shift, xproj, dtproj, bias, decay, skip, conv, init = outs
    for i in range(layers):
        def rows(name):
            first, last = places[name]
            return smalls[2 * i][first:last, :].astype(F32) + smalls[2 * i + 1][first:last, :].astype(F32)

        gain[i : i + 1, :] = gains[2 * i][0:1, :].astype(F32) + gains[2 * i + 1][0:1, :].astype(F32)
        xproj[i], dtproj[i], decay[i] = rows("xproj"), rows("dtproj"), rows("decay")
        init[i] = rows("init")
        low, high = places["taps"][0], smalls[0].shape[0]
        rest = smalls[2 * i][low:high, :].astype(F32) + smalls[2 * i + 1][low:high, :].astype(F32)

        def of(name):
            first, last = places[name]
            return rest[first - low : last - low, :]

        taps[i] = of("taps")
        shift[i : i + 1, :], bias[i : i + 1, :], skip[i : i + 1, :] = of("shift"), of("bias"), of("skip")
        for k in range(conv.shape[1]):
            conv[i, k] = of("conv")[k * seqs : (k + 1) * seqs, :]


def unpack(smalls, gains, places, seqs, width):
    layers = len(smalls)
    chans = smalls[0][0].shape[1]

    def size(name):
        return places[name][1] - places[name][0]

    shapes = [
        (layers, width), (layers, size("taps"), chans), (layers, chans), (layers, size("xproj"), chans),
        (layers, size("dtproj"), chans), (layers, chans), (layers, size("decay"), chans), (layers, chans),
        (layers, size("conv") // seqs, seqs, chans), (layers, size("init"), chans),
    ]
    args = [value for pair in smalls for value in pair] + [value for pair in gains for value in pair]
    return pl.pallas_call(
        functools.partial(unpack_kernel, layers, places, seqs),
        in_specs=whole(len(args)),
        out_specs=whole(len(shapes)),
        out_shape=[jax.ShapeDtypeStruct(shape, F32) for shape in shapes],
        compiler_params=params(),
        cost_estimate=estimate(3),
        name="unpack",
    )(*args)


def passed_along(value, axis, by):
    peers = lax.axis_size(axis)
    pairs = [(i, i + by) for i in range(peers) if 0 <= i + by < peers]
    return lax.ppermute(value, axis, pairs)


def to_segments(value):
    seqs, tokens, width = value.shape
    return value.reshape(seqs, G, tokens // G, width).transpose(0, 2, 1, 3)


def from_segments(value):
    seqs, length, _, width = value.shape
    return value.transpose(0, 2, 1, 3).reshape(seqs, length * G, width)


def local(
    hidden_in,
    norm_gain,
    in_weight,
    conv_weight,
    conv_bias,
    xproj_weight,
    dtproj_weight,
    dt_bias,
    decay_log,
    skip_gain,
    out_weight,
    conv_state,
    scan_state,
    out_cotangent,
):
    layers = in_weight.shape[0]
    rank = dtproj_weight.shape[1]
    states = decay_log.shape[1]
    seqs, tokens, _ = hidden_in.shape
    length = tokens // G
    rows = seqs * tokens
    chans = in_weight.shape[3]
    model = hidden_in.shape[2] * lax.axis_size("chan")
    taps = conv_weight.shape[1]
    is_first = lax.axis_index("seq") == 0

    first = to_segments(hidden_in).reshape(rows, -1)
    hidden = first.astype(F32)
    full, gains, flats = gather_first(first, norm_gain, in_weight)
    grad = to_segments(out_cotangent).reshape(rows, -1)
    grad_rows = lax.all_gather(grad, "chan", axis=1, tiled=True)
    grad = grad.astype(F32)
    saved = []
    for i in range(layers):
        wide = full[:rows].astype(F32)
        inverse = lax.rsqrt(jnp.sum(wide * wide, axis=1, keepdims=True) / model + EPS)
        normed = (wide * inverse * gains[i]).astype(BF16)
        flat_in = flats[i]
        mixed = dot(normed, flat_in, ((1,), (0,)))
        inner = mixed[:, :chans].reshape(seqs, length, G, chans)
        gate = mixed[:, chans:].reshape(seqs, length, G, chans)
        tail = inner[:, length - taps + 1 :]
        received = passed_along(tail[:, :, G - 1], "seq", 1)
        before = jnp.where(is_first, conv_state[i], received)
        head = jnp.concatenate([before[:, :, None], tail[:, :, : G - 1]], axis=2)
        padded = jnp.concatenate([head, inner], axis=1)
        pre = conv_bias[i] + sum(conv_weight[i, k] * padded[:, k : k + length] for k in range(taps))
        act = jax.nn.silu(pre)
        act_low = act.astype(BF16).reshape(rows, chans)
        projected = sum_chan(dot(act_low, xproj_weight[i], ((1,), (0,))).astype(BF16))
        rank_part = projected[:, :rank]
        maps = projected[:, rank:].reshape(seqs, tokens, 2 * states)
        delta = dot(rank_part, dtproj_weight[i], ((1,), (0,))) + dt_bias[i]
        delta = delta.reshape(seqs, length, G, chans)
        step = jax.nn.softplus(delta)
        y, gated, start, span, packs = scan_forward(
            act, step, gate, maps, decay_log[i], scan_state[i], skip_gain[i : i + 1]
        )
        gated = gated.reshape(rows, chans)
        saved.append(
            (hidden, inverse, normed, flat_in, mixed, gate, head, act, act_low, rank_part, maps, delta, step,
             span, packs, y, gated, start)
        )
        if i + 1 < layers:
            hidden, full = forward_boundary(gated, out_weight, i, hidden)
        else:
            branch = dot(gated, out_weight[i], ((1,), (0,))).astype(BF16)
            branch_sum = lax.psum_scatter(branch, "chan", scatter_dimension=1, tiled=True)

    def finish(i, sums):
        nonlocal in_grads, out_grads
        in_grads = place(
            place_pairs_kernel, [*sums["inner"].total(), *sums["gate"].total()], in_grads, i, layers, model // 4, (2,)
        )
        out_grads = place(place_rows_kernel, list(sums["out"].total()), out_grads, i, layers, chans // 2, ())

    smalls = [None] * layers
    in_grads = out_grads = None
    before_sums = None
    for i in reversed(range(layers)):
        (hidden_i, inverse, normed, flat_in, mixed, gate, head, act, act_low, rank_part, maps, delta, step,
         span, packs, y, gated, start) = saved[i]
        sums = {}
        sums["out"] = Summed(dot(gated, grad_rows, ((0,), (0,))).astype(BF16), True)
        grad_gated = dot(grad_rows, out_weight[i], ((1,), (1,)))
        grad_gated = grad_gated.reshape(seqs, length, G, chans)
        last = i == layers - 1
        if last:
            scanned = scan_adjoint_and_backward(
                act, step, delta, gate, y, grad_gated, maps, decay_log[i], start, span, packs, skip_gain[i : i + 1],
                dtproj_weight[i],
            )
        else:
            suffix, back_packs = scan_adjoint(step, gate, grad_gated, maps, decay_log[i], span)
            back_packs = after(back_packs, sums["out"])
            sums["out"].across()
            scanned = scan_backward(
                act, step, delta, gate, y, grad_gated, maps, decay_log[i], start, suffix, span, back_packs, packs,
                skip_gain[i : i + 1], dtproj_weight[i],
            )
        gact, gpre, ggate, proj_part, gdecay, gskip, ginit = after(scanned, sums["out"])
        sums["out"].across() if last else sums["out"].step()
        gpre = gpre.reshape(rows, chans)
        ggate = ggate.reshape(rows, chans)
        proj_part = proj_part.reshape(rows, -1)
        sums["gate"] = Summed(dot(normed, ggate, ((0,), (0,))).astype(BF16), True)
        proj_part = after(proj_part, sums["gate"])
        sums["gate"].across()
        grad_proj = sum_chan(proj_part)
        if not last:
            grad_proj = after(grad_proj, sums["out"])
        gmixed, packed = mid_backward(
            grad_proj, xproj_weight[i].T, gact, mixed.reshape(seqs, length, G, -1), head, act_low, conv_weight[i],
            conv_bias[i : i + 1], rank_part, gpre, ggate, gdecay, gskip, ginit,
        )
        gmixed, packed = after((gmixed, packed), sums["out" if last else "gate"])
        if last:
            gmixed, branch_sum = lax.optimization_barrier((gmixed, branch_sum))
            hidden = hidden + branch_sum.astype(F32)
        sums["out" if last else "gate"].step()
        sums["small"] = Summed(packed, False)
        sums["inner"] = Summed(dot(normed, gmixed[:, :chans], ((0,), (0,))).astype(BF16), True)
        inner_sums = jnp.sum(gmixed.astype(F32) * mixed, axis=1)
        gmixed = after(gmixed, sums["inner"], sums["small"])
        sums["inner"].across()
        sums["small"].across()
        outs = backward_boundary(
            gmixed, flat_in, grad, hidden_i, inverse, norm_gain[i : i + 1], inner_sums, i > 0
        )
        if last:
            outs = after(outs, sums["gate"], sums["inner"], sums["small"])
            sums["gate"].step()
        else:
            outs = after(outs, sums["inner"], sums["small"])
        grad = outs[0]
        if i > 0:
            grad_rows = outs[2]
        sums["inner"].step()
        sums["gain"] = Summed(outs[1].astype(BF16), False)
        smalls[i] = sums
        if before_sums is not None:
            finish(i + 1, before_sums)
        before_sums = sums
    finish(0, before_sums)
    places, _ = rows_of_packed(xproj_weight.shape[2], rank, states, seqs, taps)
    gain, taps_grad, shift, xproj, dtproj, bias, decay, skip, conv, init = unpack(
        [one["small"].last() for one in smalls], [one["gain"].last() for one in smalls], places, seqs,
        norm_gain.shape[1],
    )

    def back_out(value):
        return from_segments(value.reshape(seqs, length, G, -1))

    return (
        back_out(hidden),
        back_out(grad),
        gain,
        in_grads,
        taps_grad,
        shift,
        xproj.transpose(0, 2, 1),
        dtproj,
        bias,
        decay,
        skip,
        out_grads,
        conv.transpose(0, 2, 1, 3),
        init.reshape(scan_state.shape),
    )


def solution(mesh):
    return jax.shard_map(
        local,
        mesh=mesh,
        in_specs=(
            P(None, "seq", "chan"),
            P(None, "chan"),
            P(None, None, None, "chan"),
            P(None, None, "chan"),
            P(None, "chan"),
            P(None, "chan", None),
            P(None, None, "chan"),
            P(None, "chan"),
            P(None, None, "chan"),
            P(None, "chan"),
            P(None, "chan", None),
            P(None, None, None, "chan"),
            P(None, None, None, "chan"),
            P(None, "seq", "chan"),
        ),
        out_specs=(
            P(None, "seq", "chan"),
            P(None, "seq", "chan"),
            P(None, "chan"),
            P(None, None, None, "chan"),
            P(None, None, "chan"),
            P(None, "chan"),
            P(None, "chan", None),
            P(None, None, "chan"),
            P(None, "chan"),
            P(None, None, "chan"),
            P(None, "chan"),
            P(None, "chan", None),
            P(None, None, None, "chan"),
            P(None, None, None, "chan"),
        ),
        check_vma=False,
    )
```
